32 devices in a mesh: lon: 8 (over z, y), lat: 4 (over x, core).
Axes of the slice: x: 2, y: 2, z: 4, core: 2. Of those that a mesh axis runs over, the one named last changes fastest.
Arguments:
- ocean_state: float32 [4, 8, 64, 1024], P(None, None, 'lat', 'lon'), may hold values from -5 to 5
- thickness: float32 [8, 64, 1024], P(None, 'lat', 'lon'), may hold values from 0.5 to 2
- wet_mask: int32 [8, 64, 1024], P(None, 'lat', 'lon'), may hold values 0 or 1
- mode_counts: int32 [64], P('lat'), may hold values from 1 to 64, as said below
- row_flags: int32 [64], P('lat'), may hold values from 0 to 1, as said below
Outputs:
- ocean_next: float32 [4, 8, 64, 1024], P(None, None, 'lat', 'lon')
The draws below stay inside these ranges and needn't reach their ends.
Inputs may be any that keep to these rules, and one draw needn't show every extreme that they name: `mode_counts`: mode counts lie in the range; row 0 keeps 64. `row_flags`: only rows among the first 16 or the last 16 are flagged; the first and the last row always are.
All inputs are finite; a program needn't handle non-finite values. No bound on the sum of `wet_mask` on one device may be relied on, other than what follows from the above.
Results may differ from the reference program's by a relative error of at most 0.0003.
Values sent between devices are 32-bit elements; how exact they have to be, the bound alone decides.
No kernel may reach another device: no remote copies, remote signals or barrier semaphores. Data moves between devices by JAX's collectives and lax.ppermute only.
A program may use at most 64 MiB of HBM per device.

```python
import math
import jax
import jax.numpy as jnp
from jax import lax

LEV = 8
FBAND = 16
MAXM = 64
NLAT = 64
NLON = 1024


def draw_mode_counts(key, part):
    counts = jax.random.randint(key, (NLAT,), 1, MAXM + 1, dtype=jnp.int32)
    rows = jnp.arange(NLAT, dtype=jnp.int32)
    return jnp.where(rows == 0, MAXM, counts).astype(jnp.int32)


def draw_row_flags(key, part):
    rows = jnp.arange(NLAT, dtype=jnp.int32)
    coin = jax.random.randint(key, (NLAT,), 0, 4, dtype=jnp.int32) > 0
    near = (rows < FBAND) | (rows >= NLAT - FBAND)
    ends = (rows == 0) | (rows == NLAT - 1)
    return (near & (coin | ends)).astype(jnp.int32)


def with_ends(values, stream_key, smallest, high):
    longest = values.shape.index(max(values.shape))
    spots = []
    for shift in (0, 1):
        where = [jax.random.randint(jax.random.fold_in(stream_key, axis), (), 0, length) for axis, length in enumerate(values.shape)]
        where[longest] = (where[longest] + shift) % values.shape[longest]
        spots.append(tuple(where))
    return values.at[spots[0]].set(smallest).at[spots[1]].set(high)


def block_scale(own_key, extent, pieces, smallest, largest):
    loudness = 1.0
    for position, parts in pieces:
        heights = jax.random.uniform(jax.random.fold_in(jax.random.fold_in(own_key, 6), position), (parts,), jnp.float32, smallest / len(pieces), largest / len(pieces))
        loudness = loudness * jnp.repeat(jnp.exp(heights), extent[position] // parts).reshape((-1,) + (1,) * (len(extent) - 1 - position))
    return loudness


def scatter_about(key, shape, scale, limit, cuts=(), kind=jnp.bfloat16):
    loudness = block_scale(key, shape, cuts, -0.22, 0.18) if cuts else 1.0
    array = jax.random.normal(key, shape, jnp.float32) * scale * loudness
    return jnp.minimum(jnp.maximum(array, -limit), limit).astype(kind)


def setup_inputs(seed: int = 0) -> dict:
    streams_of = jax.random.split(jax.random.key(seed), 6)
    ocean_state = scatter_about(streams_of[0], (4, LEV, NLAT, NLON), 1.0, 5.0, ((2, 4), (3, 8)), jnp.float32)
    thickness = jnp.clip(jnp.exp(math.log(2.0) - 1.3862944 * jax.random.uniform(streams_of[1], (LEV, NLAT, NLON), jnp.float32) ** block_scale(streams_of[1], (LEV, NLAT, NLON), ((1, 4), (2, 8)), -0.2, 0.2)), 0.5, 2.0)
    wet_mask = with_ends((jax.random.randint(streams_of[2], (LEV, NLAT, NLON), 0, 5) < 4).astype(jnp.int32), jax.random.fold_in(streams_of[2], 1), 0, 1)
    mode_counts = draw_mode_counts(jax.random.fold_in(streams_of[5], 71), 0)
    row_flags = draw_row_flags(jax.random.fold_in(streams_of[5], 71), 0)
    return dict(ocean_state=ocean_state, thickness=thickness, wet_mask=wet_mask, mode_counts=mode_counts, row_flags=row_flags)


lat_edge = 1.3
diffusion = 0.05
vertical_mix = 0.5
time_step = 0.05


def advance(padded, u_pad, v_pad, static, centre, faces):
    thick = static[0]
    wet = static[1]
    inv_c = 1.0 / centre
    east_u = 0.5 * (u_pad[:, :, :-1] + u_pad[:, :, 1:])
    east_h = 0.5 * (thick[:, :, :-1] + thick[:, :, 1:]) * wet[:, :, :-1] * wet[:, :, 1:]
    flux_e = east_h[None] * (east_u[None] * 0.5 * (padded[..., :-1] + padded[..., 1:])
                             - diffusion * (padded[..., 1:] - padded[..., :-1]) * inv_c[:, None])
    zonal = (flux_e[..., 1:] - flux_e[..., :-1])[:, :, 1:-1, :] * inv_c[1:-1, None]
    north_v = 0.5 * (v_pad[:, :-1, :] + v_pad[:, 1:, :])
    north_h = 0.5 * (thick[:, :-1, :] + thick[:, 1:, :]) * wet[:, :-1, :] * wet[:, 1:, :] * faces[:, None]
    flux_n = north_h[None] * (north_v[None] * 0.5 * (padded[:, :, :-1] + padded[:, :, 1:])
                              - diffusion * (padded[:, :, 1:] - padded[:, :, :-1]))
    merid = (flux_n[:, :, 1:] - flux_n[:, :, :-1])[..., 1:-1] * inv_c[1:-1, None]
    inner = padded[:, :, 1:-1, 1:-1]
    wet_in = wet[:, 1:-1, 1:-1]
    thick_in = jnp.where(wet_in > 0, thick[:, 1:-1, 1:-1], 1.0)
    coupling = wet_in[:-1] * wet_in[1:] * vertical_mix / (0.5 * (thick_in[:-1] + thick_in[1:]))
    vmix = coupling[None] * (inner[:, 1:] - inner[:, :-1])
    empty = jnp.zeros_like(vmix[:, :1])
    vert = jnp.concatenate([vmix, empty], axis=1) - jnp.concatenate([empty, vmix], axis=1)
    return inner + wet_in[None] * time_step * (vert - zonal - merid) / thick_in[None]


def mode_basis(index, length, modes):
    turns = (jnp.arange(modes, dtype=jnp.int32)[None, :] * index[:, None]) % length
    angle = turns.astype(jnp.float32) * (2.0 * math.pi / length)
    return jnp.concatenate([jnp.cos(angle), jnp.sin(angle)], axis=1)


def mode_weights(counts, modes, length):
    order = jnp.arange(modes).astype(jnp.float32)
    keep = (order[None, :] < counts[:, None]).astype(jnp.float32)
    scale = jnp.where(order == 0, 1.0, 2.0) / length
    weights = keep * scale[None, :]
    return jnp.concatenate([weights, weights], axis=1)


def widen(x):
    x = jnp.concatenate([x[..., -1:], x, x[..., :1]], axis=-1)
    return jnp.pad(x, [(0, 0)] * (x.ndim - 2) + [(1, 1), (0, 0)])


def reference(ocean_state, thickness, wet_mask, mode_counts, row_flags):
    wet = wet_mask.astype(jnp.float32)
    static = widen(jnp.stack([thickness, wet]))
    rows = jnp.arange(-1, NLAT + 1).astype(jnp.float32)
    centre = jnp.cos(lat_edge * (2.0 * (rows + 0.5) / NLAT - 1.0))
    faces = jnp.cos(lat_edge * (2.0 * (rows[:-1] + 1.0) / NLAT - 1.0))
    state = ocean_state
    for step in range(2):
        padded = widen(state)
        fresh = []
        for field in range(4):
            fresh.append(advance(padded[field:field + 1], padded[2], padded[3], static, centre, faces)[0])
        state = jnp.stack(fresh)
    basis = mode_basis(jnp.arange(NLON, dtype=jnp.int32), NLON, MAXM)
    bands = []
    for lower in (0, NLAT - FBAND):
        band = state[:, :, lower:lower + FBAND, :]
        flat = band.reshape(4 * LEV * FBAND, NLON)
        counts = mode_counts[lower:lower + FBAND].astype(jnp.float32)
        row_counts = jnp.broadcast_to(counts[None, None, :], (4, LEV, FBAND)).reshape(-1)
        totals = jnp.dot(flat, basis, precision=lax.Precision.HIGHEST, preferred_element_type=jnp.float32)
        smooth = jnp.dot(totals * mode_weights(row_counts, MAXM, NLON), basis.T,
                         precision=lax.Precision.HIGHEST, preferred_element_type=jnp.float32)
        smooth = smooth.reshape(4, LEV, FBAND, NLON)
        flags = row_flags[lower:lower + FBAND].astype(jnp.float32)
        wet_band = wet[:, lower:lower + FBAND, :]
        bands.append(band + flags[None, None, :, None] * wet_band[None] * (smooth - band))
    return jnp.concatenate([bands[0], state[:, :, FBAND:NLAT - FBAND, :], bands[1]], axis=2)
```

```python
import math

import jax
import jax.numpy as jnp
from jax import lax
from jax.sharding import PartitionSpec as P

FBAND = 16
MAXM = 64


lat_edge = 1.3
diffusion = 0.05
vertical_mix = 0.5
time_step = 0.05


def advance(padded, u_pad, v_pad, static, centre, faces):
    thick = static[0]
    wet = static[1]
    inv_c = 1.0 / centre
    east_u = 0.5 * (u_pad[:, :, :-1] + u_pad[:, :, 1:])
    east_h = 0.5 * (thick[:, :, :-1] + thick[:, :, 1:]) * wet[:, :, :-1] * wet[:, :, 1:]
    flux_e = east_h[None] * (
        east_u[None] * 0.5 * (padded[..., :-1] + padded[..., 1:])
        - diffusion * (padded[..., 1:] - padded[..., :-1]) * inv_c[:, None]
    )
    zonal = (flux_e[..., 1:] - flux_e[..., :-1])[:, :, 1:-1, :] * inv_c[1:-1, None]
    north_v = 0.5 * (v_pad[:, :-1, :] + v_pad[:, 1:, :])
    north_h = (
        0.5 * (thick[:, :-1, :] + thick[:, 1:, :]) * wet[:, :-1, :] * wet[:, 1:, :] * faces[:, None]
    )
    flux_n = north_h[None] * (
        north_v[None] * 0.5 * (padded[:, :, :-1] + padded[:, :, 1:])
        - diffusion * (padded[:, :, 1:] - padded[:, :, :-1])
    )
    merid = (flux_n[:, :, 1:] - flux_n[:, :, :-1])[..., 1:-1] * inv_c[1:-1, None]
    inner = padded[:, :, 1:-1, 1:-1]
    wet_in = wet[:, 1:-1, 1:-1]
    thick_in = jnp.where(wet_in > 0, thick[:, 1:-1, 1:-1], 1.0)
    coupling = wet_in[:-1] * wet_in[1:] * vertical_mix / (0.5 * (thick_in[:-1] + thick_in[1:]))
    vmix = coupling[None] * (inner[:, 1:] - inner[:, :-1])
    empty = jnp.zeros_like(vmix[:, :1])
    vert = jnp.concatenate([vmix, empty], axis=1) - jnp.concatenate([empty, vmix], axis=1)
    return inner + wet_in[None] * time_step * (vert - zonal - merid) / thick_in[None]


def mode_basis(index, length, modes):
    turns = jnp.arange(modes, dtype=jnp.int32)[None, :] * index[:, None] % length
    angle = turns.astype(jnp.float32) * (2.0 * math.pi / length)
    return jnp.concatenate([jnp.cos(angle), jnp.sin(angle)], axis=1)


def mode_weights(counts, modes, length):
    order = jnp.arange(modes).astype(jnp.float32)
    keep = (order[None, :] < counts[:, None]).astype(jnp.float32)
    scale = jnp.where(order == 0, 1.0, 2.0) / length
    weights = keep * scale[None, :]
    return jnp.concatenate([weights, weights], axis=1)


def swap_edges(before_src, after_src, axis, wrap):
    peers = lax.axis_size(axis)
    up = [(i, (i + 1) % peers) for i in range(peers if wrap else peers - 1)]
    down = [(j, i) for i, j in up]
    return lax.ppermute(before_src, axis, up), lax.ppermute(after_src, axis, down)


def widen(fields, width):
    rows, lanes = fields.shape[2:]
    below, above = swap_edges(
        fields[:, :, rows - width :], fields[:, :, :width], "lat", False
    )
    fields = jnp.concatenate([below, fields, above], axis=2)
    shape = fields.shape[:3] + (width,)
    west, east = swap_edges(
        fields[..., lanes - width :].reshape(-1, 128),
        fields[..., :width].reshape(-1, 128),
        "lon",
        True,
    )
    return jnp.concatenate([west.reshape(shape), fields, east.reshape(shape)], axis=3)


def shards(ocean_state, thickness, wet_mask, mode_counts, row_flags):
    wet = wet_mask.astype(jnp.float32)
    levels, rows, lanes = ocean_state.shape[1:]
    lon_peers = lax.axis_size("lon")
    nlat = rows * lax.axis_size("lat")
    nlon = lanes * lon_peers
    lat_pos = lax.axis_index("lat")
    lon_pos = lax.axis_index("lon")
    joined = widen(
        jnp.concatenate([ocean_state, thickness[None], wet[None]], axis=0), 2
    )
    place = (lat_pos * rows - 2 + jnp.arange(rows + 4, dtype=jnp.int32)).astype(
        jnp.float32
    )
    centre = jnp.cos(lat_edge * (2.0 * (place + 0.5) / nlat - 1.0))
    faces = jnp.cos(lat_edge * (2.0 * (place[:-1] + 1.0) / nlat - 1.0))
    fields = joined[:4]
    fixed = joined[4:]
    fields = advance(fields, fields[2], fields[3], fixed, centre, faces)
    state = advance(
        fields, fields[2], fields[3], fixed[:, :, 1:-1, 1:-1], centre[1:-1], faces[1:-1]
    )
    total = 4 * levels * rows
    part = total // lon_peers
    flat = state.reshape(total, lanes)
    index = lon_pos * lanes + jnp.arange(lanes, dtype=jnp.int32)
    basis = mode_basis(index, nlon, MAXM)
    partial_sum = jnp.dot(
        flat, basis, precision=lax.Precision.HIGHEST, preferred_element_type=jnp.float32
    )
    pieces = lax.all_to_all(partial_sum, "lon", 0, 0, tiled=True)
    mine = pieces.reshape(lon_peers, part, 2 * MAXM).sum(axis=0)
    totals = lax.all_to_all(
        jnp.broadcast_to(mine[None], (lon_peers, part, 2 * MAXM)), "lon", 0, 0
    ).reshape(total, 2 * MAXM)
    counts = mode_counts.astype(jnp.float32)
    row_counts = jnp.broadcast_to(counts[None], (4 * levels, rows)).reshape(total)
    smooth = jnp.dot(
        totals * mode_weights(row_counts, MAXM, nlon),
        basis.T,
        precision=lax.Precision.HIGHEST,
        preferred_element_type=jnp.float32,
    ).reshape(state.shape)
    flags = row_flags.astype(jnp.float32)
    return state + flags[None, None, :, None] * wet[None] * (smooth - state)


def solution(mesh):
    in_specs = (
        P(None, None, "lat", "lon"),
        P(None, "lat", "lon"),
        P(None, "lat", "lon"),
        P("lat"),
        P("lat"),
    )
    out_specs = P(None, None, "lat", "lon")
    return jax.shard_map(shards, mesh=mesh, in_specs=in_specs, out_specs=out_specs, check_vma=False)
```

```python
import math

import jax
import jax.numpy as jnp
import numpy as np
from jax import lax
from jax.sharding import PartitionSpec as P

FBAND = 16
MAXM = 64


lat_edge = 1.3
diffusion = 0.05
vertical_mix = 0.5
time_step = 0.05


def advance(padded, u_pad, v_pad, static, centre, faces):
    thick = static[0]
    wet = static[1]
    inv_c = 1.0 / centre
    east_u = 0.5 * (u_pad[:, :, :-1] + u_pad[:, :, 1:])
    east_h = 0.5 * (thick[:, :, :-1] + thick[:, :, 1:]) * wet[:, :, :-1] * wet[:, :, 1:]
    flux_e = east_h[None] * (
        east_u[None] * 0.5 * (padded[..., :-1] + padded[..., 1:])
        - diffusion * (padded[..., 1:] - padded[..., :-1]) * inv_c[:, None]
    )
    zonal = (flux_e[..., 1:] - flux_e[..., :-1])[:, :, 1:-1, :] * inv_c[1:-1, None]
    north_v = 0.5 * (v_pad[:, :-1, :] + v_pad[:, 1:, :])
    north_h = (
        0.5 * (thick[:, :-1, :] + thick[:, 1:, :]) * wet[:, :-1, :] * wet[:, 1:, :] * faces[:, None]
    )
    flux_n = north_h[None] * (
        north_v[None] * 0.5 * (padded[:, :, :-1] + padded[:, :, 1:])
        - diffusion * (padded[:, :, 1:] - padded[:, :, :-1])
    )
    merid = (flux_n[:, :, 1:] - flux_n[:, :, :-1])[..., 1:-1] * inv_c[1:-1, None]
    inner = padded[:, :, 1:-1, 1:-1]
    wet_in = wet[:, 1:-1, 1:-1]
    thick_in = jnp.where(wet_in > 0, thick[:, 1:-1, 1:-1], 1.0)
    coupling = wet_in[:-1] * wet_in[1:] * vertical_mix / (0.5 * (thick_in[:-1] + thick_in[1:]))
    vmix = coupling[None] * (inner[:, 1:] - inner[:, :-1])
    empty = jnp.zeros_like(vmix[:, :1])
    vert = jnp.concatenate([vmix, empty], axis=1) - jnp.concatenate([empty, vmix], axis=1)
    return inner + wet_in[None] * time_step * (vert - zonal - merid) / thick_in[None]


def mode_basis(length, modes):
    turns = np.arange(modes)[None, :] * np.arange(length)[:, None] % length
    angle = turns * (2.0 * math.pi / length)
    return np.concatenate([np.cos(angle), np.sin(angle)], axis=1).astype(np.float32)


def mode_weights(counts, modes, length):
    order = jnp.arange(modes).astype(jnp.float32)
    keep = (order[None, :] < counts[:, None]).astype(jnp.float32)
    scale = jnp.where(order == 0, 1.0, 2.0) / length
    weights = keep * scale[None, :]
    return jnp.concatenate([weights, weights], axis=1)


def swap_edges(before_src, after_src, axis):
    peers = lax.axis_size(axis)
    up = [(i, (i + 1) % peers) for i in range(peers)]
    down = [(j, i) for i, j in up]
    return lax.ppermute(before_src, axis, up), lax.ppermute(after_src, axis, down)


def widen(fields, width):
    rows, lanes = fields.shape[2:]
    below, above = swap_edges(
        fields[:, :, rows - width :], fields[:, :, :width], "lat"
    )
    lat_pos = lax.axis_index("lat")
    below = jnp.where(lat_pos > 0, below, 0.0)
    above = jnp.where(lat_pos < lax.axis_size("lat") - 1, above, 0.0)
    fields = jnp.concatenate([below, fields, above], axis=2)
    shape = fields.shape[:3] + (width,)
    west, east = swap_edges(
        fields[..., lanes - width :].reshape(-1, 128),
        fields[..., :width].reshape(-1, 128),
        "lon",
    )
    return jnp.concatenate([west.reshape(shape), fields, east.reshape(shape)], axis=3)


def shards(ocean_state, thickness, wet_mask, mode_counts, row_flags):
    wet = wet_mask.astype(jnp.float32)
    levels, rows, lanes = ocean_state.shape[1:]
    lon_peers = lax.axis_size("lon")
    nlat = rows * lax.axis_size("lat")
    nlon = lanes * lon_peers
    lat_pos = lax.axis_index("lat")
    joined = widen(
        jnp.concatenate([ocean_state, thickness[None], wet[None]], axis=0), 2
    )
    place = (lat_pos * rows - 2 + jnp.arange(rows + 4, dtype=jnp.int32)).astype(
        jnp.float32
    )
    centre = jnp.cos(lat_edge * (2.0 * (place + 0.5) / nlat - 1.0))
    faces = jnp.cos(lat_edge * (2.0 * (place[:-1] + 1.0) / nlat - 1.0))
    fields = joined[:4]
    fixed = joined[4:]
    fields = advance(fields, fields[2], fields[3], fixed, centre, faces)
    state = advance(
        fields, fields[2], fields[3], fixed[:, :, 1:-1, 1:-1], centre[1:-1], faces[1:-1]
    )
    total = 4 * levels * rows
    part = total // lon_peers
    basis = jnp.asarray(mode_basis(nlon, MAXM)).reshape(lon_peers, lanes, 2 * MAXM)
    circles = lax.all_to_all(
        state.reshape(lon_peers, part, lanes), "lon", 0, 0, tiled=True
    )
    totals = jnp.einsum(
        "opi,oim->pm",
        circles,
        basis,
        precision=lax.Precision.HIGHEST,
        preferred_element_type=jnp.float32,
    )
    counts = mode_counts.astype(jnp.float32)
    row_counts = lax.dynamic_slice(
        jnp.broadcast_to(counts[None], (4 * levels, rows)).reshape(total),
        (lax.axis_index("lon") * part,),
        (part,),
    )
    smooth = jnp.einsum(
        "pm,oim->opi",
        totals * mode_weights(row_counts, MAXM, nlon),
        basis,
        precision=lax.Precision.HIGHEST,
        preferred_element_type=jnp.float32,
    )
    smooth = lax.all_to_all(smooth, "lon", 0, 0, tiled=True).reshape(state.shape)
    flags = row_flags.astype(jnp.float32)
    return state + flags[None, None, :, None] * wet[None] * (smooth - state)


def solution(mesh):
    in_specs = (
        P(None, None, "lat", "lon"),
        P(None, "lat", "lon"),
        P(None, "lat", "lon"),
        P("lat"),
        P("lat"),
    )
    out_specs = P(None, None, "lat", "lon")
    return jax.shard_map(shards, mesh=mesh, in_specs=in_specs, out_specs=out_specs, check_vma=False)
```

```python
import math

import jax
import jax.numpy as jnp
import numpy as np
from jax import lax
from jax.experimental import pallas as pl
from jax.experimental.pallas import tpu as pltpu
from jax.sharding import PartitionSpec as P

MAXM = 64
LANES = 128
GROUP = 16


lat_edge = 1.3
diffusion = 0.05
vertical_mix = 0.5
time_step = 0.05


def roll(x, shift, axis):
    shift %= x.shape[axis]
    return pltpu.roll(x, shift, axis) if shift else x


def east(x):
    return roll(x, -1, 1)


def west(x):
    return roll(x, 1, 1)


def north(x):
    return roll(x, -1, 0)


def south(x):
    return roll(x, 1, 0)


def lane_of(shape):
    return lax.broadcasted_iota(jnp.int32, shape, 1)


def face_terms(h, w, inv_c, face):
    open_e = 0.5 * (h + east(h)) * (w * east(w))
    open_n = 0.5 * (h + north(h)) * (w * north(w)) * face
    return 0.25 * open_e, diffusion * open_e * inv_c, 0.25 * open_n, diffusion * open_n


def advance(fields, terms, scale, scale_c, vertical):
    quarter_e, spread_e, quarter_n, spread_n = terms
    u, v = fields[2], fields[3]
    speed_e = quarter_e * (u + east(u))
    speed_n = quarter_n * (v + north(v))
    here_e, there_e = speed_e + spread_e, speed_e - spread_e
    here_n, there_n = speed_n + spread_n, speed_n - spread_n
    fresh = []
    for q, vert in zip(fields, vertical):
        flux_e = here_e * q + there_e * east(q)
        flux_n = here_n * q + there_n * north(q)
        spread = (flux_e - west(flux_e)) + (flux_n - south(flux_n))
        fresh.append(q + scale * vert - scale_c * spread)
    return fresh


def pack_kernel(state_ref, thick_ref, wet_ref, halo_ref, first_ref, last_ref):
    levels, rows, lanes = thick_ref.shape
    lane = lane_of((8, LANES))
    for t in range(rows // 8 + 1):
        first = jnp.zeros((8, LANES), jnp.float32)
        last = jnp.zeros((8, LANES), jnp.float32)
        part = slice(8 * t, 8 * t + 8)
        for f in range(6):
            for k in range(levels):
                if t == rows // 8:
                    x = halo_ref[f, k]
                elif f < 4:
                    x = state_ref[f, k, part]
                elif f == 4:
                    x = thick_ref[k, part]
                else:
                    x = wet_ref[k, part].astype(jnp.float32)
                at = GROUP * f + 2 * k
                mine = (lane >= at) & (lane < at + 2)
                first = jnp.where(mine, roll(x, at, 1), first)
                last = jnp.where(mine, roll(x, at + 2 - lanes, 1), last)
        first_ref[part] = first
        last_ref[part] = last


def inner_kernel(
    state_ref, thick_ref, wet_ref, halo_ref, table_ref, out_ref, own_ref, q_ref, term_ref
):
    levels, rows, lanes = thick_ref.shape
    full = rows + 8
    inv_c, face = table_ref[0], table_ref[1]

    def load(f, k):
        if f < 4:
            own = state_ref[f, k]
        elif f == 4:
            own = thick_ref[k]
        else:
            own = wet_ref[k].astype(jnp.float32)
        return jnp.concatenate([own, halo_ref[f, k]], axis=0)

    lane = lane_of((full, LANES))
    for f in range(6):
        own = jnp.zeros((full, LANES), jnp.float32)
        for k in range(levels):
            x = load(f, k)
            q_ref[f, k] = x
            at = GROUP * k + 2
            own = jnp.where((lane >= at) & (lane < at + 4), roll(x, at, 1), own)
            at = GROUP * k + 8
            own = jnp.where(
                (lane >= at) & (lane < at + 4), roll(x, at + 4 - lanes, 1), own
            )
        own_ref[f] = own

    def solid(k):
        return jnp.where(q_ref[5, k] > 0, q_ref[4, k], 1.0)

    for k in range(levels):
        h, w, hs = q_ref[4, k], q_ref[5, k], solid(k)
        for i, term in enumerate(face_terms(h, w, inv_c, face)):
            term_ref[i, k] = term
        scale = time_step * w / hs
        term_ref[4, k] = scale
        term_ref[5, k] = scale * inv_c
        if k + 1 < levels:
            term_ref[6, k] = w * q_ref[5, k + 1] * vertical_mix / (0.5 * (hs + solid(k + 1)))

    def step(source, target, part):
        for k in range(levels):
            fields = [source[f, k] for f in range(4)]
            vertical = []
            for f in range(4):
                vert = jnp.zeros((full, LANES), jnp.float32)
                if k + 1 < levels:
                    vert = term_ref[6, k] * (source[f, k + 1] - fields[f])
                if k:
                    vert = vert - term_ref[6, k - 1] * (fields[f] - source[f, k - 1])
                vertical.append(vert)
            terms = [term_ref[i, k] for i in range(4)]
            fresh = advance(fields, terms, term_ref[4, k], term_ref[5, k], vertical)
            for f in range(4):
                target[f, k] = fresh[f][:part]

    middle = q_ref.at[6:10]
    step(q_ref, middle, full)
    step(middle, out_ref, rows)


def edge_kernel(inner_ref, own_ref, west_ref, east_ref, table_ref, out_ref):
    levels, rows, lanes = inner_ref.shape[1:]
    full = rows + 8
    lane = lane_of((full, LANES))
    inv_c, face = table_ref[0], table_ref[1]
    from_west, from_east = west_ref[...], east_ref[...]
    tiles = []
    for f in range(6):
        x = own_ref[f]
        for k in range(levels):
            src = GROUP * f + 2 * k
            at = GROUP * k
            x = jnp.where((lane >= at) & (lane < at + 2), roll(from_west, at - src, 1), x)
            at = GROUP * k + 12
            x = jnp.where((lane >= at) & (lane < at + 2), roll(from_east, at - src, 1), x)
        tiles.append(x)
    fields, h, w = tiles[:4], tiles[4], tiles[5]

    def deeper(x):
        return roll(x, -GROUP, 1)

    def shallower(x):
        return roll(x, GROUP, 1)

    hs = jnp.where(w > 0, h, 1.0)
    terms = face_terms(h, w, inv_c, face)
    scale = time_step * w / hs
    scale_c = scale * inv_c
    couple = w * deeper(w) * vertical_mix / (0.5 * (hs + deeper(hs)))
    couple = jnp.where(lane < GROUP * (levels - 1), couple, 0.0)
    for _ in range(2):
        vertical = []
        for q in fields:
            down = couple * (deeper(q) - q)
            vertical.append(down - shallower(down))
        fields = advance(fields, terms, scale, scale_c, vertical)
    lane = lane_of((rows, LANES))
    for f in range(4):
        x = fields[f][:rows]
        for k in range(levels):
            left = roll(x, -(GROUP * k + 2), 1)
            right = roll(x, lanes - 2 - (GROUP * k + 10), 1)
            out_ref[f, k] = jnp.where(
                lane < 2, left, jnp.where(lane >= lanes - 2, right, inner_ref[f, k])
            )


def call(kernel, outs, scratch=(), cost=None):
    vmem = pl.BlockSpec(memory_space=pltpu.VMEM)
    shapes = [jax.ShapeDtypeStruct(s, jnp.float32) for s in outs]

    def run(*args):
        return pl.pallas_call(
            kernel,
            out_shape=shapes,
            in_specs=[vmem] * len(args),
            out_specs=[vmem] * len(outs),
            scratch_shapes=[pltpu.VMEM(s, jnp.float32) for s in scratch],
            compiler_params=pltpu.CompilerParams(vmem_limit_bytes=24 << 20),
            cost_estimate=cost,
        )(*args)

    return run


def swap_edges(before_src, after_src, axis):
    peers = lax.axis_size(axis)
    up = [(i, (i + 1) % peers) for i in range(peers)]
    down = [(j, i) for i, j in up]
    return lax.ppermute(before_src, axis, up), lax.ppermute(after_src, axis, down)


def mode_basis(length, modes):
    turns = np.arange(modes)[None, :] * np.arange(length)[:, None] % length
    angle = turns * (2.0 * math.pi / length)
    return np.concatenate([np.cos(angle), np.sin(angle)], axis=1).astype(np.float32)


def mode_weights(counts, modes, length):
    order = jnp.arange(modes).astype(jnp.float32)
    keep = (order[None, :] < counts[:, None]).astype(jnp.float32)
    scale = jnp.where(order == 0, 1.0, 2.0) / length
    weights = keep * scale[None, :]
    return jnp.concatenate([weights, weights], axis=1)


def row_table(lat_pos, rows, nlat):
    place = np.arange(rows + 8)
    place = np.where(place < rows + 2, place, np.where(place < rows + 6, 0, place - rows - 8))
    place = (lat_pos * rows + jnp.asarray(place, jnp.int32)).astype(jnp.float32)
    centre = jnp.cos(lat_edge * (2.0 * (place + 0.5) / nlat - 1.0))
    faces = jnp.cos(lat_edge * (2.0 * (place + 1.0) / nlat - 1.0))
    table = jnp.stack([1.0 / centre, faces])
    return jnp.broadcast_to(table[:, :, None], table.shape + (LANES,))


def shards(ocean_state, thickness, wet_mask, mode_counts, row_flags):
    levels, rows, lanes = ocean_state.shape[1:]
    assert rows % 8 == 0 and lanes == LANES and levels * GROUP <= LANES
    lon_peers = lax.axis_size("lon")
    lat_peers = lax.axis_size("lat")
    nlat = rows * lat_peers
    nlon = lanes * lon_peers
    lat_pos = lax.axis_index("lat")
    table = row_table(lat_pos, rows, nlat)

    def edge_rows(part):
        return jnp.concatenate(
            [
                ocean_state[:, :, part],
                thickness[None, :, part],
                wet_mask[None, :, part].astype(jnp.float32),
            ]
        )

    below, above = swap_edges(
        edge_rows(slice(rows - 2, rows)), edge_rows(slice(0, 2)), "lat"
    )
    below = jnp.where(lat_pos > 0, below, 0.0)
    above = jnp.where(lat_pos < lat_peers - 1, above, 0.0)
    halo = jnp.concatenate(
        [above, jnp.zeros((6, levels, 4, lanes), jnp.float32), below], axis=2
    )
    full = rows + 8
    first, last = call(pack_kernel, [(full, LANES)] * 2)(
        ocean_state, thickness, wet_mask, halo
    )
    from_west, from_east = swap_edges(last, first, "lon")
    cells = levels * full * lanes
    inner, own = call(
        inner_kernel,
        [ocean_state.shape, (6, full, LANES)],
        [(10, levels, full, lanes), (7, levels, full, lanes)],
        pl.CostEstimate(
            flops=300 * cells, transcendentals=2 * cells, bytes_accessed=60 * cells
        ),
    )(ocean_state, thickness, wet_mask, halo, table)
    state = call(edge_kernel, [ocean_state.shape])(
        inner, own, from_west, from_east, table
    )[0]

    total = 4 * levels * rows
    part = total // lon_peers
    basis = jnp.asarray(mode_basis(nlon, MAXM)).reshape(lon_peers, lanes, 2 * MAXM)
    circles = lax.all_to_all(
        state.reshape(lon_peers, part, lanes), "lon", 0, 0, tiled=True
    )
    totals = jnp.einsum(
        "opi,oim->pm",
        circles,
        basis,
        precision=lax.Precision.HIGHEST,
        preferred_element_type=jnp.float32,
    )
    counts = mode_counts.astype(jnp.float32)
    row_counts = lax.dynamic_slice(
        jnp.broadcast_to(counts[None], (4 * levels, rows)).reshape(total),
        (lax.axis_index("lon") * part,),
        (part,),
    )
    smooth = jnp.einsum(
        "pm,oim->opi",
        totals * mode_weights(row_counts, MAXM, nlon),
        basis,
        precision=lax.Precision.HIGHEST,
        preferred_element_type=jnp.float32,
    )
    smooth = lax.all_to_all(smooth, "lon", 0, 0, tiled=True).reshape(state.shape)
    flags = row_flags.astype(jnp.float32)
    wet = wet_mask.astype(jnp.float32)
    return state + flags[None, None, :, None] * wet[None] * (smooth - state)


def solution(mesh):
    in_specs = (
        P(None, None, "lat", "lon"),
        P(None, "lat", "lon"),
        P(None, "lat", "lon"),
        P("lat"),
        P("lat"),
    )
    out_specs = P(None, None, "lat", "lon")
    return jax.shard_map(shards, mesh=mesh, in_specs=in_specs, out_specs=out_specs, check_vma=False)
```

```python
import math

import jax
import jax.numpy as jnp
import numpy as np
from jax import lax
from jax.experimental import pallas as pl
from jax.experimental.pallas import tpu as pltpu
from jax.sharding import PartitionSpec as P

MAXM = 64
LANES = 128
GROUP = 16


lat_edge = 1.3
diffusion = 0.05
vertical_mix = 0.5
time_step = 0.05


def roll(x, shift, axis):
    shift %= x.shape[axis]
    return pltpu.roll(x, shift, axis) if shift else x


def east(x):
    return roll(x, -1, 1)


def west(x):
    return roll(x, 1, 1)


def north(x):
    return roll(x, -1, 0)


def south(x):
    return roll(x, 1, 0)


def lane_of(shape):
    return lax.broadcasted_iota(jnp.int32, shape, 1)


def east_terms(h, w, inv_c):
    open_e = 0.5 * (h + east(h)) * (w * east(w))
    return 0.25 * open_e, diffusion * open_e * inv_c


def north_terms(h, w, face):
    open_n = 0.5 * (h + north(h)) * (w * north(w)) * face
    return 0.25 * open_n, diffusion * open_n


def advance(fields, terms, scale, scale_c, vertical):
    quarter_e, spread_e, quarter_n, spread_n = terms
    u, v = fields[2], fields[3]
    speed_e = quarter_e * (u + east(u))
    speed_n = quarter_n * (v + north(v))
    here_e, there_e = speed_e + spread_e, speed_e - spread_e
    here_n, there_n = speed_n + spread_n, speed_n - spread_n
    fresh = []
    for q, vert in zip(fields, vertical):
        flux_e = here_e * q + there_e * east(q)
        flux_n = here_n * q + there_n * north(q)
        spread = (flux_e - west(flux_e)) + (flux_n - south(flux_n))
        fresh.append(q + scale * vert - scale_c * spread)
    return fresh


def own_columns(load, levels, lanes, rows):
    lane = lane_of((rows, LANES))
    own = jnp.zeros((rows, LANES), jnp.float32)
    for k in range(levels):
        x = load(k)
        at = GROUP * k + 2
        own = jnp.where((lane >= at) & (lane < at + 4), roll(x, at, 1), own)
        at = GROUP * k + 8
        own = jnp.where((lane >= at) & (lane < at + 4), roll(x, at + 4 - lanes, 1), own)
    return own


def row_terms(thick, wet, inv_c, levels, term_ref):
    w, h = wet(0), thick(0)
    hs = jnp.where(w > 0, h, 1.0)
    for k in range(levels):
        term_ref[0, k], term_ref[1, k] = east_terms(h, w, inv_c)
        scale = time_step * w / hs
        term_ref[2, k] = scale
        term_ref[3, k] = scale * inv_c
        if k + 1 < levels:
            w_next, h_next = wet(k + 1), thick(k + 1)
            hs_next = jnp.where(w_next > 0, h_next, 1.0)
            term_ref[4, k] = w * w_next * vertical_mix / (0.5 * (hs + hs_next))
            w, h, hs = w_next, h_next, hs_next


def ready_kernel(state_ref, thick_ref, wet_ref, table_ref, own_ref, term_ref):
    levels, rows, lanes = thick_ref.shape

    def thick(k):
        return thick_ref[k]

    def wet(k):
        return wet_ref[k].astype(jnp.float32)

    for f in range(4):
        own_ref[f] = own_columns(lambda k, f=f: state_ref[f, k], levels, lanes, rows)
    own_ref[4] = own_columns(thick, levels, lanes, rows)
    own_ref[5] = own_columns(wet, levels, lanes, rows)
    row_terms(thick, wet, table_ref[0, :rows], levels, term_ref)


def pack_kernel(
    state_ref, thick_ref, wet_ref, below_ref, above_ref, first_ref, last_ref, halo_ref
):
    levels, rows, lanes = thick_ref.shape
    lat_pos = lax.axis_index("lat")
    with_below = jnp.where(lat_pos > 0, 1.0, 0.0)
    with_above = jnp.where(lat_pos < lax.axis_size("lat") - 1, 1.0, 0.0)
    lane = lane_of((8, LANES))
    for f in range(6):
        for k in range(levels):
            halo_ref[f, k, 0:2] = above_ref[f, k] * with_above
            halo_ref[f, k, 2:6] = jnp.zeros((4, lanes), jnp.float32)
            halo_ref[f, k, 6:8] = below_ref[f, k] * with_below
    for t in range(rows // 8 + 1):
        first = jnp.zeros((8, LANES), jnp.float32)
        last = jnp.zeros((8, LANES), jnp.float32)
        part = slice(8 * t, 8 * t + 8)
        for f in range(6):
            for k in range(levels):
                if t == rows // 8:
                    x = halo_ref[f, k]
                elif f < 4:
                    x = state_ref[f, k, part]
                elif f == 4:
                    x = thick_ref[k, part]
                else:
                    x = wet_ref[k, part].astype(jnp.float32)
                at = GROUP * f + 2 * k
                mine = (lane >= at) & (lane < at + 2)
                first = jnp.where(mine, roll(x, at, 1), first)
                last = jnp.where(mine, roll(x, at + 2 - lanes, 1), last)
        first_ref[part] = first
        last_ref[part] = last


def inner_kernel(
    state_ref,
    thick_ref,
    wet_ref,
    halo_ref,
    table_ref,
    own_ref,
    term_ref,
    out_ref,
    edge_ref,
    halo_term_ref,
    north_ref,
):
    levels, rows, lanes = thick_ref.shape
    full = rows + 8
    face = table_ref[1]

    def joined(x, y):
        return jnp.concatenate([x, y], axis=0)

    def halo(f):
        return lambda k: halo_ref[f, k]

    for f in range(6):
        edge_ref[f, :rows] = own_ref[f]
        edge_ref[f, rows:] = own_columns(halo(f), levels, lanes, 8)
    row_terms(halo(4), halo(5), table_ref[0, rows:], levels, halo_term_ref)
    for k in range(levels):
        h = joined(thick_ref[k], halo_ref[4, k])
        w = joined(wet_ref[k].astype(jnp.float32), halo_ref[5, k])
        north_ref[0, k], north_ref[1, k] = north_terms(h, w, face)
        for f in range(4):
            out_ref[0, f, k] = joined(state_ref[f, k], halo_ref[f, k])

    def term(i, k):
        return joined(term_ref[i, k], halo_term_ref[i, k])

    def step(i, _):
        source, target = out_ref.at[i], out_ref.at[i + 1]
        fields = [source[f, 0] for f in range(4)]
        above = [jnp.zeros((full, LANES), jnp.float32)] * 4
        for k in range(levels):
            deeper = below = above
            if k + 1 < levels:
                couple = term(4, k)
                deeper = [source[f, k + 1] for f in range(4)]
                below = [couple * (d - q) for d, q in zip(deeper, fields)]
                vertical = [b - a for b, a in zip(below, above)]
            else:
                vertical = [-a for a in above]
            terms = term(0, k), term(1, k), north_ref[0, k], north_ref[1, k]
            fresh = advance(fields, terms, term(2, k), term(3, k), vertical)
            for f in range(4):
                target[f, k] = fresh[f]
            fields, above = deeper, below
        return 0

    lax.fori_loop(0, 2, step, 0)


def edge_kernel(
    inner_ref, own_ref, west_ref, east_ref, table_ref, out_ref, send_ref, tile_ref, term_ref, sems
):
    levels, rows, lanes = out_ref.shape[1:]
    full = rows + 8
    lane = lane_of((full, LANES))
    inv_c, face = table_ref[0], table_ref[1]
    from_west, from_east = west_ref[...], east_ref[...]

    def joined(f):
        x = own_ref[f]
        for k in range(levels):
            src = GROUP * f + 2 * k
            at = GROUP * k
            x = jnp.where((lane >= at) & (lane < at + 2), roll(from_west, at - src, 1), x)
            at = GROUP * k + 12
            x = jnp.where((lane >= at) & (lane < at + 2), roll(from_east, at - src, 1), x)
        return x

    def deeper(x):
        return roll(x, -GROUP, 1)

    def shallower(x):
        return roll(x, GROUP, 1)

    h, w = joined(4), joined(5)
    for f in range(4):
        tile_ref[f] = joined(f)
    hs = jnp.where(w > 0, h, 1.0)
    scale = time_step * w / hs
    couple = w * deeper(w) * vertical_mix / (0.5 * (hs + deeper(hs)))
    couple = jnp.where(lane < GROUP * (levels - 1), couple, 0.0)
    terms = east_terms(h, w, inv_c) + north_terms(h, w, face)
    for i, term in enumerate(terms + (scale, scale * inv_c, couple)):
        term_ref[i] = term

    def step(_, __):
        terms = [term_ref[i] for i in range(7)]
        fields = [tile_ref[f] for f in range(4)]
        vertical = []
        for q in fields:
            down = terms[6] * (deeper(q) - q)
            vertical.append(down - shallower(down))
        for f, q in enumerate(advance(fields, terms[:4], terms[4], terms[5], vertical)):
            tile_ref[f] = q
        return 0

    lax.fori_loop(0, 2, step, 0)
    lane = lane_of((rows, LANES))
    for f in range(4):
        x = tile_ref[f, :rows]
        for k in range(levels):
            left = roll(x, -(GROUP * k + 2), 1)
            right = roll(x, lanes - 2 - (GROUP * k + 10), 1)
            out_ref[f, k] = jnp.where(
                lane < 2,
                left,
                jnp.where(lane >= lanes - 2, right, inner_ref[2, f, k, :rows]),
            )
        pltpu.make_async_copy(out_ref.at[f], send_ref.at[f], sems.at[f]).start()
    for f in range(4):
        pltpu.make_async_copy(out_ref.at[f], send_ref.at[f], sems.at[f]).wait()


def product(a, b, dims):
    return lax.dot_general(
        a,
        b,
        (dims, ((), ())),
        precision=lax.Precision.HIGHEST,
        preferred_element_type=jnp.float32,
    )


def filter_kernel(circle_ref, basis_ref, weight_ref, out_ref, totals_ref, piece_ref, sems):
    pieces = circle_ref.shape[0]
    total = jnp.zeros(totals_ref.shape, jnp.float32)
    for o in range(pieces):
        total = total + product(circle_ref[o], basis_ref[o], ((1,), (0,)))
    totals_ref[...] = total * weight_ref[...]
    copies = []
    for o in range(pieces):
        piece_ref[o] = product(totals_ref[...], basis_ref[o], ((1,), (1,)))
        copies.append(pltpu.make_async_copy(piece_ref.at[o], out_ref.at[o], sems.at[o]))
        copies[-1].start()
    for copy in copies:
        copy.wait()


def blend_kernel(state_ref, smooth_ref, wet_ref, flag_ref, out_ref, piece_ref, sems):
    levels = wet_ref.shape[0]
    flag = flag_ref[...]
    copies = []
    for f in range(4):
        for k in range(levels):
            state = state_ref[f, k]
            gate = flag * wet_ref[k].astype(jnp.float32)
            piece_ref[f, k] = state + gate * (smooth_ref[f, k] - state)
        copies.append(pltpu.make_async_copy(piece_ref.at[f], out_ref.at[f], sems.at[f]))
        copies[-1].start()
    for copy in copies:
        copy.wait()


def call(kernel, outs, scratch=(), sems=0, sent=False, flops=0):
    vmem = pl.BlockSpec(memory_space=pltpu.VMEM)
    specs = [vmem] * len(outs)
    if sent:
        specs[-1] = pl.BlockSpec(memory_space=pl.ANY)
    buffers = [pltpu.VMEM(s, jnp.float32) for s in scratch]
    if sems:
        buffers.append(pltpu.SemaphoreType.DMA((sems,)))
    cost = pl.CostEstimate(
        flops=flops, transcendentals=0, bytes_accessed=4 * sum(map(math.prod, outs))
    )

    def run(*args):
        return pl.pallas_call(
            kernel,
            out_shape=[jax.ShapeDtypeStruct(s, jnp.float32) for s in outs],
            in_specs=[vmem] * len(args),
            out_specs=specs,
            scratch_shapes=buffers,
            compiler_params=pltpu.CompilerParams(vmem_limit_bytes=24 << 20),
            cost_estimate=cost,
        )(*args)

    return run


def swap_edges(before_src, after_src, axis):
    peers = lax.axis_size(axis)
    up = [(i, (i + 1) % peers) for i in range(peers)]
    down = [(j, i) for i, j in up]
    return lax.ppermute(before_src, axis, up), lax.ppermute(after_src, axis, down)


def mode_basis(length, modes):
    turns = np.arange(modes)[None, :] * np.arange(length)[:, None] % length
    angle = turns * (2.0 * math.pi / length)
    return np.concatenate([np.cos(angle), np.sin(angle)], axis=1).astype(np.float32)


def mode_weights(counts, modes, length):
    order = jnp.arange(modes).astype(jnp.float32)
    keep = (order[None, :] < counts[:, None]).astype(jnp.float32)
    scale = jnp.where(order == 0, 1.0, 2.0) / length
    weights = keep * scale[None, :]
    return jnp.concatenate([weights, weights], axis=1)


def row_table(lat_pos, rows, nlat):
    place = np.arange(rows + 8)
    place = np.where(place < rows + 2, place, np.where(place < rows + 6, 0, place - rows - 8))
    place = (lat_pos * rows + jnp.asarray(place, jnp.int32)).astype(jnp.float32)
    centre = jnp.cos(lat_edge * (2.0 * (place + 0.5) / nlat - 1.0))
    faces = jnp.cos(lat_edge * (2.0 * (place + 1.0) / nlat - 1.0))
    table = jnp.stack([1.0 / centre, faces])
    return jnp.broadcast_to(table[:, :, None], table.shape + (LANES,))


def shards(ocean_state, thickness, wet_mask, mode_counts, row_flags):
    levels, rows, lanes = ocean_state.shape[1:]
    assert rows % 8 == 0 and lanes == LANES and levels * GROUP <= LANES
    lon_peers = lax.axis_size("lon")
    lat_peers = lax.axis_size("lat")
    nlat = rows * lat_peers
    nlon = lanes * lon_peers
    full = rows + 8
    total = 4 * levels * rows
    part = total // lon_peers
    table = row_table(lax.axis_index("lat"), rows, nlat)
    block = (ocean_state, thickness, wet_mask)
    cells = 4 * levels * full * lanes

    def edge_rows(part):
        return jnp.concatenate(
            [
                ocean_state[:, :, part],
                thickness[None, :, part],
                wet_mask[None, :, part].astype(jnp.float32),
            ]
        )

    below, above = swap_edges(
        edge_rows(slice(rows - 2, rows)), edge_rows(slice(0, 2)), "lat"
    )
    own, terms = call(
        ready_kernel, [(6, rows, LANES), (5, levels, rows, lanes)], flops=20 * cells
    )(*block, table)
    first, last, halo = call(
        pack_kernel, [(full, LANES)] * 2 + [(6, levels, 8, lanes)]
    )(*block, below, above)
    from_west, from_east = swap_edges(last, first, "lon")
    inner, edges = call(
        inner_kernel,
        [(3, 4, levels, full, lanes), (6, full, LANES)],
        [(5, levels, 8, lanes), (2, levels, full, lanes)],
        flops=60 * cells,
    )(*block, halo, table, own, terms)
    state, sent = call(
        edge_kernel,
        [ocean_state.shape] * 2,
        [(4, full, LANES), (7, full, LANES)],
        sems=4,
        sent=True,
    )(inner, edges, from_west, from_east, table)

    basis = jnp.asarray(mode_basis(nlon, MAXM)).reshape(lon_peers, lanes, 2 * MAXM)
    counts = mode_counts.astype(jnp.float32)
    row_counts = lax.dynamic_slice(
        jnp.broadcast_to(counts[None], (4 * levels, rows)).reshape(total),
        (lax.axis_index("lon") * part,),
        (part,),
    )
    weights = mode_weights(row_counts, MAXM, nlon)
    circles = lax.all_to_all(
        sent.reshape(lon_peers, part, lanes), "lon", 0, 0, tiled=True
    )
    smooth = call(
        filter_kernel,
        [circles.shape],
        [(part, 2 * MAXM), circles.shape],
        sems=lon_peers,
        sent=True,
    )(circles, basis, weights)[0]
    smooth = lax.all_to_all(smooth, "lon", 0, 0, tiled=True).reshape(ocean_state.shape)
    flags = jnp.broadcast_to(row_flags.astype(jnp.float32)[:, None], (rows, lanes))
    return call(blend_kernel, [ocean_state.shape], [ocean_state.shape], sems=4, sent=True)(
        state, smooth, wet_mask, flags
    )[0]


def solution(mesh):
    in_specs = (
        P(None, None, "lat", "lon"),
        P(None, "lat", "lon"),
        P(None, "lat", "lon"),
        P("lat"),
        P("lat"),
    )
    out_specs = P(None, None, "lat", "lon")
    return jax.shard_map(shards, mesh=mesh, in_specs=in_specs, out_specs=out_specs, check_vma=False)
```

```python
import math

import jax
import jax.numpy as jnp
import ml_dtypes
import numpy as np
from jax import lax
from jax.experimental import pallas as pl
from jax.experimental.pallas import tpu as pltpu
from jax.sharding import PartitionSpec as P

MAXM = 64
LANES = 128
GROUP = 16


lat_edge = 1.3
diffusion = 0.05
vertical_mix = 0.5
time_step = 0.05


def roll(x, shift, axis):
    shift %= x.shape[axis]
    return pltpu.roll(x, shift, axis) if shift else x


def east(x):
    return roll(x, -1, 1)


def west(x):
    return roll(x, 1, 1)


def north(x):
    return roll(x, -1, 0)


def south(x):
    return roll(x, 1, 0)


def lane_of(shape):
    return lax.broadcasted_iota(jnp.int32, shape, 1)


def east_terms(h, w, inv_c):
    open_e = 0.5 * (h + east(h)) * (w * east(w))
    return 0.25 * open_e, diffusion * open_e * inv_c


def north_terms(h, w, face):
    open_n = 0.5 * (h + north(h)) * (w * north(w)) * face
    return 0.25 * open_n, diffusion * open_n


def advance(fields, terms, scale, scale_c, vertical):
    quarter_e, spread_e, quarter_n, spread_n = terms
    u, v = fields[2], fields[3]
    speed_e = quarter_e * (u + east(u))
    speed_n = quarter_n * (v + north(v))
    here_e, there_e = speed_e + spread_e, speed_e - spread_e
    here_n, there_n = speed_n + spread_n, speed_n - spread_n
    fresh = []
    for q, vert in zip(fields, vertical):
        flux_e = here_e * q + there_e * east(q)
        flux_n = here_n * q + there_n * north(q)
        spread = (flux_e - west(flux_e)) + (flux_n - south(flux_n))
        fresh.append(q + scale * vert - scale_c * spread)
    return fresh


def own_columns(load, levels, lanes, rows):
    lane = lane_of((rows, LANES))
    own = jnp.zeros((rows, LANES), jnp.float32)
    for k in range(levels):
        x = load(k)
        at = GROUP * k + 2
        own = jnp.where((lane >= at) & (lane < at + 4), roll(x, at, 1), own)
        at = GROUP * k + 8
        own = jnp.where((lane >= at) & (lane < at + 4), roll(x, at + 4 - lanes, 1), own)
    return own


def row_terms(thick, wet, inv_c, levels, term_ref):
    w, h = wet(0), thick(0)
    hs = jnp.where(w > 0, h, 1.0)
    for k in range(levels):
        term_ref[0, k], term_ref[1, k] = east_terms(h, w, inv_c)
        scale = time_step * w / hs
        term_ref[2, k] = scale
        term_ref[3, k] = scale * inv_c
        if k + 1 < levels:
            w_next, h_next = wet(k + 1), thick(k + 1)
            hs_next = jnp.where(w_next > 0, h_next, 1.0)
            term_ref[4, k] = w * w_next * vertical_mix / (0.5 * (hs + hs_next))
            w, h, hs = w_next, h_next, hs_next


def load_kernel(
    state_any, thick_any, wet_any, state_ref, thick_ref, wet_ref, first_ref, last_ref, raw_ref, sems
):
    levels, rows = thick_ref.shape[:2]
    moves = [(wet_any, raw_ref), (thick_any, thick_ref)]
    moves += [(state_any.at[f], state_ref.at[f]) for f in range(4)]
    copies = [pltpu.make_async_copy(*pair, sems.at[i]) for i, pair in enumerate(moves)]
    for copy in copies:
        copy.start()
    copies[0].wait()
    for k in range(levels):
        wet_ref[k] = raw_ref[k].astype(jnp.float32)
    for copy in copies[1:]:
        copy.wait()
    for f in range(6):
        for k in range(levels):
            x = state_ref.at[f, k] if f < 4 else (thick_ref, wet_ref)[f - 4].at[k]
            first_ref[f, k] = x[0:2]
            last_ref[f, k] = x[rows - 2 : rows]


def ready_kernel(state_ref, thick_ref, wet_ref, table_ref, own_ref, term_ref):
    levels, rows, lanes = thick_ref.shape

    def thick(k):
        return thick_ref[k]

    def wet(k):
        return wet_ref[k]

    for f in range(4):
        own_ref[f] = own_columns(lambda k, f=f: state_ref[f, k], levels, lanes, rows)
    own_ref[4] = own_columns(thick, levels, lanes, rows)
    own_ref[5] = own_columns(wet, levels, lanes, rows)
    row_terms(thick, wet, table_ref[0, :rows], levels, term_ref)


def pack_kernel(
    state_ref, thick_ref, wet_ref, below_ref, above_ref, first_ref, last_ref, halo_ref
):
    levels, rows, lanes = thick_ref.shape
    lat_pos = lax.axis_index("lat")
    with_below = jnp.where(lat_pos > 0, 1.0, 0.0)
    with_above = jnp.where(lat_pos < lax.axis_size("lat") - 1, 1.0, 0.0)
    lane = lane_of((8, LANES))
    for f in range(6):
        for k in range(levels):
            halo_ref[f, k, 0:2] = above_ref[f, k] * with_above
            halo_ref[f, k, 2:6] = jnp.zeros((4, lanes), jnp.float32)
            halo_ref[f, k, 6:8] = below_ref[f, k] * with_below
    for t in range(rows // 8 + 1):
        first = jnp.zeros((8, LANES), jnp.float32)
        last = jnp.zeros((8, LANES), jnp.float32)
        part = slice(8 * t, 8 * t + 8)
        for f in range(6):
            for k in range(levels):
                if t == rows // 8:
                    x = halo_ref[f, k]
                elif f < 4:
                    x = state_ref[f, k, part]
                elif f == 4:
                    x = thick_ref[k, part]
                else:
                    x = wet_ref[k, part]
                at = GROUP * f + 2 * k
                mine = (lane >= at) & (lane < at + 2)
                first = jnp.where(mine, roll(x, at, 1), first)
                last = jnp.where(mine, roll(x, at + 2 - lanes, 1), last)
        first_ref[part] = first
        last_ref[part] = last


def inner_kernel(
    state_ref,
    thick_ref,
    wet_ref,
    halo_ref,
    table_ref,
    own_ref,
    term_ref,
    out_ref,
    edge_ref,
    halo_term_ref,
    north_ref,
):
    levels, rows, lanes = thick_ref.shape
    full = rows + 8
    face = table_ref[1]

    def joined(x, y):
        return jnp.concatenate([x, y], axis=0)

    def halo(f):
        return lambda k: halo_ref[f, k]

    for f in range(6):
        edge_ref[f, :rows] = own_ref[f]
        edge_ref[f, rows:] = own_columns(halo(f), levels, lanes, 8)
    row_terms(halo(4), halo(5), table_ref[0, rows:], levels, halo_term_ref)
    for k in range(levels):
        h = joined(thick_ref[k], halo_ref[4, k])
        w = joined(wet_ref[k], halo_ref[5, k])
        north_ref[0, k], north_ref[1, k] = north_terms(h, w, face)
        for f in range(4):
            out_ref[0, f, k] = joined(state_ref[f, k], halo_ref[f, k])

    def term(i, k):
        return joined(term_ref[i, k], halo_term_ref[i, k])

    def step(i, _):
        source, target = out_ref.at[i], out_ref.at[i + 1]
        fields = [source[f, 0] for f in range(4)]
        above = [jnp.zeros((full, LANES), jnp.float32)] * 4
        for k in range(levels):
            deeper = below = above
            if k + 1 < levels:
                couple = term(4, k)
                deeper = [source[f, k + 1] for f in range(4)]
                below = [couple * (d - q) for d, q in zip(deeper, fields)]
                vertical = [b - a for b, a in zip(below, above)]
            else:
                vertical = [-a for a in above]
            terms = term(0, k), term(1, k), north_ref[0, k], north_ref[1, k]
            fresh = advance(fields, terms, term(2, k), term(3, k), vertical)
            for f in range(4):
                target[f, k] = fresh[f]
            fields, above = deeper, below
        return 0

    lax.fori_loop(0, 2, step, 0)


def edge_kernel(
    inner_ref, own_ref, west_ref, east_ref, table_ref, out_ref, send_ref, tile_ref, term_ref, sems
):
    levels, rows, lanes = out_ref.shape[1:]
    full = rows + 8
    lane = lane_of((full, LANES))
    inv_c, face = table_ref[0], table_ref[1]
    from_west, from_east = west_ref[...], east_ref[...]

    def joined(f):
        x = own_ref[f]
        for k in range(levels):
            src = GROUP * f + 2 * k
            at = GROUP * k
            x = jnp.where((lane >= at) & (lane < at + 2), roll(from_west, at - src, 1), x)
            at = GROUP * k + 12
            x = jnp.where((lane >= at) & (lane < at + 2), roll(from_east, at - src, 1), x)
        return x

    def deeper(x):
        return roll(x, -GROUP, 1)

    def shallower(x):
        return roll(x, GROUP, 1)

    h, w = joined(4), joined(5)
    for f in range(4):
        tile_ref[f] = joined(f)
    hs = jnp.where(w > 0, h, 1.0)
    scale = time_step * w / hs
    couple = w * deeper(w) * vertical_mix / (0.5 * (hs + deeper(hs)))
    couple = jnp.where(lane < GROUP * (levels - 1), couple, 0.0)
    terms = east_terms(h, w, inv_c) + north_terms(h, w, face)
    for i, term in enumerate(terms + (scale, scale * inv_c, couple)):
        term_ref[i] = term

    def step(_, __):
        terms = [term_ref[i] for i in range(7)]
        fields = [tile_ref[f] for f in range(4)]
        vertical = []
        for q in fields:
            down = terms[6] * (deeper(q) - q)
            vertical.append(down - shallower(down))
        for f, q in enumerate(advance(fields, terms[:4], terms[4], terms[5], vertical)):
            tile_ref[f] = q
        return 0

    lax.fori_loop(0, 2, step, 0)
    lane = lane_of((rows, LANES))
    for f in range(4):
        x = tile_ref[f, :rows]
        for k in range(levels):
            left = roll(x, -(GROUP * k + 2), 1)
            right = roll(x, lanes - 2 - (GROUP * k + 10), 1)
            out_ref[f, k] = jnp.where(
                lane < 2,
                left,
                jnp.where(lane >= lanes - 2, right, inner_ref[2, f, k, :rows]),
            )
        pltpu.make_async_copy(out_ref.at[f], send_ref.at[f], sems.at[f]).start()
    for f in range(4):
        pltpu.make_async_copy(out_ref.at[f], send_ref.at[f], sems.at[f]).wait()


def split(x):
    high = x.astype(jnp.bfloat16)
    return high, (x - high.astype(jnp.float32)).astype(jnp.bfloat16)


def product(a, b, dims):
    return lax.dot_general(a, b, (dims, ((), ())), preferred_element_type=jnp.float32)


def filter_kernel(circle_ref, basis_ref, weight_ref, out_ref, piece_ref, sems):
    pieces, part, lanes = circle_ref.shape
    modes = weight_ref.shape[1]
    pairs = range(0, pieces, 2)
    total = jnp.zeros((2 * part, 2 * modes), jnp.float32)
    for o in pairs:
        parts = zip(split(circle_ref[o]), split(circle_ref[o + 1]))
        x = jnp.concatenate([jnp.concatenate(p, axis=1) for p in parts], axis=0)
        total = total + product(x, basis_ref[lanes * o : lanes * (o + 2)], ((1,), (0,)))
    total = total[:part] + total[part:]
    total = (total[:, :modes] + total[:, modes:]) * weight_ref[...]
    y = jnp.concatenate([jnp.concatenate([p, p], axis=1) for p in split(total)], axis=0)
    copies = []
    for o in pairs:
        x = product(y, basis_ref[lanes * o : lanes * (o + 2)], ((1,), (1,)))
        x = x[:part] + x[part:]
        piece_ref[o] = x[:, :lanes]
        piece_ref[o + 1] = x[:, lanes:]
        both = pl.ds(o, 2)
        copies.append(
            pltpu.make_async_copy(piece_ref.at[both], out_ref.at[both], sems.at[o // 2])
        )
        copies[-1].start()
    for copy in copies:
        copy.wait()


def blend_kernel(state_ref, smooth_ref, wet_ref, flag_ref, out_ref, piece_ref, sems):
    levels = wet_ref.shape[0]
    flag = flag_ref[...]
    copies = []
    for f in range(4):
        for k in range(levels):
            state = state_ref[f, k]
            gate = flag * wet_ref[k]
            piece_ref[f, k] = state + gate * (smooth_ref[f, k] - state)
        copies.append(pltpu.make_async_copy(piece_ref.at[f], out_ref.at[f], sems.at[f]))
        copies[-1].start()
    for copy in copies:
        copy.wait()


def call(kernel, outs, scratch=(), sems=0, raw=False, sent=False, flops=0):
    vmem = pl.BlockSpec(memory_space=pltpu.VMEM)
    away = pl.BlockSpec(memory_space=pl.ANY)
    specs = [vmem] * len(outs)
    if sent:
        specs[-1] = away
    buffers = [pltpu.VMEM(s, jnp.float32) if isinstance(s, tuple) else s for s in scratch]
    if sems:
        buffers.append(pltpu.SemaphoreType.DMA((sems,)))
    cost = pl.CostEstimate(
        flops=flops, transcendentals=0, bytes_accessed=4 * sum(map(math.prod, outs))
    )

    def run(*args):
        if raw:
            args = [pltpu.with_memory_space_constraint(x, pltpu.HBM) for x in args]
        return pl.pallas_call(
            kernel,
            out_shape=[jax.ShapeDtypeStruct(s, jnp.float32) for s in outs],
            in_specs=[away if raw else vmem] * len(args),
            out_specs=specs,
            scratch_shapes=buffers,
            compiler_params=pltpu.CompilerParams(vmem_limit_bytes=24 << 20),
            cost_estimate=cost,
        )(*args)

    return run


def swap_edges(before_src, after_src, axis):
    peers = lax.axis_size(axis)
    up = [(i, (i + 1) % peers) for i in range(peers)]
    down = [(j, i) for i, j in up]
    return lax.ppermute(before_src, axis, up), lax.ppermute(after_src, axis, down)


def mode_basis(length, modes):
    turns = np.arange(modes)[None, :] * np.arange(length)[:, None] % length
    angle = turns * (2.0 * math.pi / length)
    basis = np.concatenate([np.cos(angle), np.sin(angle)], axis=1).astype(np.float32)
    high = basis.astype(ml_dtypes.bfloat16)
    low = (basis - high.astype(np.float32)).astype(ml_dtypes.bfloat16)
    return np.concatenate([high, low], axis=1)


def mode_weights(counts, modes, length):
    order = jnp.arange(modes).astype(jnp.float32)
    keep = (order[None, :] < counts[:, None]).astype(jnp.float32)
    scale = jnp.where(order == 0, 1.0, 2.0) / length
    weights = keep * scale[None, :]
    return jnp.concatenate([weights, weights], axis=1)


def row_table(lat_pos, rows, nlat):
    place = np.arange(rows + 8)
    place = np.where(place < rows + 2, place, np.where(place < rows + 6, 0, place - rows - 8))
    place = (lat_pos * rows + jnp.asarray(place, jnp.int32)).astype(jnp.float32)
    centre = jnp.cos(lat_edge * (2.0 * (place + 0.5) / nlat - 1.0))
    faces = jnp.cos(lat_edge * (2.0 * (place + 1.0) / nlat - 1.0))
    table = jnp.stack([1.0 / centre, faces])
    return jnp.broadcast_to(table[:, :, None], table.shape + (LANES,))


def shards(ocean_state, thickness, wet_mask, mode_counts, row_flags):
    levels, rows, lanes = ocean_state.shape[1:]
    assert rows % 8 == 0 and lanes == LANES and levels * GROUP <= LANES
    lon_peers = lax.axis_size("lon")
    lat_peers = lax.axis_size("lat")
    nlat = rows * lat_peers
    nlon = lanes * lon_peers
    full = rows + 8
    total = 4 * levels * rows
    part = total // lon_peers
    table = row_table(lax.axis_index("lat"), rows, nlat)
    cells = 4 * levels * full * lanes
    edge_rows = (6, levels, 2, lanes)

    *block, first, last = call(
        load_kernel,
        [ocean_state.shape, thickness.shape, thickness.shape, edge_rows, edge_rows],
        [pltpu.VMEM(thickness.shape, jnp.int32)],
        sems=6,
        raw=True,
    )(ocean_state, thickness, wet_mask)
    below, above = swap_edges(last, first, "lat")
    own, terms = call(
        ready_kernel, [(6, rows, LANES), (5, levels, rows, lanes)], flops=20 * cells
    )(*block, table)
    below, above, own, terms = lax.optimization_barrier((below, above, own, terms))
    first, last, halo = call(
        pack_kernel, [(full, LANES)] * 2 + [(6, levels, 8, lanes)]
    )(*block, below, above)
    from_west, from_east = swap_edges(last, first, "lon")
    inner, edges = call(
        inner_kernel,
        [(3, 4, levels, full, lanes), (6, full, LANES)],
        [(5, levels, 8, lanes), (2, levels, full, lanes)],
        flops=60 * cells,
    )(*block, halo, table, own, terms)
    state, sent = call(
        edge_kernel,
        [ocean_state.shape] * 2,
        [(4, full, LANES), (7, full, LANES)],
        sems=4,
        sent=True,
    )(inner, edges, from_west, from_east, table)

    basis = jnp.asarray(mode_basis(nlon, MAXM))
    counts = mode_counts.astype(jnp.float32)
    row_counts = lax.dynamic_slice(
        jnp.broadcast_to(counts[None], (4 * levels, rows)).reshape(total),
        (lax.axis_index("lon") * part,),
        (part,),
    )
    weights = mode_weights(row_counts, MAXM, nlon)
    circles = lax.all_to_all(
        sent.reshape(lon_peers, part, lanes), "lon", 0, 0, tiled=True
    )
    smooth = call(
        filter_kernel,
        [circles.shape],
        [circles.shape],
        sems=lon_peers // 2,
        sent=True,
    )(circles, basis, weights)[0]
    smooth = lax.all_to_all(smooth, "lon", 0, 0, tiled=True).reshape(ocean_state.shape)
    flags = jnp.broadcast_to(row_flags.astype(jnp.float32)[:, None], (rows, lanes))
    return call(blend_kernel, [ocean_state.shape], [ocean_state.shape], sems=4, sent=True)(
        state, smooth, block[2], flags
    )[0]


def solution(mesh):
    in_specs = (
        P(None, None, "lat", "lon"),
        P(None, "lat", "lon"),
        P(None, "lat", "lon"),
        P("lat"),
        P("lat"),
    )
    out_specs = P(None, None, "lat", "lon")
    return jax.shard_map(shards, mesh=mesh, in_specs=in_specs, out_specs=out_specs, check_vma=False)
```

```python
import math

import jax
import jax.numpy as jnp
import ml_dtypes
import numpy as np
from jax import lax
from jax.experimental import pallas as pl
from jax.experimental.pallas import tpu as pltpu
from jax.sharding import PartitionSpec as P

FBAND = 16
MAXM = 64
LANES = 128
GROUP = 16


lat_edge = 1.3
diffusion = 0.05
vertical_mix = 0.5
time_step = 0.05


def roll(x, shift, axis):
    shift %= x.shape[axis]
    return pltpu.roll(x, shift, axis) if shift else x


def east(x):
    return roll(x, -1, 1)


def west(x):
    return roll(x, 1, 1)


def north(x):
    return roll(x, -1, 0)


def south(x):
    return roll(x, 1, 0)


def lane_of(shape):
    return lax.broadcasted_iota(jnp.int32, shape, 1)


def east_terms(h, w, inv_c):
    open_e = 0.5 * (h + east(h)) * (w * east(w))
    return 0.25 * open_e, diffusion * open_e * inv_c


def north_terms(h, w, face):
    open_n = 0.5 * (h + north(h)) * (w * north(w)) * face
    return 0.25 * open_n, diffusion * open_n


def advance(fields, terms, scale, scale_c, vertical):
    quarter_e, spread_e, quarter_n, spread_n = terms
    u, v = fields[2], fields[3]
    speed_e = quarter_e * (u + east(u))
    speed_n = quarter_n * (v + north(v))
    here_e, there_e = speed_e + spread_e, speed_e - spread_e
    here_n, there_n = speed_n + spread_n, speed_n - spread_n
    fresh = []
    for q, vert in zip(fields, vertical):
        flux_e = here_e * q + there_e * east(q)
        flux_n = here_n * q + there_n * north(q)
        spread = (flux_e - west(flux_e)) + (flux_n - south(flux_n))
        fresh.append(q + scale * vert - scale_c * spread)
    return fresh


def own_columns(load, levels, lanes, rows):
    lane = lane_of((rows, LANES))
    own = jnp.zeros((rows, LANES), jnp.float32)
    for k in range(levels):
        x = load(k)
        at = GROUP * k + 2
        own = jnp.where((lane >= at) & (lane < at + 4), roll(x, at, 1), own)
        at = GROUP * k + 8
        own = jnp.where((lane >= at) & (lane < at + 4), roll(x, at + 4 - lanes, 1), own)
    return own


def row_terms(thick, wet, inv_c, levels, term_ref):
    w, h = wet(0), thick(0)
    hs = jnp.where(w > 0, h, 1.0)
    for k in range(levels):
        term_ref[0, k], term_ref[1, k] = east_terms(h, w, inv_c)
        scale = time_step * w / hs
        term_ref[2, k] = scale
        term_ref[3, k] = scale * inv_c
        if k + 1 < levels:
            w_next, h_next = wet(k + 1), thick(k + 1)
            hs_next = jnp.where(w_next > 0, h_next, 1.0)
            term_ref[4, k] = w * w_next * vertical_mix / (0.5 * (hs + hs_next))
            w, h, hs = w_next, h_next, hs_next


def load_kernel(
    state_any, thick_any, wet_any, state_ref, thick_ref, wet_ref, first_ref, last_ref, raw_ref, sems
):
    levels, rows = thick_ref.shape[:2]
    moves = [(wet_any, raw_ref), (thick_any, thick_ref)]
    moves += [(state_any.at[f], state_ref.at[f]) for f in range(4)]
    copies = [pltpu.make_async_copy(*pair, sems.at[i]) for i, pair in enumerate(moves)]
    for copy in copies:
        copy.start()
    copies[0].wait()
    for k in range(levels):
        wet_ref[k] = raw_ref[k].astype(jnp.float32)
    for copy in copies[1:]:
        copy.wait()
    for f in range(6):
        for k in range(levels):
            x = state_ref.at[f, k] if f < 4 else (thick_ref, wet_ref)[f - 4].at[k]
            first_ref[f, k] = x[0:2]
            last_ref[f, k] = x[rows - 2 : rows]


def ready_kernel(state_ref, thick_ref, wet_ref, table_ref, own_ref, term_ref):
    levels, rows, lanes = thick_ref.shape

    def thick(k):
        return thick_ref[k]

    def wet(k):
        return wet_ref[k]

    for f in range(4):
        own_ref[f] = own_columns(lambda k, f=f: state_ref[f, k], levels, lanes, rows)
    own_ref[4] = own_columns(thick, levels, lanes, rows)
    own_ref[5] = own_columns(wet, levels, lanes, rows)
    row_terms(thick, wet, table_ref[0, :rows], levels, term_ref)


def pack_kernel(
    state_ref, thick_ref, wet_ref, below_ref, above_ref, first_ref, last_ref, halo_ref
):
    levels, rows, lanes = thick_ref.shape
    lat_pos = lax.axis_index("lat")
    with_below = jnp.where(lat_pos > 0, 1.0, 0.0)
    with_above = jnp.where(lat_pos < lax.axis_size("lat") - 1, 1.0, 0.0)
    lane = lane_of((8, LANES))
    for f in range(6):
        for k in range(levels):
            halo_ref[f, k, 0:2] = above_ref[f, k] * with_above
            halo_ref[f, k, 2:6] = jnp.zeros((4, lanes), jnp.float32)
            halo_ref[f, k, 6:8] = below_ref[f, k] * with_below
    for t in range(rows // 8 + 1):
        first = jnp.zeros((8, LANES), jnp.float32)
        last = jnp.zeros((8, LANES), jnp.float32)
        part = slice(8 * t, 8 * t + 8)
        for f in range(6):
            for k in range(levels):
                if t == rows // 8:
                    x = halo_ref[f, k]
                elif f < 4:
                    x = state_ref[f, k, part]
                elif f == 4:
                    x = thick_ref[k, part]
                else:
                    x = wet_ref[k, part]
                at = GROUP * f + 2 * k
                mine = (lane >= at) & (lane < at + 2)
                first = jnp.where(mine, roll(x, at, 1), first)
                last = jnp.where(mine, roll(x, at + 2 - lanes, 1), last)
        first_ref[part] = first
        last_ref[part] = last


def inner_kernel(
    state_ref,
    thick_ref,
    wet_ref,
    halo_ref,
    table_ref,
    own_ref,
    term_ref,
    out_ref,
    edge_ref,
    halo_term_ref,
    north_ref,
):
    levels, rows, lanes = thick_ref.shape
    full = rows + 8
    face = table_ref[1]

    def joined(x, y):
        return jnp.concatenate([x, y], axis=0)

    def halo(f):
        return lambda k: halo_ref[f, k]

    for f in range(6):
        edge_ref[f, :rows] = own_ref[f]
        edge_ref[f, rows:] = own_columns(halo(f), levels, lanes, 8)
    row_terms(halo(4), halo(5), table_ref[0, rows:], levels, halo_term_ref)
    for k in range(levels):
        h = joined(thick_ref[k], halo_ref[4, k])
        w = joined(wet_ref[k], halo_ref[5, k])
        north_ref[0, k], north_ref[1, k] = north_terms(h, w, face)
        for f in range(4):
            out_ref[0, f, k] = joined(state_ref[f, k], halo_ref[f, k])

    def term(i, k):
        return joined(term_ref[i, k], halo_term_ref[i, k])

    def step(i, _):
        source, target = out_ref.at[i], out_ref.at[i + 1]
        fields = [source[f, 0] for f in range(4)]
        above = [jnp.zeros((full, LANES), jnp.float32)] * 4
        for k in range(levels):
            deeper = below = above
            if k + 1 < levels:
                couple = term(4, k)
                deeper = [source[f, k + 1] for f in range(4)]
                below = [couple * (d - q) for d, q in zip(deeper, fields)]
                vertical = [b - a for b, a in zip(below, above)]
            else:
                vertical = [-a for a in above]
            terms = term(0, k), term(1, k), north_ref[0, k], north_ref[1, k]
            fresh = advance(fields, terms, term(2, k), term(3, k), vertical)
            for f in range(4):
                target[f, k] = fresh[f]
            fields, above = deeper, below
        return 0

    lax.fori_loop(0, 2, step, 0)


def edge_kernel(
    inner_ref, own_ref, west_ref, east_ref, table_ref, out_ref, send_ref, tile_ref, term_ref, sems
):
    levels, rows, lanes = out_ref.shape[1:]
    full = rows + 8
    lane = lane_of((full, LANES))
    inv_c, face = table_ref[0], table_ref[1]
    from_west, from_east = west_ref[...], east_ref[...]

    def joined(f):
        x = own_ref[f]
        for k in range(levels):
            src = GROUP * f + 2 * k
            at = GROUP * k
            x = jnp.where((lane >= at) & (lane < at + 2), roll(from_west, at - src, 1), x)
            at = GROUP * k + 12
            x = jnp.where((lane >= at) & (lane < at + 2), roll(from_east, at - src, 1), x)
        return x

    def deeper(x):
        return roll(x, -GROUP, 1)

    def shallower(x):
        return roll(x, GROUP, 1)

    h, w = joined(4), joined(5)
    for f in range(4):
        tile_ref[f] = joined(f)
    hs = jnp.where(w > 0, h, 1.0)
    scale = time_step * w / hs
    couple = w * deeper(w) * vertical_mix / (0.5 * (hs + deeper(hs)))
    couple = jnp.where(lane < GROUP * (levels - 1), couple, 0.0)
    terms = east_terms(h, w, inv_c) + north_terms(h, w, face)
    for i, term in enumerate(terms + (scale, scale * inv_c, couple)):
        term_ref[i] = term

    def step(_, __):
        terms = [term_ref[i] for i in range(7)]
        fields = [tile_ref[f] for f in range(4)]
        vertical = []
        for q in fields:
            down = terms[6] * (deeper(q) - q)
            vertical.append(down - shallower(down))
        for f, q in enumerate(advance(fields, terms[:4], terms[4], terms[5], vertical)):
            tile_ref[f] = q
        return 0

    lax.fori_loop(0, 2, step, 0)
    lane = lane_of((rows, LANES))
    for f in range(4):
        x = tile_ref[f, :rows]
        for k in range(levels):
            left = roll(x, -(GROUP * k + 2), 1)
            right = roll(x, lanes - 2 - (GROUP * k + 10), 1)
            out_ref[f, k] = jnp.where(
                lane < 2,
                left,
                jnp.where(lane >= lanes - 2, right, inner_ref[2, f, k, :rows]),
            )
        pltpu.make_async_copy(out_ref.at[f], send_ref.at[f], sems.at[f]).start()
    for f in range(4):
        pltpu.make_async_copy(out_ref.at[f], send_ref.at[f], sems.at[f]).wait()


def split(x):
    high = x.astype(jnp.bfloat16)
    return high, (x - high.astype(jnp.float32)).astype(jnp.bfloat16)


def product(a, b, dims):
    return lax.dot_general(a, b, (dims, ((), ())), preferred_element_type=jnp.float32)


def filter_kernel(circle_ref, basis_ref, weight_ref, out_ref, piece_ref, sems):
    pieces, part, lanes = circle_ref.shape
    modes = weight_ref.shape[1]
    pairs = range(0, pieces, 2)
    total = jnp.zeros((2 * part, 2 * modes), jnp.float32)
    for o in pairs:
        parts = zip(split(circle_ref[o]), split(circle_ref[o + 1]))
        x = jnp.concatenate([jnp.concatenate(p, axis=1) for p in parts], axis=0)
        total = total + product(x, basis_ref[lanes * o : lanes * (o + 2)], ((1,), (0,)))
    total = total[:part] + total[part:]
    total = (total[:, :modes] + total[:, modes:]) * weight_ref[...]
    y = jnp.concatenate([jnp.concatenate([p, p], axis=1) for p in split(total)], axis=0)
    copies = []
    for o in pairs:
        x = product(y, basis_ref[lanes * o : lanes * (o + 2)], ((1,), (1,)))
        x = x[:part] + x[part:]
        piece_ref[o] = x[:, :lanes]
        piece_ref[o + 1] = x[:, lanes:]
        both = pl.ds(o, 2)
        copies.append(
            pltpu.make_async_copy(piece_ref.at[both], out_ref.at[both], sems.at[o // 2])
        )
        copies[-1].start()
    for copy in copies:
        copy.wait()


def blend_kernel(state_ref, smooth_ref, wet_ref, flag_ref, out_ref, piece_ref, sems):
    levels = wet_ref.shape[0]
    flag = flag_ref[...]
    copies = []
    for f in range(4):
        for k in range(levels):
            state = state_ref[f, k]
            gate = flag * wet_ref[k]
            piece_ref[f, k] = state + gate * (smooth_ref[f, k] - state)
        copies.append(pltpu.make_async_copy(piece_ref.at[f], out_ref.at[f], sems.at[f]))
        copies[-1].start()
    for copy in copies:
        copy.wait()


def call(kernel, outs, scratch=(), sems=0, raw=False, sent=False, flops=0):
    vmem = pl.BlockSpec(memory_space=pltpu.VMEM)
    away = pl.BlockSpec(memory_space=pl.ANY)
    specs = [vmem] * len(outs)
    if sent:
        specs[-1] = away
    buffers = [pltpu.VMEM(s, jnp.float32) if isinstance(s, tuple) else s for s in scratch]
    if sems:
        buffers.append(pltpu.SemaphoreType.DMA((sems,)))
    cost = pl.CostEstimate(
        flops=flops, transcendentals=0, bytes_accessed=4 * sum(map(math.prod, outs))
    )

    def run(*args):
        if raw:
            args = [pltpu.with_memory_space_constraint(x, pltpu.HBM) for x in args]
        return pl.pallas_call(
            kernel,
            out_shape=[jax.ShapeDtypeStruct(s, jnp.float32) for s in outs],
            in_specs=[away if raw else vmem] * len(args),
            out_specs=specs,
            scratch_shapes=buffers,
            compiler_params=pltpu.CompilerParams(vmem_limit_bytes=24 << 20),
            cost_estimate=cost,
        )(*args)

    return run


def swap_edges(before_src, after_src, axis):
    peers = lax.axis_size(axis)
    up = [(i, (i + 1) % peers) for i in range(peers)]
    down = [(j, i) for i, j in up]
    return lax.ppermute(before_src, axis, up), lax.ppermute(after_src, axis, down)


def mode_basis(length, modes):
    turns = np.arange(modes)[None, :] * np.arange(length)[:, None] % length
    angle = turns * (2.0 * math.pi / length)
    basis = np.concatenate([np.cos(angle), np.sin(angle)], axis=1).astype(np.float32)
    high = basis.astype(ml_dtypes.bfloat16)
    low = (basis - high.astype(np.float32)).astype(ml_dtypes.bfloat16)
    return np.concatenate([high, low], axis=1)


def mode_weights(counts, modes, length):
    order = jnp.arange(modes).astype(jnp.float32)
    keep = (order[None, :] < counts[:, None]).astype(jnp.float32)
    scale = jnp.where(order == 0, 1.0, 2.0) / length
    weights = keep * scale[None, :]
    return jnp.concatenate([weights, weights], axis=1)


def row_table(lat_pos, rows, nlat):
    place = np.arange(rows + 8)
    place = np.where(place < rows + 2, place, np.where(place < rows + 6, 0, place - rows - 8))
    place = (lat_pos * rows + jnp.asarray(place, jnp.int32)).astype(jnp.float32)
    centre = jnp.cos(lat_edge * (2.0 * (place + 0.5) / nlat - 1.0))
    faces = jnp.cos(lat_edge * (2.0 * (place + 1.0) / nlat - 1.0))
    table = jnp.stack([1.0 / centre, faces])
    return jnp.broadcast_to(table[:, :, None], table.shape + (LANES,))


def shards(ocean_state, thickness, wet_mask, mode_counts, row_flags):
    levels, rows, lanes = ocean_state.shape[1:]
    assert rows % 8 == 0 and lanes == LANES and levels * GROUP <= LANES
    lon_peers = lax.axis_size("lon")
    lat_peers = lax.axis_size("lat")
    nlat = rows * lat_peers
    nlon = lanes * lon_peers
    full = rows + 8
    total = 4 * levels * rows
    part = total // lon_peers
    lat_pos = lax.axis_index("lat")
    table = row_table(lat_pos, rows, nlat)
    cells = 4 * levels * full * lanes
    edge_rows = (6, levels, 2, lanes)

    *block, first, last = call(
        load_kernel,
        [ocean_state.shape, thickness.shape, thickness.shape, edge_rows, edge_rows],
        [pltpu.VMEM(thickness.shape, jnp.int32)],
        sems=6,
        raw=True,
    )(ocean_state, thickness, wet_mask)
    below, above = swap_edges(last, first, "lat")
    own, terms = call(
        ready_kernel, [(6, rows, LANES), (5, levels, rows, lanes)], flops=20 * cells
    )(*block, table)
    below, above, own, terms = lax.optimization_barrier((below, above, own, terms))
    first, last, halo = call(
        pack_kernel, [(full, LANES)] * 2 + [(6, levels, 8, lanes)]
    )(*block, below, above)
    from_west, from_east = swap_edges(last, first, "lon")
    inner, edges = call(
        inner_kernel,
        [(3, 4, levels, full, lanes), (6, full, LANES)],
        [(5, levels, 8, lanes), (2, levels, full, lanes)],
        flops=60 * cells,
    )(*block, halo, table, own, terms)
    state, sent = call(
        edge_kernel,
        [ocean_state.shape] * 2,
        [(4, full, LANES), (7, full, LANES)],
        sems=4,
        sent=True,
    )(inner, edges, from_west, from_east, table)

    basis = lax.optimization_barrier(jnp.asarray(mode_basis(nlon, MAXM)))

    def filtered(state, sent, wet):
        counts = mode_counts.astype(jnp.float32)
        row_counts = lax.dynamic_slice(
            jnp.broadcast_to(counts[None], (4 * levels, rows)).reshape(total),
            (lax.axis_index("lon") * part,),
            (part,),
        )
        weights = mode_weights(row_counts, MAXM, nlon)
        circles = lax.all_to_all(
            sent.reshape(lon_peers, part, lanes), "lon", 0, 0, tiled=True
        )
        smooth = call(
            filter_kernel, [circles.shape], [circles.shape], sems=lon_peers // 2, sent=True
        )(circles, basis, weights)[0]
        smooth = lax.all_to_all(smooth, "lon", 0, 0, tiled=True).reshape(state.shape)
        flags = jnp.broadcast_to(row_flags.astype(jnp.float32)[:, None], (rows, lanes))
        return call(blend_kernel, [state.shape], [state.shape], sems=4, sent=True)(
            state, smooth, wet, flags
        )[0]

    first_row = lat_pos * rows
    banded = (first_row < FBAND) | (first_row + rows > nlat - FBAND)
    return lax.cond(banded, filtered, lambda state, sent, wet: sent, state, sent, block[2])


def solution(mesh):
    in_specs = (
        P(None, None, "lat", "lon"),
        P(None, "lat", "lon"),
        P(None, "lat", "lon"),
        P("lat"),
        P("lat"),
    )
    out_specs = P(None, None, "lat", "lon")
    return jax.shard_map(shards, mesh=mesh, in_specs=in_specs, out_specs=out_specs, check_vma=False)
```

```python
import math

import jax
import jax.numpy as jnp
import ml_dtypes
import numpy as np
from jax import lax
from jax.experimental import pallas as pl
from jax.experimental.pallas import tpu as pltpu
from jax.sharding import PartitionSpec as P

FBAND = 16
MAXM = 64
LANES = 128
GROUP = 16


lat_edge = 1.3
diffusion = 0.05
vertical_mix = 0.5
time_step = 0.05


def roll(x, shift, axis):
    shift %= x.shape[axis]
    return pltpu.roll(x, shift, axis) if shift else x


def east(x):
    return roll(x, -1, 1)


def west(x):
    return roll(x, 1, 1)


def north(x):
    return roll(x, -1, 0)


def south(x):
    return roll(x, 1, 0)


def lane_of(shape):
    return lax.broadcasted_iota(jnp.int32, shape, 1)


def east_terms(h, w, inv_c):
    open_e = 0.5 * (h + east(h)) * (w * east(w))
    return 0.25 * open_e, diffusion * open_e * inv_c


def north_terms(h, w, face):
    open_n = 0.5 * (h + north(h)) * (w * north(w)) * face
    return 0.25 * open_n, diffusion * open_n


def advance(fields, terms, scale, scale_c, vertical):
    quarter_e, spread_e, quarter_n, spread_n = terms
    u, v = fields[2], fields[3]
    speed_e = quarter_e * (u + east(u))
    speed_n = quarter_n * (v + north(v))
    here_e, there_e = speed_e + spread_e, speed_e - spread_e
    here_n, there_n = speed_n + spread_n, speed_n - spread_n
    fresh = []
    for q, vert in zip(fields, vertical):
        flux_e = here_e * q + there_e * east(q)
        flux_n = here_n * q + there_n * north(q)
        spread = (flux_e - west(flux_e)) + (flux_n - south(flux_n))
        fresh.append(q + scale * vert - scale_c * spread)
    return fresh


def own_columns(load, levels, lanes, rows):
    lane = lane_of((rows, LANES))
    own = jnp.zeros((rows, LANES), jnp.float32)
    for k in range(levels):
        x = load(k)
        at = GROUP * k + 2
        own = jnp.where((lane >= at) & (lane < at + 4), roll(x, at, 1), own)
        at = GROUP * k + 8
        own = jnp.where((lane >= at) & (lane < at + 4), roll(x, at + 4 - lanes, 1), own)
    return own


def row_terms(thick, wet, inv_c, levels, term_ref):
    w, h = wet(0), thick(0)
    hs = jnp.where(w > 0, h, 1.0)
    for k in range(levels):
        term_ref[0, k], term_ref[1, k] = east_terms(h, w, inv_c)
        scale = time_step * w / hs
        term_ref[2, k] = scale
        term_ref[3, k] = scale * inv_c
        if k + 1 < levels:
            w_next, h_next = wet(k + 1), thick(k + 1)
            hs_next = jnp.where(w_next > 0, h_next, 1.0)
            term_ref[4, k] = w * w_next * vertical_mix / (0.5 * (hs + hs_next))
            w, h, hs = w_next, h_next, hs_next


def load_kernel(
    state_any, thick_any, wet_any, state_ref, thick_ref, wet_ref, first_ref, last_ref, raw_ref, sems
):
    levels, rows = thick_ref.shape[:2]
    moves = [(wet_any, raw_ref), (thick_any, thick_ref)]
    moves += [(state_any.at[f], state_ref.at[f]) for f in range(4)]
    copies = [pltpu.make_async_copy(*pair, sems.at[i]) for i, pair in enumerate(moves)]
    for copy in copies:
        copy.start()
    copies[0].wait()
    for k in range(levels):
        wet_ref[k] = raw_ref[k].astype(jnp.float32)
    for copy in copies[1:]:
        copy.wait()
    for f in range(6):
        for k in range(levels):
            x = state_ref.at[f, k] if f < 4 else (thick_ref, wet_ref)[f - 4].at[k]
            first_ref[f, k] = x[0:2]
            last_ref[f, k] = x[rows - 2 : rows]


def ready_kernel(state_ref, thick_ref, wet_ref, table_ref, own_ref, term_ref):
    levels, rows, lanes = thick_ref.shape

    def thick(k):
        return thick_ref[k]

    def wet(k):
        return wet_ref[k]

    for f in range(4):
        own_ref[f] = own_columns(lambda k, f=f: state_ref[f, k], levels, lanes, rows)
    own_ref[4] = own_columns(thick, levels, lanes, rows)
    own_ref[5] = own_columns(wet, levels, lanes, rows)
    row_terms(thick, wet, table_ref[0, :rows], levels, term_ref)


def pack_kernel(state_ref, thick_ref, wet_ref, halo_ref, first_ref, last_ref):
    levels, rows, lanes = thick_ref.shape
    lane = lane_of((8, LANES))
    for t in range(rows // 8 + 1):
        first = jnp.zeros((8, LANES), jnp.float32)
        last = jnp.zeros((8, LANES), jnp.float32)
        part = slice(8 * t, 8 * t + 8)
        for f in range(6):
            for k in range(levels):
                if t == rows // 8:
                    x = halo_ref[f, k]
                elif f < 4:
                    x = state_ref[f, k, part]
                elif f == 4:
                    x = thick_ref[k, part]
                else:
                    x = wet_ref[k, part]
                at = GROUP * f + 2 * k
                mine = (lane >= at) & (lane < at + 2)
                first = jnp.where(mine, roll(x, at, 1), first)
                last = jnp.where(mine, roll(x, at + 2 - lanes, 1), last)
        first_ref[part] = first
        last_ref[part] = last


def inner_kernel(
    state_ref,
    thick_ref,
    wet_ref,
    below_ref,
    above_ref,
    table_ref,
    own_ref,
    term_ref,
    out_ref,
    edge_ref,
    halo_ref,
    halo_term_ref,
    north_ref,
):
    levels, rows, lanes = thick_ref.shape
    full = rows + 8
    face = table_ref[1]
    lat_pos = lax.axis_index("lat")
    with_below = jnp.where(lat_pos > 0, 1.0, 0.0)
    with_above = jnp.where(lat_pos < lax.axis_size("lat") - 1, 1.0, 0.0)
    for f in range(6):
        for k in range(levels):
            halo_ref[f, k, 0:2] = above_ref[f, k] * with_above
            halo_ref[f, k, 2:6] = jnp.zeros((4, lanes), jnp.float32)
            halo_ref[f, k, 6:8] = below_ref[f, k] * with_below

    def joined(x, y):
        return jnp.concatenate([x, y], axis=0)

    def halo(f):
        return lambda k: halo_ref[f, k]

    for f in range(6):
        edge_ref[f, :rows] = own_ref[f]
        edge_ref[f, rows:] = own_columns(halo(f), levels, lanes, 8)
    row_terms(halo(4), halo(5), table_ref[0, rows:], levels, halo_term_ref)
    for k in range(levels):
        h = joined(thick_ref[k], halo_ref[4, k])
        w = joined(wet_ref[k], halo_ref[5, k])
        north_ref[0, k], north_ref[1, k] = north_terms(h, w, face)
        for f in range(4):
            out_ref[0, f, k] = joined(state_ref[f, k], halo_ref[f, k])

    def term(i, k):
        return joined(term_ref[i, k], halo_term_ref[i, k])

    def step(i, _):
        source, target = out_ref.at[i], out_ref.at[i + 1]
        fields = [source[f, 0] for f in range(4)]
        above = [jnp.zeros((full, LANES), jnp.float32)] * 4
        for k in range(levels):
            deeper = below = above
            if k + 1 < levels:
                couple = term(4, k)
                deeper = [source[f, k + 1] for f in range(4)]
                below = [couple * (d - q) for d, q in zip(deeper, fields)]
                vertical = [b - a for b, a in zip(below, above)]
            else:
                vertical = [-a for a in above]
            terms = term(0, k), term(1, k), north_ref[0, k], north_ref[1, k]
            fresh = advance(fields, terms, term(2, k), term(3, k), vertical)
            for f in range(4):
                target[f, k] = fresh[f]
            fields, above = deeper, below
        return 0

    lax.fori_loop(0, 2, step, 0)


def step_tile(tile_ref, h, w, levels, table_ref, term_ref):
    inv_c, face = table_ref[0], table_ref[1]
    lane = lane_of(h.shape)

    def deeper(x):
        return roll(x, -GROUP, 1)

    def shallower(x):
        return roll(x, GROUP, 1)

    hs = jnp.where(w > 0, h, 1.0)
    scale = time_step * w / hs
    couple = w * deeper(w) * vertical_mix / (0.5 * (hs + deeper(hs)))
    couple = jnp.where(lane < GROUP * (levels - 1), couple, 0.0)
    terms = east_terms(h, w, inv_c) + north_terms(h, w, face)
    for i, term in enumerate(terms + (scale, scale * inv_c, couple)):
        term_ref[i] = term

    def step(_, __):
        terms = [term_ref[i] for i in range(7)]
        fields = [tile_ref[f] for f in range(4)]
        vertical = []
        for q in fields:
            down = terms[6] * (deeper(q) - q)
            vertical.append(down - shallower(down))
        for f, q in enumerate(advance(fields, terms[:4], terms[4], terms[5], vertical)):
            tile_ref[f] = q
        return 0

    lax.fori_loop(0, 2, step, 0)


def edge_kernel(
    inner_ref, own_ref, west_ref, east_ref, table_ref, out_ref, send_ref, tile_ref, term_ref, sems
):
    levels, rows, lanes = out_ref.shape[1:]
    full = rows + 8
    lane = lane_of((full, LANES))
    from_west, from_east = west_ref[...], east_ref[...]

    def joined(f):
        x = own_ref[f]
        for k in range(levels):
            src = GROUP * f + 2 * k
            at = GROUP * k
            x = jnp.where((lane >= at) & (lane < at + 2), roll(from_west, at - src, 1), x)
            at = GROUP * k + 12
            x = jnp.where((lane >= at) & (lane < at + 2), roll(from_east, at - src, 1), x)
        return x

    for f in range(4):
        tile_ref[f] = joined(f)
    step_tile(tile_ref, joined(4), joined(5), levels, table_ref, term_ref)
    lane = lane_of((rows, LANES))
    for f in range(4):
        x = tile_ref[f, :rows]
        for k in range(levels):
            left = roll(x, -(GROUP * k + 2), 1)
            right = roll(x, lanes - 2 - (GROUP * k + 10), 1)
            out_ref[f, k] = jnp.where(
                lane < 2,
                left,
                jnp.where(lane >= lanes - 2, right, inner_ref[2, f, k, :rows]),
            )
        pltpu.make_async_copy(out_ref.at[f], send_ref.at[f], sems.at[f]).start()
    for f in range(4):
        pltpu.make_async_copy(out_ref.at[f], send_ref.at[f], sems.at[f]).wait()


def split(x):
    high = x.astype(jnp.bfloat16)
    return high, (x - high.astype(jnp.float32)).astype(jnp.bfloat16)


def product(a, b, dims):
    return lax.dot_general(a, b, (dims, ((), ())), preferred_element_type=jnp.float32)


def within(lane, low, high):
    c = lane % GROUP
    return (c >= low) & (c < high)


def pairs_of_rows(tiles, t, place):
    sub = lax.broadcasted_iota(jnp.int32, tiles[0].shape, 0) // 2
    for y in range(4):
        made = roll(tiles[0], -2 * y, 0)
        for x in range(1, 4):
            made = jnp.where(sub == x, roll(tiles[x], 2 * (x - y), 0), made)
        place(y, made)


def send_kernel(inner_ref, own_ref, out_ref, piece_ref, raw_ref, sems):
    levels, full = inner_ref.shape[2:4]
    rows = full - 8
    peers = out_ref.shape[0]
    main = 8 * levels
    c = lane_of((full, LANES)) % GROUP
    for i in range(3):
        a, b = own_ref[2 * i], own_ref[2 * i + 1]
        one = jnp.where(c < 4, roll(a, -2, 1), roll(a, -4, 1))
        two = jnp.where(c < 12, roll(b, 6, 1), roll(b, 4, 1))
        both = jnp.where(c < 8, one, two)
        raw_ref[i, 0:2] = both[full - 2 : full]
        raw_ref[i, 2 : rows + 4] = both[: rows + 2]
        raw_ref[i, rows + 4 : full] = jnp.zeros((4, LANES), jnp.float32)
    copies = []
    for t in range(rows // 8):
        for k in range(levels):
            tiles = [inner_ref[2, f, k, 8 * t : 8 * t + 8] for f in range(4)]

            def place(y, tile, t=t, k=k):
                piece_ref[4 * t + y, 8 * k : 8 * k + 8] = tile

            pairs_of_rows(tiles, t, place)
        for p in range(4 * t, 4 * t + 4):
            for i in range(3):
                piece_ref[p, main + 8 * i : main + 8 * i + 8] = raw_ref[i, 2 * p : 2 * p + 8]
        part = pl.ds(4 * t, 4)
        copies.append(pltpu.make_async_copy(piece_ref.at[part], out_ref.at[part], sems.at[t]))
        copies[-1].start()
    assert 4 * (rows // 8) == peers
    for copy in copies:
        copy.wait()


def circle_kernel(
    circle_ref,
    table_ref,
    basis_ref,
    joint_basis_ref,
    weight_ref,
    out_ref,
    tile_ref,
    term_ref,
    joint_ref,
    piece_ref,
    sems,
):
    peers = circle_ref.shape[0]
    main, modes = weight_ref.shape
    levels = main // 8
    lanes = LANES
    lane = lane_of((8, LANES))
    left, right = within(lane, 4, 8), within(lane, 8, 12)
    for o in range(peers):
        after = (o + 1) % peers
        for i in range(3):
            at = pl.ds(main + 8 * i, 8)
            x, y = circle_ref[o, at], circle_ref[after, at]
            one = jnp.where(left, x, jnp.where(right, roll(y, 8, 1), 0.0))
            two = jnp.where(left, roll(x, -8, 1), jnp.where(right, y, 0.0))
            tile_ref[2 * i, 8 * o : 8 * o + 8] = one
            tile_ref[2 * i + 1, 8 * o : 8 * o + 8] = two
    step_tile(tile_ref, tile_ref[4], tile_ref[5], levels, table_ref, term_ref)
    sub = lax.broadcasted_iota(jnp.int32, (8, LANES), 0) // 2
    for o in range(peers):
        made = jnp.zeros((8, LANES), jnp.float32)
        for f in range(4):
            x = tile_ref[f, 8 * o : 8 * o + 8]
            made = jnp.where(sub == f, roll(x, 2 * f - 2, 0), made)
        joint_ref[8 * o : 8 * o + 8] = jnp.where(within(lane, 6, 10), made, 0.0)
    lane_main = lane_of((main, LANES))
    inside = (lane_main >= 2) & (lane_main < lanes - 2)
    level = lax.broadcasted_iota(jnp.int32, (main, LANES), 0) // 8
    at_level = lane_main // GROUP == level

    def block(o):
        return jnp.where(inside, circle_ref[o, :main], 0.0)

    def joint(o):
        x = joint_ref[8 * o : 8 * o + 8]
        return jnp.where(at_level, jnp.concatenate([x] * levels, axis=0), 0.0)

    total = jnp.zeros((2 * main, 2 * modes), jnp.float32)
    for o in range(0, peers, 2):
        span = slice(lanes * o, lanes * (o + 2))
        for source, basis in ((block, basis_ref), (joint, joint_basis_ref)):
            parts = zip(split(source(o)), split(source(o + 1)))
            x = jnp.concatenate([jnp.concatenate(p, axis=1) for p in parts], axis=0)
            total = total + product(x, basis[span], ((1,), (0,)))
    total = total[:main] + total[main:]
    total = (total[:, :modes] + total[:, modes:]) * weight_ref[...]
    y = jnp.concatenate([jnp.concatenate([p, p], axis=1) for p in split(total)], axis=0)
    copies = []
    for o in range(0, peers, 2):
        x = product(y, basis_ref[lanes * o : lanes * (o + 2)], ((1,), (1,)))
        x = x[:main] + x[main:]
        for i in range(2):
            before = (o + i - 1) % peers
            piece_ref[o + i, :main] = x[:, lanes * i : lanes * (i + 1)]
            piece_ref[o + i, main:] = jnp.where(
                lane % GROUP < 8,
                joint_ref[8 * (o + i) : 8 * (o + i) + 8],
                joint_ref[8 * before : 8 * before + 8],
            )
        both = pl.ds(o, 2)
        copies.append(
            pltpu.make_async_copy(piece_ref.at[both], out_ref.at[both], sems.at[o // 2])
        )
        copies[-1].start()
    for copy in copies:
        copy.wait()


def join_kernel(inner_ref, piece_ref, wet_ref, flag_ref, out_ref, made_ref, sems):
    levels, rows, lanes = wet_ref.shape
    main = 8 * levels
    lane = lane_of((8, LANES))

    def edges_of(t, into):
        tiles = [piece_ref[4 * t + x, main : main + 8] for x in range(4)]
        pairs_of_rows(tiles, t, into)

    for t in range(rows // 8):
        part = slice(8 * t, 8 * t + 8)
        flag = flag_ref[part]
        edges = {}
        edges_of(t, edges.__setitem__)
        for k in range(levels):
            tiles = [piece_ref[4 * t + x, 8 * k : 8 * k + 8] for x in range(4)]
            gate = flag * wet_ref[k, part]

            def place(f, smooth, k=k, gate=gate, part=part, edges=edges):
                first = roll(edges[f], -(GROUP * k + 8), 1)
                last = roll(edges[f], lanes - 2 - (GROUP * k + 6), 1)
                state = jnp.where(
                    lane < 2,
                    first,
                    jnp.where(lane >= lanes - 2, last, inner_ref[2, f, k, part]),
                )
                made_ref[f, k, part] = state + gate * (smooth - state)

            pairs_of_rows(tiles, t, place)
    copies = []
    for f in range(4):
        copies.append(pltpu.make_async_copy(made_ref.at[f], out_ref.at[f], sems.at[f]))
        copies[-1].start()
    for copy in copies:
        copy.wait()


def filter_kernel(circle_ref, basis_ref, weight_ref, out_ref, piece_ref, sems):
    pieces, part, lanes = circle_ref.shape
    modes = weight_ref.shape[1]
    pairs = range(0, pieces, 2)
    total = jnp.zeros((2 * part, 2 * modes), jnp.float32)
    for o in pairs:
        parts = zip(split(circle_ref[o]), split(circle_ref[o + 1]))
        x = jnp.concatenate([jnp.concatenate(p, axis=1) for p in parts], axis=0)
        total = total + product(x, basis_ref[lanes * o : lanes * (o + 2)], ((1,), (0,)))
    total = total[:part] + total[part:]
    total = (total[:, :modes] + total[:, modes:]) * weight_ref[...]
    y = jnp.concatenate([jnp.concatenate([p, p], axis=1) for p in split(total)], axis=0)
    copies = []
    for o in pairs:
        x = product(y, basis_ref[lanes * o : lanes * (o + 2)], ((1,), (1,)))
        x = x[:part] + x[part:]
        piece_ref[o] = x[:, :lanes]
        piece_ref[o + 1] = x[:, lanes:]
        both = pl.ds(o, 2)
        copies.append(
            pltpu.make_async_copy(piece_ref.at[both], out_ref.at[both], sems.at[o // 2])
        )
        copies[-1].start()
    for copy in copies:
        copy.wait()


def blend_kernel(state_ref, smooth_ref, wet_ref, flag_ref, out_ref, piece_ref, sems):
    levels = wet_ref.shape[0]
    flag = flag_ref[...]
    copies = []
    for f in range(4):
        for k in range(levels):
            state = state_ref[f, k]
            gate = flag * wet_ref[k]
            piece_ref[f, k] = state + gate * (smooth_ref[f, k] - state)
        copies.append(pltpu.make_async_copy(piece_ref.at[f], out_ref.at[f], sems.at[f]))
        copies[-1].start()
    for copy in copies:
        copy.wait()


def call(kernel, outs, scratch=(), sems=0, raw=False, sent=False, flops=0):
    vmem = pl.BlockSpec(memory_space=pltpu.VMEM)
    away = pl.BlockSpec(memory_space=pl.ANY)
    specs = [vmem] * len(outs)
    if sent:
        specs[-1] = away
    buffers = [pltpu.VMEM(s, jnp.float32) if isinstance(s, tuple) else s for s in scratch]
    if sems:
        buffers.append(pltpu.SemaphoreType.DMA((sems,)))
    cost = pl.CostEstimate(
        flops=flops, transcendentals=0, bytes_accessed=4 * sum(map(math.prod, outs))
    )

    def run(*args):
        if raw:
            args = [pltpu.with_memory_space_constraint(x, pltpu.HBM) for x in args]
        return pl.pallas_call(
            kernel,
            out_shape=[jax.ShapeDtypeStruct(s, jnp.float32) for s in outs],
            in_specs=[away if raw else vmem] * len(args),
            out_specs=specs,
            scratch_shapes=buffers,
            compiler_params=pltpu.CompilerParams(vmem_limit_bytes=24 << 20),
            cost_estimate=cost,
        )(*args)

    return run


def swap_edges(before_src, after_src, axis):
    peers = lax.axis_size(axis)
    up = [(i, (i + 1) % peers) for i in range(peers)]
    down = [(j, i) for i, j in up]
    return lax.ppermute(before_src, axis, up), lax.ppermute(after_src, axis, down)


def mode_basis(length, modes):
    turns = np.arange(modes)[None, :] * np.arange(length)[:, None] % length
    angle = turns * (2.0 * math.pi / length)
    basis = np.concatenate([np.cos(angle), np.sin(angle)], axis=1).astype(np.float32)
    high = basis.astype(ml_dtypes.bfloat16)
    low = (basis - high.astype(np.float32)).astype(ml_dtypes.bfloat16)
    return np.concatenate([high, low], axis=1)


def joint_basis(basis, lanes):
    length = basis.shape[0]
    joint, lane = np.divmod(np.arange(length), lanes)
    c = lane % GROUP
    column = (lanes * (joint + 1) + c - 8) % length
    return np.where(((c >= 6) & (c < 10))[:, None], basis[column], np.zeros_like(basis))


def mode_weights(counts, modes, length):
    order = jnp.arange(modes).astype(jnp.float32)
    keep = (order[None, :] < counts[:, None]).astype(jnp.float32)
    scale = jnp.where(order == 0, 1.0, 2.0) / length
    weights = keep * scale[None, :]
    return jnp.concatenate([weights, weights], axis=1)


def row_table(place, nlat):
    place = place.astype(jnp.float32)
    centre = jnp.cos(lat_edge * (2.0 * (place + 0.5) / nlat - 1.0))
    faces = jnp.cos(lat_edge * (2.0 * (place + 1.0) / nlat - 1.0))
    table = jnp.stack([1.0 / centre, faces])
    return jnp.broadcast_to(table[:, :, None], table.shape + (LANES,))


def ring_rows(rows):
    place = np.arange(rows + 8)
    return np.where(place < rows + 2, place, np.where(place < rows + 6, 0, place - rows - 8))


def shards(ocean_state, thickness, wet_mask, mode_counts, row_flags):
    levels, rows, lanes = ocean_state.shape[1:]
    assert rows % 8 == 0 and lanes == LANES and levels * GROUP <= LANES
    lon_peers = lax.axis_size("lon")
    lat_peers = lax.axis_size("lat")
    nlat = rows * lat_peers
    nlon = lanes * lon_peers
    full = rows + 8
    total = 4 * levels * rows
    part = total // lon_peers
    lat_pos = lax.axis_index("lat")
    first_row = lat_pos * rows
    table = row_table(first_row + jnp.asarray(ring_rows(rows), jnp.int32), nlat)
    cells = 4 * levels * full * lanes
    edge_rows = (6, levels, 2, lanes)

    *block, first, last = call(
        load_kernel,
        [ocean_state.shape, thickness.shape, thickness.shape, edge_rows, edge_rows],
        [pltpu.VMEM(thickness.shape, jnp.int32)],
        sems=6,
        raw=True,
    )(ocean_state, thickness, wet_mask)
    below, above = swap_edges(last, first, "lat")
    own, terms = call(
        ready_kernel, [(6, rows, LANES), (5, levels, rows, lanes)], flops=20 * cells
    )(*block, table)
    below, above, own, terms = lax.optimization_barrier((below, above, own, terms))
    inner, edges, halo = call(
        inner_kernel,
        [(3, 4, levels, full, lanes), (6, full, LANES), (6, levels, 8, lanes)],
        [(5, levels, 8, lanes), (2, levels, full, lanes)],
        flops=60 * cells,
    )(*block, below, above, table, own, terms)

    def exchanged():
        first, last = call(pack_kernel, [(full, LANES)] * 2)(*block, halo)
        from_west, from_east = swap_edges(last, first, "lon")
        return call(
            edge_kernel,
            [ocean_state.shape] * 2,
            [(4, full, LANES), (7, full, LANES)],
            sems=4,
            sent=True,
        )(inner, edges, from_west, from_east, table)

    banded = (first_row < FBAND) | (first_row + rows > nlat - FBAND)
    flags = jnp.broadcast_to(row_flags.astype(jnp.float32)[:, None], (rows, lanes))
    counts = mode_counts.astype(jnp.float32)
    modes = mode_basis(nlon, MAXM)
    basis, at_joints = lax.optimization_barrier(
        (jnp.asarray(modes), jnp.asarray(joint_basis(modes, lanes)))
    )
    lon_pos = lax.axis_index("lon")

    def circled():
        main = 8 * levels
        sent = call(
            send_kernel,
            [(lon_peers, main + 24, lanes)],
            [(lon_peers, main + 24, lanes), (3, full, lanes)],
            sems=rows // 8,
            sent=True,
        )(inner, edges)[0]
        circles = lax.all_to_all(sent, "lon", 0, 0, tiled=True)
        place = first_row + 2 * lon_pos - 2 + jnp.minimum(jnp.arange(8, dtype=jnp.int32), 5)
        joint_table = jnp.tile(row_table(place, nlat), (1, lon_peers, 1))
        row_counts = jnp.tile(lax.dynamic_slice(counts, (2 * lon_pos,), (2,)), 4 * levels)
        pieces = call(
            circle_kernel,
            [(lon_peers, main + 8, lanes)],
            [
                (6, 8 * lon_peers, lanes),
                (7, 8 * lon_peers, lanes),
                (8 * lon_peers, lanes),
                (lon_peers, main + 8, lanes),
            ],
            sems=lon_peers // 2,
            sent=True,
        )(circles, joint_table, basis, at_joints, mode_weights(row_counts, MAXM, nlon))[0]
        pieces = lax.all_to_all(pieces, "lon", 0, 0, tiled=True)
        return call(join_kernel, [ocean_state.shape], [ocean_state.shape], sems=4, sent=True)(
            inner, pieces, block[2], flags
        )[0]

    if rows == 2 * lon_peers:
        return lax.cond(banded, circled, lambda: exchanged()[1])

    state, sent = exchanged()

    def filtered():
        row_counts = lax.dynamic_slice(
            jnp.broadcast_to(counts[None], (4 * levels, rows)).reshape(total),
            (lon_pos * part,),
            (part,),
        )
        circles = lax.all_to_all(
            sent.reshape(lon_peers, part, lanes), "lon", 0, 0, tiled=True
        )
        smooth = call(
            filter_kernel, [circles.shape], [circles.shape], sems=lon_peers // 2, sent=True
        )(circles, basis, mode_weights(row_counts, MAXM, nlon))[0]
        smooth = lax.all_to_all(smooth, "lon", 0, 0, tiled=True).reshape(state.shape)
        return call(blend_kernel, [state.shape], [state.shape], sems=4, sent=True)(
            state, smooth, block[2], flags
        )[0]

    return lax.cond(banded, filtered, lambda: sent)


def solution(mesh):
    in_specs = (
        P(None, None, "lat", "lon"),
        P(None, "lat", "lon"),
        P(None, "lat", "lon"),
        P("lat"),
        P("lat"),
    )
    out_specs = P(None, None, "lat", "lon")
    return jax.shard_map(shards, mesh=mesh, in_specs=in_specs, out_specs=out_specs, check_vma=False)
```

```python
import math

import jax
import jax.numpy as jnp
import ml_dtypes
import numpy as np
from jax import lax
from jax.experimental import pallas as pl
from jax.experimental.pallas import tpu as pltpu
from jax.sharding import PartitionSpec as P

FBAND = 16
MAXM = 64
LANES = 128
GROUP = 16


lat_edge = 1.3
diffusion = 0.05
vertical_mix = 0.5
time_step = 0.05


def roll(x, shift, axis):
    shift %= x.shape[axis]
    return pltpu.roll(x, shift, axis) if shift else x


def east(x):
    return roll(x, -1, 1)


def west(x):
    return roll(x, 1, 1)


def north(x):
    return roll(x, -1, 0)


def south(x):
    return roll(x, 1, 0)


def lane_of(shape):
    return lax.broadcasted_iota(jnp.int32, shape, 1)


def east_terms(h, w, inv_c):
    open_e = 0.5 * (h + east(h)) * (w * east(w))
    return 0.25 * open_e, diffusion * open_e * inv_c


def north_terms(h, w, face):
    open_n = 0.5 * (h + north(h)) * (w * north(w)) * face
    return 0.25 * open_n, diffusion * open_n


def advance(fields, terms, scale, scale_c, vertical):
    quarter_e, spread_e, quarter_n, spread_n = terms
    u, v = fields[2], fields[3]
    speed_e = quarter_e * (u + east(u))
    speed_n = quarter_n * (v + north(v))
    here_e, there_e = speed_e + spread_e, speed_e - spread_e
    here_n, there_n = speed_n + spread_n, speed_n - spread_n
    fresh = []
    for q, vert in zip(fields, vertical):
        flux_e = here_e * q + there_e * east(q)
        flux_n = here_n * q + there_n * north(q)
        spread = (flux_e - west(flux_e)) + (flux_n - south(flux_n))
        fresh.append(q + scale * vert - scale_c * spread)
    return fresh


def own_columns(load, levels, lanes, rows):
    lane = lane_of((rows, LANES))
    own = jnp.zeros((rows, LANES), jnp.float32)
    for k in range(levels):
        x = load(k)
        at = GROUP * k + 2
        own = jnp.where((lane >= at) & (lane < at + 4), roll(x, at, 1), own)
        at = GROUP * k + 8
        own = jnp.where((lane >= at) & (lane < at + 4), roll(x, at + 4 - lanes, 1), own)
    return own


def row_terms(thick, wet, inv_c, levels, term_ref):
    w, h = wet(0), thick(0)
    hs = jnp.where(w > 0, h, 1.0)
    for k in range(levels):
        term_ref[0, k], term_ref[1, k] = east_terms(h, w, inv_c)
        scale = time_step * w / hs
        term_ref[2, k] = scale
        term_ref[3, k] = scale * inv_c
        if k + 1 < levels:
            w_next, h_next = wet(k + 1), thick(k + 1)
            hs_next = jnp.where(w_next > 0, h_next, 1.0)
            term_ref[4, k] = w * w_next * vertical_mix / (0.5 * (hs + hs_next))
            w, h, hs = w_next, h_next, hs_next


def load_kernel(
    state_any,
    thick_any,
    wet_any,
    flag_any,
    count_any,
    state_ref,
    thick_ref,
    wet_ref,
    first_ref,
    last_ref,
    flag_ref,
    count_ref,
    raw_ref,
    raw_flag_ref,
    raw_count_ref,
    sems,
):
    levels, rows = thick_ref.shape[:2]
    moves = [(flag_any, raw_flag_ref), (count_any, raw_count_ref), (wet_any, raw_ref)]
    moves += [(thick_any, thick_ref)]
    moves += [(state_any.at[f], state_ref.at[f]) for f in range(4)]
    copies = [pltpu.make_async_copy(*pair, sems.at[i]) for i, pair in enumerate(moves)]
    for copy in copies:
        copy.start()
    for copy in copies[:3]:
        copy.wait()
    shape = (rows, rows)
    diagonal = lax.broadcasted_iota(jnp.int32, shape, 0) == lane_of(shape)
    for raw, ref in ((raw_flag_ref, flag_ref), (raw_count_ref, count_ref)):
        spread = jnp.broadcast_to(raw[...].astype(jnp.float32), shape)
        value = jnp.sum(jnp.where(diagonal, spread, 0.0), axis=1, keepdims=True)
        ref[...] = jnp.broadcast_to(value, (rows, LANES))
    for k in range(levels):
        wet_ref[k] = raw_ref[k].astype(jnp.float32)
    for copy in copies[3:]:
        copy.wait()
    for f in range(6):
        for k in range(levels):
            x = state_ref.at[f, k] if f < 4 else (thick_ref, wet_ref)[f - 4].at[k]
            first_ref[f, k] = x[0:2]
            last_ref[f, k] = x[rows - 2 : rows]


def ready_kernel(state_ref, thick_ref, wet_ref, table_ref, own_ref, term_ref):
    levels, rows, lanes = thick_ref.shape

    def thick(k):
        return thick_ref[k]

    def wet(k):
        return wet_ref[k]

    for f in range(4):
        own_ref[f] = own_columns(lambda k, f=f: state_ref[f, k], levels, lanes, rows)
    own_ref[4] = own_columns(thick, levels, lanes, rows)
    own_ref[5] = own_columns(wet, levels, lanes, rows)
    row_terms(thick, wet, table_ref[0, :rows], levels, term_ref)


def pack_kernel(state_ref, thick_ref, wet_ref, halo_ref, first_ref, last_ref):
    levels, rows, lanes = thick_ref.shape
    lane = lane_of((8, LANES))
    for t in range(rows // 8 + 1):
        first = jnp.zeros((8, LANES), jnp.float32)
        last = jnp.zeros((8, LANES), jnp.float32)
        part = slice(8 * t, 8 * t + 8)
        for f in range(6):
            for k in range(levels):
                if t == rows // 8:
                    x = halo_ref[f, k]
                elif f < 4:
                    x = state_ref[f, k, part]
                elif f == 4:
                    x = thick_ref[k, part]
                else:
                    x = wet_ref[k, part]
                at = GROUP * f + 2 * k
                mine = (lane >= at) & (lane < at + 2)
                first = jnp.where(mine, roll(x, at, 1), first)
                last = jnp.where(mine, roll(x, at + 2 - lanes, 1), last)
        first_ref[part] = first
        last_ref[part] = last


def inner_kernel(
    state_ref,
    thick_ref,
    wet_ref,
    below_ref,
    above_ref,
    table_ref,
    own_ref,
    term_ref,
    out_ref,
    edge_ref,
    halo_ref,
    halo_term_ref,
    north_ref,
):
    levels, rows, lanes = thick_ref.shape
    full = rows + 8
    face = table_ref[1]
    lat_pos = lax.axis_index("lat")
    with_below = jnp.where(lat_pos > 0, 1.0, 0.0)
    with_above = jnp.where(lat_pos < lax.axis_size("lat") - 1, 1.0, 0.0)
    for f in range(6):
        for k in range(levels):
            halo_ref[f, k, 0:2] = above_ref[f, k] * with_above
            halo_ref[f, k, 2:6] = jnp.zeros((4, lanes), jnp.float32)
            halo_ref[f, k, 6:8] = below_ref[f, k] * with_below

    def joined(x, y):
        return jnp.concatenate([x, y], axis=0)

    def halo(f):
        return lambda k: halo_ref[f, k]

    for f in range(6):
        edge_ref[f, :rows] = own_ref[f]
        edge_ref[f, rows:] = own_columns(halo(f), levels, lanes, 8)
    row_terms(halo(4), halo(5), table_ref[0, rows:], levels, halo_term_ref)
    for k in range(levels):
        h = joined(thick_ref[k], halo_ref[4, k])
        w = joined(wet_ref[k], halo_ref[5, k])
        north_ref[0, k], north_ref[1, k] = north_terms(h, w, face)
        for f in range(4):
            out_ref[0, f, k] = joined(state_ref[f, k], halo_ref[f, k])

    def term(i, k):
        return joined(term_ref[i, k], halo_term_ref[i, k])

    def step(i, _):
        source, target = out_ref.at[i], out_ref.at[i + 1]
        fields = [source[f, 0] for f in range(4)]
        above = [jnp.zeros((full, LANES), jnp.float32)] * 4
        for k in range(levels):
            deeper = below = above
            if k + 1 < levels:
                couple = term(4, k)
                deeper = [source[f, k + 1] for f in range(4)]
                below = [couple * (d - q) for d, q in zip(deeper, fields)]
                vertical = [b - a for b, a in zip(below, above)]
            else:
                vertical = [-a for a in above]
            terms = term(0, k), term(1, k), north_ref[0, k], north_ref[1, k]
            fresh = advance(fields, terms, term(2, k), term(3, k), vertical)
            for f in range(4):
                target[f, k] = fresh[f]
            fields, above = deeper, below
        return 0

    lax.fori_loop(0, 2, step, 0)


def step_tile(tile_ref, h, w, levels, table_ref, term_ref):
    inv_c, face = table_ref[0], table_ref[1]
    lane = lane_of(h.shape)

    def deeper(x):
        return roll(x, -GROUP, 1)

    def shallower(x):
        return roll(x, GROUP, 1)

    hs = jnp.where(w > 0, h, 1.0)
    scale = time_step * w / hs
    couple = w * deeper(w) * vertical_mix / (0.5 * (hs + deeper(hs)))
    couple = jnp.where(lane < GROUP * (levels - 1), couple, 0.0)
    terms = east_terms(h, w, inv_c) + north_terms(h, w, face)
    for i, term in enumerate(terms + (scale, scale * inv_c, couple)):
        term_ref[i] = term

    def step(_, __):
        terms = [term_ref[i] for i in range(7)]
        fields = [tile_ref[f] for f in range(4)]
        vertical = []
        for q in fields:
            down = terms[6] * (deeper(q) - q)
            vertical.append(down - shallower(down))
        for f, q in enumerate(advance(fields, terms[:4], terms[4], terms[5], vertical)):
            tile_ref[f] = q
        return 0

    lax.fori_loop(0, 2, step, 0)


def edge_kernel(
    inner_ref, own_ref, west_ref, east_ref, table_ref, out_ref, send_ref, tile_ref, term_ref, sems
):
    levels, rows, lanes = out_ref.shape[1:]
    full = rows + 8
    lane = lane_of((full, LANES))
    from_west, from_east = west_ref[...], east_ref[...]

    def joined(f):
        x = own_ref[f]
        for k in range(levels):
            src = GROUP * f + 2 * k
            at = GROUP * k
            x = jnp.where((lane >= at) & (lane < at + 2), roll(from_west, at - src, 1), x)
            at = GROUP * k + 12
            x = jnp.where((lane >= at) & (lane < at + 2), roll(from_east, at - src, 1), x)
        return x

    for f in range(4):
        tile_ref[f] = joined(f)
    step_tile(tile_ref, joined(4), joined(5), levels, table_ref, term_ref)
    lane = lane_of((rows, LANES))
    for f in range(4):
        x = tile_ref[f, :rows]
        for k in range(levels):
            left = roll(x, -(GROUP * k + 2), 1)
            right = roll(x, lanes - 2 - (GROUP * k + 10), 1)
            out_ref[f, k] = jnp.where(
                lane < 2,
                left,
                jnp.where(lane >= lanes - 2, right, inner_ref[2, f, k, :rows]),
            )
        pltpu.make_async_copy(out_ref.at[f], send_ref.at[f], sems.at[f]).start()
    for f in range(4):
        pltpu.make_async_copy(out_ref.at[f], send_ref.at[f], sems.at[f]).wait()


def split(x):
    high = x.astype(jnp.bfloat16)
    return high, (x - high.astype(jnp.float32)).astype(jnp.bfloat16)


def product(a, b, dims):
    return lax.dot_general(a, b, (dims, ((), ())), preferred_element_type=jnp.float32)


def pairs_of_rows(tiles, t, place):
    sub = lax.broadcasted_iota(jnp.int32, tiles[0].shape, 0) // 2
    for y in range(4):
        made = roll(tiles[0], -2 * y, 0)
        for x in range(1, 4):
            made = jnp.where(sub == x, roll(tiles[x], 2 * (x - y), 0), made)
        place(y, made)


def send_kernel(inner_ref, own_ref, out_ref, raw_ref):
    levels, full = inner_ref.shape[2:4]
    rows = full - 8
    main = 8 * levels
    c = lane_of((full, LANES)) % GROUP
    for i in range(3):
        a, b = own_ref[2 * i], own_ref[2 * i + 1]
        one = jnp.where(c < 4, roll(a, -2, 1), roll(a, -4, 1))
        two = jnp.where(c < 12, roll(b, 6, 1), roll(b, 4, 1))
        both = jnp.where(c < 8, one, two)
        raw_ref[i, 0:2] = both[full - 2 : full]
        raw_ref[i, 2 : rows + 4] = both[: rows + 2]
        raw_ref[i, rows + 4 : full] = jnp.zeros((4, LANES), jnp.float32)
    for t in range(rows // 8):
        for k in range(levels):
            tiles = [inner_ref[2, f, k, 8 * t : 8 * t + 8] for f in range(4)]

            def place(y, tile, t=t, k=k):
                out_ref[4 * t + y, 8 * k : 8 * k + 8] = tile

            pairs_of_rows(tiles, t, place)
        for p in range(4 * t, 4 * t + 4):
            for i in range(3):
                out_ref[p, main + 8 * i : main + 8 * i + 8] = raw_ref[i, 2 * p : 2 * p + 8]


def circle_kernel(
    circle_ref,
    table_ref,
    basis_ref,
    joint_basis_ref,
    count_ref,
    out_ref,
    tile_ref,
    term_ref,
    joint_ref,
):
    peers = circle_ref.shape[0]
    modes = basis_ref.shape[1] // 2
    length = basis_ref.shape[0]
    main = circle_ref.shape[1] - 24
    levels = main // 8
    lanes = LANES
    lane = lane_of((8, LANES))
    c = lane % GROUP
    for j in range(0, peers, 2):
        part = slice(4 * j, 4 * j + 8)
        for i in range(3):
            x, y, z = (
                circle_ref[(j + d) % peers, main + 8 * i : main + 8 * i + 8] for d in range(3)
            )
            for f, shift in ((2 * i, 0), (2 * i + 1, -8)):
                middle = jnp.where(c < 12, roll(y, 4 + shift, 1), roll(z, 12 + shift, 1))
                tile_ref[f, part] = jnp.where(c < 4, roll(x, shift - 4, 1), middle)
    step_tile(tile_ref, tile_ref[4], tile_ref[5], levels, table_ref, term_ref)
    sub = lax.broadcasted_iota(jnp.int32, (8, LANES), 0) // 2
    right = (c % 8 >= 2) & (c % 8 < 6)
    for j in range(peers // 2):
        made = jnp.zeros((8, LANES), jnp.float32)
        for f in range(4):
            x = tile_ref[f, 8 * j : 8 * j + 8]
            made = jnp.where(sub == f, roll(x, 2 * f - 2, 0), made)
        joint_ref[8 * j : 8 * j + 8] = jnp.where(right, made, 0.0)
    lane_main = lane_of((main, LANES))
    row_main = lax.broadcasted_iota(jnp.int32, (main, LANES), 0)
    inside = (lane_main >= 2) & (lane_main < lanes - 2)
    at_level = lane_main // GROUP == row_main // 8

    def block(o):
        return jnp.where(inside, circle_ref[o, :main], 0.0)

    def joint(j):
        x = joint_ref[8 * j : 8 * j + 8]
        return jnp.where(at_level, jnp.concatenate([x] * levels, axis=0), 0.0)

    total = jnp.zeros((2 * main, 2 * modes), jnp.float32)
    for source, basis, count in (
        (block, basis_ref, peers),
        (joint, joint_basis_ref, peers // 2),
    ):
        for o in range(0, count, 2):
            parts = zip(split(source(o)), split(source(o + 1)))
            x = jnp.concatenate([jnp.concatenate(p, axis=1) for p in parts], axis=0)
            total = total + product(x, basis[lanes * o : lanes * (o + 2)], ((1,), (0,)))
    total = total[:main] + total[main:]
    counts = count_ref[...]
    row = lax.broadcasted_iota(jnp.int32, counts.shape, 0)
    own = 2 * lax.axis_index("lon")
    even, odd = (
        jnp.sum(jnp.where(row == own + r, counts, 0.0), axis=0, keepdims=True) for r in (0, 1)
    )
    limit = jnp.where(row_main % 2 == 0, even, odd)
    order = (lane_main % (modes // 2)).astype(jnp.float32)
    weight = jnp.where(order < limit, jnp.where(order == 0.0, 1.0 / length, 2.0 / length), 0.0)
    total = (total[:, :modes] + total[:, modes:]) * weight
    y = jnp.concatenate([jnp.concatenate([p, p], axis=1) for p in split(total)], axis=0)
    for o in range(0, peers, 2):
        x = product(y, basis_ref[lanes * o : lanes * (o + 2)], ((1,), (1,)))
        x = x[:main] + x[main:]
        out_ref[o, :main] = x[:, :lanes]
        out_ref[o + 1, :main] = x[:, lanes:]
        before = (4 * o - 8) % (4 * peers)
        here = joint_ref[4 * o : 4 * o + 8]
        out_ref[o, main:] = jnp.where(
            c < 8, roll(joint_ref[before : before + 8], -8, 1), roll(here, 8, 1)
        )
        out_ref[o + 1, main:] = here


def join_kernel(inner_ref, piece_ref, wet_ref, flag_ref, out_ref, made_ref, sems):
    levels, rows, lanes = wet_ref.shape
    main = 8 * levels
    lane = lane_of((8, LANES))

    def edges_of(t, into):
        tiles = [piece_ref[4 * t + x, main : main + 8] for x in range(4)]
        pairs_of_rows(tiles, t, into)

    for t in range(rows // 8):
        part = slice(8 * t, 8 * t + 8)
        flag = flag_ref[part]
        edges = {}
        edges_of(t, edges.__setitem__)
        for k in range(levels):
            tiles = [piece_ref[4 * t + x, 8 * k : 8 * k + 8] for x in range(4)]
            gate = flag * wet_ref[k, part]

            def place(f, smooth, k=k, gate=gate, part=part, edges=edges):
                first = roll(edges[f], -(GROUP * k + 4), 1)
                last = roll(edges[f], lanes - 2 - (GROUP * k + 10), 1)
                state = jnp.where(
                    lane < 2,
                    first,
                    jnp.where(lane >= lanes - 2, last, inner_ref[2, f, k, part]),
                )
                made_ref[f, k, part] = state + gate * (smooth - state)

            pairs_of_rows(tiles, t, place)
    copies = []
    for f in range(4):
        copies.append(pltpu.make_async_copy(made_ref.at[f], out_ref.at[f], sems.at[f]))
        copies[-1].start()
    for copy in copies:
        copy.wait()


def filter_kernel(circle_ref, basis_ref, weight_ref, out_ref, piece_ref, sems):
    pieces, part, lanes = circle_ref.shape
    modes = weight_ref.shape[1]
    pairs = range(0, pieces, 2)
    total = jnp.zeros((2 * part, 2 * modes), jnp.float32)
    for o in pairs:
        parts = zip(split(circle_ref[o]), split(circle_ref[o + 1]))
        x = jnp.concatenate([jnp.concatenate(p, axis=1) for p in parts], axis=0)
        total = total + product(x, basis_ref[lanes * o : lanes * (o + 2)], ((1,), (0,)))
    total = total[:part] + total[part:]
    total = (total[:, :modes] + total[:, modes:]) * weight_ref[...]
    y = jnp.concatenate([jnp.concatenate([p, p], axis=1) for p in split(total)], axis=0)
    copies = []
    for o in pairs:
        x = product(y, basis_ref[lanes * o : lanes * (o + 2)], ((1,), (1,)))
        x = x[:part] + x[part:]
        piece_ref[o] = x[:, :lanes]
        piece_ref[o + 1] = x[:, lanes:]
        both = pl.ds(o, 2)
        copies.append(
            pltpu.make_async_copy(piece_ref.at[both], out_ref.at[both], sems.at[o // 2])
        )
        copies[-1].start()
    for copy in copies:
        copy.wait()


def blend_kernel(state_ref, smooth_ref, wet_ref, flag_ref, out_ref, piece_ref, sems):
    levels = wet_ref.shape[0]
    flag = flag_ref[...]
    copies = []
    for f in range(4):
        for k in range(levels):
            state = state_ref[f, k]
            gate = flag * wet_ref[k]
            piece_ref[f, k] = state + gate * (smooth_ref[f, k] - state)
        copies.append(pltpu.make_async_copy(piece_ref.at[f], out_ref.at[f], sems.at[f]))
        copies[-1].start()
    for copy in copies:
        copy.wait()


def call(kernel, outs, scratch=(), sems=0, raw=False, sent=False, flops=0):
    vmem = pl.BlockSpec(memory_space=pltpu.VMEM)
    away = pl.BlockSpec(memory_space=pl.ANY)
    specs = [vmem] * len(outs)
    shapes = [jax.ShapeDtypeStruct(s, jnp.float32) for s in outs]
    if sent:
        specs[-1] = away
        shapes[-1] = pltpu.HBM(outs[-1], jnp.float32)
    buffers = [pltpu.VMEM(s, jnp.float32) if isinstance(s, tuple) else s for s in scratch]
    if sems:
        buffers.append(pltpu.SemaphoreType.DMA((sems,)))
    cost = pl.CostEstimate(
        flops=flops, transcendentals=0, bytes_accessed=4 * sum(map(math.prod, outs))
    )

    def run(*args):
        if raw:
            args = [pltpu.with_memory_space_constraint(x, pltpu.HBM) for x in args]
        return pl.pallas_call(
            kernel,
            out_shape=shapes,
            in_specs=[away if raw else vmem] * len(args),
            out_specs=specs,
            scratch_shapes=buffers,
            compiler_params=pltpu.CompilerParams(vmem_limit_bytes=24 << 20),
            cost_estimate=cost,
        )(*args)

    return run


def swap_edges(before_src, after_src, axis):
    peers = lax.axis_size(axis)
    up = [(i, (i + 1) % peers) for i in range(peers)]
    down = [(j, i) for i, j in up]
    return lax.ppermute(before_src, axis, up), lax.ppermute(after_src, axis, down)


def mode_basis(length, modes):
    turns = np.arange(modes)[None, :] * np.arange(length)[:, None] % length
    angle = turns * (2.0 * math.pi / length)
    basis = np.concatenate([np.cos(angle), np.sin(angle)], axis=1).astype(np.float32)
    high = basis.astype(ml_dtypes.bfloat16)
    low = (basis - high.astype(np.float32)).astype(ml_dtypes.bfloat16)
    return np.concatenate([high, low], axis=1)


def joint_basis(basis, lanes):
    length = basis.shape[0]
    tile, lane = np.divmod(np.arange(length // 2), lanes)
    half, c = np.divmod(lane % GROUP, 8)
    column = (lanes * (2 * tile + half + 1) + c - 4) % length
    return np.where(((c >= 2) & (c < 6))[:, None], basis[column], np.zeros_like(basis[column]))


def mode_weights(counts, modes, length):
    order = jnp.arange(modes).astype(jnp.float32)
    keep = (order[None, :] < counts[:, None]).astype(jnp.float32)
    scale = jnp.where(order == 0, 1.0, 2.0) / length
    weights = keep * scale[None, :]
    return jnp.concatenate([weights, weights], axis=1)


def row_table(place, nlat):
    place = place.astype(jnp.float32)
    centre = jnp.cos(lat_edge * (2.0 * (place + 0.5) / nlat - 1.0))
    faces = jnp.cos(lat_edge * (2.0 * (place + 1.0) / nlat - 1.0))
    table = jnp.stack([1.0 / centre, faces])
    return jnp.broadcast_to(table[:, :, None], table.shape + (LANES,))


def ring_rows(rows):
    place = jnp.arange(rows + 8, dtype=jnp.int32)
    return jnp.where(place < rows + 2, place, jnp.where(place < rows + 6, 0, place - rows - 8))


def shards(ocean_state, thickness, wet_mask, mode_counts, row_flags):
    levels, rows, lanes = ocean_state.shape[1:]
    assert rows % 8 == 0 and lanes == LANES and levels * GROUP <= LANES
    lon_peers = lax.axis_size("lon")
    lat_peers = lax.axis_size("lat")
    nlat = rows * lat_peers
    nlon = lanes * lon_peers
    full = rows + 8
    total = 4 * levels * rows
    part = total // lon_peers
    lat_pos = lax.axis_index("lat")
    first_row = lat_pos * rows
    table = row_table(first_row + ring_rows(rows), nlat)
    cells = 4 * levels * full * lanes
    edge_rows = (6, levels, 2, lanes)

    *block, first, last, flags, counts = call(
        load_kernel,
        [ocean_state.shape, thickness.shape, thickness.shape, edge_rows, edge_rows]
        + [(rows, lanes)] * 2,
        [pltpu.VMEM(shape, jnp.int32) for shape in (thickness.shape, (1, rows), (1, rows))],
        sems=8,
        raw=True,
    )(ocean_state, thickness, wet_mask, row_flags[None], mode_counts[None])
    below, above = swap_edges(last, first, "lat")
    own, terms = call(
        ready_kernel, [(6, rows, LANES), (5, levels, rows, lanes)], flops=20 * cells
    )(*block, table)
    below, above, own, terms = lax.optimization_barrier((below, above, own, terms))
    inner, edges, halo = call(
        inner_kernel,
        [(3, 4, levels, full, lanes), (6, full, LANES), (6, levels, 8, lanes)],
        [(5, levels, 8, lanes), (2, levels, full, lanes)],
        flops=60 * cells,
    )(*block, below, above, table, own, terms)

    def exchanged():
        first, last = call(pack_kernel, [(full, LANES)] * 2)(*block, halo)
        from_west, from_east = swap_edges(last, first, "lon")
        return call(
            edge_kernel,
            [ocean_state.shape] * 2,
            [(4, full, LANES), (7, full, LANES)],
            sems=4,
            sent=True,
        )(inner, edges, from_west, from_east, table)

    banded = (first_row < FBAND) | (first_row + rows > nlat - FBAND)
    modes = mode_basis(nlon, MAXM)
    basis, at_joints = lax.optimization_barrier(
        (jnp.asarray(modes), jnp.asarray(joint_basis(modes, lanes)))
    )
    lon_pos = lax.axis_index("lon")
    place = first_row + 2 * lon_pos - 2 + jnp.arange(4 * lon_peers, dtype=jnp.int32) % 8
    joint_table = row_table(jnp.minimum(place, first_row + 2 * lon_pos + 3), nlat)

    def circled():
        main = 8 * levels
        sent = call(
            send_kernel, [(lon_peers, main + 24, lanes)], [(3, full, lanes)]
        )(inner, edges)[0]
        circles = lax.all_to_all(sent, "lon", 0, 0, tiled=True)
        pieces = call(
            circle_kernel,
            [(lon_peers, main + 8, lanes)],
            [
                (6, 4 * lon_peers, lanes),
                (7, 4 * lon_peers, lanes),
                (4 * lon_peers, lanes),
            ],
        )(circles, joint_table, basis, at_joints, counts)[0]
        pieces = lax.all_to_all(pieces, "lon", 0, 0, tiled=True)
        return call(join_kernel, [ocean_state.shape], [ocean_state.shape], sems=4, sent=True)(
            inner, pieces, block[2], flags
        )[0]

    if rows == 2 * lon_peers:
        return lax.cond(banded, circled, lambda: exchanged()[1])

    state, sent = exchanged()

    def filtered():
        row_counts = lax.dynamic_slice(
            jnp.broadcast_to(
                mode_counts.astype(jnp.float32)[None], (4 * levels, rows)
            ).reshape(total),
            (lon_pos * part,),
            (part,),
        )
        circles = lax.all_to_all(
            sent.reshape(lon_peers, part, lanes), "lon", 0, 0, tiled=True
        )
        smooth = call(
            filter_kernel, [circles.shape], [circles.shape], sems=lon_peers // 2, sent=True
        )(circles, basis, mode_weights(row_counts, MAXM, nlon))[0]
        smooth = lax.all_to_all(smooth, "lon", 0, 0, tiled=True).reshape(state.shape)
        return call(blend_kernel, [state.shape], [state.shape], sems=4, sent=True)(
            state, smooth, block[2], flags
        )[0]

    return lax.cond(banded, filtered, lambda: sent)


def solution(mesh):
    in_specs = (
        P(None, None, "lat", "lon"),
        P(None, "lat", "lon"),
        P(None, "lat", "lon"),
        P("lat"),
        P("lat"),
    )
    out_specs = P(None, None, "lat", "lon")
    return jax.shard_map(shards, mesh=mesh, in_specs=in_specs, out_specs=out_specs, check_vma=False)
```

```python
import functools
import math

import jax
import jax.numpy as jnp
import ml_dtypes
import numpy as np
from jax import lax
from jax.experimental import pallas as pl
from jax.experimental.pallas import tpu as pltpu
from jax.sharding import PartitionSpec as P

FBAND = 16
MAXM = 64
LANES = 128
GROUP = 16


lat_edge = 1.3
diffusion = 0.05
vertical_mix = 0.5
time_step = 0.05


def roll(x, shift, axis):
    shift %= x.shape[axis]
    return pltpu.roll(x, shift, axis) if shift else x


def east(x):
    return roll(x, -1, 1)


def west(x):
    return roll(x, 1, 1)


def north(x):
    return roll(x, -1, 0)


def south(x):
    return roll(x, 1, 0)


def lane_of(shape):
    return lax.broadcasted_iota(jnp.int32, shape, 1)


def east_terms(h, w, inv_c):
    open_e = 0.5 * (h + east(h)) * (w * east(w))
    return 0.25 * open_e, diffusion * open_e * inv_c


def north_terms(h, w, face):
    open_n = 0.5 * (h + north(h)) * (w * north(w)) * face
    return 0.25 * open_n, diffusion * open_n


def advance(fields, terms, scale, scale_c, vertical):
    quarter_e, spread_e, quarter_n, spread_n = terms
    u, v = fields[2], fields[3]
    speed_e = quarter_e * (u + east(u))
    speed_n = quarter_n * (v + north(v))
    here_e, there_e = speed_e + spread_e, speed_e - spread_e
    here_n, there_n = speed_n + spread_n, speed_n - spread_n
    fresh = []
    for q, vert in zip(fields, vertical):
        flux_e = here_e * q + there_e * east(q)
        flux_n = here_n * q + there_n * north(q)
        spread = (flux_e - west(flux_e)) + (flux_n - south(flux_n))
        fresh.append(q + scale * vert - scale_c * spread)
    return fresh


def own_columns(load, levels, lanes, rows):
    lane = lane_of((rows, LANES))
    own = jnp.zeros((rows, LANES), jnp.float32)
    for k in range(levels):
        x = load(k)
        at = GROUP * k + 2
        own = jnp.where((lane >= at) & (lane < at + 4), roll(x, at, 1), own)
        at = GROUP * k + 8
        own = jnp.where((lane >= at) & (lane < at + 4), roll(x, at + 4 - lanes, 1), own)
    return own


def row_terms(thick, wet, inv_c, levels, term_ref):
    w, h = wet(0), thick(0)
    hs = jnp.where(w > 0, h, 1.0)
    for k in range(levels):
        term_ref[0, k], term_ref[1, k] = east_terms(h, w, inv_c)
        scale = time_step * w / hs
        term_ref[2, k] = scale
        term_ref[3, k] = scale * inv_c
        if k + 1 < levels:
            w_next, h_next = wet(k + 1), thick(k + 1)
            hs_next = jnp.where(w_next > 0, h_next, 1.0)
            term_ref[4, k] = w * w_next * vertical_mix / (0.5 * (hs + hs_next))
            w, h, hs = w_next, h_next, hs_next


def load_kernel(
    paired,
    state_any,
    thick_any,
    wet_any,
    flag_any,
    count_any,
    state_ref,
    thick_ref,
    wet_ref,
    first_ref,
    last_ref,
    flag_ref,
    count_ref,
    raw_ref,
    raw_flag_ref,
    raw_count_ref,
    sems,
):
    levels, rows = thick_ref.shape[:2]
    moves = [(flag_any, raw_flag_ref), (count_any, raw_count_ref), (wet_any, raw_ref)]
    moves += [(thick_any, thick_ref)]
    moves += [(state_any.at[f], state_ref.at[f]) for f in range(4)]
    copies = [pltpu.make_async_copy(*pair, sems.at[i]) for i, pair in enumerate(moves)]
    for copy in copies:
        copy.start()
    for copy in copies[:3]:
        copy.wait()
    shape = (rows, rows)
    diagonal = lax.broadcasted_iota(jnp.int32, shape, 0) == lane_of(shape)
    for raw, ref in ((raw_flag_ref, flag_ref), (raw_count_ref, count_ref)):
        spread = jnp.broadcast_to(raw[...].astype(jnp.float32), shape)
        value = jnp.sum(jnp.where(diagonal, spread, 0.0), axis=1, keepdims=True)
        ref[...] = jnp.broadcast_to(value, (rows, LANES))
    for k in range(levels):
        wet_ref[k] = raw_ref[k].astype(jnp.float32)
    for copy in copies[3:]:
        copy.wait()
    for f in range(6):
        for k in range(levels):
            x = state_ref.at[f, k] if f < 4 else (thick_ref, wet_ref)[f - 4].at[k]
            first_ref[f, k] = x[0:2]
            last_ref[f, k] = x[rows - 2 : rows]
    if paired:
        even = lax.axis_index("lat") % 2 == 0
        for f in range(6):
            for k in range(levels):
                low, high = first_ref[f, k], last_ref[f, k]
                first_ref[f, k] = jnp.where(even, high, low)
                last_ref[f, k] = jnp.where(even, low, high)


def ready_kernel(state_ref, thick_ref, wet_ref, table_ref, own_ref, term_ref):
    levels, rows, lanes = thick_ref.shape

    def thick(k):
        return thick_ref[k]

    def wet(k):
        return wet_ref[k]

    for f in range(4):
        own_ref[f] = own_columns(lambda k, f=f: state_ref[f, k], levels, lanes, rows)
    own_ref[4] = own_columns(thick, levels, lanes, rows)
    own_ref[5] = own_columns(wet, levels, lanes, rows)
    row_terms(thick, wet, table_ref[0, :rows], levels, term_ref)


def pack_kernel(state_ref, thick_ref, wet_ref, halo_ref, first_ref, last_ref):
    levels, rows, lanes = thick_ref.shape
    lane = lane_of((8, LANES))
    for t in range(rows // 8 + 1):
        first = jnp.zeros((8, LANES), jnp.float32)
        last = jnp.zeros((8, LANES), jnp.float32)
        part = slice(8 * t, 8 * t + 8)
        for f in range(6):
            for k in range(levels):
                if t == rows // 8:
                    x = halo_ref[f, k]
                elif f < 4:
                    x = state_ref[f, k, part]
                elif f == 4:
                    x = thick_ref[k, part]
                else:
                    x = wet_ref[k, part]
                at = GROUP * f + 2 * k
                mine = (lane >= at) & (lane < at + 2)
                first = jnp.where(mine, roll(x, at, 1), first)
                last = jnp.where(mine, roll(x, at + 2 - lanes, 1), last)
        first_ref[part] = first
        last_ref[part] = last


def inner_kernel(
    state_ref,
    thick_ref,
    wet_ref,
    below_ref,
    above_ref,
    table_ref,
    own_ref,
    term_ref,
    out_ref,
    edge_ref,
    halo_ref,
    halo_term_ref,
    north_ref,
):
    levels, rows, lanes = thick_ref.shape
    full = rows + 8
    face = table_ref[1]
    lat_pos = lax.axis_index("lat")
    with_below = jnp.where(lat_pos > 0, 1.0, 0.0)
    with_above = jnp.where(lat_pos < lax.axis_size("lat") - 1, 1.0, 0.0)
    for f in range(6):
        for k in range(levels):
            halo_ref[f, k, 0:2] = above_ref[f, k] * with_above
            halo_ref[f, k, 2:6] = jnp.zeros((4, lanes), jnp.float32)
            halo_ref[f, k, 6:8] = below_ref[f, k] * with_below

    def joined(x, y):
        return jnp.concatenate([x, y], axis=0)

    def halo(f):
        return lambda k: halo_ref[f, k]

    for f in range(6):
        edge_ref[f, :rows] = own_ref[f]
        edge_ref[f, rows:] = own_columns(halo(f), levels, lanes, 8)
    row_terms(halo(4), halo(5), table_ref[0, rows:], levels, halo_term_ref)
    for k in range(levels):
        h = joined(thick_ref[k], halo_ref[4, k])
        w = joined(wet_ref[k], halo_ref[5, k])
        north_ref[0, k], north_ref[1, k] = north_terms(h, w, face)
        for f in range(4):
            out_ref[0, f, k] = joined(state_ref[f, k], halo_ref[f, k])

    def term(i, k):
        return joined(term_ref[i, k], halo_term_ref[i, k])

    def step(i, _):
        source, target = out_ref.at[i], out_ref.at[i + 1]
        fields = [source[f, 0] for f in range(4)]
        above = [jnp.zeros((full, LANES), jnp.float32)] * 4
        for k in range(levels):
            deeper = below = above
            if k + 1 < levels:
                couple = term(4, k)
                deeper = [source[f, k + 1] for f in range(4)]
                below = [couple * (d - q) for d, q in zip(deeper, fields)]
                vertical = [b - a for b, a in zip(below, above)]
            else:
                vertical = [-a for a in above]
            terms = term(0, k), term(1, k), north_ref[0, k], north_ref[1, k]
            fresh = advance(fields, terms, term(2, k), term(3, k), vertical)
            for f in range(4):
                target[f, k] = fresh[f]
            fields, above = deeper, below
        return 0

    lax.fori_loop(0, 2, step, 0)


def step_tile(tile_ref, h, w, levels, table_ref, term_ref):
    inv_c, face = table_ref[0], table_ref[1]
    lane = lane_of(h.shape)

    def deeper(x):
        return roll(x, -GROUP, 1)

    def shallower(x):
        return roll(x, GROUP, 1)

    hs = jnp.where(w > 0, h, 1.0)
    scale = time_step * w / hs
    couple = w * deeper(w) * vertical_mix / (0.5 * (hs + deeper(hs)))
    couple = jnp.where(lane < GROUP * (levels - 1), couple, 0.0)
    terms = east_terms(h, w, inv_c) + north_terms(h, w, face)
    for i, term in enumerate(terms + (scale, scale * inv_c, couple)):
        term_ref[i] = term

    def step(_, __):
        terms = [term_ref[i] for i in range(7)]
        fields = [tile_ref[f] for f in range(4)]
        vertical = []
        for q in fields:
            down = terms[6] * (deeper(q) - q)
            vertical.append(down - shallower(down))
        for f, q in enumerate(advance(fields, terms[:4], terms[4], terms[5], vertical)):
            tile_ref[f] = q
        return 0

    lax.fori_loop(0, 2, step, 0)


def edge_kernel(
    inner_ref, own_ref, west_ref, east_ref, table_ref, out_ref, send_ref, tile_ref, term_ref, sems
):
    levels, rows, lanes = out_ref.shape[1:]
    full = rows + 8
    lane = lane_of((full, LANES))
    from_west, from_east = west_ref[...], east_ref[...]

    def joined(f):
        x = own_ref[f]
        for k in range(levels):
            src = GROUP * f + 2 * k
            at = GROUP * k
            x = jnp.where((lane >= at) & (lane < at + 2), roll(from_west, at - src, 1), x)
            at = GROUP * k + 12
            x = jnp.where((lane >= at) & (lane < at + 2), roll(from_east, at - src, 1), x)
        return x

    for f in range(4):
        tile_ref[f] = joined(f)
    step_tile(tile_ref, joined(4), joined(5), levels, table_ref, term_ref)
    lane = lane_of((rows, LANES))
    for f in range(4):
        x = tile_ref[f, :rows]
        for k in range(levels):
            left = roll(x, -(GROUP * k + 2), 1)
            right = roll(x, lanes - 2 - (GROUP * k + 10), 1)
            out_ref[f, k] = jnp.where(
                lane < 2,
                left,
                jnp.where(lane >= lanes - 2, right, inner_ref[2, f, k, :rows]),
            )
        pltpu.make_async_copy(out_ref.at[f], send_ref.at[f], sems.at[f]).start()
    for f in range(4):
        pltpu.make_async_copy(out_ref.at[f], send_ref.at[f], sems.at[f]).wait()


def split(x):
    high = x.astype(jnp.bfloat16)
    return high, (x - high.astype(jnp.float32)).astype(jnp.bfloat16)


def product(a, b, dims):
    return lax.dot_general(a, b, (dims, ((), ())), preferred_element_type=jnp.float32)


def pairs_of_rows(tiles, t, place):
    sub = lax.broadcasted_iota(jnp.int32, tiles[0].shape, 0) // 2
    for y in range(4):
        made = roll(tiles[0], -2 * y, 0)
        for x in range(1, 4):
            made = jnp.where(sub == x, roll(tiles[x], 2 * (x - y), 0), made)
        place(y, made)


def step_levels(buf_ref, term_ref):
    levels, size = buf_ref.shape[2:4]

    def step(i, _):
        source, target = buf_ref.at[i], buf_ref.at[i + 1]
        fields = [source[f, 0] for f in range(4)]
        above = [jnp.zeros((size, LANES), jnp.float32)] * 4
        for k in range(levels):
            deeper = below = above
            if k + 1 < levels:
                couple = term_ref[4, k]
                deeper = [source[f, k + 1] for f in range(4)]
                below = [couple * (d - q) for d, q in zip(deeper, fields)]
                vertical = [b - a for b, a in zip(below, above)]
            else:
                vertical = [-a for a in above]
            terms = [term_ref[i, k] for i in (0, 1, 5, 6)]
            fresh = advance(fields, terms, term_ref[2, k], term_ref[3, k], vertical)
            for f in range(4):
                target[f, k] = fresh[f]
            fields, above = deeper, below
        return 0

    lax.fori_loop(0, 2, step, 0)


def closed_kernel(state_ref, thick_ref, wet_ref, table_ref, own_ref, buf_ref, term_ref):
    levels, rows, lanes = thick_ref.shape

    def thick(k):
        return thick_ref[k]

    def wet(k):
        return wet_ref[k]

    for f in range(4):
        own_ref[f] = own_columns(lambda k, f=f: state_ref[f, k], levels, lanes, rows)
    own_ref[4] = own_columns(thick, levels, lanes, rows)
    own_ref[5] = own_columns(wet, levels, lanes, rows)
    row_terms(thick, wet, table_ref[0, :rows], levels, term_ref)
    row = lax.broadcasted_iota(jnp.int32, (rows, LANES), 0)
    face = jnp.where(row < rows - 1, table_ref[1, :rows], 0.0)
    for k in range(levels):
        term_ref[5, k], term_ref[6, k] = north_terms(thick(k), wet(k), face)
        for f in range(4):
            buf_ref[0, f, k] = state_ref[f, k]
    step_levels(buf_ref, term_ref)


def end_kernel(
    state_ref,
    thick_ref,
    wet_ref,
    got_ref,
    own_ref,
    closed_ref,
    table_ref,
    out_ref,
    send_ref,
    field_ref,
    halo_ref,
    buf_ref,
    term_ref,
    raw_ref,
):
    levels, rows, lanes = thick_ref.shape
    full = rows + 8
    top = lax.axis_index("lat") == 0
    at_top = jnp.where(top, 1.0, 0.0)
    at_bottom = jnp.where(top, 0.0, 1.0)
    sub = lax.broadcasted_iota(jnp.int32, (8, LANES), 0)

    def own(f, k, part):
        return state_ref[f, k, part] if f < 4 else (thick_ref, wet_ref)[f - 4][k, part]

    for f in range(6):
        for k in range(levels):
            halo_ref[f, k, 0:2] = got_ref[f, k] * at_top
            halo_ref[f, k, 2:6] = jnp.zeros((4, lanes), jnp.float32)
            halo_ref[f, k, 6:8] = got_ref[f, k] * at_bottom
    for f in range(6):
        for k in range(levels):
            halo = halo_ref[f, k]
            beyond = jnp.where(sub < 6, roll(halo, 4, 0), 0.0)
            high = jnp.where(sub < 4, roll(own(f, k, slice(rows - 8, rows)), -4, 0), beyond)
            low = jnp.where(sub < 2, roll(halo, 2, 0), roll(own(f, k, slice(0, 8)), 2, 0))
            tile = jnp.where(top, high, low)
            if f < 4:
                buf_ref[0, f, k] = tile
            else:
                field_ref[f - 4, k] = tile

    def thick(k):
        return field_ref[0, k]

    def wet(k):
        return field_ref[1, k]

    row_terms(thick, wet, table_ref[0], levels, term_ref)
    for k in range(levels):
        term_ref[5, k], term_ref[6, k] = north_terms(thick(k), wet(k), table_ref[1])
    step_levels(buf_ref, term_ref)
    c = lane_of((full, LANES)) % GROUP

    def ring(f):
        beyond = own_columns(lambda k: halo_ref[f, k], levels, lanes, 8)
        return jnp.concatenate([own_ref[f], beyond], axis=0)

    for i in range(3):
        a, b = ring(2 * i), ring(2 * i + 1)
        one = jnp.where(c < 4, roll(a, -2, 1), roll(a, -4, 1))
        two = jnp.where(c < 12, roll(b, 6, 1), roll(b, 4, 1))
        both = jnp.where(c < 8, one, two)
        raw_ref[i, 0:2] = both[full - 2 : full]
        raw_ref[i, 2 : rows + 4] = both[: rows + 2]
        raw_ref[i, rows + 4 : full] = jnp.zeros((4, LANES), jnp.float32)
    main = 8 * levels
    last = rows // 8 - 1
    for t in range(rows // 8):
        part = slice(8 * t, 8 * t + 8)
        for k in range(levels):
            tiles = []
            for f in range(4):
                x = closed_ref[2, f, k, part]
                if t == last:
                    fixed = jnp.where(sub >= 6, roll(buf_ref[2, f, k], 4, 0), x)
                    x = jnp.where(top, fixed, x)
                if t == 0:
                    fixed = jnp.where(sub < 2, roll(buf_ref[2, f, k], -2, 0), x)
                    x = jnp.where(top, x, fixed)
                out_ref[f, k, part] = x
                tiles.append(x)

            def place(y, tile, t=t, k=k):
                send_ref[4 * t + y, 8 * k : 8 * k + 8] = tile

            pairs_of_rows(tiles, t, place)
        for p in range(4 * t, 4 * t + 4):
            for i in range(3):
                send_ref[p, main + 8 * i : main + 8 * i + 8] = raw_ref[i, 2 * p : 2 * p + 8]


def circle_kernel(
    circle_ref,
    table_ref,
    basis_ref,
    joint_basis_ref,
    count_ref,
    out_ref,
    tile_ref,
    term_ref,
    joint_ref,
):
    peers = circle_ref.shape[0]
    modes = basis_ref.shape[1] // 2
    length = basis_ref.shape[0]
    main = circle_ref.shape[1] - 24
    levels = main // 8
    lanes = LANES
    lane = lane_of((8, LANES))
    c = lane % GROUP
    for j in range(0, peers, 2):
        part = slice(4 * j, 4 * j + 8)
        for i in range(3):
            x, y, z = (
                circle_ref[(j + d) % peers, main + 8 * i : main + 8 * i + 8] for d in range(3)
            )
            for f, shift in ((2 * i, 0), (2 * i + 1, -8)):
                middle = jnp.where(c < 12, roll(y, 4 + shift, 1), roll(z, 12 + shift, 1))
                tile_ref[f, part] = jnp.where(c < 4, roll(x, shift - 4, 1), middle)
    step_tile(tile_ref, tile_ref[4], tile_ref[5], levels, table_ref, term_ref)
    sub = lax.broadcasted_iota(jnp.int32, (8, LANES), 0) // 2
    right = (c % 8 >= 2) & (c % 8 < 6)
    for j in range(peers // 2):
        made = jnp.zeros((8, LANES), jnp.float32)
        for f in range(4):
            x = tile_ref[f, 8 * j : 8 * j + 8]
            made = jnp.where(sub == f, roll(x, 2 * f - 2, 0), made)
        joint_ref[8 * j : 8 * j + 8] = jnp.where(right, made, 0.0)
    lane_main = lane_of((main, LANES))
    row_main = lax.broadcasted_iota(jnp.int32, (main, LANES), 0)
    inside = (lane_main >= 2) & (lane_main < lanes - 2)
    at_level = lane_main // GROUP == row_main // 8

    def block(o):
        return jnp.where(inside, circle_ref[o, :main], 0.0)

    def joint(j):
        x = joint_ref[8 * j : 8 * j + 8]
        return jnp.where(at_level, jnp.concatenate([x] * levels, axis=0), 0.0)

    total = jnp.zeros((2 * main, 2 * modes), jnp.float32)
    for source, basis, count in (
        (block, basis_ref, peers),
        (joint, joint_basis_ref, peers // 2),
    ):
        for o in range(0, count, 2):
            parts = zip(split(source(o)), split(source(o + 1)))
            x = jnp.concatenate([jnp.concatenate(p, axis=1) for p in parts], axis=0)
            total = total + product(x, basis[lanes * o : lanes * (o + 2)], ((1,), (0,)))
    total = total[:main] + total[main:]
    counts = count_ref[...]
    row = lax.broadcasted_iota(jnp.int32, counts.shape, 0)
    own = 2 * lax.axis_index("lon")
    even, odd = (
        jnp.sum(jnp.where(row == own + r, counts, 0.0), axis=0, keepdims=True) for r in (0, 1)
    )
    limit = jnp.where(row_main % 2 == 0, even, odd)
    order = (lane_main % (modes // 2)).astype(jnp.float32)
    weight = jnp.where(order < limit, jnp.where(order == 0.0, 1.0 / length, 2.0 / length), 0.0)
    total = (total[:, :modes] + total[:, modes:]) * weight
    y = jnp.concatenate([jnp.concatenate([p, p], axis=1) for p in split(total)], axis=0)
    for o in range(0, peers, 2):
        x = product(y, basis_ref[lanes * o : lanes * (o + 2)], ((1,), (1,)))
        x = x[:main] + x[main:]
        out_ref[o, :main] = x[:, :lanes]
        out_ref[o + 1, :main] = x[:, lanes:]
        before = (4 * o - 8) % (4 * peers)
        here = joint_ref[4 * o : 4 * o + 8]
        out_ref[o, main:] = jnp.where(
            c < 8, roll(joint_ref[before : before + 8], -8, 1), roll(here, 8, 1)
        )
        out_ref[o + 1, main:] = here


def join_kernel(state_ref, piece_ref, wet_ref, flag_ref, out_ref, made_ref, sems):
    levels, rows, lanes = wet_ref.shape
    main = 8 * levels
    lane = lane_of((8, LANES))
    edges = [{} for _ in range(rows // 8)]
    for t, into in enumerate(edges):
        tiles = [piece_ref[4 * t + x, main : main + 8] for x in range(4)]
        pairs_of_rows(tiles, t, into.__setitem__)
    copies = []
    for k in range(levels):
        for t in range(rows // 8):
            part = slice(8 * t, 8 * t + 8)
            tiles = [piece_ref[4 * t + x, 8 * k : 8 * k + 8] for x in range(4)]
            gate = flag_ref[part] * wet_ref[k, part]

            def place(f, smooth, k=k, gate=gate, part=part, edge=edges[t]):
                first = roll(edge[f], -(GROUP * k + 4), 1)
                last = roll(edge[f], lanes - 2 - (GROUP * k + 10), 1)
                state = jnp.where(
                    lane < 2, first, jnp.where(lane >= lanes - 2, last, state_ref[f, k, part])
                )
                made_ref[f, k, part] = state + gate * (smooth - state)

            pairs_of_rows(tiles, t, place)
        if k % 2:
            both = pl.ds(k - 1, 2)
            copies.append(
                pltpu.make_async_copy(
                    made_ref.at[:, both], out_ref.at[:, both], sems.at[k // 2]
                )
            )
            copies[-1].start()
    for copy in copies:
        copy.wait()


def filter_kernel(circle_ref, basis_ref, weight_ref, out_ref, piece_ref, sems):
    pieces, part, lanes = circle_ref.shape
    modes = weight_ref.shape[1]
    pairs = range(0, pieces, 2)
    total = jnp.zeros((2 * part, 2 * modes), jnp.float32)
    for o in pairs:
        parts = zip(split(circle_ref[o]), split(circle_ref[o + 1]))
        x = jnp.concatenate([jnp.concatenate(p, axis=1) for p in parts], axis=0)
        total = total + product(x, basis_ref[lanes * o : lanes * (o + 2)], ((1,), (0,)))
    total = total[:part] + total[part:]
    total = (total[:, :modes] + total[:, modes:]) * weight_ref[...]
    y = jnp.concatenate([jnp.concatenate([p, p], axis=1) for p in split(total)], axis=0)
    copies = []
    for o in pairs:
        x = product(y, basis_ref[lanes * o : lanes * (o + 2)], ((1,), (1,)))
        x = x[:part] + x[part:]
        piece_ref[o] = x[:, :lanes]
        piece_ref[o + 1] = x[:, lanes:]
        both = pl.ds(o, 2)
        copies.append(
            pltpu.make_async_copy(piece_ref.at[both], out_ref.at[both], sems.at[o // 2])
        )
        copies[-1].start()
    for copy in copies:
        copy.wait()


def blend_kernel(state_ref, smooth_ref, wet_ref, flag_ref, out_ref, piece_ref, sems):
    levels = wet_ref.shape[0]
    flag = flag_ref[...]
    copies = []
    for f in range(4):
        for k in range(levels):
            state = state_ref[f, k]
            gate = flag * wet_ref[k]
            piece_ref[f, k] = state + gate * (smooth_ref[f, k] - state)
        copies.append(pltpu.make_async_copy(piece_ref.at[f], out_ref.at[f], sems.at[f]))
        copies[-1].start()
    for copy in copies:
        copy.wait()


def call(kernel, outs, scratch=(), sems=0, raw=False, sent=False, flops=0):
    vmem = pl.BlockSpec(memory_space=pltpu.VMEM)
    away = pl.BlockSpec(memory_space=pl.ANY)
    specs = [vmem] * len(outs)
    shapes = [jax.ShapeDtypeStruct(s, jnp.float32) for s in outs]
    if sent:
        specs[-1] = away
        shapes[-1] = pltpu.HBM(outs[-1], jnp.float32)
    buffers = [pltpu.VMEM(s, jnp.float32) if isinstance(s, tuple) else s for s in scratch]
    if sems:
        buffers.append(pltpu.SemaphoreType.DMA((sems,)))
    cost = pl.CostEstimate(
        flops=flops, transcendentals=0, bytes_accessed=4 * sum(map(math.prod, outs))
    )

    def run(*args):
        if raw:
            args = [pltpu.with_memory_space_constraint(x, pltpu.HBM) for x in args]
        return pl.pallas_call(
            kernel,
            out_shape=shapes,
            in_specs=[away if raw else vmem] * len(args),
            out_specs=specs,
            scratch_shapes=buffers,
            compiler_params=pltpu.CompilerParams(vmem_limit_bytes=24 << 20),
            cost_estimate=cost,
        )(*args)

    return run


def swap_edges(before_src, after_src, axis):
    peers = lax.axis_size(axis)
    up = [(i, (i + 1) % peers) for i in range(peers)]
    down = [(j, i) for i, j in up]
    return lax.ppermute(before_src, axis, up), lax.ppermute(after_src, axis, down)


def mode_basis(length, modes):
    turns = np.arange(modes)[None, :] * np.arange(length)[:, None] % length
    angle = turns * (2.0 * math.pi / length)
    basis = np.concatenate([np.cos(angle), np.sin(angle)], axis=1).astype(np.float32)
    high = basis.astype(ml_dtypes.bfloat16)
    low = (basis - high.astype(np.float32)).astype(ml_dtypes.bfloat16)
    return np.concatenate([high, low], axis=1)


def joint_basis(basis, lanes):
    length = basis.shape[0]
    tile, lane = np.divmod(np.arange(length // 2), lanes)
    half, c = np.divmod(lane % GROUP, 8)
    column = (lanes * (2 * tile + half + 1) + c - 4) % length
    return np.where(((c >= 2) & (c < 6))[:, None], basis[column], np.zeros_like(basis[column]))


def mode_weights(counts, modes, length):
    order = jnp.arange(modes).astype(jnp.float32)
    keep = (order[None, :] < counts[:, None]).astype(jnp.float32)
    scale = jnp.where(order == 0, 1.0, 2.0) / length
    weights = keep * scale[None, :]
    return jnp.concatenate([weights, weights], axis=1)


def row_table(place, nlat):
    place = place.astype(jnp.float32)
    centre = jnp.cos(lat_edge * (2.0 * (place + 0.5) / nlat - 1.0))
    faces = jnp.cos(lat_edge * (2.0 * (place + 1.0) / nlat - 1.0))
    table = jnp.stack([1.0 / centre, faces])
    return jnp.broadcast_to(table[:, :, None], table.shape + (LANES,))


def ring_rows(rows):
    place = jnp.arange(rows + 8, dtype=jnp.int32)
    return jnp.where(place < rows + 2, place, jnp.where(place < rows + 6, 0, place - rows - 8))


def shards(ocean_state, thickness, wet_mask, mode_counts, row_flags):
    levels, rows, lanes = ocean_state.shape[1:]
    assert rows % 8 == 0 and lanes == LANES and levels * GROUP <= LANES
    lon_peers = lax.axis_size("lon")
    lat_peers = lax.axis_size("lat")
    nlat = rows * lat_peers
    nlon = lanes * lon_peers
    full = rows + 8
    total = 4 * levels * rows
    part = total // lon_peers
    lat_pos = lax.axis_index("lat")
    first_row = lat_pos * rows
    table = row_table(first_row + ring_rows(rows), nlat)
    cells = 4 * levels * full * lanes
    edge_rows = (6, levels, 2, lanes)

    paired = rows == 2 * lon_peers and rows >= FBAND and lat_peers % 2 == 0 and levels % 2 == 0
    *block, first, last, flags, counts = call(
        functools.partial(load_kernel, paired),
        [ocean_state.shape, thickness.shape, thickness.shape, edge_rows, edge_rows]
        + [(rows, lanes)] * 2,
        [pltpu.VMEM(shape, jnp.int32) for shape in (thickness.shape, (1, rows), (1, rows))],
        sems=8,
        raw=True,
    )(ocean_state, thickness, wet_mask, row_flags[None], mode_counts[None])

    def ready():
        return call(
            ready_kernel, [(6, rows, LANES), (5, levels, rows, lanes)], flops=20 * cells
        )(*block, table)

    def exchanged(below, above, own, terms):
        inner, edges, halo = call(
            inner_kernel,
            [(3, 4, levels, full, lanes), (6, full, LANES), (6, levels, 8, lanes)],
            [(5, levels, 8, lanes), (2, levels, full, lanes)],
            flops=60 * cells,
        )(*block, below, above, table, own, terms)
        first, last = call(pack_kernel, [(full, LANES)] * 2)(*block, halo)
        from_west, from_east = swap_edges(last, first, "lon")
        return call(
            edge_kernel,
            [ocean_state.shape] * 2,
            [(4, full, LANES), (7, full, LANES)],
            sems=4,
            sent=True,
        )(inner, edges, from_west, from_east, table)

    banded = (first_row < FBAND) | (first_row + rows > nlat - FBAND)
    modes = mode_basis(nlon, MAXM)
    basis, at_joints = lax.optimization_barrier(
        (jnp.asarray(modes), jnp.asarray(joint_basis(modes, lanes)))
    )
    lon_pos = lax.axis_index("lon")
    place = first_row + 2 * lon_pos - 2 + jnp.arange(4 * lon_peers, dtype=jnp.int32) % 8
    joint_table = row_table(jnp.minimum(place, first_row + 2 * lon_pos + 3), nlat)

    def circled(got, own, closed):
        main = 8 * levels
        tile = (levels, 8, lanes)
        state, sent = call(
            end_kernel,
            [ocean_state.shape, (lon_peers, main + 24, lanes)],
            [(2,) + tile, (6,) + tile, (3, 4) + tile, (7,) + tile, (3, full, lanes)],
        )(*block, got, own, closed, end_table)
        circles = lax.all_to_all(sent, "lon", 0, 0, tiled=True)
        pieces = call(
            circle_kernel,
            [(lon_peers, main + 8, lanes)],
            [
                (6, 4 * lon_peers, lanes),
                (7, 4 * lon_peers, lanes),
                (4 * lon_peers, lanes),
            ],
        )(circles, joint_table, basis, at_joints, counts)[0]
        pieces = lax.all_to_all(pieces, "lon", 0, 0, tiled=True)
        return call(
            join_kernel, [ocean_state.shape], [ocean_state.shape], sems=levels // 2, sent=True
        )(state, pieces, block[2], flags)[0]

    def between(got, *_):
        pairs = [(i, i + 1) for i in range(1, lat_peers - 1, 2)]
        other = lax.ppermute(last, "lat", pairs + [(j, i) for i, j in pairs])
        even = lat_pos % 2 == 0
        below, above = jnp.where(even, other, got), jnp.where(even, got, other)
        return exchanged(below, above, *ready())[1]

    if paired:
        ends = jnp.where(lat_pos == 0, first_row + rows - 4, first_row - 2)
        end_place = ends + jnp.minimum(jnp.arange(8, dtype=jnp.int32), 5)
        end_table = row_table(end_place, nlat)
        got = lax.ppermute(first, "lat", [(i, i ^ 1) for i in range(lat_peers)])
        own, closed = call(
            closed_kernel,
            [(6, rows, LANES), (3, 4, levels, rows, lanes)],
            [(7, levels, rows, lanes)],
            flops=60 * cells,
        )(*block, table)
        got, own, closed = lax.optimization_barrier((got, own, closed))
        return lax.cond(banded, circled, between, got, own, closed)

    below, above = swap_edges(last, first, "lat")
    state, sent = exchanged(*lax.optimization_barrier((below, above, *ready())))

    def filtered():
        row_counts = lax.dynamic_slice(
            jnp.broadcast_to(
                mode_counts.astype(jnp.float32)[None], (4 * levels, rows)
            ).reshape(total),
            (lon_pos * part,),
            (part,),
        )
        circles = lax.all_to_all(
            sent.reshape(lon_peers, part, lanes), "lon", 0, 0, tiled=True
        )
        smooth = call(
            filter_kernel, [circles.shape], [circles.shape], sems=lon_peers // 2, sent=True
        )(circles, basis, mode_weights(row_counts, MAXM, nlon))[0]
        smooth = lax.all_to_all(smooth, "lon", 0, 0, tiled=True).reshape(state.shape)
        return call(blend_kernel, [state.shape], [state.shape], sems=4, sent=True)(
            state, smooth, block[2], flags
        )[0]

    return lax.cond(banded, filtered, lambda: sent)


def solution(mesh):
    in_specs = (
        P(None, None, "lat", "lon"),
        P(None, "lat", "lon"),
        P(None, "lat", "lon"),
        P("lat"),
        P("lat"),
    )
    out_specs = P(None, None, "lat", "lon")
    return jax.shard_map(shards, mesh=mesh, in_specs=in_specs, out_specs=out_specs, check_vma=False)
```

```python
import functools
import math

import jax
import jax.numpy as jnp
import ml_dtypes
import numpy as np
from jax import lax
from jax.experimental import pallas as pl
from jax.experimental.pallas import tpu as pltpu
from jax.sharding import PartitionSpec as P

FBAND = 16
MAXM = 64
LANES = 128
GROUP = 16


lat_edge = 1.3
diffusion = 0.05
vertical_mix = 0.5
time_step = 0.05


def roll(x, shift, axis):
    shift %= x.shape[axis]
    return pltpu.roll(x, shift, axis) if shift else x


def east(x):
    return roll(x, -1, 1)


def west(x):
    return roll(x, 1, 1)


def north(x):
    return roll(x, -1, 0)


def south(x):
    return roll(x, 1, 0)


def lane_of(shape):
    return lax.broadcasted_iota(jnp.int32, shape, 1)


def east_terms(h, w, inv_c):
    open_e = 0.5 * (h + east(h)) * (w * east(w))
    return 0.25 * open_e, diffusion * open_e * inv_c


def north_terms(h, w, face):
    open_n = 0.5 * (h + north(h)) * (w * north(w)) * face
    return 0.25 * open_n, diffusion * open_n


def advance(fields, terms, scale, scale_c, vertical):
    quarter_e, spread_e, quarter_n, spread_n = terms
    u, v = fields[2], fields[3]
    speed_e = quarter_e * (u + east(u))
    speed_n = quarter_n * (v + north(v))
    here_e, there_e = speed_e + spread_e, speed_e - spread_e
    here_n, there_n = speed_n + spread_n, speed_n - spread_n
    fresh = []
    for q, vert in zip(fields, vertical):
        flux_e = here_e * q + there_e * east(q)
        flux_n = here_n * q + there_n * north(q)
        spread = (flux_e - west(flux_e)) + (flux_n - south(flux_n))
        fresh.append(q + scale * vert - scale_c * spread)
    return fresh


def own_columns(load, levels, lanes, rows):
    lane = lane_of((rows, LANES))
    own = jnp.zeros((rows, LANES), jnp.float32)
    for k in range(levels):
        x = load(k)
        at = GROUP * k + 2
        own = jnp.where((lane >= at) & (lane < at + 4), roll(x, at, 1), own)
        at = GROUP * k + 8
        own = jnp.where((lane >= at) & (lane < at + 4), roll(x, at + 4 - lanes, 1), own)
    return own


def row_terms(thick, wet, inv_c, levels, term_ref):
    w, h = wet(0), thick(0)
    hs = jnp.where(w > 0, h, 1.0)
    for k in range(levels):
        term_ref[0, k], term_ref[1, k] = east_terms(h, w, inv_c)
        scale = time_step * w / hs
        term_ref[2, k] = scale
        term_ref[3, k] = scale * inv_c
        if k + 1 < levels:
            w_next, h_next = wet(k + 1), thick(k + 1)
            hs_next = jnp.where(w_next > 0, h_next, 1.0)
            term_ref[4, k] = w * w_next * vertical_mix / (0.5 * (hs + hs_next))
            w, h, hs = w_next, h_next, hs_next


def fill_table(ref, place, nlat):
    place = place.astype(jnp.float32)
    ref[0] = 1.0 / jnp.cos(lat_edge * (2.0 * (place + 0.5) / nlat - 1.0))
    ref[1] = jnp.cos(lat_edge * (2.0 * (place + 1.0) / nlat - 1.0))


def ring_rows(rows):
    place = lax.broadcasted_iota(jnp.int32, (rows + 8, LANES), 0)
    return jnp.where(place < rows + 2, place, jnp.where(place < rows + 6, 0, place - rows - 8))


def load_kernel(
    paired,
    state_any,
    thick_any,
    wet_any,
    flag_any,
    count_any,
    state_ref,
    thick_ref,
    wet_ref,
    first_ref,
    last_ref,
    flag_ref,
    count_ref,
    table_ref,
    end_table_ref,
    joint_table_ref,
    raw_ref,
    raw_flag_ref,
    raw_count_ref,
    sems,
):
    levels, rows = thick_ref.shape[:2]
    moves = [(flag_any, raw_flag_ref), (count_any, raw_count_ref), (wet_any, raw_ref)]
    moves += [(thick_any, thick_ref)]
    moves += [(state_any.at[f], state_ref.at[f]) for f in range(4)]
    copies = [pltpu.make_async_copy(*pair, sems.at[i]) for i, pair in enumerate(moves)]
    for copy in copies:
        copy.start()
    nlat = rows * lax.axis_size("lat")
    lat_pos = lax.axis_index("lat")
    first_row = lat_pos * rows
    fill_table(table_ref, first_row + ring_rows(rows), nlat)
    if paired:
        six = jnp.minimum(lax.broadcasted_iota(jnp.int32, (8, LANES), 0), 5)
        end = jnp.where(lat_pos == 0, rows - 4, -2)
        fill_table(end_table_ref, first_row + end + six, nlat)
        fill_table(joint_table_ref, first_row + 2 * lax.axis_index("lon") - 2 + six, nlat)
    for copy in copies[:3]:
        copy.wait()
    shape = (rows, rows)
    diagonal = lax.broadcasted_iota(jnp.int32, shape, 0) == lane_of(shape)
    for raw, ref in ((raw_flag_ref, flag_ref), (raw_count_ref, count_ref)):
        spread = jnp.broadcast_to(raw[...].astype(jnp.float32), shape)
        value = jnp.sum(jnp.where(diagonal, spread, 0.0), axis=1, keepdims=True)
        ref[...] = jnp.broadcast_to(value, (rows, LANES))
    for k in range(levels):
        wet_ref[k] = raw_ref[k].astype(jnp.float32)
    for copy in copies[3:]:
        copy.wait()
    for f in range(6):
        for k in range(levels):
            x = state_ref.at[f, k] if f < 4 else (thick_ref, wet_ref)[f - 4].at[k]
            first_ref[f, k] = x[0:2]
            last_ref[f, k] = x[rows - 2 : rows]
    if paired:
        even = lax.axis_index("lat") % 2 == 0
        for f in range(6):
            for k in range(levels):
                low, high = first_ref[f, k], last_ref[f, k]
                first_ref[f, k] = jnp.where(even, high, low)
                last_ref[f, k] = jnp.where(even, low, high)


def ready_kernel(state_ref, thick_ref, wet_ref, table_ref, own_ref, term_ref):
    levels, rows, lanes = thick_ref.shape

    def thick(k):
        return thick_ref[k]

    def wet(k):
        return wet_ref[k]

    for f in range(4):
        own_ref[f] = own_columns(lambda k, f=f: state_ref[f, k], levels, lanes, rows)
    own_ref[4] = own_columns(thick, levels, lanes, rows)
    own_ref[5] = own_columns(wet, levels, lanes, rows)
    row_terms(thick, wet, table_ref[0, :rows], levels, term_ref)


def pack_kernel(state_ref, thick_ref, wet_ref, halo_ref, first_ref, last_ref):
    levels, rows, lanes = thick_ref.shape
    lane = lane_of((8, LANES))
    for t in range(rows // 8 + 1):
        first = jnp.zeros((8, LANES), jnp.float32)
        last = jnp.zeros((8, LANES), jnp.float32)
        part = slice(8 * t, 8 * t + 8)
        for f in range(6):
            for k in range(levels):
                if t == rows // 8:
                    x = halo_ref[f, k]
                elif f < 4:
                    x = state_ref[f, k, part]
                elif f == 4:
                    x = thick_ref[k, part]
                else:
                    x = wet_ref[k, part]
                at = GROUP * f + 2 * k
                mine = (lane >= at) & (lane < at + 2)
                first = jnp.where(mine, roll(x, at, 1), first)
                last = jnp.where(mine, roll(x, at + 2 - lanes, 1), last)
        first_ref[part] = first
        last_ref[part] = last


def inner_kernel(
    state_ref,
    thick_ref,
    wet_ref,
    below_ref,
    above_ref,
    table_ref,
    own_ref,
    term_ref,
    out_ref,
    edge_ref,
    halo_ref,
    halo_term_ref,
    north_ref,
):
    levels, rows, lanes = thick_ref.shape
    full = rows + 8
    face = table_ref[1]
    lat_pos = lax.axis_index("lat")
    with_below = jnp.where(lat_pos > 0, 1.0, 0.0)
    with_above = jnp.where(lat_pos < lax.axis_size("lat") - 1, 1.0, 0.0)
    for f in range(6):
        for k in range(levels):
            halo_ref[f, k, 0:2] = above_ref[f, k] * with_above
            halo_ref[f, k, 2:6] = jnp.zeros((4, lanes), jnp.float32)
            halo_ref[f, k, 6:8] = below_ref[f, k] * with_below

    def joined(x, y):
        return jnp.concatenate([x, y], axis=0)

    def halo(f):
        return lambda k: halo_ref[f, k]

    for f in range(6):
        edge_ref[f, :rows] = own_ref[f]
        edge_ref[f, rows:] = own_columns(halo(f), levels, lanes, 8)
    row_terms(halo(4), halo(5), table_ref[0, rows:], levels, halo_term_ref)
    for k in range(levels):
        h = joined(thick_ref[k], halo_ref[4, k])
        w = joined(wet_ref[k], halo_ref[5, k])
        north_ref[0, k], north_ref[1, k] = north_terms(h, w, face)
        for f in range(4):
            out_ref[0, f, k] = joined(state_ref[f, k], halo_ref[f, k])

    def term(i, k):
        return joined(term_ref[i, k], halo_term_ref[i, k])

    def step(i, _):
        source, target = out_ref.at[i], out_ref.at[i + 1]
        fields = [source[f, 0] for f in range(4)]
        above = [jnp.zeros((full, LANES), jnp.float32)] * 4
        for k in range(levels):
            deeper = below = above
            if k + 1 < levels:
                couple = term(4, k)
                deeper = [source[f, k + 1] for f in range(4)]
                below = [couple * (d - q) for d, q in zip(deeper, fields)]
                vertical = [b - a for b, a in zip(below, above)]
            else:
                vertical = [-a for a in above]
            terms = term(0, k), term(1, k), north_ref[0, k], north_ref[1, k]
            fresh = advance(fields, terms, term(2, k), term(3, k), vertical)
            for f in range(4):
                target[f, k] = fresh[f]
            fields, above = deeper, below
        return 0

    lax.fori_loop(0, 2, step, 0)


def step_tile(tile_ref, h, w, levels, inv_c, face, term_ref):
    lane = lane_of(h.shape)

    def deeper(x):
        return roll(x, -GROUP, 1)

    def shallower(x):
        return roll(x, GROUP, 1)

    hs = jnp.where(w > 0, h, 1.0)
    scale = time_step * w / hs
    couple = w * deeper(w) * vertical_mix / (0.5 * (hs + deeper(hs)))
    couple = jnp.where(lane < GROUP * (levels - 1), couple, 0.0)
    terms = east_terms(h, w, inv_c) + north_terms(h, w, face)
    for i, term in enumerate(terms + (scale, scale * inv_c, couple)):
        term_ref[i] = term

    def step():
        terms = [term_ref[i] for i in range(7)]
        fields = [tile_ref[f] for f in range(4)]
        vertical = []
        for q in fields:
            down = terms[6] * (deeper(q) - q)
            vertical.append(down - shallower(down))
        for f, q in enumerate(advance(fields, terms[:4], terms[4], terms[5], vertical)):
            tile_ref[f] = q

    step()
    step()


def edge_kernel(
    inner_ref, own_ref, west_ref, east_ref, table_ref, out_ref, send_ref, tile_ref, term_ref, sems
):
    levels, rows, lanes = out_ref.shape[1:]
    full = rows + 8
    lane = lane_of((full, LANES))
    from_west, from_east = west_ref[...], east_ref[...]

    def joined(f):
        x = own_ref[f]
        for k in range(levels):
            src = GROUP * f + 2 * k
            at = GROUP * k
            x = jnp.where((lane >= at) & (lane < at + 2), roll(from_west, at - src, 1), x)
            at = GROUP * k + 12
            x = jnp.where((lane >= at) & (lane < at + 2), roll(from_east, at - src, 1), x)
        return x

    for f in range(4):
        tile_ref[f] = joined(f)
    step_tile(tile_ref, joined(4), joined(5), levels, table_ref[0], table_ref[1], term_ref)
    lane = lane_of((rows, LANES))
    for f in range(4):
        x = tile_ref[f, :rows]
        for k in range(levels):
            left = roll(x, -(GROUP * k + 2), 1)
            right = roll(x, lanes - 2 - (GROUP * k + 10), 1)
            out_ref[f, k] = jnp.where(
                lane < 2,
                left,
                jnp.where(lane >= lanes - 2, right, inner_ref[2, f, k, :rows]),
            )
        pltpu.make_async_copy(out_ref.at[f], send_ref.at[f], sems.at[f]).start()
    for f in range(4):
        pltpu.make_async_copy(out_ref.at[f], send_ref.at[f], sems.at[f]).wait()


def split(x):
    high = x.astype(jnp.bfloat16)
    return high, (x - high.astype(jnp.float32)).astype(jnp.bfloat16)


def product(a, b, dims):
    return lax.dot_general(a, b, (dims, ((), ())), preferred_element_type=jnp.float32)


def pairs_of_rows(tiles, t, place):
    sub = lax.broadcasted_iota(jnp.int32, tiles[0].shape, 0) // 2
    for y in range(4):
        made = roll(tiles[0], -2 * y, 0)
        for x in range(1, 4):
            made = jnp.where(sub == x, roll(tiles[x], 2 * (x - y), 0), made)
        place(y, made)


def step_levels(buf_ref, term_ref, loop):
    levels, size = buf_ref.shape[2:4]

    def step(i, _):
        source, target = buf_ref.at[i], buf_ref.at[i + 1]
        fields = [source[f, 0] for f in range(4)]
        above = [jnp.zeros((size, LANES), jnp.float32)] * 4
        for k in range(levels):
            deeper = below = above
            if k + 1 < levels:
                couple = term_ref[4, k]
                deeper = [source[f, k + 1] for f in range(4)]
                below = [couple * (d - q) for d, q in zip(deeper, fields)]
                vertical = [b - a for b, a in zip(below, above)]
            else:
                vertical = [-a for a in above]
            terms = [term_ref[i, k] for i in (0, 1, 5, 6)]
            fresh = advance(fields, terms, term_ref[2, k], term_ref[3, k], vertical)
            for f in range(4):
                target[f, k] = fresh[f]
            fields, above = deeper, below
        return 0

    if loop:
        lax.fori_loop(0, 2, step, 0)
    else:
        step(1, step(0, 0))


def closed_kernel(state_ref, thick_ref, wet_ref, table_ref, own_ref, buf_ref, term_ref):
    levels, rows, lanes = thick_ref.shape

    def thick(k):
        return thick_ref[k]

    def wet(k):
        return wet_ref[k]

    for f in range(4):
        own_ref[f] = own_columns(lambda k, f=f: state_ref[f, k], levels, lanes, rows)
    own_ref[4] = own_columns(thick, levels, lanes, rows)
    own_ref[5] = own_columns(wet, levels, lanes, rows)
    row_terms(thick, wet, table_ref[0, :rows], levels, term_ref)
    row = lax.broadcasted_iota(jnp.int32, (rows, LANES), 0)
    face = jnp.where(row < rows - 1, table_ref[1, :rows], 0.0)
    for k in range(levels):
        term_ref[5, k], term_ref[6, k] = north_terms(thick(k), wet(k), face)
        for f in range(4):
            buf_ref[0, f, k] = state_ref[f, k]
    step_levels(buf_ref, term_ref, True)


def end_kernel(
    state_ref,
    thick_ref,
    wet_ref,
    got_ref,
    own_ref,
    closed_ref,
    table_ref,
    out_ref,
    send_ref,
    field_ref,
    halo_ref,
    buf_ref,
    term_ref,
    raw_ref,
):
    levels, rows, lanes = thick_ref.shape
    full = rows + 8
    top = lax.axis_index("lat") == 0
    at_top = jnp.where(top, 1.0, 0.0)
    at_bottom = jnp.where(top, 0.0, 1.0)
    sub = lax.broadcasted_iota(jnp.int32, (8, LANES), 0)

    def own(f, k, part):
        return state_ref[f, k, part] if f < 4 else (thick_ref, wet_ref)[f - 4][k, part]

    for f in range(6):
        for k in range(levels):
            halo_ref[f, k, 0:2] = got_ref[f, k] * at_top
            halo_ref[f, k, 2:6] = jnp.zeros((4, lanes), jnp.float32)
            halo_ref[f, k, 6:8] = got_ref[f, k] * at_bottom
    for f in range(6):
        for k in range(levels):
            halo = halo_ref[f, k]
            beyond = jnp.where(sub < 6, roll(halo, 4, 0), 0.0)
            high = jnp.where(sub < 4, roll(own(f, k, slice(rows - 8, rows)), -4, 0), beyond)
            low = jnp.where(sub < 2, roll(halo, 2, 0), roll(own(f, k, slice(0, 8)), 2, 0))
            tile = jnp.where(top, high, low)
            if f < 4:
                buf_ref[0, f, k] = tile
            else:
                field_ref[f - 4, k] = tile

    def thick(k):
        return field_ref[0, k]

    def wet(k):
        return field_ref[1, k]

    row_terms(thick, wet, table_ref[0], levels, term_ref)
    for k in range(levels):
        term_ref[5, k], term_ref[6, k] = north_terms(thick(k), wet(k), table_ref[1])
    step_levels(buf_ref, term_ref, False)
    c = lane_of((full, LANES)) % GROUP

    def ring(f):
        beyond = own_columns(lambda k: halo_ref[f, k], levels, lanes, 8)
        return jnp.concatenate([own_ref[f], beyond], axis=0)

    for i in range(3):
        a, b = ring(2 * i), ring(2 * i + 1)
        one = jnp.where(c < 4, roll(a, -2, 1), roll(a, -4, 1))
        two = jnp.where(c < 12, roll(b, 6, 1), roll(b, 4, 1))
        both = jnp.where(c < 8, one, two)
        raw_ref[i, 0:2] = both[full - 2 : full]
        raw_ref[i, 2 : rows + 4] = both[: rows + 2]
        raw_ref[i, rows + 4 : full] = jnp.zeros((4, LANES), jnp.float32)
    main = 8 * levels
    last = rows // 8 - 1
    for t in range(rows // 8):
        part = slice(8 * t, 8 * t + 8)
        for k in range(levels):
            tiles = []
            for f in range(4):
                x = closed_ref[2, f, k, part]
                if t == last:
                    fixed = jnp.where(sub >= 6, roll(buf_ref[2, f, k], 4, 0), x)
                    x = jnp.where(top, fixed, x)
                if t == 0:
                    fixed = jnp.where(sub < 2, roll(buf_ref[2, f, k], -2, 0), x)
                    x = jnp.where(top, x, fixed)
                out_ref[f, k, part] = x
                tiles.append(x)

            def place(y, tile, t=t, k=k):
                send_ref[4 * t + y, 8 * k : 8 * k + 8] = tile

            pairs_of_rows(tiles, t, place)
        for p in range(4 * t, 4 * t + 4):
            for i in range(3):
                send_ref[p, main + 8 * i : main + 8 * i + 8] = raw_ref[i, 2 * p : 2 * p + 8]


def circle_kernel(
    circle_ref,
    table_ref,
    basis_ref,
    joint_basis_ref,
    count_ref,
    out_ref,
    tile_ref,
    term_ref,
    joint_ref,
):
    peers = circle_ref.shape[0]
    modes = basis_ref.shape[1] // 2
    length = basis_ref.shape[0]
    main = circle_ref.shape[1] - 24
    levels = main // 8
    lanes = LANES
    lane = lane_of((8, LANES))
    c = lane % GROUP
    for j in range(0, peers, 2):
        part = slice(4 * j, 4 * j + 8)
        for i in range(3):
            x, y, z = (
                circle_ref[(j + d) % peers, main + 8 * i : main + 8 * i + 8] for d in range(3)
            )
            for f, shift in ((2 * i, 0), (2 * i + 1, -8)):
                middle = jnp.where(c < 12, roll(y, 4 + shift, 1), roll(z, 12 + shift, 1))
                tile_ref[f, part] = jnp.where(c < 4, roll(x, shift - 4, 1), middle)
    inv_c, face = (jnp.concatenate([table_ref[i]] * (peers // 2), axis=0) for i in (0, 1))
    step_tile(tile_ref, tile_ref[4], tile_ref[5], levels, inv_c, face, term_ref)
    sub = lax.broadcasted_iota(jnp.int32, (8, LANES), 0) // 2
    right = (c % 8 >= 2) & (c % 8 < 6)
    for j in range(peers // 2):
        made = jnp.zeros((8, LANES), jnp.float32)
        for f in range(4):
            x = tile_ref[f, 8 * j : 8 * j + 8]
            made = jnp.where(sub == f, roll(x, 2 * f - 2, 0), made)
        joint_ref[8 * j : 8 * j + 8] = jnp.where(right, made, 0.0)
    lane_main = lane_of((main, LANES))
    row_main = lax.broadcasted_iota(jnp.int32, (main, LANES), 0)
    inside = (lane_main >= 2) & (lane_main < lanes - 2)
    at_level = lane_main // GROUP == row_main // 8

    def block(o):
        return jnp.where(inside, circle_ref[o, :main], 0.0)

    def joint(j):
        x = joint_ref[8 * j : 8 * j + 8]
        return jnp.where(at_level, jnp.concatenate([x] * levels, axis=0), 0.0)

    total = jnp.zeros((2 * main, 2 * modes), jnp.float32)
    for source, basis, count in (
        (block, basis_ref, peers),
        (joint, joint_basis_ref, peers // 2),
    ):
        for o in range(0, count, 2):
            parts = zip(split(source(o)), split(source(o + 1)))
            x = jnp.concatenate([jnp.concatenate(p, axis=1) for p in parts], axis=0)
            total = total + product(x, basis[lanes * o : lanes * (o + 2)], ((1,), (0,)))
    total = total[:main] + total[main:]
    counts = count_ref[...]
    row = lax.broadcasted_iota(jnp.int32, counts.shape, 0)
    own = 2 * lax.axis_index("lon")
    even, odd = (
        jnp.sum(jnp.where(row == own + r, counts, 0.0), axis=0, keepdims=True) for r in (0, 1)
    )
    limit = jnp.where(row_main % 2 == 0, even, odd)
    order = (lane_main % (modes // 2)).astype(jnp.float32)
    weight = jnp.where(order < limit, jnp.where(order == 0.0, 1.0 / length, 2.0 / length), 0.0)
    total = (total[:, :modes] + total[:, modes:]) * weight
    y = jnp.concatenate([jnp.concatenate([p, p], axis=1) for p in split(total)], axis=0)
    for o in range(0, peers, 2):
        x = product(y, basis_ref[lanes * o : lanes * (o + 2)], ((1,), (1,)))
        x = x[:main] + x[main:]
        out_ref[o, :main] = x[:, :lanes]
        out_ref[o + 1, :main] = x[:, lanes:]
        before = (4 * o - 8) % (4 * peers)
        here = joint_ref[4 * o : 4 * o + 8]
        out_ref[o, main:] = jnp.where(
            c < 8, roll(joint_ref[before : before + 8], -8, 1), roll(here, 8, 1)
        )
        out_ref[o + 1, main:] = here


def join_kernel(state_ref, piece_ref, wet_ref, flag_ref, out_ref, made_ref, sems):
    levels, rows, lanes = wet_ref.shape
    main = 8 * levels
    lane = lane_of((8, LANES))
    edges = [{} for _ in range(rows // 8)]
    for t, into in enumerate(edges):
        tiles = [piece_ref[4 * t + x, main : main + 8] for x in range(4)]
        pairs_of_rows(tiles, t, into.__setitem__)
    copies = []
    for k in range(levels):
        for t in range(rows // 8):
            part = slice(8 * t, 8 * t + 8)
            tiles = [piece_ref[4 * t + x, 8 * k : 8 * k + 8] for x in range(4)]
            gate = flag_ref[part] * wet_ref[k, part]

            def place(f, smooth, k=k, gate=gate, part=part, edge=edges[t]):
                first = roll(edge[f], -(GROUP * k + 4), 1)
                last = roll(edge[f], lanes - 2 - (GROUP * k + 10), 1)
                state = jnp.where(
                    lane < 2, first, jnp.where(lane >= lanes - 2, last, state_ref[f, k, part])
                )
                made_ref[f, k, part] = state + gate * (smooth - state)

            pairs_of_rows(tiles, t, place)
        if k % 2:
            both = pl.ds(k - 1, 2)
            copies.append(
                pltpu.make_async_copy(
                    made_ref.at[:, both], out_ref.at[:, both], sems.at[k // 2]
                )
            )
            copies[-1].start()
    for copy in copies:
        copy.wait()


def filter_kernel(circle_ref, basis_ref, weight_ref, out_ref, piece_ref, sems):
    pieces, part, lanes = circle_ref.shape
    modes = weight_ref.shape[1]
    pairs = range(0, pieces, 2)
    total = jnp.zeros((2 * part, 2 * modes), jnp.float32)
    for o in pairs:
        parts = zip(split(circle_ref[o]), split(circle_ref[o + 1]))
        x = jnp.concatenate([jnp.concatenate(p, axis=1) for p in parts], axis=0)
        total = total + product(x, basis_ref[lanes * o : lanes * (o + 2)], ((1,), (0,)))
    total = total[:part] + total[part:]
    total = (total[:, :modes] + total[:, modes:]) * weight_ref[...]
    y = jnp.concatenate([jnp.concatenate([p, p], axis=1) for p in split(total)], axis=0)
    copies = []
    for o in pairs:
        x = product(y, basis_ref[lanes * o : lanes * (o + 2)], ((1,), (1,)))
        x = x[:part] + x[part:]
        piece_ref[o] = x[:, :lanes]
        piece_ref[o + 1] = x[:, lanes:]
        both = pl.ds(o, 2)
        copies.append(
            pltpu.make_async_copy(piece_ref.at[both], out_ref.at[both], sems.at[o // 2])
        )
        copies[-1].start()
    for copy in copies:
        copy.wait()


def blend_kernel(state_ref, smooth_ref, wet_ref, flag_ref, out_ref, piece_ref, sems):
    levels = wet_ref.shape[0]
    flag = flag_ref[...]
    copies = []
    for f in range(4):
        for k in range(levels):
            state = state_ref[f, k]
            gate = flag * wet_ref[k]
            piece_ref[f, k] = state + gate * (smooth_ref[f, k] - state)
        copies.append(pltpu.make_async_copy(piece_ref.at[f], out_ref.at[f], sems.at[f]))
        copies[-1].start()
    for copy in copies:
        copy.wait()


def call(kernel, outs, scratch=(), sems=0, raw=False, sent=False, flops=0):
    vmem = pl.BlockSpec(memory_space=pltpu.VMEM)
    away = pl.BlockSpec(memory_space=pl.ANY)
    specs = [vmem] * len(outs)
    shapes = [jax.ShapeDtypeStruct(s, jnp.float32) for s in outs]
    if sent:
        specs[-1] = away
        shapes[-1] = pltpu.HBM(outs[-1], jnp.float32)
    buffers = [pltpu.VMEM(s, jnp.float32) if isinstance(s, tuple) else s for s in scratch]
    if sems:
        buffers.append(pltpu.SemaphoreType.DMA((sems,)))
    cost = pl.CostEstimate(
        flops=flops, transcendentals=0, bytes_accessed=4 * sum(map(math.prod, outs))
    )

    def run(*args):
        if raw:
            args = [pltpu.with_memory_space_constraint(x, pltpu.HBM) for x in args]
        return pl.pallas_call(
            kernel,
            out_shape=shapes,
            in_specs=[away if raw else vmem] * len(args),
            out_specs=specs,
            scratch_shapes=buffers,
            compiler_params=pltpu.CompilerParams(vmem_limit_bytes=24 << 20),
            cost_estimate=cost,
        )(*args)

    return run


def swap_edges(before_src, after_src, axis):
    peers = lax.axis_size(axis)
    up = [(i, (i + 1) % peers) for i in range(peers)]
    down = [(j, i) for i, j in up]
    return lax.ppermute(before_src, axis, up), lax.ppermute(after_src, axis, down)


def mode_basis(length, modes):
    turns = np.arange(modes)[None, :] * np.arange(length)[:, None] % length
    angle = turns * (2.0 * math.pi / length)
    basis = np.concatenate([np.cos(angle), np.sin(angle)], axis=1).astype(np.float32)
    high = basis.astype(ml_dtypes.bfloat16)
    low = (basis - high.astype(np.float32)).astype(ml_dtypes.bfloat16)
    return np.concatenate([high, low], axis=1)


def joint_basis(basis, lanes):
    length = basis.shape[0]
    tile, lane = np.divmod(np.arange(length // 2), lanes)
    half, c = np.divmod(lane % GROUP, 8)
    column = (lanes * (2 * tile + half + 1) + c - 4) % length
    return np.where(((c >= 2) & (c < 6))[:, None], basis[column], np.zeros_like(basis[column]))


def mode_weights(counts, modes, length):
    order = jnp.arange(modes).astype(jnp.float32)
    keep = (order[None, :] < counts[:, None]).astype(jnp.float32)
    scale = jnp.where(order == 0, 1.0, 2.0) / length
    weights = keep * scale[None, :]
    return jnp.concatenate([weights, weights], axis=1)


def shards(ocean_state, thickness, wet_mask, mode_counts, row_flags):
    levels, rows, lanes = ocean_state.shape[1:]
    assert rows % 8 == 0 and lanes == LANES and levels * GROUP <= LANES
    lon_peers = lax.axis_size("lon")
    lat_peers = lax.axis_size("lat")
    nlat = rows * lat_peers
    nlon = lanes * lon_peers
    full = rows + 8
    total = 4 * levels * rows
    part = total // lon_peers
    lat_pos = lax.axis_index("lat")
    first_row = lat_pos * rows
    cells = 4 * levels * full * lanes
    edge_rows = (6, levels, 2, lanes)

    paired = rows == 2 * lon_peers and rows >= FBAND and lat_peers % 2 == 0 and levels % 2 == 0
    *block, first, last, flags, counts, table, end_table, joint_table = call(
        functools.partial(load_kernel, paired),
        [ocean_state.shape, thickness.shape, thickness.shape, edge_rows, edge_rows]
        + [(rows, lanes)] * 2
        + [(2, full, lanes), (2, 8, lanes), (2, 8, lanes)],
        [pltpu.VMEM(shape, jnp.int32) for shape in (thickness.shape, (1, rows), (1, rows))],
        sems=8,
        raw=True,
    )(ocean_state, thickness, wet_mask, row_flags[None], mode_counts[None])

    def ready():
        return call(
            ready_kernel, [(6, rows, LANES), (5, levels, rows, lanes)], flops=20 * cells
        )(*block, table)

    def exchanged(below, above, own, terms):
        inner, edges, halo = call(
            inner_kernel,
            [(3, 4, levels, full, lanes), (6, full, LANES), (6, levels, 8, lanes)],
            [(5, levels, 8, lanes), (2, levels, full, lanes)],
            flops=60 * cells,
        )(*block, below, above, table, own, terms)
        first, last = call(pack_kernel, [(full, LANES)] * 2)(*block, halo)
        from_west, from_east = swap_edges(last, first, "lon")
        return call(
            edge_kernel,
            [ocean_state.shape] * 2,
            [(4, full, LANES), (7, full, LANES)],
            sems=4,
            sent=True,
        )(inner, edges, from_west, from_east, table)

    banded = (first_row < FBAND) | (first_row + rows > nlat - FBAND)
    modes = mode_basis(nlon, MAXM)
    basis, at_joints = lax.optimization_barrier(
        (jnp.asarray(modes), jnp.asarray(joint_basis(modes, lanes)))
    )
    lon_pos = lax.axis_index("lon")

    def circled(got, own, closed):
        main = 8 * levels
        tile = (levels, 8, lanes)
        state, sent = call(
            end_kernel,
            [ocean_state.shape, (lon_peers, main + 24, lanes)],
            [(2,) + tile, (6,) + tile, (3, 4) + tile, (7,) + tile, (3, full, lanes)],
        )(*block, got, own, closed, end_table)
        circles = lax.all_to_all(sent, "lon", 0, 0, tiled=True)
        pieces = call(
            circle_kernel,
            [(lon_peers, main + 8, lanes)],
            [
                (6, 4 * lon_peers, lanes),
                (7, 4 * lon_peers, lanes),
                (4 * lon_peers, lanes),
            ],
        )(circles, joint_table, basis, at_joints, counts)[0]
        pieces = lax.all_to_all(pieces, "lon", 0, 0, tiled=True)
        return call(
            join_kernel, [ocean_state.shape], [ocean_state.shape], sems=levels // 2, sent=True
        )(state, pieces, block[2], flags)[0]

    def between(got, *_):
        pairs = [(i, i + 1) for i in range(1, lat_peers - 1, 2)]
        other = lax.ppermute(last, "lat", pairs + [(j, i) for i, j in pairs])
        even = lat_pos % 2 == 0
        below, above = jnp.where(even, other, got), jnp.where(even, got, other)
        return exchanged(below, above, *ready())[1]

    if paired:
        got = lax.ppermute(first, "lat", [(i, i ^ 1) for i in range(lat_peers)])
        own, closed = call(
            closed_kernel,
            [(6, rows, LANES), (3, 4, levels, rows, lanes)],
            [(7, levels, rows, lanes)],
            flops=60 * cells,
        )(*block, table)
        got, own, closed = lax.optimization_barrier((got, own, closed))
        return lax.cond(banded, circled, between, got, own, closed)

    below, above = swap_edges(last, first, "lat")
    state, sent = exchanged(*lax.optimization_barrier((below, above, *ready())))

    def filtered():
        row_counts = lax.dynamic_slice(
            jnp.broadcast_to(
                mode_counts.astype(jnp.float32)[None], (4 * levels, rows)
            ).reshape(total),
            (lon_pos * part,),
            (part,),
        )
        circles = lax.all_to_all(
            sent.reshape(lon_peers, part, lanes), "lon", 0, 0, tiled=True
        )
        smooth = call(
            filter_kernel, [circles.shape], [circles.shape], sems=lon_peers // 2, sent=True
        )(circles, basis, mode_weights(row_counts, MAXM, nlon))[0]
        smooth = lax.all_to_all(smooth, "lon", 0, 0, tiled=True).reshape(state.shape)
        return call(blend_kernel, [state.shape], [state.shape], sems=4, sent=True)(
            state, smooth, block[2], flags
        )[0]

    return lax.cond(banded, filtered, lambda: sent)


def solution(mesh):
    in_specs = (
        P(None, None, "lat", "lon"),
        P(None, "lat", "lon"),
        P(None, "lat", "lon"),
        P("lat"),
        P("lat"),
    )
    out_specs = P(None, None, "lat", "lon")
    return jax.shard_map(shards, mesh=mesh, in_specs=in_specs, out_specs=out_specs, check_vma=False)
```

```python
import functools
import math

import jax
import jax.numpy as jnp
import ml_dtypes
import numpy as np
from jax import lax
from jax.experimental import pallas as pl
from jax.experimental.pallas import tpu as pltpu
from jax.sharding import PartitionSpec as P

FBAND = 16
MAXM = 64
LANES = 128
DEGREE = LANES // 2
GROUP = 16


lat_edge = 1.3
diffusion = 0.05
vertical_mix = 0.5
time_step = 0.05


def roll(x, shift, axis):
    shift %= x.shape[axis]
    return pltpu.roll(x, shift, axis) if shift else x


def east(x):
    return roll(x, -1, 1)


def west(x):
    return roll(x, 1, 1)


def north(x):
    return roll(x, -1, 0)


def south(x):
    return roll(x, 1, 0)


def lane_of(shape):
    return lax.broadcasted_iota(jnp.int32, shape, 1)


def east_terms(h, w, inv_c):
    open_e = 0.5 * (h + east(h)) * (w * east(w))
    return 0.25 * open_e, diffusion * open_e * inv_c


def north_terms(h, w, face):
    open_n = 0.5 * (h + north(h)) * (w * north(w)) * face
    return 0.25 * open_n, diffusion * open_n


def advance(fields, terms, scale, scale_c, vertical):
    quarter_e, spread_e, quarter_n, spread_n = terms
    u, v = fields[2], fields[3]
    speed_e = quarter_e * (u + east(u))
    speed_n = quarter_n * (v + north(v))
    here_e, there_e = speed_e + spread_e, speed_e - spread_e
    here_n, there_n = speed_n + spread_n, speed_n - spread_n
    fresh = []
    for q, vert in zip(fields, vertical):
        flux_e = here_e * q + there_e * east(q)
        flux_n = here_n * q + there_n * north(q)
        spread = (flux_e - west(flux_e)) + (flux_n - south(flux_n))
        fresh.append(q + scale * vert - scale_c * spread)
    return fresh


def own_columns(load, levels, lanes, rows):
    lane = lane_of((rows, LANES))
    own = jnp.zeros((rows, LANES), jnp.float32)
    for k in range(levels):
        x = load(k)
        at = GROUP * k + 2
        own = jnp.where((lane >= at) & (lane < at + 4), roll(x, at, 1), own)
        at = GROUP * k + 8
        own = jnp.where((lane >= at) & (lane < at + 4), roll(x, at + 4 - lanes, 1), own)
    return own


def row_terms(thick, wet, inv_c, levels, term_ref):
    w, h = wet(0), thick(0)
    hs = jnp.where(w > 0, h, 1.0)
    for k in range(levels):
        term_ref[0, k], term_ref[1, k] = east_terms(h, w, inv_c)
        scale = time_step * w / hs
        term_ref[2, k] = scale
        term_ref[3, k] = scale * inv_c
        if k + 1 < levels:
            w_next, h_next = wet(k + 1), thick(k + 1)
            hs_next = jnp.where(w_next > 0, h_next, 1.0)
            term_ref[4, k] = w * w_next * vertical_mix / (0.5 * (hs + hs_next))
            w, h, hs = w_next, h_next, hs_next


def fill_table(ref, place, nlat):
    place = place.astype(jnp.float32)
    ref[0] = 1.0 / jnp.cos(lat_edge * (2.0 * (place + 0.5) / nlat - 1.0))
    ref[1] = jnp.cos(lat_edge * (2.0 * (place + 1.0) / nlat - 1.0))


def ring_rows(rows):
    place = lax.broadcasted_iota(jnp.int32, (rows + 8, LANES), 0)
    return jnp.where(place < rows + 2, place, jnp.where(place < rows + 6, 0, place - rows - 8))


def load_kernel(
    paired,
    state_any,
    thick_any,
    wet_any,
    flag_any,
    count_any,
    state_ref,
    thick_ref,
    wet_ref,
    first_ref,
    last_ref,
    flag_ref,
    count_ref,
    table_ref,
    end_table_ref,
    joint_table_ref,
    raw_ref,
    raw_flag_ref,
    raw_count_ref,
    sems,
):
    levels, rows = thick_ref.shape[:2]
    moves = [(flag_any, raw_flag_ref), (count_any, raw_count_ref), (wet_any, raw_ref)]
    moves += [(thick_any, thick_ref)]
    moves += [(state_any.at[f], state_ref.at[f]) for f in range(4)]
    copies = [pltpu.make_async_copy(*pair, sems.at[i]) for i, pair in enumerate(moves)]
    for copy in copies:
        copy.start()
    nlat = rows * lax.axis_size("lat")
    lat_pos = lax.axis_index("lat")
    first_row = lat_pos * rows
    fill_table(table_ref, first_row + ring_rows(rows), nlat)
    if paired:
        six = jnp.minimum(lax.broadcasted_iota(jnp.int32, (8, LANES), 0), 5)
        end = jnp.where(lat_pos == 0, rows - 4, -2)
        fill_table(end_table_ref, first_row + end + six, nlat)
        fill_table(joint_table_ref, first_row + 2 * lax.axis_index("lon") - 2 + six, nlat)
    for copy in copies[:3]:
        copy.wait()
    shape = (rows, rows)
    diagonal = lax.broadcasted_iota(jnp.int32, shape, 0) == lane_of(shape)
    for raw, ref in ((raw_flag_ref, flag_ref), (raw_count_ref, count_ref)):
        spread = jnp.broadcast_to(raw[...].astype(jnp.float32), shape)
        value = jnp.sum(jnp.where(diagonal, spread, 0.0), axis=1, keepdims=True)
        ref[...] = jnp.broadcast_to(value, (rows, LANES))
    for k in range(levels):
        wet_ref[k] = raw_ref[k].astype(jnp.float32)
    for copy in copies[3:]:
        copy.wait()
    for f in range(6):
        for k in range(levels):
            x = state_ref.at[f, k] if f < 4 else (thick_ref, wet_ref)[f - 4].at[k]
            first_ref[f, k] = x[0:2]
            last_ref[f, k] = x[rows - 2 : rows]
    if paired:
        even = lax.axis_index("lat") % 2 == 0
        for f in range(6):
            for k in range(levels):
                low, high = first_ref[f, k], last_ref[f, k]
                first_ref[f, k] = jnp.where(even, high, low)
                last_ref[f, k] = jnp.where(even, low, high)


def ready_kernel(state_ref, thick_ref, wet_ref, table_ref, own_ref, term_ref):
    levels, rows, lanes = thick_ref.shape

    def thick(k):
        return thick_ref[k]

    def wet(k):
        return wet_ref[k]

    for f in range(4):
        own_ref[f] = own_columns(lambda k, f=f: state_ref[f, k], levels, lanes, rows)
    own_ref[4] = own_columns(thick, levels, lanes, rows)
    own_ref[5] = own_columns(wet, levels, lanes, rows)
    row_terms(thick, wet, table_ref[0, :rows], levels, term_ref)


def pack_kernel(state_ref, thick_ref, wet_ref, halo_ref, first_ref, last_ref):
    levels, rows, lanes = thick_ref.shape
    lane = lane_of((8, LANES))
    for t in range(rows // 8 + 1):
        first = jnp.zeros((8, LANES), jnp.float32)
        last = jnp.zeros((8, LANES), jnp.float32)
        part = slice(8 * t, 8 * t + 8)
        for f in range(6):
            for k in range(levels):
                if t == rows // 8:
                    x = halo_ref[f, k]
                elif f < 4:
                    x = state_ref[f, k, part]
                elif f == 4:
                    x = thick_ref[k, part]
                else:
                    x = wet_ref[k, part]
                at = GROUP * f + 2 * k
                mine = (lane >= at) & (lane < at + 2)
                first = jnp.where(mine, roll(x, at, 1), first)
                last = jnp.where(mine, roll(x, at + 2 - lanes, 1), last)
        first_ref[part] = first
        last_ref[part] = last


def inner_kernel(
    state_ref,
    thick_ref,
    wet_ref,
    below_ref,
    above_ref,
    table_ref,
    own_ref,
    term_ref,
    out_ref,
    edge_ref,
    halo_ref,
    halo_term_ref,
    north_ref,
):
    levels, rows, lanes = thick_ref.shape
    full = rows + 8
    face = table_ref[1]
    lat_pos = lax.axis_index("lat")
    with_below = jnp.where(lat_pos > 0, 1.0, 0.0)
    with_above = jnp.where(lat_pos < lax.axis_size("lat") - 1, 1.0, 0.0)
    for f in range(6):
        for k in range(levels):
            halo_ref[f, k, 0:2] = above_ref[f, k] * with_above
            halo_ref[f, k, 2:6] = jnp.zeros((4, lanes), jnp.float32)
            halo_ref[f, k, 6:8] = below_ref[f, k] * with_below

    def joined(x, y):
        return jnp.concatenate([x, y], axis=0)

    def halo(f):
        return lambda k: halo_ref[f, k]

    for f in range(6):
        edge_ref[f, :rows] = own_ref[f]
        edge_ref[f, rows:] = own_columns(halo(f), levels, lanes, 8)
    row_terms(halo(4), halo(5), table_ref[0, rows:], levels, halo_term_ref)
    for k in range(levels):
        h = joined(thick_ref[k], halo_ref[4, k])
        w = joined(wet_ref[k], halo_ref[5, k])
        north_ref[0, k], north_ref[1, k] = north_terms(h, w, face)
        for f in range(4):
            out_ref[0, f, k] = joined(state_ref[f, k], halo_ref[f, k])

    def term(i, k):
        return joined(term_ref[i, k], halo_term_ref[i, k])

    def step(i, _):
        source, target = out_ref.at[i], out_ref.at[i + 1]
        fields = [source[f, 0] for f in range(4)]
        above = [jnp.zeros((full, LANES), jnp.float32)] * 4
        for k in range(levels):
            deeper = below = above
            if k + 1 < levels:
                couple = term(4, k)
                deeper = [source[f, k + 1] for f in range(4)]
                below = [couple * (d - q) for d, q in zip(deeper, fields)]
                vertical = [b - a for b, a in zip(below, above)]
            else:
                vertical = [-a for a in above]
            terms = term(0, k), term(1, k), north_ref[0, k], north_ref[1, k]
            fresh = advance(fields, terms, term(2, k), term(3, k), vertical)
            for f in range(4):
                target[f, k] = fresh[f]
            fields, above = deeper, below
        return 0

    lax.fori_loop(0, 2, step, 0)


def step_tile(tile_ref, h, w, levels, inv_c, face, term_ref):
    lane = lane_of(h.shape)

    def deeper(x):
        return roll(x, -GROUP, 1)

    def shallower(x):
        return roll(x, GROUP, 1)

    hs = jnp.where(w > 0, h, 1.0)
    scale = time_step * w / hs
    couple = w * deeper(w) * vertical_mix / (0.5 * (hs + deeper(hs)))
    couple = jnp.where(lane < GROUP * (levels - 1), couple, 0.0)
    terms = east_terms(h, w, inv_c) + north_terms(h, w, face)
    for i, term in enumerate(terms + (scale, scale * inv_c, couple)):
        term_ref[i] = term

    def step():
        terms = [term_ref[i] for i in range(7)]
        fields = [tile_ref[f] for f in range(4)]
        vertical = []
        for q in fields:
            down = terms[6] * (deeper(q) - q)
            vertical.append(down - shallower(down))
        for f, q in enumerate(advance(fields, terms[:4], terms[4], terms[5], vertical)):
            tile_ref[f] = q

    step()
    step()


def edge_kernel(
    inner_ref, own_ref, west_ref, east_ref, table_ref, out_ref, send_ref, tile_ref, term_ref, sems
):
    levels, rows, lanes = out_ref.shape[1:]
    full = rows + 8
    lane = lane_of((full, LANES))
    from_west, from_east = west_ref[...], east_ref[...]

    def joined(f):
        x = own_ref[f]
        for k in range(levels):
            src = GROUP * f + 2 * k
            at = GROUP * k
            x = jnp.where((lane >= at) & (lane < at + 2), roll(from_west, at - src, 1), x)
            at = GROUP * k + 12
            x = jnp.where((lane >= at) & (lane < at + 2), roll(from_east, at - src, 1), x)
        return x

    for f in range(4):
        tile_ref[f] = joined(f)
    step_tile(tile_ref, joined(4), joined(5), levels, table_ref[0], table_ref[1], term_ref)
    lane = lane_of((rows, LANES))
    for f in range(4):
        x = tile_ref[f, :rows]
        for k in range(levels):
            left = roll(x, -(GROUP * k + 2), 1)
            right = roll(x, lanes - 2 - (GROUP * k + 10), 1)
            out_ref[f, k] = jnp.where(
                lane < 2,
                left,
                jnp.where(lane >= lanes - 2, right, inner_ref[2, f, k, :rows]),
            )
        pltpu.make_async_copy(out_ref.at[f], send_ref.at[f], sems.at[f]).start()
    for f in range(4):
        pltpu.make_async_copy(out_ref.at[f], send_ref.at[f], sems.at[f]).wait()


def split(x):
    high = x.astype(jnp.bfloat16)
    return high, (x - high.astype(jnp.float32)).astype(jnp.bfloat16)


def product(a, b, dims):
    return lax.dot_general(a, b, (dims, ((), ())), preferred_element_type=jnp.float32)


def unpack(x):
    left = lane_of(x.shape) < DEGREE
    return jnp.concatenate([jnp.where(left, x, 0.0), jnp.where(left, 0.0, x)], axis=0)


def pairs_of_rows(tiles, t, place):
    sub = lax.broadcasted_iota(jnp.int32, tiles[0].shape, 0) // 2
    for y in range(4):
        made = roll(tiles[0], -2 * y, 0)
        for x in range(1, 4):
            made = jnp.where(sub == x, roll(tiles[x], 2 * (x - y), 0), made)
        place(y, made)


def step_levels(buf_ref, term_ref, loop):
    levels, size = buf_ref.shape[2:4]

    def step(i, _):
        source, target = buf_ref.at[i], buf_ref.at[i + 1]
        fields = [source[f, 0] for f in range(4)]
        above = [jnp.zeros((size, LANES), jnp.float32)] * 4
        for k in range(levels):
            deeper = below = above
            if k + 1 < levels:
                couple = term_ref[4, k]
                deeper = [source[f, k + 1] for f in range(4)]
                below = [couple * (d - q) for d, q in zip(deeper, fields)]
                vertical = [b - a for b, a in zip(below, above)]
            else:
                vertical = [-a for a in above]
            terms = [term_ref[i, k] for i in (0, 1, 5, 6)]
            fresh = advance(fields, terms, term_ref[2, k], term_ref[3, k], vertical)
            for f in range(4):
                target[f, k] = fresh[f]
            fields, above = deeper, below
        return 0

    if loop:
        lax.fori_loop(0, 2, step, 0)
    else:
        step(1, step(0, 0))


def closed_kernel(state_ref, thick_ref, wet_ref, table_ref, own_ref, buf_ref, term_ref):
    levels, rows, lanes = thick_ref.shape

    def thick(k):
        return thick_ref[k]

    def wet(k):
        return wet_ref[k]

    for f in range(4):
        own_ref[f] = own_columns(lambda k, f=f: state_ref[f, k], levels, lanes, rows)
    own_ref[4] = own_columns(thick, levels, lanes, rows)
    own_ref[5] = own_columns(wet, levels, lanes, rows)
    row_terms(thick, wet, table_ref[0, :rows], levels, term_ref)
    row = lax.broadcasted_iota(jnp.int32, (rows, LANES), 0)
    face = jnp.where(row < rows - 1, table_ref[1, :rows], 0.0)
    for k in range(levels):
        term_ref[5, k], term_ref[6, k] = north_terms(thick(k), wet(k), face)
        for f in range(4):
            buf_ref[0, f, k] = state_ref[f, k]
    step_levels(buf_ref, term_ref, True)


def end_kernel(
    state_ref,
    thick_ref,
    wet_ref,
    got_ref,
    own_ref,
    closed_ref,
    table_ref,
    sums_ref,
    out_ref,
    send_ref,
    field_ref,
    halo_ref,
    buf_ref,
    term_ref,
    raw_ref,
    main_ref,
):
    levels, rows, lanes = thick_ref.shape
    full = rows + 8
    top = lax.axis_index("lat") == 0
    at_top = jnp.where(top, 1.0, 0.0)
    at_bottom = jnp.where(top, 0.0, 1.0)
    sub = lax.broadcasted_iota(jnp.int32, (8, LANES), 0)

    def own(f, k, part):
        return state_ref[f, k, part] if f < 4 else (thick_ref, wet_ref)[f - 4][k, part]

    for f in range(6):
        for k in range(levels):
            halo_ref[f, k, 0:2] = got_ref[f, k] * at_top
            halo_ref[f, k, 2:6] = jnp.zeros((4, lanes), jnp.float32)
            halo_ref[f, k, 6:8] = got_ref[f, k] * at_bottom
    for f in range(6):
        for k in range(levels):
            halo = halo_ref[f, k]
            beyond = jnp.where(sub < 6, roll(halo, 4, 0), 0.0)
            high = jnp.where(sub < 4, roll(own(f, k, slice(rows - 8, rows)), -4, 0), beyond)
            low = jnp.where(sub < 2, roll(halo, 2, 0), roll(own(f, k, slice(0, 8)), 2, 0))
            tile = jnp.where(top, high, low)
            if f < 4:
                buf_ref[0, f, k] = tile
            else:
                field_ref[f - 4, k] = tile

    def thick(k):
        return field_ref[0, k]

    def wet(k):
        return field_ref[1, k]

    row_terms(thick, wet, table_ref[0], levels, term_ref)
    for k in range(levels):
        term_ref[5, k], term_ref[6, k] = north_terms(thick(k), wet(k), table_ref[1])
    step_levels(buf_ref, term_ref, False)
    c = lane_of((full, LANES)) % GROUP

    def ring(f):
        beyond = own_columns(lambda k: halo_ref[f, k], levels, lanes, 8)
        return jnp.concatenate([own_ref[f], beyond], axis=0)

    for i in range(3):
        a, b = ring(2 * i), ring(2 * i + 1)
        one = jnp.where(c < 4, roll(a, -2, 1), roll(a, -4, 1))
        two = jnp.where(c < 12, roll(b, 6, 1), roll(b, 4, 1))
        both = jnp.where(c < 8, one, two)
        raw_ref[i, 0:2] = both[full - 2 : full]
        raw_ref[i, 2 : rows + 4] = both[: rows + 2]
        raw_ref[i, rows + 4 : full] = jnp.zeros((4, LANES), jnp.float32)
    main = 8 * levels
    half = main // 2
    last = rows // 8 - 1
    for t in range(rows // 8):
        part = slice(8 * t, 8 * t + 8)
        for k in range(levels):
            tiles = []
            for f in range(4):
                x = closed_ref[2, f, k, part]
                if t == last:
                    fixed = jnp.where(sub >= 6, roll(buf_ref[2, f, k], 4, 0), x)
                    x = jnp.where(top, fixed, x)
                if t == 0:
                    fixed = jnp.where(sub < 2, roll(buf_ref[2, f, k], -2, 0), x)
                    x = jnp.where(top, x, fixed)
                out_ref[f, k, part] = x
                tiles.append(x)

            def place(y, tile, t=t, k=k):
                at = main * (4 * t + y) + 8 * k
                main_ref[at : at + 8] = tile

            pairs_of_rows(tiles, t, place)
        for p in range(4 * t, 4 * t + 4):
            for i in range(3):
                send_ref[p, half + 8 * i : half + 8 * i + 8] = raw_ref[i, 2 * p : 2 * p + 8]
    x = jnp.concatenate(split(main_ref[...]), axis=1)
    x = product(x, jnp.concatenate([sums_ref[...]] * 2, axis=0), ((1,), (0,)))
    x = x + roll(x, DEGREE, 1)
    left = lane_of((half, LANES)) < DEGREE
    for p in range(send_ref.shape[0]):
        at = main * p
        send_ref[p, :half] = jnp.where(left, x[at : at + half], x[at + half : at + main])


def circle_kernel(
    circle_ref,
    table_ref,
    basis_ref,
    joint_basis_ref,
    count_ref,
    out_ref,
    tile_ref,
    term_ref,
    joint_ref,
):
    peers = circle_ref.shape[0]
    modes = basis_ref.shape[1] // 2
    length = basis_ref.shape[0]
    half = circle_ref.shape[1] - 24
    main = 2 * half
    levels = main // 8
    lanes = LANES
    lane = lane_of((8, LANES))
    c = lane % GROUP
    for j in range(0, peers, 2):
        part = slice(4 * j, 4 * j + 8)
        for i in range(3):
            x, y, z = (
                circle_ref[(j + d) % peers, half + 8 * i : half + 8 * i + 8] for d in range(3)
            )
            for f, shift in ((2 * i, 0), (2 * i + 1, -8)):
                middle = jnp.where(c < 12, roll(y, 4 + shift, 1), roll(z, 12 + shift, 1))
                tile_ref[f, part] = jnp.where(c < 4, roll(x, shift - 4, 1), middle)
    inv_c, face = (jnp.concatenate([table_ref[i]] * (peers // 2), axis=0) for i in (0, 1))
    step_tile(tile_ref, tile_ref[4], tile_ref[5], levels, inv_c, face, term_ref)
    sub = lax.broadcasted_iota(jnp.int32, (8, LANES), 0) // 2
    right = (c % 8 >= 2) & (c % 8 < 6)
    for j in range(peers // 2):
        made = jnp.zeros((8, LANES), jnp.float32)
        for f in range(4):
            x = tile_ref[f, 8 * j : 8 * j + 8]
            made = jnp.where(sub == f, roll(x, 2 * f - 2, 0), made)
        joint_ref[8 * j : 8 * j + 8] = jnp.where(right, made, 0.0)
    lane_main = lane_of((main, LANES))
    row_main = lax.broadcasted_iota(jnp.int32, (main, LANES), 0)
    at_level = lane_main // GROUP == row_main // 8

    def block(o):
        return unpack(circle_ref[o, :half])

    def joint(j):
        x = joint_ref[8 * j : 8 * j + 8]
        return jnp.where(at_level, jnp.concatenate([x] * levels, axis=0), 0.0)

    total = jnp.zeros((2 * main, 2 * modes), jnp.float32)
    for source, basis, count in (
        (block, basis_ref, peers),
        (joint, joint_basis_ref, peers // 2),
    ):
        for o in range(0, count, 2):
            parts = zip(split(source(o)), split(source(o + 1)))
            x = jnp.concatenate([jnp.concatenate(p, axis=1) for p in parts], axis=0)
            total = total + product(x, basis[lanes * o : lanes * (o + 2)], ((1,), (0,)))
    total = total[:main] + total[main:]
    counts = count_ref[...]
    row = lax.broadcasted_iota(jnp.int32, counts.shape, 0)
    own = 2 * lax.axis_index("lon")
    even, odd = (
        jnp.sum(jnp.where(row == own + r, counts, 0.0), axis=0, keepdims=True) for r in (0, 1)
    )
    limit = jnp.where(row_main % 2 == 0, even, odd)
    order = (lane_main % (modes // 2)).astype(jnp.float32)
    weight = jnp.where(order < limit, jnp.where(order == 0.0, 1.0 / length, 2.0 / length), 0.0)
    total = (total[:, :modes] + total[:, modes:]) * weight
    y = jnp.concatenate([jnp.concatenate([p, p], axis=1) for p in split(total)], axis=0)
    for o in range(0, peers, 2):
        x = product(y, basis_ref[lanes * o : lanes * (o + 2)], ((1,), (1,)))
        x = x[:main] + x[main:]
        left = lane_of((half, LANES)) < DEGREE
        out_ref[o, :half] = jnp.where(left, x[:half, :lanes], x[half:, :lanes])
        out_ref[o + 1, :half] = jnp.where(left, x[:half, lanes:], x[half:, lanes:])
        before = (4 * o - 8) % (4 * peers)
        here = joint_ref[4 * o : 4 * o + 8]
        out_ref[o, half:] = jnp.where(
            c < 8, roll(joint_ref[before : before + 8], -8, 1), roll(here, 8, 1)
        )
        out_ref[o + 1, half:] = here


def join_kernel(
    state_ref, piece_ref, wet_ref, flag_ref, columns_ref, out_ref, made_ref, smooth_ref, sems
):
    levels, rows, lanes = wet_ref.shape
    main = 8 * levels
    half = main // 2
    lane = lane_of((8, LANES))
    x = jnp.concatenate(
        [unpack(piece_ref[p, :half]) for p in range(piece_ref.shape[0])], axis=0
    )
    x = jnp.concatenate(split(x), axis=1)
    x = product(x, jnp.concatenate([columns_ref[...]] * 2, axis=0), ((1,), (0,)))
    smooth_ref[...] = x[:, :lanes] + x[:, lanes:]
    edges = [{} for _ in range(rows // 8)]
    for t, into in enumerate(edges):
        tiles = [piece_ref[4 * t + x, half : half + 8] for x in range(4)]
        pairs_of_rows(tiles, t, into.__setitem__)
    copies = []
    for k in range(levels):
        for t in range(rows // 8):
            part = slice(8 * t, 8 * t + 8)
            starts = [main * (4 * t + x) + 8 * k for x in range(4)]
            tiles = [smooth_ref[at : at + 8] for at in starts]
            gate = flag_ref[part] * wet_ref[k, part]

            def place(f, smooth, k=k, gate=gate, part=part, edge=edges[t]):
                first = roll(edge[f], -(GROUP * k + 4), 1)
                last = roll(edge[f], lanes - 2 - (GROUP * k + 10), 1)
                state = jnp.where(
                    lane < 2, first, jnp.where(lane >= lanes - 2, last, state_ref[f, k, part])
                )
                made_ref[f, k, part] = state + gate * (smooth - state)

            pairs_of_rows(tiles, t, place)
        if k % 2:
            both = pl.ds(k - 1, 2)
            copies.append(
                pltpu.make_async_copy(
                    made_ref.at[:, both], out_ref.at[:, both], sems.at[k // 2]
                )
            )
            copies[-1].start()
    for copy in copies:
        copy.wait()


def filter_kernel(circle_ref, basis_ref, weight_ref, out_ref, piece_ref, sems):
    pieces, part, lanes = circle_ref.shape
    modes = weight_ref.shape[1]
    pairs = range(0, pieces, 2)
    total = jnp.zeros((2 * part, 2 * modes), jnp.float32)
    for o in pairs:
        parts = zip(split(circle_ref[o]), split(circle_ref[o + 1]))
        x = jnp.concatenate([jnp.concatenate(p, axis=1) for p in parts], axis=0)
        total = total + product(x, basis_ref[lanes * o : lanes * (o + 2)], ((1,), (0,)))
    total = total[:part] + total[part:]
    total = (total[:, :modes] + total[:, modes:]) * weight_ref[...]
    y = jnp.concatenate([jnp.concatenate([p, p], axis=1) for p in split(total)], axis=0)
    copies = []
    for o in pairs:
        x = product(y, basis_ref[lanes * o : lanes * (o + 2)], ((1,), (1,)))
        x = x[:part] + x[part:]
        piece_ref[o] = x[:, :lanes]
        piece_ref[o + 1] = x[:, lanes:]
        both = pl.ds(o, 2)
        copies.append(
            pltpu.make_async_copy(piece_ref.at[both], out_ref.at[both], sems.at[o // 2])
        )
        copies[-1].start()
    for copy in copies:
        copy.wait()


def blend_kernel(state_ref, smooth_ref, wet_ref, flag_ref, out_ref, piece_ref, sems):
    levels = wet_ref.shape[0]
    flag = flag_ref[...]
    copies = []
    for f in range(4):
        for k in range(levels):
            state = state_ref[f, k]
            gate = flag * wet_ref[k]
            piece_ref[f, k] = state + gate * (smooth_ref[f, k] - state)
        copies.append(pltpu.make_async_copy(piece_ref.at[f], out_ref.at[f], sems.at[f]))
        copies[-1].start()
    for copy in copies:
        copy.wait()


def call(kernel, outs, scratch=(), sems=0, raw=False, sent=False, flops=0):
    vmem = pl.BlockSpec(memory_space=pltpu.VMEM)
    away = pl.BlockSpec(memory_space=pl.ANY)
    specs = [vmem] * len(outs)
    shapes = [jax.ShapeDtypeStruct(s, jnp.float32) for s in outs]
    if sent:
        specs[-1] = away
        shapes[-1] = pltpu.HBM(outs[-1], jnp.float32)
    buffers = [pltpu.VMEM(s, jnp.float32) if isinstance(s, tuple) else s for s in scratch]
    if sems:
        buffers.append(pltpu.SemaphoreType.DMA((sems,)))
    cost = pl.CostEstimate(
        flops=flops, transcendentals=0, bytes_accessed=4 * sum(map(math.prod, outs))
    )

    def run(*args):
        if raw:
            args = [pltpu.with_memory_space_constraint(x, pltpu.HBM) for x in args]
        return pl.pallas_call(
            kernel,
            out_shape=shapes,
            in_specs=[away if raw else vmem] * len(args),
            out_specs=specs,
            scratch_shapes=buffers,
            compiler_params=pltpu.CompilerParams(vmem_limit_bytes=24 << 20),
            cost_estimate=cost,
        )(*args)

    return run


def swap_edges(before_src, after_src, axis):
    peers = lax.axis_size(axis)
    up = [(i, (i + 1) % peers) for i in range(peers)]
    down = [(j, i) for i, j in up]
    return lax.ppermute(before_src, axis, up), lax.ppermute(after_src, axis, down)


def mode_basis(length, modes):
    turns = np.arange(modes)[None, :] * np.arange(length)[:, None] % length
    angle = turns * (2.0 * math.pi / length)
    basis = np.concatenate([np.cos(angle), np.sin(angle)], axis=1).astype(np.float32)
    high = basis.astype(ml_dtypes.bfloat16)
    low = (basis - high.astype(np.float32)).astype(ml_dtypes.bfloat16)
    return np.concatenate([high, low], axis=1)


def two_parts(x):
    x = x.astype(np.float32)
    high = x.astype(ml_dtypes.bfloat16)
    return np.concatenate([high, (x - high.astype(np.float32)).astype(ml_dtypes.bfloat16)], axis=1)


def polynomials(lanes):
    x = (2.0 * np.arange(lanes) + 1.0 - lanes) / lanes
    return np.cos(np.arange(DEGREE)[None, :] * np.arccos(x)[:, None])


def block_coefficients(length, lanes, modes):
    nodes = 4 * DEGREE
    turn = (np.arange(nodes) + 0.5) * math.pi / nodes
    at_nodes = np.cos(np.arange(DEGREE)[:, None] * turn[None, :])
    at_nodes *= np.where(np.arange(DEGREE) == 0, 1.0, 2.0)[:, None] / nodes
    parts = []
    for block in range(length // lanes):
        place = (np.cos(turn) * lanes + lanes - 1.0) / 2.0 + lanes * block
        angle = np.arange(modes)[None, :] * place[:, None] * (2.0 * math.pi / length)
        values = np.concatenate([np.cos(angle), np.sin(angle)], axis=1)
        parts.append((at_nodes[:, :, None] * values[None]).sum(axis=1))
    return np.stack(parts)


def joint_basis(basis, lanes):
    length = basis.shape[0]
    tile, lane = np.divmod(np.arange(length // 2), lanes)
    half, c = np.divmod(lane % GROUP, 8)
    column = (lanes * (2 * tile + half + 1) + c - 4) % length
    return np.where(((c >= 2) & (c < 6))[:, None], basis[column], np.zeros_like(basis[column]))


def mode_weights(counts, modes, length):
    order = jnp.arange(modes).astype(jnp.float32)
    keep = (order[None, :] < counts[:, None]).astype(jnp.float32)
    scale = jnp.where(order == 0, 1.0, 2.0) / length
    weights = keep * scale[None, :]
    return jnp.concatenate([weights, weights], axis=1)


def shards(ocean_state, thickness, wet_mask, mode_counts, row_flags):
    levels, rows, lanes = ocean_state.shape[1:]
    assert rows % 8 == 0 and lanes == LANES and levels * GROUP <= LANES
    lon_peers = lax.axis_size("lon")
    lat_peers = lax.axis_size("lat")
    nlat = rows * lat_peers
    nlon = lanes * lon_peers
    full = rows + 8
    total = 4 * levels * rows
    part = total // lon_peers
    lat_pos = lax.axis_index("lat")
    first_row = lat_pos * rows
    cells = 4 * levels * full * lanes
    edge_rows = (6, levels, 2, lanes)

    paired = rows == 2 * lon_peers and rows >= FBAND and lat_peers % 2 == 0 and levels % 2 == 0
    paired = paired and math.pi * (MAXM - 1) * lanes / nlon <= DEGREE / 2.5
    *block, first, last, flags, counts, table, end_table, joint_table = call(
        functools.partial(load_kernel, paired),
        [ocean_state.shape, thickness.shape, thickness.shape, edge_rows, edge_rows]
        + [(rows, lanes)] * 2
        + [(2, full, lanes), (2, 8, lanes), (2, 8, lanes)],
        [pltpu.VMEM(shape, jnp.int32) for shape in (thickness.shape, (1, rows), (1, rows))],
        sems=8,
        raw=True,
    )(ocean_state, thickness, wet_mask, row_flags[None], mode_counts[None])

    def ready():
        return call(
            ready_kernel, [(6, rows, LANES), (5, levels, rows, lanes)], flops=20 * cells
        )(*block, table)

    def exchanged(below, above, own, terms):
        inner, edges, halo = call(
            inner_kernel,
            [(3, 4, levels, full, lanes), (6, full, LANES), (6, levels, 8, lanes)],
            [(5, levels, 8, lanes), (2, levels, full, lanes)],
            flops=60 * cells,
        )(*block, below, above, table, own, terms)
        first, last = call(pack_kernel, [(full, LANES)] * 2)(*block, halo)
        from_west, from_east = swap_edges(last, first, "lon")
        return call(
            edge_kernel,
            [ocean_state.shape] * 2,
            [(4, full, LANES), (7, full, LANES)],
            sems=4,
            sent=True,
        )(inner, edges, from_west, from_east, table)

    banded = (first_row < FBAND) | (first_row + rows > nlat - FBAND)
    modes = mode_basis(nlon, MAXM)
    tables = [modes]
    if paired:
        coefficients = block_coefficients(nlon, lanes, MAXM)
        coefficients = np.concatenate([coefficients] * 2, axis=1).reshape(nlon, 2 * MAXM)
        columns = polynomials(lanes)
        inside = (np.arange(lanes) >= 2) & (np.arange(lanes) < lanes - 2)
        tables = [
            two_parts(coefficients),
            joint_basis(modes, lanes),
            two_parts(columns * inside[:, None]),
            two_parts(np.concatenate([columns.T] * 2, axis=0)),
        ]
    tables = lax.optimization_barrier([jnp.asarray(table) for table in tables])
    lon_pos = lax.axis_index("lon")

    def circled(got, own, closed):
        half = 4 * levels
        tile = (levels, 8, lanes)
        to_modes, at_joints, to_sums, to_columns = tables
        state, sent = call(
            end_kernel,
            [ocean_state.shape, (lon_peers, half + 24, lanes)],
            [(2,) + tile, (6,) + tile, (3, 4) + tile, (7,) + tile, (3, full, lanes)]
            + [(total, lanes)],
        )(*block, got, own, closed, end_table, to_sums)
        circles = lax.all_to_all(sent, "lon", 0, 0, tiled=True)
        pieces = call(
            circle_kernel,
            [(lon_peers, half + 8, lanes)],
            [
                (6, 4 * lon_peers, lanes),
                (7, 4 * lon_peers, lanes),
                (4 * lon_peers, lanes),
            ],
        )(circles, joint_table, to_modes, at_joints, counts)[0]
        pieces = lax.all_to_all(pieces, "lon", 0, 0, tiled=True)
        return call(
            join_kernel,
            [ocean_state.shape],
            [ocean_state.shape, (total, lanes)],
            sems=levels // 2,
            sent=True,
        )(state, pieces, block[2], flags, to_columns)[0]

    def between(got, *_):
        pairs = [(i, i + 1) for i in range(1, lat_peers - 1, 2)]
        other = lax.ppermute(last, "lat", pairs + [(j, i) for i, j in pairs])
        even = lat_pos % 2 == 0
        below, above = jnp.where(even, other, got), jnp.where(even, got, other)
        return exchanged(below, above, *ready())[1]

    if paired:
        got = lax.ppermute(first, "lat", [(i, i ^ 1) for i in range(lat_peers)])
        own, closed = call(
            closed_kernel,
            [(6, rows, LANES), (3, 4, levels, rows, lanes)],
            [(7, levels, rows, lanes)],
            flops=60 * cells,
        )(*block, table)
        got, own, closed = lax.optimization_barrier((got, own, closed))
        return lax.cond(banded, circled, between, got, own, closed)

    below, above = swap_edges(last, first, "lat")
    state, sent = exchanged(*lax.optimization_barrier((below, above, *ready())))

    def filtered():
        row_counts = lax.dynamic_slice(
            jnp.broadcast_to(
                mode_counts.astype(jnp.float32)[None], (4 * levels, rows)
            ).reshape(total),
            (lon_pos * part,),
            (part,),
        )
        circles = lax.all_to_all(
            sent.reshape(lon_peers, part, lanes), "lon", 0, 0, tiled=True
        )
        smooth = call(
            filter_kernel, [circles.shape], [circles.shape], sems=lon_peers // 2, sent=True
        )(circles, tables[0], mode_weights(row_counts, MAXM, nlon))[0]
        smooth = lax.all_to_all(smooth, "lon", 0, 0, tiled=True).reshape(state.shape)
        return call(blend_kernel, [state.shape], [state.shape], sems=4, sent=True)(
            state, smooth, block[2], flags
        )[0]

    return lax.cond(banded, filtered, lambda: sent)


def solution(mesh):
    in_specs = (
        P(None, None, "lat", "lon"),
        P(None, "lat", "lon"),
        P(None, "lat", "lon"),
        P("lat"),
        P("lat"),
    )
    out_specs = P(None, None, "lat", "lon")
    return jax.shard_map(shards, mesh=mesh, in_specs=in_specs, out_specs=out_specs, check_vma=False)
```

```python
import functools
import math

import jax
import jax.numpy as jnp
import ml_dtypes
import numpy as np
from jax import lax
from jax.experimental import pallas as pl
from jax.experimental.pallas import tpu as pltpu
from jax.sharding import PartitionSpec as P

FBAND = 16
MAXM = 64
LANES = 128
DEGREE = LANES // 2
GROUP = 16


lat_edge = 1.3
diffusion = 0.05
vertical_mix = 0.5
time_step = 0.05


def roll(x, shift, axis):
    shift %= x.shape[axis]
    return pltpu.roll(x, shift, axis) if shift else x


def east(x):
    return roll(x, -1, 1)


def west(x):
    return roll(x, 1, 1)


def north(x):
    return roll(x, -1, 0)


def south(x):
    return roll(x, 1, 0)


def lane_of(shape):
    return lax.broadcasted_iota(jnp.int32, shape, 1)


def east_terms(h, w, inv_c):
    open_e = 0.5 * (h + east(h)) * (w * east(w))
    return 0.25 * open_e, diffusion * open_e * inv_c


def north_terms(h, w, face):
    open_n = 0.5 * (h + north(h)) * (w * north(w)) * face
    return 0.25 * open_n, diffusion * open_n


def advance(fields, terms, scale, scale_c, vertical):
    quarter_e, spread_e, quarter_n, spread_n = terms
    u, v = fields[2], fields[3]
    speed_e = quarter_e * (u + east(u))
    speed_n = quarter_n * (v + north(v))
    here_e, there_e = speed_e + spread_e, speed_e - spread_e
    here_n, there_n = speed_n + spread_n, speed_n - spread_n
    fresh = []
    for q, vert in zip(fields, vertical):
        flux_e = here_e * q + there_e * east(q)
        flux_n = here_n * q + there_n * north(q)
        spread = (flux_e - west(flux_e)) + (flux_n - south(flux_n))
        fresh.append(q + scale * vert - scale_c * spread)
    return fresh


def own_columns(load, levels, lanes, rows):
    lane = lane_of((rows, LANES))
    own = jnp.zeros((rows, LANES), jnp.float32)
    for k in range(levels):
        x = load(k)
        at = GROUP * k + 2
        own = jnp.where((lane >= at) & (lane < at + 4), roll(x, at, 1), own)
        at = GROUP * k + 8
        own = jnp.where((lane >= at) & (lane < at + 4), roll(x, at + 4 - lanes, 1), own)
    return own


def row_terms(thick, wet, inv_c, levels, term_ref):
    w, h = wet(0), thick(0)
    hs = jnp.where(w > 0, h, 1.0)
    for k in range(levels):
        term_ref[0, k], term_ref[1, k] = east_terms(h, w, inv_c)
        scale = time_step * w / hs
        term_ref[2, k] = scale
        term_ref[3, k] = scale * inv_c
        if k + 1 < levels:
            w_next, h_next = wet(k + 1), thick(k + 1)
            hs_next = jnp.where(w_next > 0, h_next, 1.0)
            term_ref[4, k] = w * w_next * vertical_mix / (0.5 * (hs + hs_next))
            w, h, hs = w_next, h_next, hs_next


def fill_table(ref, place, nlat):
    place = place.astype(jnp.float32)
    ref[0] = 1.0 / jnp.cos(lat_edge * (2.0 * (place + 0.5) / nlat - 1.0))
    ref[1] = jnp.cos(lat_edge * (2.0 * (place + 1.0) / nlat - 1.0))


def ring_rows(rows):
    place = lax.broadcasted_iota(jnp.int32, (rows + 8, LANES), 0)
    return jnp.where(place < rows + 2, place, jnp.where(place < rows + 6, 0, place - rows - 8))


def load_kernel(
    paired,
    state_any,
    thick_any,
    wet_any,
    flag_any,
    count_any,
    sums_any,
    state_ref,
    thick_ref,
    wet_ref,
    first_ref,
    last_ref,
    flag_ref,
    count_ref,
    table_ref,
    end_table_ref,
    joint_table_ref,
    sums_ref,
    raw_ref,
    raw_flag_ref,
    raw_count_ref,
    sems,
):
    levels, rows = thick_ref.shape[:2]
    moves = [(flag_any, raw_flag_ref), (count_any, raw_count_ref), (wet_any, raw_ref)]
    moves += [(thick_any, thick_ref), (sums_any, sums_ref)]
    moves += [(state_any.at[f], state_ref.at[f]) for f in range(4)]
    copies = [pltpu.make_async_copy(*pair, sems.at[i]) for i, pair in enumerate(moves)]
    for copy in copies:
        copy.start()
    nlat = rows * lax.axis_size("lat")
    lat_pos = lax.axis_index("lat")
    first_row = lat_pos * rows
    fill_table(table_ref, first_row + ring_rows(rows), nlat)
    if paired:
        six = jnp.minimum(lax.broadcasted_iota(jnp.int32, (8, LANES), 0), 5)
        end = jnp.where(lat_pos == 0, rows - 4, -2)
        fill_table(end_table_ref, first_row + end + six, nlat)
        fill_table(joint_table_ref, first_row + 2 * lax.axis_index("lon") - 2 + six, nlat)
    for copy in copies[:3]:
        copy.wait()
    shape = (rows, rows)
    diagonal = lax.broadcasted_iota(jnp.int32, shape, 0) == lane_of(shape)
    for raw, ref in ((raw_flag_ref, flag_ref), (raw_count_ref, count_ref)):
        spread = jnp.broadcast_to(raw[...].astype(jnp.float32), shape)
        value = jnp.sum(jnp.where(diagonal, spread, 0.0), axis=1, keepdims=True)
        ref[...] = jnp.broadcast_to(value, (rows, LANES))
    for k in range(levels):
        wet_ref[k] = raw_ref[k].astype(jnp.float32)
    for copy in copies[3:]:
        copy.wait()
    for f in range(6):
        for k in range(levels):
            x = state_ref.at[f, k] if f < 4 else (thick_ref, wet_ref)[f - 4].at[k]
            first_ref[f, k] = x[0:2]
            last_ref[f, k] = x[rows - 2 : rows]
    if paired:
        even = lax.axis_index("lat") % 2 == 0
        for f in range(6):
            for k in range(levels):
                low, high = first_ref[f, k], last_ref[f, k]
                first_ref[f, k] = jnp.where(even, high, low)
                last_ref[f, k] = jnp.where(even, low, high)


def ready_kernel(state_ref, thick_ref, wet_ref, table_ref, own_ref, term_ref):
    levels, rows, lanes = thick_ref.shape

    def thick(k):
        return thick_ref[k]

    def wet(k):
        return wet_ref[k]

    for f in range(4):
        own_ref[f] = own_columns(lambda k, f=f: state_ref[f, k], levels, lanes, rows)
    own_ref[4] = own_columns(thick, levels, lanes, rows)
    own_ref[5] = own_columns(wet, levels, lanes, rows)
    row_terms(thick, wet, table_ref[0, :rows], levels, term_ref)


def pack_kernel(state_ref, thick_ref, wet_ref, halo_ref, first_ref, last_ref):
    levels, rows, lanes = thick_ref.shape
    lane = lane_of((8, LANES))
    for t in range(rows // 8 + 1):
        first = jnp.zeros((8, LANES), jnp.float32)
        last = jnp.zeros((8, LANES), jnp.float32)
        part = slice(8 * t, 8 * t + 8)
        for f in range(6):
            for k in range(levels):
                if t == rows // 8:
                    x = halo_ref[f, k]
                elif f < 4:
                    x = state_ref[f, k, part]
                elif f == 4:
                    x = thick_ref[k, part]
                else:
                    x = wet_ref[k, part]
                at = GROUP * f + 2 * k
                mine = (lane >= at) & (lane < at + 2)
                first = jnp.where(mine, roll(x, at, 1), first)
                last = jnp.where(mine, roll(x, at + 2 - lanes, 1), last)
        first_ref[part] = first
        last_ref[part] = last


def inner_kernel(
    state_ref,
    thick_ref,
    wet_ref,
    below_ref,
    above_ref,
    table_ref,
    own_ref,
    term_ref,
    out_ref,
    edge_ref,
    halo_ref,
    halo_term_ref,
    north_ref,
):
    levels, rows, lanes = thick_ref.shape
    full = rows + 8
    face = table_ref[1]
    lat_pos = lax.axis_index("lat")
    with_below = jnp.where(lat_pos > 0, 1.0, 0.0)
    with_above = jnp.where(lat_pos < lax.axis_size("lat") - 1, 1.0, 0.0)
    for f in range(6):
        for k in range(levels):
            halo_ref[f, k, 0:2] = above_ref[f, k] * with_above
            halo_ref[f, k, 2:6] = jnp.zeros((4, lanes), jnp.float32)
            halo_ref[f, k, 6:8] = below_ref[f, k] * with_below

    def joined(x, y):
        return jnp.concatenate([x, y], axis=0)

    def halo(f):
        return lambda k: halo_ref[f, k]

    for f in range(6):
        edge_ref[f, :rows] = own_ref[f]
        edge_ref[f, rows:] = own_columns(halo(f), levels, lanes, 8)
    row_terms(halo(4), halo(5), table_ref[0, rows:], levels, halo_term_ref)
    for k in range(levels):
        h = joined(thick_ref[k], halo_ref[4, k])
        w = joined(wet_ref[k], halo_ref[5, k])
        north_ref[0, k], north_ref[1, k] = north_terms(h, w, face)
        for f in range(4):
            out_ref[0, f, k] = joined(state_ref[f, k], halo_ref[f, k])

    def term(i, k):
        return joined(term_ref[i, k], halo_term_ref[i, k])

    def step(i, _):
        source, target = out_ref.at[i], out_ref.at[i + 1]
        fields = [source[f, 0] for f in range(4)]
        above = [jnp.zeros((full, LANES), jnp.float32)] * 4
        for k in range(levels):
            deeper = below = above
            if k + 1 < levels:
                couple = term(4, k)
                deeper = [source[f, k + 1] for f in range(4)]
                below = [couple * (d - q) for d, q in zip(deeper, fields)]
                vertical = [b - a for b, a in zip(below, above)]
            else:
                vertical = [-a for a in above]
            terms = term(0, k), term(1, k), north_ref[0, k], north_ref[1, k]
            fresh = advance(fields, terms, term(2, k), term(3, k), vertical)
            for f in range(4):
                target[f, k] = fresh[f]
            fields, above = deeper, below
        return 0

    lax.fori_loop(0, 2, step, 0)


def step_tile(tile_ref, h, w, levels, inv_c, face, term_ref):
    lane = lane_of(h.shape)

    def deeper(x):
        return roll(x, -GROUP, 1)

    def shallower(x):
        return roll(x, GROUP, 1)

    hs = jnp.where(w > 0, h, 1.0)
    scale = time_step * w / hs
    couple = w * deeper(w) * vertical_mix / (0.5 * (hs + deeper(hs)))
    couple = jnp.where(lane < GROUP * (levels - 1), couple, 0.0)
    terms = east_terms(h, w, inv_c) + north_terms(h, w, face)
    for i, term in enumerate(terms + (scale, scale * inv_c, couple)):
        term_ref[i] = term

    def step():
        terms = [term_ref[i] for i in range(7)]
        fields = [tile_ref[f] for f in range(4)]
        vertical = []
        for q in fields:
            down = terms[6] * (deeper(q) - q)
            vertical.append(down - shallower(down))
        for f, q in enumerate(advance(fields, terms[:4], terms[4], terms[5], vertical)):
            tile_ref[f] = q

    step()
    step()


def edge_kernel(
    inner_ref, own_ref, west_ref, east_ref, table_ref, out_ref, send_ref, tile_ref, term_ref, sems
):
    levels, rows, lanes = out_ref.shape[1:]
    full = rows + 8
    lane = lane_of((full, LANES))
    from_west, from_east = west_ref[...], east_ref[...]

    def joined(f):
        x = own_ref[f]
        for k in range(levels):
            src = GROUP * f + 2 * k
            at = GROUP * k
            x = jnp.where((lane >= at) & (lane < at + 2), roll(from_west, at - src, 1), x)
            at = GROUP * k + 12
            x = jnp.where((lane >= at) & (lane < at + 2), roll(from_east, at - src, 1), x)
        return x

    for f in range(4):
        tile_ref[f] = joined(f)
    step_tile(tile_ref, joined(4), joined(5), levels, table_ref[0], table_ref[1], term_ref)
    lane = lane_of((rows, LANES))
    for f in range(4):
        x = tile_ref[f, :rows]
        for k in range(levels):
            left = roll(x, -(GROUP * k + 2), 1)
            right = roll(x, lanes - 2 - (GROUP * k + 10), 1)
            out_ref[f, k] = jnp.where(
                lane < 2,
                left,
                jnp.where(lane >= lanes - 2, right, inner_ref[2, f, k, :rows]),
            )
        pltpu.make_async_copy(out_ref.at[f], send_ref.at[f], sems.at[f]).start()
    for f in range(4):
        pltpu.make_async_copy(out_ref.at[f], send_ref.at[f], sems.at[f]).wait()


def split(x):
    high = x.astype(jnp.bfloat16)
    return high, (x - high.astype(jnp.float32)).astype(jnp.bfloat16)


def product(a, b, dims):
    return lax.dot_general(a, b, (dims, ((), ())), preferred_element_type=jnp.float32)


def unpack(x):
    left = lane_of(x.shape) < DEGREE
    return jnp.concatenate([jnp.where(left, x, 0.0), jnp.where(left, 0.0, x)], axis=0)


def pairs_of_rows(tiles, t, place):
    sub = lax.broadcasted_iota(jnp.int32, tiles[0].shape, 0) // 2
    for y in range(4):
        made = roll(tiles[0], -2 * y, 0)
        for x in range(1, 4):
            made = jnp.where(sub == x, roll(tiles[x], 2 * (x - y), 0), made)
        place(y, made)


def step_levels(buf_ref, term_ref, loop):
    levels, size = buf_ref.shape[2:4]

    def step(i, _):
        source, target = buf_ref.at[i], buf_ref.at[i + 1]
        fields = [source[f, 0] for f in range(4)]
        above = [jnp.zeros((size, LANES), jnp.float32)] * 4
        for k in range(levels):
            deeper = below = above
            if k + 1 < levels:
                couple = term_ref[4, k]
                deeper = [source[f, k + 1] for f in range(4)]
                below = [couple * (d - q) for d, q in zip(deeper, fields)]
                vertical = [b - a for b, a in zip(below, above)]
            else:
                vertical = [-a for a in above]
            terms = [term_ref[i, k] for i in (0, 1, 5, 6)]
            fresh = advance(fields, terms, term_ref[2, k], term_ref[3, k], vertical)
            for f in range(4):
                target[f, k] = fresh[f]
            fields, above = deeper, below
        return 0

    if loop:
        lax.fori_loop(0, 2, step, 0)
    else:
        step(1, step(0, 0))


def closed_kernel(state_ref, thick_ref, wet_ref, table_ref, own_ref, buf_ref, term_ref):
    levels, rows, lanes = thick_ref.shape

    def thick(k):
        return thick_ref[k]

    def wet(k):
        return wet_ref[k]

    for f in range(4):
        own_ref[f] = own_columns(lambda k, f=f: state_ref[f, k], levels, lanes, rows)
    own_ref[4] = own_columns(thick, levels, lanes, rows)
    own_ref[5] = own_columns(wet, levels, lanes, rows)
    row_terms(thick, wet, table_ref[0, :rows], levels, term_ref)
    row = lax.broadcasted_iota(jnp.int32, (rows, LANES), 0)
    face = jnp.where(row < rows - 1, table_ref[1, :rows], 0.0)
    for k in range(levels):
        term_ref[5, k], term_ref[6, k] = north_terms(thick(k), wet(k), face)
        for f in range(4):
            buf_ref[0, f, k] = state_ref[f, k]
    step_levels(buf_ref, term_ref, True)


def end_kernel(
    state_ref,
    thick_ref,
    wet_ref,
    got_ref,
    own_ref,
    closed_ref,
    table_ref,
    sums_ref,
    out_ref,
    send_ref,
    field_ref,
    halo_ref,
    buf_ref,
    term_ref,
    raw_ref,
    main_ref,
):
    levels, rows, lanes = thick_ref.shape
    full = rows + 8
    top = lax.axis_index("lat") == 0
    at_top = jnp.where(top, 1.0, 0.0)
    at_bottom = jnp.where(top, 0.0, 1.0)
    sub = lax.broadcasted_iota(jnp.int32, (8, LANES), 0)

    def own(f, k, part):
        return state_ref[f, k, part] if f < 4 else (thick_ref, wet_ref)[f - 4][k, part]

    for f in range(6):
        for k in range(levels):
            halo_ref[f, k, 0:2] = got_ref[f, k] * at_top
            halo_ref[f, k, 2:6] = jnp.zeros((4, lanes), jnp.float32)
            halo_ref[f, k, 6:8] = got_ref[f, k] * at_bottom
    for f in range(6):
        for k in range(levels):
            halo = halo_ref[f, k]
            beyond = jnp.where(sub < 6, roll(halo, 4, 0), 0.0)
            high = jnp.where(sub < 4, roll(own(f, k, slice(rows - 8, rows)), -4, 0), beyond)
            low = jnp.where(sub < 2, roll(halo, 2, 0), roll(own(f, k, slice(0, 8)), 2, 0))
            tile = jnp.where(top, high, low)
            if f < 4:
                buf_ref[0, f, k] = tile
            else:
                field_ref[f - 4, k] = tile

    def thick(k):
        return field_ref[0, k]

    def wet(k):
        return field_ref[1, k]

    row_terms(thick, wet, table_ref[0], levels, term_ref)
    for k in range(levels):
        term_ref[5, k], term_ref[6, k] = north_terms(thick(k), wet(k), table_ref[1])
    step_levels(buf_ref, term_ref, False)
    c = lane_of((full, LANES)) % GROUP

    def ring(f):
        beyond = own_columns(lambda k: halo_ref[f, k], levels, lanes, 8)
        return jnp.concatenate([own_ref[f], beyond], axis=0)

    for i in range(3):
        a, b = ring(2 * i), ring(2 * i + 1)
        one = jnp.where(c < 4, roll(a, -2, 1), roll(a, -4, 1))
        two = jnp.where(c < 12, roll(b, 6, 1), roll(b, 4, 1))
        both = jnp.where(c < 8, one, two)
        raw_ref[i, 0:2] = both[full - 2 : full]
        raw_ref[i, 2 : rows + 4] = both[: rows + 2]
        raw_ref[i, rows + 4 : full] = jnp.zeros((4, LANES), jnp.float32)
    main = 8 * levels
    half = main // 2
    last = rows // 8 - 1
    for t in range(rows // 8):
        part = slice(8 * t, 8 * t + 8)
        for k in range(levels):
            tiles = []
            for f in range(4):
                x = closed_ref[2, f, k, part]
                if t == last:
                    fixed = jnp.where(sub >= 6, roll(buf_ref[2, f, k], 4, 0), x)
                    x = jnp.where(top, fixed, x)
                if t == 0:
                    fixed = jnp.where(sub < 2, roll(buf_ref[2, f, k], -2, 0), x)
                    x = jnp.where(top, x, fixed)
                out_ref[f, k, part] = x
                tiles.append(x)

            def place(y, tile, t=t, k=k):
                at = main * (4 * t + y) + 8 * k
                main_ref[at : at + 8] = tile

            pairs_of_rows(tiles, t, place)
        for p in range(4 * t, 4 * t + 4):
            for i in range(3):
                send_ref[p, half + 8 * i : half + 8 * i + 8] = raw_ref[i, 2 * p : 2 * p + 8]
    x = jnp.concatenate(split(main_ref[...]), axis=1)
    x = product(x, jnp.concatenate([sums_ref[...]] * 2, axis=0), ((1,), (0,)))
    x = x + roll(x, DEGREE, 1)
    left = lane_of((half, LANES)) < DEGREE
    for p in range(send_ref.shape[0]):
        at = main * p
        send_ref[p, :half] = jnp.where(left, x[at : at + half], x[at + half : at + main])


def circle_kernel(
    circle_ref,
    table_ref,
    basis_ref,
    joint_basis_ref,
    count_ref,
    out_ref,
    tile_ref,
    term_ref,
    joint_ref,
):
    peers = circle_ref.shape[0]
    modes = basis_ref.shape[1] // 2
    length = basis_ref.shape[0]
    half = circle_ref.shape[1] - 24
    main = 2 * half
    levels = main // 8
    lanes = LANES
    lane = lane_of((8, LANES))
    c = lane % GROUP
    for j in range(0, peers, 2):
        part = slice(4 * j, 4 * j + 8)
        for i in range(3):
            x, y, z = (
                circle_ref[(j + d) % peers, half + 8 * i : half + 8 * i + 8] for d in range(3)
            )
            for f, shift in ((2 * i, 0), (2 * i + 1, -8)):
                middle = jnp.where(c < 12, roll(y, 4 + shift, 1), roll(z, 12 + shift, 1))
                tile_ref[f, part] = jnp.where(c < 4, roll(x, shift - 4, 1), middle)
    inv_c, face = (jnp.concatenate([table_ref[i]] * (peers // 2), axis=0) for i in (0, 1))
    step_tile(tile_ref, tile_ref[4], tile_ref[5], levels, inv_c, face, term_ref)
    sub = lax.broadcasted_iota(jnp.int32, (8, LANES), 0) // 2
    right = (c % 8 >= 2) & (c % 8 < 6)
    for j in range(peers // 2):
        made = jnp.zeros((8, LANES), jnp.float32)
        for f in range(4):
            x = tile_ref[f, 8 * j : 8 * j + 8]
            made = jnp.where(sub == f, roll(x, 2 * f - 2, 0), made)
        joint_ref[8 * j : 8 * j + 8] = jnp.where(right, made, 0.0)
    lane_main = lane_of((main, LANES))
    row_main = lax.broadcasted_iota(jnp.int32, (main, LANES), 0)
    at_level = lane_main // GROUP == row_main // 8

    def block(o):
        return unpack(circle_ref[o, :half])

    def joint(j):
        x = joint_ref[8 * j : 8 * j + 8]
        return jnp.where(at_level, jnp.concatenate([x] * levels, axis=0), 0.0)

    total = jnp.zeros((2 * main, 2 * modes), jnp.float32)
    for source, basis, count in (
        (block, basis_ref, peers),
        (joint, joint_basis_ref, peers // 2),
    ):
        for o in range(0, count, 2):
            parts = zip(split(source(o)), split(source(o + 1)))
            x = jnp.concatenate([jnp.concatenate(p, axis=1) for p in parts], axis=0)
            total = total + product(x, basis[lanes * o : lanes * (o + 2)], ((1,), (0,)))
    total = total[:main] + total[main:]
    counts = count_ref[...]
    row = lax.broadcasted_iota(jnp.int32, counts.shape, 0)
    own = 2 * lax.axis_index("lon")
    even, odd = (
        jnp.sum(jnp.where(row == own + r, counts, 0.0), axis=0, keepdims=True) for r in (0, 1)
    )
    limit = jnp.where(row_main % 2 == 0, even, odd)
    order = (lane_main % (modes // 2)).astype(jnp.float32)
    weight = jnp.where(order < limit, jnp.where(order == 0.0, 1.0 / length, 2.0 / length), 0.0)
    total = (total[:, :modes] + total[:, modes:]) * weight
    y = jnp.concatenate([jnp.concatenate([p, p], axis=1) for p in split(total)], axis=0)
    for o in range(0, peers, 2):
        x = product(y, basis_ref[lanes * o : lanes * (o + 2)], ((1,), (1,)))
        x = x[:main] + x[main:]
        left = lane_of((half, LANES)) < DEGREE
        out_ref[o, :half] = jnp.where(left, x[:half, :lanes], x[half:, :lanes])
        out_ref[o + 1, :half] = jnp.where(left, x[:half, lanes:], x[half:, lanes:])
        before = (4 * o - 8) % (4 * peers)
        here = joint_ref[4 * o : 4 * o + 8]
        out_ref[o, half:] = jnp.where(
            c < 8, roll(joint_ref[before : before + 8], -8, 1), roll(here, 8, 1)
        )
        out_ref[o + 1, half:] = here


def join_kernel(
    state_ref, piece_ref, wet_ref, flag_ref, columns_ref, out_ref, made_ref, smooth_ref, sems
):
    levels, rows, lanes = wet_ref.shape
    main = 8 * levels
    half = main // 2
    lane = lane_of((8, LANES))
    x = jnp.concatenate(
        [unpack(piece_ref[p, :half]) for p in range(piece_ref.shape[0])], axis=0
    )
    x = jnp.concatenate(split(x), axis=1)
    x = product(x, jnp.concatenate([columns_ref[...]] * 2, axis=0), ((1,), (0,)))
    smooth_ref[...] = x[:, :lanes] + x[:, lanes:]
    edges = [{} for _ in range(rows // 8)]
    for t, into in enumerate(edges):
        tiles = [piece_ref[4 * t + x, half : half + 8] for x in range(4)]
        pairs_of_rows(tiles, t, into.__setitem__)
    copies = []
    for k in range(levels):
        for t in range(rows // 8):
            part = slice(8 * t, 8 * t + 8)
            starts = [main * (4 * t + x) + 8 * k for x in range(4)]
            tiles = [smooth_ref[at : at + 8] for at in starts]
            gate = flag_ref[part] * wet_ref[k, part]

            def place(f, smooth, k=k, gate=gate, part=part, edge=edges[t]):
                first = roll(edge[f], -(GROUP * k + 4), 1)
                last = roll(edge[f], lanes - 2 - (GROUP * k + 10), 1)
                state = jnp.where(
                    lane < 2, first, jnp.where(lane >= lanes - 2, last, state_ref[f, k, part])
                )
                made_ref[f, k, part] = state + gate * (smooth - state)

            pairs_of_rows(tiles, t, place)
        if k % 2:
            both = pl.ds(k - 1, 2)
            copies.append(
                pltpu.make_async_copy(
                    made_ref.at[:, both], out_ref.at[:, both], sems.at[k // 2]
                )
            )
            copies[-1].start()
    for copy in copies:
        copy.wait()


def filter_kernel(circle_ref, basis_ref, weight_ref, out_ref, piece_ref, sems):
    pieces, part, lanes = circle_ref.shape
    modes = weight_ref.shape[1]
    pairs = range(0, pieces, 2)
    total = jnp.zeros((2 * part, 2 * modes), jnp.float32)
    for o in pairs:
        parts = zip(split(circle_ref[o]), split(circle_ref[o + 1]))
        x = jnp.concatenate([jnp.concatenate(p, axis=1) for p in parts], axis=0)
        total = total + product(x, basis_ref[lanes * o : lanes * (o + 2)], ((1,), (0,)))
    total = total[:part] + total[part:]
    total = (total[:, :modes] + total[:, modes:]) * weight_ref[...]
    y = jnp.concatenate([jnp.concatenate([p, p], axis=1) for p in split(total)], axis=0)
    copies = []
    for o in pairs:
        x = product(y, basis_ref[lanes * o : lanes * (o + 2)], ((1,), (1,)))
        x = x[:part] + x[part:]
        piece_ref[o] = x[:, :lanes]
        piece_ref[o + 1] = x[:, lanes:]
        both = pl.ds(o, 2)
        copies.append(
            pltpu.make_async_copy(piece_ref.at[both], out_ref.at[both], sems.at[o // 2])
        )
        copies[-1].start()
    for copy in copies:
        copy.wait()


def blend_kernel(state_ref, smooth_ref, wet_ref, flag_ref, out_ref, piece_ref, sems):
    levels = wet_ref.shape[0]
    flag = flag_ref[...]
    copies = []
    for f in range(4):
        for k in range(levels):
            state = state_ref[f, k]
            gate = flag * wet_ref[k]
            piece_ref[f, k] = state + gate * (smooth_ref[f, k] - state)
        copies.append(pltpu.make_async_copy(piece_ref.at[f], out_ref.at[f], sems.at[f]))
        copies[-1].start()
    for copy in copies:
        copy.wait()


def call(kernel, outs, scratch=(), sems=0, raw=False, sent=False, flops=0):
    vmem = pl.BlockSpec(memory_space=pltpu.VMEM)
    away = pl.BlockSpec(memory_space=pl.ANY)
    specs = [vmem] * len(outs)
    shapes = [jax.ShapeDtypeStruct(s, jnp.float32) if isinstance(s, tuple) else s for s in outs]
    if sent:
        specs[-1] = away
        shapes[-1] = pltpu.HBM(outs[-1], jnp.float32)
    buffers = [pltpu.VMEM(s, jnp.float32) if isinstance(s, tuple) else s for s in scratch]
    if sems:
        buffers.append(pltpu.SemaphoreType.DMA((sems,)))
    cost = pl.CostEstimate(
        flops=flops,
        transcendentals=0,
        bytes_accessed=4 * sum(math.prod(s.shape) for s in shapes),
    )

    def run(*args):
        if raw:
            args = [pltpu.with_memory_space_constraint(x, pltpu.HBM) for x in args]
        return pl.pallas_call(
            kernel,
            out_shape=shapes,
            in_specs=[away if raw else vmem] * len(args),
            out_specs=specs,
            scratch_shapes=buffers,
            compiler_params=pltpu.CompilerParams(vmem_limit_bytes=24 << 20),
            cost_estimate=cost,
        )(*args)

    return run


def swap_edges(before_src, after_src, axis):
    peers = lax.axis_size(axis)
    up = [(i, (i + 1) % peers) for i in range(peers)]
    down = [(j, i) for i, j in up]
    return lax.ppermute(before_src, axis, up), lax.ppermute(after_src, axis, down)


def mode_basis(length, modes):
    turns = np.arange(modes)[None, :] * np.arange(length)[:, None] % length
    angle = turns * (2.0 * math.pi / length)
    basis = np.concatenate([np.cos(angle), np.sin(angle)], axis=1).astype(np.float32)
    high = basis.astype(ml_dtypes.bfloat16)
    low = (basis - high.astype(np.float32)).astype(ml_dtypes.bfloat16)
    return np.concatenate([high, low], axis=1)


def two_parts(x):
    x = x.astype(np.float32)
    high = x.astype(ml_dtypes.bfloat16)
    return np.concatenate([high, (x - high.astype(np.float32)).astype(ml_dtypes.bfloat16)], axis=1)


def polynomials(lanes):
    x = (2.0 * np.arange(lanes) + 1.0 - lanes) / lanes
    return np.cos(np.arange(DEGREE)[None, :] * np.arccos(x)[:, None])


def block_coefficients(length, lanes, modes):
    nodes = 4 * DEGREE
    turn = (np.arange(nodes) + 0.5) * math.pi / nodes
    at_nodes = np.cos(np.arange(DEGREE)[:, None] * turn[None, :])
    at_nodes *= np.where(np.arange(DEGREE) == 0, 1.0, 2.0)[:, None] / nodes
    parts = []
    for block in range(length // lanes):
        place = (np.cos(turn) * lanes + lanes - 1.0) / 2.0 + lanes * block
        angle = np.arange(modes)[None, :] * place[:, None] * (2.0 * math.pi / length)
        values = np.concatenate([np.cos(angle), np.sin(angle)], axis=1)
        parts.append((at_nodes[:, :, None] * values[None]).sum(axis=1))
    return np.stack(parts)


def joint_basis(basis, lanes):
    length = basis.shape[0]
    tile, lane = np.divmod(np.arange(length // 2), lanes)
    half, c = np.divmod(lane % GROUP, 8)
    column = (lanes * (2 * tile + half + 1) + c - 4) % length
    return np.where(((c >= 2) & (c < 6))[:, None], basis[column], np.zeros_like(basis[column]))


def mode_weights(counts, modes, length):
    order = jnp.arange(modes).astype(jnp.float32)
    keep = (order[None, :] < counts[:, None]).astype(jnp.float32)
    scale = jnp.where(order == 0, 1.0, 2.0) / length
    weights = keep * scale[None, :]
    return jnp.concatenate([weights, weights], axis=1)


def shards(ocean_state, thickness, wet_mask, mode_counts, row_flags):
    levels, rows, lanes = ocean_state.shape[1:]
    assert rows % 8 == 0 and lanes == LANES and levels * GROUP <= LANES
    lon_peers = lax.axis_size("lon")
    lat_peers = lax.axis_size("lat")
    nlat = rows * lat_peers
    nlon = lanes * lon_peers
    full = rows + 8
    total = 4 * levels * rows
    part = total // lon_peers
    lat_pos = lax.axis_index("lat")
    first_row = lat_pos * rows
    cells = 4 * levels * full * lanes
    edge_rows = (6, levels, 2, lanes)

    paired = rows == 2 * lon_peers and rows >= FBAND and lat_peers % 2 == 0 and levels % 2 == 0
    paired = paired and math.pi * (MAXM - 1) * lanes / nlon <= DEGREE / 2.5
    columns = polynomials(lanes)
    inside = (np.arange(lanes) >= 2) & (np.arange(lanes) < lanes - 2)
    sums = jnp.asarray(two_parts(columns * inside[:, None]))
    *block, first, last, flags, counts, table, end_table, joint_table, to_sums = call(
        functools.partial(load_kernel, paired),
        [ocean_state.shape, thickness.shape, thickness.shape, edge_rows, edge_rows]
        + [(rows, lanes)] * 2
        + [(2, full, lanes), (2, 8, lanes), (2, 8, lanes)]
        + [jax.ShapeDtypeStruct(sums.shape, sums.dtype)],
        [pltpu.VMEM(shape, jnp.int32) for shape in (thickness.shape, (1, rows), (1, rows))],
        sems=9,
        raw=True,
    )(ocean_state, thickness, wet_mask, row_flags[None], mode_counts[None], sums)

    def ready():
        return call(
            ready_kernel, [(6, rows, LANES), (5, levels, rows, lanes)], flops=20 * cells
        )(*block, table)

    def exchanged(below, above, own, terms):
        inner, edges, halo = call(
            inner_kernel,
            [(3, 4, levels, full, lanes), (6, full, LANES), (6, levels, 8, lanes)],
            [(5, levels, 8, lanes), (2, levels, full, lanes)],
            flops=60 * cells,
        )(*block, below, above, table, own, terms)
        first, last = call(pack_kernel, [(full, LANES)] * 2)(*block, halo)
        from_west, from_east = swap_edges(last, first, "lon")
        return call(
            edge_kernel,
            [ocean_state.shape] * 2,
            [(4, full, LANES), (7, full, LANES)],
            sems=4,
            sent=True,
        )(inner, edges, from_west, from_east, table)

    banded = (first_row < FBAND) | (first_row + rows > nlat - FBAND)
    modes = mode_basis(nlon, MAXM)
    tables = [modes]
    if paired:
        coefficients = block_coefficients(nlon, lanes, MAXM)
        coefficients = np.concatenate([coefficients] * 2, axis=1).reshape(nlon, 2 * MAXM)
        tables = [
            two_parts(coefficients),
            joint_basis(modes, lanes),
            two_parts(np.concatenate([columns.T] * 2, axis=0)),
        ]
    tables = lax.optimization_barrier([jnp.asarray(table) for table in tables])
    lon_pos = lax.axis_index("lon")

    def circled(got, own, closed):
        half = 4 * levels
        tile = (levels, 8, lanes)
        to_modes, at_joints, to_columns = tables
        state, sent = call(
            end_kernel,
            [ocean_state.shape, (lon_peers, half + 24, lanes)],
            [(2,) + tile, (6,) + tile, (3, 4) + tile, (7,) + tile, (3, full, lanes)]
            + [(total, lanes)],
        )(*block, got, own, closed, end_table, to_sums)
        circles = lax.all_to_all(sent, "lon", 0, 0, tiled=True)
        pieces = call(
            circle_kernel,
            [(lon_peers, half + 8, lanes)],
            [
                (6, 4 * lon_peers, lanes),
                (7, 4 * lon_peers, lanes),
                (4 * lon_peers, lanes),
            ],
        )(circles, joint_table, to_modes, at_joints, counts)[0]
        pieces = lax.all_to_all(pieces, "lon", 0, 0, tiled=True)
        return call(
            join_kernel,
            [ocean_state.shape],
            [ocean_state.shape, (total, lanes)],
            sems=levels // 2,
            sent=True,
        )(state, pieces, block[2], flags, to_columns)[0]

    def between(got, *_):
        pairs = [(i, i + 1) for i in range(1, lat_peers - 1, 2)]
        other = lax.ppermute(last, "lat", pairs + [(j, i) for i, j in pairs])
        even = lat_pos % 2 == 0
        below, above = jnp.where(even, other, got), jnp.where(even, got, other)
        return exchanged(below, above, *ready())[1]

    if paired:
        got = lax.ppermute(first, "lat", [(i, i ^ 1) for i in range(lat_peers)])
        own, closed = call(
            closed_kernel,
            [(6, rows, LANES), (3, 4, levels, rows, lanes)],
            [(7, levels, rows, lanes)],
            flops=60 * cells,
        )(*block, table)
        got, own, closed = lax.optimization_barrier((got, own, closed))
        return lax.cond(banded, circled, between, got, own, closed)

    below, above = swap_edges(last, first, "lat")
    state, sent = exchanged(*lax.optimization_barrier((below, above, *ready())))

    def filtered():
        row_counts = lax.dynamic_slice(
            jnp.broadcast_to(
                mode_counts.astype(jnp.float32)[None], (4 * levels, rows)
            ).reshape(total),
            (lon_pos * part,),
            (part,),
        )
        circles = lax.all_to_all(
            sent.reshape(lon_peers, part, lanes), "lon", 0, 0, tiled=True
        )
        smooth = call(
            filter_kernel, [circles.shape], [circles.shape], sems=lon_peers // 2, sent=True
        )(circles, tables[0], mode_weights(row_counts, MAXM, nlon))[0]
        smooth = lax.all_to_all(smooth, "lon", 0, 0, tiled=True).reshape(state.shape)
        return call(blend_kernel, [state.shape], [state.shape], sems=4, sent=True)(
            state, smooth, block[2], flags
        )[0]

    return lax.cond(banded, filtered, lambda: sent)


def solution(mesh):
    in_specs = (
        P(None, None, "lat", "lon"),
        P(None, "lat", "lon"),
        P(None, "lat", "lon"),
        P("lat"),
        P("lat"),
    )
    out_specs = P(None, None, "lat", "lon")
    return jax.shard_map(shards, mesh=mesh, in_specs=in_specs, out_specs=out_specs, check_vma=False)
```

```python
import functools
import math

import jax
import jax.numpy as jnp
import ml_dtypes
import numpy as np
from jax import lax
from jax.experimental import pallas as pl
from jax.experimental.pallas import tpu as pltpu
from jax.sharding import PartitionSpec as P

FBAND = 16
MAXM = 64
LANES = 128
SUMS = 32
PACKED = LANES // SUMS
GROUP = 16


lat_edge = 1.3
diffusion = 0.05
vertical_mix = 0.5
time_step = 0.05


def roll(x, shift, axis):
    shift %= x.shape[axis]
    return pltpu.roll(x, shift, axis) if shift else x


def east(x):
    return roll(x, -1, 1)


def west(x):
    return roll(x, 1, 1)


def north(x):
    return roll(x, -1, 0)


def south(x):
    return roll(x, 1, 0)


def lane_of(shape):
    return lax.broadcasted_iota(jnp.int32, shape, 1)


def east_terms(h, w, inv_c):
    open_e = 0.5 * (h + east(h)) * (w * east(w))
    return 0.25 * open_e, diffusion * open_e * inv_c


def north_terms(h, w, face):
    open_n = 0.5 * (h + north(h)) * (w * north(w)) * face
    return 0.25 * open_n, diffusion * open_n


def advance(fields, terms, scale, scale_c, vertical):
    quarter_e, spread_e, quarter_n, spread_n = terms
    u, v = fields[2], fields[3]
    speed_e = quarter_e * (u + east(u))
    speed_n = quarter_n * (v + north(v))
    here_e, there_e = speed_e + spread_e, speed_e - spread_e
    here_n, there_n = speed_n + spread_n, speed_n - spread_n
    fresh = []
    for q, vert in zip(fields, vertical):
        flux_e = here_e * q + there_e * east(q)
        flux_n = here_n * q + there_n * north(q)
        spread = (flux_e - west(flux_e)) + (flux_n - south(flux_n))
        fresh.append(q + scale * vert - scale_c * spread)
    return fresh


def own_columns(load, levels, lanes, rows):
    lane = lane_of((rows, LANES))
    own = jnp.zeros((rows, LANES), jnp.float32)
    for k in range(levels):
        x = load(k)
        at = GROUP * k + 2
        own = jnp.where((lane >= at) & (lane < at + 4), roll(x, at, 1), own)
        at = GROUP * k + 8
        own = jnp.where((lane >= at) & (lane < at + 4), roll(x, at + 4 - lanes, 1), own)
    return own


def row_terms(thick, wet, inv_c, levels, term_ref):
    w, h = wet(0), thick(0)
    hs = jnp.where(w > 0, h, 1.0)
    for k in range(levels):
        term_ref[0, k], term_ref[1, k] = east_terms(h, w, inv_c)
        scale = time_step * w / hs
        term_ref[2, k] = scale
        term_ref[3, k] = scale * inv_c
        if k + 1 < levels:
            w_next, h_next = wet(k + 1), thick(k + 1)
            hs_next = jnp.where(w_next > 0, h_next, 1.0)
            term_ref[4, k] = w * w_next * vertical_mix / (0.5 * (hs + hs_next))
            w, h, hs = w_next, h_next, hs_next


def fill_table(ref, place, nlat):
    place = place.astype(jnp.float32)
    ref[0] = 1.0 / jnp.cos(lat_edge * (2.0 * (place + 0.5) / nlat - 1.0))
    ref[1] = jnp.cos(lat_edge * (2.0 * (place + 1.0) / nlat - 1.0))


def ring_rows(rows):
    place = lax.broadcasted_iota(jnp.int32, (rows + 8, LANES), 0)
    return jnp.where(place < rows + 2, place, jnp.where(place < rows + 6, 0, place - rows - 8))


def load_kernel(
    paired,
    state_any,
    thick_any,
    wet_any,
    flag_any,
    count_any,
    sums_any,
    state_ref,
    thick_ref,
    wet_ref,
    first_ref,
    last_ref,
    flag_ref,
    count_ref,
    table_ref,
    end_table_ref,
    joint_table_ref,
    sums_ref,
    raw_ref,
    raw_flag_ref,
    raw_count_ref,
    sems,
):
    levels, rows = thick_ref.shape[:2]
    moves = [(flag_any, raw_flag_ref), (count_any, raw_count_ref), (wet_any, raw_ref)]
    moves += [(thick_any, thick_ref), (sums_any, sums_ref)]
    moves += [(state_any.at[f], state_ref.at[f]) for f in range(4)]
    copies = [pltpu.make_async_copy(*pair, sems.at[i]) for i, pair in enumerate(moves)]
    for copy in copies:
        copy.start()
    nlat = rows * lax.axis_size("lat")
    lat_pos = lax.axis_index("lat")
    first_row = lat_pos * rows
    fill_table(table_ref, first_row + ring_rows(rows), nlat)
    if paired:
        six = jnp.minimum(lax.broadcasted_iota(jnp.int32, (8, LANES), 0), 5)
        end = jnp.where(lat_pos == 0, rows - 4, -2)
        fill_table(end_table_ref, first_row + end + six, nlat)
        fill_table(joint_table_ref, first_row + 2 * lax.axis_index("lon") - 2 + six, nlat)
    for copy in copies[:3]:
        copy.wait()
    shape = (rows, rows)
    diagonal = lax.broadcasted_iota(jnp.int32, shape, 0) == lane_of(shape)
    for raw, ref in ((raw_flag_ref, flag_ref), (raw_count_ref, count_ref)):
        spread = jnp.broadcast_to(raw[...].astype(jnp.float32), shape)
        value = jnp.sum(jnp.where(diagonal, spread, 0.0), axis=1, keepdims=True)
        ref[...] = jnp.broadcast_to(value, (rows, LANES))
    for k in range(levels):
        wet_ref[k] = raw_ref[k].astype(jnp.float32)
    for copy in copies[3:]:
        copy.wait()
    for f in range(6):
        for k in range(levels):
            x = state_ref.at[f, k] if f < 4 else (thick_ref, wet_ref)[f - 4].at[k]
            first_ref[f, k] = x[0:2]
            last_ref[f, k] = x[rows - 2 : rows]
    if paired:
        even = lax.axis_index("lat") % 2 == 0
        for f in range(6):
            for k in range(levels):
                low, high = first_ref[f, k], last_ref[f, k]
                first_ref[f, k] = jnp.where(even, high, low)
                last_ref[f, k] = jnp.where(even, low, high)


def ready_kernel(state_ref, thick_ref, wet_ref, table_ref, own_ref, term_ref):
    levels, rows, lanes = thick_ref.shape

    def thick(k):
        return thick_ref[k]

    def wet(k):
        return wet_ref[k]

    for f in range(4):
        own_ref[f] = own_columns(lambda k, f=f: state_ref[f, k], levels, lanes, rows)
    own_ref[4] = own_columns(thick, levels, lanes, rows)
    own_ref[5] = own_columns(wet, levels, lanes, rows)
    row_terms(thick, wet, table_ref[0, :rows], levels, term_ref)


def pack_kernel(state_ref, thick_ref, wet_ref, halo_ref, first_ref, last_ref):
    levels, rows, lanes = thick_ref.shape
    lane = lane_of((8, LANES))
    for t in range(rows // 8 + 1):
        first = jnp.zeros((8, LANES), jnp.float32)
        last = jnp.zeros((8, LANES), jnp.float32)
        part = slice(8 * t, 8 * t + 8)
        for f in range(6):
            for k in range(levels):
                if t == rows // 8:
                    x = halo_ref[f, k]
                elif f < 4:
                    x = state_ref[f, k, part]
                elif f == 4:
                    x = thick_ref[k, part]
                else:
                    x = wet_ref[k, part]
                at = GROUP * f + 2 * k
                mine = (lane >= at) & (lane < at + 2)
                first = jnp.where(mine, roll(x, at, 1), first)
                last = jnp.where(mine, roll(x, at + 2 - lanes, 1), last)
        first_ref[part] = first
        last_ref[part] = last


def inner_kernel(
    state_ref,
    thick_ref,
    wet_ref,
    below_ref,
    above_ref,
    table_ref,
    own_ref,
    term_ref,
    out_ref,
    edge_ref,
    halo_ref,
    halo_term_ref,
    north_ref,
):
    levels, rows, lanes = thick_ref.shape
    full = rows + 8
    face = table_ref[1]
    lat_pos = lax.axis_index("lat")
    with_below = jnp.where(lat_pos > 0, 1.0, 0.0)
    with_above = jnp.where(lat_pos < lax.axis_size("lat") - 1, 1.0, 0.0)
    for f in range(6):
        for k in range(levels):
            halo_ref[f, k, 0:2] = above_ref[f, k] * with_above
            halo_ref[f, k, 2:6] = jnp.zeros((4, lanes), jnp.float32)
            halo_ref[f, k, 6:8] = below_ref[f, k] * with_below

    def joined(x, y):
        return jnp.concatenate([x, y], axis=0)

    def halo(f):
        return lambda k: halo_ref[f, k]

    for f in range(6):
        edge_ref[f, :rows] = own_ref[f]
        edge_ref[f, rows:] = own_columns(halo(f), levels, lanes, 8)
    row_terms(halo(4), halo(5), table_ref[0, rows:], levels, halo_term_ref)
    for k in range(levels):
        h = joined(thick_ref[k], halo_ref[4, k])
        w = joined(wet_ref[k], halo_ref[5, k])
        north_ref[0, k], north_ref[1, k] = north_terms(h, w, face)
        for f in range(4):
            out_ref[0, f, k] = joined(state_ref[f, k], halo_ref[f, k])

    def term(i, k):
        return joined(term_ref[i, k], halo_term_ref[i, k])

    def step(i, _):
        source, target = out_ref.at[i], out_ref.at[i + 1]
        fields = [source[f, 0] for f in range(4)]
        above = [jnp.zeros((full, LANES), jnp.float32)] * 4
        for k in range(levels):
            deeper = below = above
            if k + 1 < levels:
                couple = term(4, k)
                deeper = [source[f, k + 1] for f in range(4)]
                below = [couple * (d - q) for d, q in zip(deeper, fields)]
                vertical = [b - a for b, a in zip(below, above)]
            else:
                vertical = [-a for a in above]
            terms = term(0, k), term(1, k), north_ref[0, k], north_ref[1, k]
            fresh = advance(fields, terms, term(2, k), term(3, k), vertical)
            for f in range(4):
                target[f, k] = fresh[f]
            fields, above = deeper, below
        return 0

    lax.fori_loop(0, 2, step, 0)


def step_tile(tile_ref, h, w, levels, inv_c, face, term_ref):
    lane = lane_of(h.shape)

    def deeper(x):
        return roll(x, -GROUP, 1)

    def shallower(x):
        return roll(x, GROUP, 1)

    hs = jnp.where(w > 0, h, 1.0)
    scale = time_step * w / hs
    couple = w * deeper(w) * vertical_mix / (0.5 * (hs + deeper(hs)))
    couple = jnp.where(lane < GROUP * (levels - 1), couple, 0.0)
    terms = east_terms(h, w, inv_c) + north_terms(h, w, face)
    for i, term in enumerate(terms + (scale, scale * inv_c, couple)):
        term_ref[i] = term

    def step():
        terms = [term_ref[i] for i in range(7)]
        fields = [tile_ref[f] for f in range(4)]
        vertical = []
        for q in fields:
            down = terms[6] * (deeper(q) - q)
            vertical.append(down - shallower(down))
        for f, q in enumerate(advance(fields, terms[:4], terms[4], terms[5], vertical)):
            tile_ref[f] = q

    step()
    step()


def edge_kernel(
    inner_ref, own_ref, west_ref, east_ref, table_ref, out_ref, send_ref, tile_ref, term_ref, sems
):
    levels, rows, lanes = out_ref.shape[1:]
    full = rows + 8
    lane = lane_of((full, LANES))
    from_west, from_east = west_ref[...], east_ref[...]

    def joined(f):
        x = own_ref[f]
        for k in range(levels):
            src = GROUP * f + 2 * k
            at = GROUP * k
            x = jnp.where((lane >= at) & (lane < at + 2), roll(from_west, at - src, 1), x)
            at = GROUP * k + 12
            x = jnp.where((lane >= at) & (lane < at + 2), roll(from_east, at - src, 1), x)
        return x

    for f in range(4):
        tile_ref[f] = joined(f)
    step_tile(tile_ref, joined(4), joined(5), levels, table_ref[0], table_ref[1], term_ref)
    lane = lane_of((rows, LANES))
    for f in range(4):
        x = tile_ref[f, :rows]
        for k in range(levels):
            left = roll(x, -(GROUP * k + 2), 1)
            right = roll(x, lanes - 2 - (GROUP * k + 10), 1)
            out_ref[f, k] = jnp.where(
                lane < 2,
                left,
                jnp.where(lane >= lanes - 2, right, inner_ref[2, f, k, :rows]),
            )
        pltpu.make_async_copy(out_ref.at[f], send_ref.at[f], sems.at[f]).start()
    for f in range(4):
        pltpu.make_async_copy(out_ref.at[f], send_ref.at[f], sems.at[f]).wait()


def split(x):
    high = x.astype(jnp.bfloat16)
    return high, (x - high.astype(jnp.float32)).astype(jnp.bfloat16)


def product(a, b, dims):
    return lax.dot_general(a, b, (dims, ((), ())), preferred_element_type=jnp.float32)


def unpack(x):
    part = lane_of(x.shape) // SUMS
    return jnp.concatenate([jnp.where(part == g, x, 0.0) for g in range(PACKED)], axis=0)


def pack(x):
    size = x.shape[0] // PACKED
    made = x[:size]
    part = lane_of(made.shape) // SUMS
    for g in range(1, PACKED):
        made = jnp.where(part == g, x[size * g : size * (g + 1)], made)
    return made


def pairs_of_rows(tiles, t, place):
    sub = lax.broadcasted_iota(jnp.int32, tiles[0].shape, 0) // 2
    for y in range(4):
        made = roll(tiles[0], -2 * y, 0)
        for x in range(1, 4):
            made = jnp.where(sub == x, roll(tiles[x], 2 * (x - y), 0), made)
        place(y, made)


def step_levels(buf_ref, term_ref, loop):
    levels, size = buf_ref.shape[2:4]

    def step(i, _):
        source, target = buf_ref.at[i], buf_ref.at[i + 1]
        fields = [source[f, 0] for f in range(4)]
        above = [jnp.zeros((size, LANES), jnp.float32)] * 4
        for k in range(levels):
            deeper = below = above
            if k + 1 < levels:
                couple = term_ref[4, k]
                deeper = [source[f, k + 1] for f in range(4)]
                below = [couple * (d - q) for d, q in zip(deeper, fields)]
                vertical = [b - a for b, a in zip(below, above)]
            else:
                vertical = [-a for a in above]
            terms = [term_ref[i, k] for i in (0, 1, 5, 6)]
            fresh = advance(fields, terms, term_ref[2, k], term_ref[3, k], vertical)
            for f in range(4):
                target[f, k] = fresh[f]
            fields, above = deeper, below
        return 0

    if loop:
        lax.fori_loop(0, 2, step, 0)
    else:
        step(1, step(0, 0))


def closed_kernel(state_ref, thick_ref, wet_ref, table_ref, own_ref, buf_ref, term_ref):
    levels, rows, lanes = thick_ref.shape

    def thick(k):
        return thick_ref[k]

    def wet(k):
        return wet_ref[k]

    for f in range(4):
        own_ref[f] = own_columns(lambda k, f=f: state_ref[f, k], levels, lanes, rows)
    own_ref[4] = own_columns(thick, levels, lanes, rows)
    own_ref[5] = own_columns(wet, levels, lanes, rows)
    row_terms(thick, wet, table_ref[0, :rows], levels, term_ref)
    row = lax.broadcasted_iota(jnp.int32, (rows, LANES), 0)
    face = jnp.where(row < rows - 1, table_ref[1, :rows], 0.0)
    for k in range(levels):
        term_ref[5, k], term_ref[6, k] = north_terms(thick(k), wet(k), face)
        for f in range(4):
            buf_ref[0, f, k] = state_ref[f, k]
    step_levels(buf_ref, term_ref, True)


def end_kernel(
    state_ref,
    thick_ref,
    wet_ref,
    got_ref,
    own_ref,
    closed_ref,
    table_ref,
    sums_ref,
    out_ref,
    send_ref,
    field_ref,
    halo_ref,
    buf_ref,
    term_ref,
    raw_ref,
    main_ref,
):
    levels, rows, lanes = thick_ref.shape
    full = rows + 8
    top = lax.axis_index("lat") == 0
    at_top = jnp.where(top, 1.0, 0.0)
    at_bottom = jnp.where(top, 0.0, 1.0)
    sub = lax.broadcasted_iota(jnp.int32, (8, LANES), 0)

    def own(f, k, part):
        return state_ref[f, k, part] if f < 4 else (thick_ref, wet_ref)[f - 4][k, part]

    for f in range(6):
        for k in range(levels):
            halo_ref[f, k, 0:2] = got_ref[f, k] * at_top
            halo_ref[f, k, 2:6] = jnp.zeros((4, lanes), jnp.float32)
            halo_ref[f, k, 6:8] = got_ref[f, k] * at_bottom
    for f in range(6):
        for k in range(levels):
            halo = halo_ref[f, k]
            beyond = jnp.where(sub < 6, roll(halo, 4, 0), 0.0)
            high = jnp.where(sub < 4, roll(own(f, k, slice(rows - 8, rows)), -4, 0), beyond)
            low = jnp.where(sub < 2, roll(halo, 2, 0), roll(own(f, k, slice(0, 8)), 2, 0))
            tile = jnp.where(top, high, low)
            if f < 4:
                buf_ref[0, f, k] = tile
            else:
                field_ref[f - 4, k] = tile

    def thick(k):
        return field_ref[0, k]

    def wet(k):
        return field_ref[1, k]

    row_terms(thick, wet, table_ref[0], levels, term_ref)
    for k in range(levels):
        term_ref[5, k], term_ref[6, k] = north_terms(thick(k), wet(k), table_ref[1])
    step_levels(buf_ref, term_ref, False)
    c = lane_of((full, LANES)) % GROUP

    def ring(f):
        beyond = own_columns(lambda k: halo_ref[f, k], levels, lanes, 8)
        return jnp.concatenate([own_ref[f], beyond], axis=0)

    for i in range(3):
        a, b = ring(2 * i), ring(2 * i + 1)
        one = jnp.where(c < 4, roll(a, -2, 1), roll(a, -4, 1))
        two = jnp.where(c < 12, roll(b, 6, 1), roll(b, 4, 1))
        both = jnp.where(c < 8, one, two)
        raw_ref[i, 0:2] = both[full - 2 : full]
        raw_ref[i, 2 : rows + 4] = both[: rows + 2]
        raw_ref[i, rows + 4 : full] = jnp.zeros((4, LANES), jnp.float32)
    main = 8 * levels
    few = main // PACKED
    last = rows // 8 - 1
    for t in range(rows // 8):
        part = slice(8 * t, 8 * t + 8)
        for k in range(levels):
            tiles = []
            for f in range(4):
                x = closed_ref[2, f, k, part]
                if t == last:
                    fixed = jnp.where(sub >= 6, roll(buf_ref[2, f, k], 4, 0), x)
                    x = jnp.where(top, fixed, x)
                if t == 0:
                    fixed = jnp.where(sub < 2, roll(buf_ref[2, f, k], -2, 0), x)
                    x = jnp.where(top, x, fixed)
                out_ref[f, k, part] = x
                tiles.append(x)

            def place(y, tile, t=t, k=k):
                at = main * (4 * t + y) + 8 * k
                main_ref[at : at + 8] = tile

            pairs_of_rows(tiles, t, place)
        for p in range(4 * t, 4 * t + 4):
            for i in range(3):
                send_ref[p, few + 8 * i : few + 8 * i + 8] = raw_ref[i, 2 * p : 2 * p + 8]
    x = jnp.concatenate(split(main_ref[...]), axis=1)
    x = product(x, jnp.concatenate([sums_ref[...]] * 2, axis=0), ((1,), (0,)))
    x = x + roll(x, SUMS, 1)
    for p in range(send_ref.shape[0]):
        send_ref[p, :few] = pack(x[main * p : main * (p + 1)])


def circle_kernel(
    circle_ref,
    table_ref,
    basis_ref,
    joint_basis_ref,
    count_ref,
    out_ref,
    tile_ref,
    term_ref,
    joint_ref,
):
    peers = circle_ref.shape[0]
    modes = basis_ref.shape[1] // 2
    length = basis_ref.shape[0]
    few = circle_ref.shape[1] - 24
    main = PACKED * few
    levels = main // 8
    lanes = LANES
    lane = lane_of((8, LANES))
    c = lane % GROUP
    for j in range(0, peers, 2):
        part = slice(4 * j, 4 * j + 8)
        for i in range(3):
            x, y, z = (
                circle_ref[(j + d) % peers, few + 8 * i : few + 8 * i + 8] for d in range(3)
            )
            for f, shift in ((2 * i, 0), (2 * i + 1, -8)):
                middle = jnp.where(c < 12, roll(y, 4 + shift, 1), roll(z, 12 + shift, 1))
                tile_ref[f, part] = jnp.where(c < 4, roll(x, shift - 4, 1), middle)
    inv_c, face = (jnp.concatenate([table_ref[i]] * (peers // 2), axis=0) for i in (0, 1))
    step_tile(tile_ref, tile_ref[4], tile_ref[5], levels, inv_c, face, term_ref)
    sub = lax.broadcasted_iota(jnp.int32, (8, LANES), 0) // 2
    right = (c % 8 >= 2) & (c % 8 < 6)
    for j in range(peers // 2):
        made = jnp.zeros((8, LANES), jnp.float32)
        for f in range(4):
            x = tile_ref[f, 8 * j : 8 * j + 8]
            made = jnp.where(sub == f, roll(x, 2 * f - 2, 0), made)
        joint_ref[8 * j : 8 * j + 8] = jnp.where(right, made, 0.0)
    lane_main = lane_of((main, LANES))
    row_main = lax.broadcasted_iota(jnp.int32, (main, LANES), 0)
    at_level = lane_main // GROUP == row_main // 8

    def block(o):
        return unpack(circle_ref[o, :few])

    def joint(j):
        x = joint_ref[8 * j : 8 * j + 8]
        return jnp.where(at_level, jnp.concatenate([x] * levels, axis=0), 0.0)

    total = jnp.zeros((2 * main, 2 * modes), jnp.float32)
    for source, basis, count in (
        (block, basis_ref, peers),
        (joint, joint_basis_ref, peers // 2),
    ):
        for o in range(0, count, 2):
            parts = zip(split(source(o)), split(source(o + 1)))
            x = jnp.concatenate([jnp.concatenate(p, axis=1) for p in parts], axis=0)
            total = total + product(x, basis[lanes * o : lanes * (o + 2)], ((1,), (0,)))
    total = total[:main] + total[main:]
    counts = count_ref[...]
    row = lax.broadcasted_iota(jnp.int32, counts.shape, 0)
    own = 2 * lax.axis_index("lon")
    even, odd = (
        jnp.sum(jnp.where(row == own + r, counts, 0.0), axis=0, keepdims=True) for r in (0, 1)
    )
    limit = jnp.where(row_main % 2 == 0, even, odd)
    order = (lane_main % (modes // 2)).astype(jnp.float32)
    weight = jnp.where(order < limit, jnp.where(order == 0.0, 1.0 / length, 2.0 / length), 0.0)
    total = (total[:, :modes] + total[:, modes:]) * weight
    y = jnp.concatenate([jnp.concatenate([p, p], axis=1) for p in split(total)], axis=0)
    for o in range(0, peers, 2):
        x = product(y, basis_ref[lanes * o : lanes * (o + 2)], ((1,), (1,)))
        x = x[:main] + x[main:]
        out_ref[o, :few] = pack(x[:, :lanes])
        out_ref[o + 1, :few] = pack(x[:, lanes:])
        before = (4 * o - 8) % (4 * peers)
        here = joint_ref[4 * o : 4 * o + 8]
        out_ref[o, few:] = jnp.where(
            c < 8, roll(joint_ref[before : before + 8], -8, 1), roll(here, 8, 1)
        )
        out_ref[o + 1, few:] = here


def join_kernel(
    state_ref, piece_ref, wet_ref, flag_ref, columns_ref, out_ref, made_ref, smooth_ref, sems
):
    levels, rows, lanes = wet_ref.shape
    main = 8 * levels
    few = main // PACKED
    lane = lane_of((8, LANES))
    x = jnp.concatenate(
        [unpack(piece_ref[p, :few]) for p in range(piece_ref.shape[0])], axis=0
    )
    x = jnp.concatenate(split(x), axis=1)
    x = product(x, jnp.concatenate([columns_ref[...]] * 2, axis=0), ((1,), (0,)))
    smooth_ref[...] = x[:, :lanes] + x[:, lanes:]
    edges = [{} for _ in range(rows // 8)]
    for t, into in enumerate(edges):
        tiles = [piece_ref[4 * t + x, few : few + 8] for x in range(4)]
        pairs_of_rows(tiles, t, into.__setitem__)
    copies = []
    for k in range(levels):
        for t in range(rows // 8):
            part = slice(8 * t, 8 * t + 8)
            starts = [main * (4 * t + x) + 8 * k for x in range(4)]
            tiles = [smooth_ref[at : at + 8] for at in starts]
            gate = flag_ref[part] * wet_ref[k, part]

            def place(f, smooth, k=k, gate=gate, part=part, edge=edges[t]):
                first = roll(edge[f], -(GROUP * k + 4), 1)
                last = roll(edge[f], lanes - 2 - (GROUP * k + 10), 1)
                state = jnp.where(
                    lane < 2, first, jnp.where(lane >= lanes - 2, last, state_ref[f, k, part])
                )
                made_ref[f, k, part] = state + gate * (smooth - state)

            pairs_of_rows(tiles, t, place)
        if k % 2:
            both = pl.ds(k - 1, 2)
            copies.append(
                pltpu.make_async_copy(
                    made_ref.at[:, both], out_ref.at[:, both], sems.at[k // 2]
                )
            )
            copies[-1].start()
    for copy in copies:
        copy.wait()


def filter_kernel(circle_ref, basis_ref, weight_ref, out_ref, piece_ref, sems):
    pieces, part, lanes = circle_ref.shape
    modes = weight_ref.shape[1]
    pairs = range(0, pieces, 2)
    total = jnp.zeros((2 * part, 2 * modes), jnp.float32)
    for o in pairs:
        parts = zip(split(circle_ref[o]), split(circle_ref[o + 1]))
        x = jnp.concatenate([jnp.concatenate(p, axis=1) for p in parts], axis=0)
        total = total + product(x, basis_ref[lanes * o : lanes * (o + 2)], ((1,), (0,)))
    total = total[:part] + total[part:]
    total = (total[:, :modes] + total[:, modes:]) * weight_ref[...]
    y = jnp.concatenate([jnp.concatenate([p, p], axis=1) for p in split(total)], axis=0)
    copies = []
    for o in pairs:
        x = product(y, basis_ref[lanes * o : lanes * (o + 2)], ((1,), (1,)))
        x = x[:part] + x[part:]
        piece_ref[o] = x[:, :lanes]
        piece_ref[o + 1] = x[:, lanes:]
        both = pl.ds(o, 2)
        copies.append(
            pltpu.make_async_copy(piece_ref.at[both], out_ref.at[both], sems.at[o // 2])
        )
        copies[-1].start()
    for copy in copies:
        copy.wait()


def blend_kernel(state_ref, smooth_ref, wet_ref, flag_ref, out_ref, piece_ref, sems):
    levels = wet_ref.shape[0]
    flag = flag_ref[...]
    copies = []
    for f in range(4):
        for k in range(levels):
            state = state_ref[f, k]
            gate = flag * wet_ref[k]
            piece_ref[f, k] = state + gate * (smooth_ref[f, k] - state)
        copies.append(pltpu.make_async_copy(piece_ref.at[f], out_ref.at[f], sems.at[f]))
        copies[-1].start()
    for copy in copies:
        copy.wait()


def call(kernel, outs, scratch=(), sems=0, raw=False, sent=False, flops=0):
    vmem = pl.BlockSpec(memory_space=pltpu.VMEM)
    away = pl.BlockSpec(memory_space=pl.ANY)
    specs = [vmem] * len(outs)
    shapes = [jax.ShapeDtypeStruct(s, jnp.float32) if isinstance(s, tuple) else s for s in outs]
    if sent:
        specs[-1] = away
        shapes[-1] = pltpu.HBM(outs[-1], jnp.float32)
    buffers = [pltpu.VMEM(s, jnp.float32) if isinstance(s, tuple) else s for s in scratch]
    if sems:
        buffers.append(pltpu.SemaphoreType.DMA((sems,)))
    cost = pl.CostEstimate(
        flops=flops,
        transcendentals=0,
        bytes_accessed=4 * sum(math.prod(s.shape) for s in shapes),
    )

    def run(*args):
        if raw:
            args = [pltpu.with_memory_space_constraint(x, pltpu.HBM) for x in args]
        return pl.pallas_call(
            kernel,
            out_shape=shapes,
            in_specs=[away if raw else vmem] * len(args),
            out_specs=specs,
            scratch_shapes=buffers,
            compiler_params=pltpu.CompilerParams(vmem_limit_bytes=24 << 20),
            cost_estimate=cost,
        )(*args)

    return run


def swap_edges(before_src, after_src, axis):
    peers = lax.axis_size(axis)
    up = [(i, (i + 1) % peers) for i in range(peers)]
    down = [(j, i) for i, j in up]
    return lax.ppermute(before_src, axis, up), lax.ppermute(after_src, axis, down)


def mode_basis(length, modes):
    turns = np.arange(modes)[None, :] * np.arange(length)[:, None] % length
    angle = turns * (2.0 * math.pi / length)
    basis = np.concatenate([np.cos(angle), np.sin(angle)], axis=1).astype(np.float32)
    high = basis.astype(ml_dtypes.bfloat16)
    low = (basis - high.astype(np.float32)).astype(ml_dtypes.bfloat16)
    return np.concatenate([high, low], axis=1)


def two_parts(x):
    x = x.astype(np.float32)
    high = x.astype(ml_dtypes.bfloat16)
    return np.concatenate([high, (x - high.astype(np.float32)).astype(ml_dtypes.bfloat16)], axis=1)


def on_grid(x):
    return np.round(x * 2.0**32) / 2.0**32


def sequences(length, lanes, modes):
    at = np.arange(lanes)
    band = 2.0 * math.pi * (modes - 0.5) / length
    along = ((lanes - 1 - 2.0 * at) / 2.0) ** 2 * math.cos(band)
    beside = at[1:] * (lanes - at[1:]) / 2.0
    matrix = np.diag(along) + np.diag(beside, 1) + np.diag(beside, -1)
    most = np.linalg.eigh(matrix)[1][:, ::-1][:, :SUMS]
    order = np.where(np.arange(SUMS)[None, :] % 2 == 0, 1.0, at[:, None] - (lanes - 1) / 2.0)
    return on_grid(most * np.sign((most * order).sum(axis=0))[None, :])


def block_coefficients(length, lanes, modes, columns):
    turns = np.arange(modes)[None, :] * np.arange(length)[:, None] % length
    angle = turns * (2.0 * math.pi / length)
    wave = np.concatenate([np.cos(angle), np.sin(angle)], axis=1).reshape(-1, lanes, 2 * modes)
    made = on_grid(np.einsum("in,oim->onm", columns, wave, optimize=False))
    rest = wave - np.einsum("in,onm->oim", columns, made, optimize=False)
    return made, np.abs(rest).max()


def joint_basis(basis, lanes):
    length = basis.shape[0]
    tile, lane = np.divmod(np.arange(length // 2), lanes)
    half, c = np.divmod(lane % GROUP, 8)
    column = (lanes * (2 * tile + half + 1) + c - 4) % length
    return np.where(((c >= 2) & (c < 6))[:, None], basis[column], np.zeros_like(basis[column]))


def mode_weights(counts, modes, length):
    order = jnp.arange(modes).astype(jnp.float32)
    keep = (order[None, :] < counts[:, None]).astype(jnp.float32)
    scale = jnp.where(order == 0, 1.0, 2.0) / length
    weights = keep * scale[None, :]
    return jnp.concatenate([weights, weights], axis=1)


def shards(ocean_state, thickness, wet_mask, mode_counts, row_flags):
    levels, rows, lanes = ocean_state.shape[1:]
    assert rows % 8 == 0 and lanes == LANES and levels * GROUP <= LANES
    lon_peers = lax.axis_size("lon")
    lat_peers = lax.axis_size("lat")
    nlat = rows * lat_peers
    nlon = lanes * lon_peers
    full = rows + 8
    total = 4 * levels * rows
    part = total // lon_peers
    lat_pos = lax.axis_index("lat")
    first_row = lat_pos * rows
    cells = 4 * levels * full * lanes
    edge_rows = (6, levels, 2, lanes)

    paired = rows == 2 * lon_peers and rows >= FBAND and lat_peers % 2 == 0 and levels % 2 == 0
    columns = sequences(nlon, lanes, MAXM)
    if paired:
        coefficients, rest = block_coefficients(nlon, lanes, MAXM, columns)
        paired = bool(rest < 1e-8)
    inside = (np.arange(lanes) >= 2) & (np.arange(lanes) < lanes - 2)
    sums = jnp.asarray(np.tile(two_parts(columns * inside[:, None]), (1, PACKED // 2)))
    *block, first, last, flags, counts, table, end_table, joint_table, to_sums = call(
        functools.partial(load_kernel, paired),
        [ocean_state.shape, thickness.shape, thickness.shape, edge_rows, edge_rows]
        + [(rows, lanes)] * 2
        + [(2, full, lanes), (2, 8, lanes), (2, 8, lanes)]
        + [jax.ShapeDtypeStruct(sums.shape, sums.dtype)],
        [pltpu.VMEM(shape, jnp.int32) for shape in (thickness.shape, (1, rows), (1, rows))],
        sems=9,
        raw=True,
    )(ocean_state, thickness, wet_mask, row_flags[None], mode_counts[None], sums)

    def ready():
        return call(
            ready_kernel, [(6, rows, LANES), (5, levels, rows, lanes)], flops=20 * cells
        )(*block, table)

    def exchanged(below, above, own, terms):
        inner, edges, halo = call(
            inner_kernel,
            [(3, 4, levels, full, lanes), (6, full, LANES), (6, levels, 8, lanes)],
            [(5, levels, 8, lanes), (2, levels, full, lanes)],
            flops=60 * cells,
        )(*block, below, above, table, own, terms)
        first, last = call(pack_kernel, [(full, LANES)] * 2)(*block, halo)
        from_west, from_east = swap_edges(last, first, "lon")
        return call(
            edge_kernel,
            [ocean_state.shape] * 2,
            [(4, full, LANES), (7, full, LANES)],
            sems=4,
            sent=True,
        )(inner, edges, from_west, from_east, table)

    banded = (first_row < FBAND) | (first_row + rows > nlat - FBAND)
    modes = mode_basis(nlon, MAXM)
    tables = [modes]
    if paired:
        coefficients = np.concatenate([coefficients] * PACKED, axis=1).reshape(nlon, 2 * MAXM)
        tables = [
            two_parts(coefficients),
            joint_basis(modes, lanes),
            two_parts(np.concatenate([columns.T] * PACKED, axis=0)),
        ]
    tables = lax.optimization_barrier([jnp.asarray(table) for table in tables])
    lon_pos = lax.axis_index("lon")

    def circled(got, own, closed):
        few = 8 * levels // PACKED
        tile = (levels, 8, lanes)
        to_modes, at_joints, to_columns = tables
        state, sent = call(
            end_kernel,
            [ocean_state.shape, (lon_peers, few + 24, lanes)],
            [(2,) + tile, (6,) + tile, (3, 4) + tile, (7,) + tile, (3, full, lanes)]
            + [(total, lanes)],
        )(*block, got, own, closed, end_table, to_sums)
        circles = lax.all_to_all(sent, "lon", 0, 0, tiled=True)
        pieces = call(
            circle_kernel,
            [(lon_peers, few + 8, lanes)],
            [
                (6, 4 * lon_peers, lanes),
                (7, 4 * lon_peers, lanes),
                (4 * lon_peers, lanes),
            ],
        )(circles, joint_table, to_modes, at_joints, counts)[0]
        pieces = lax.all_to_all(pieces, "lon", 0, 0, tiled=True)
        return call(
            join_kernel,
            [ocean_state.shape],
            [ocean_state.shape, (total, lanes)],
            sems=levels // 2,
            sent=True,
        )(state, pieces, block[2], flags, to_columns)[0]

    def between(got, *_):
        pairs = [(i, i + 1) for i in range(1, lat_peers - 1, 2)]
        other = lax.ppermute(last, "lat", pairs + [(j, i) for i, j in pairs])
        even = lat_pos % 2 == 0
        below, above = jnp.where(even, other, got), jnp.where(even, got, other)
        return exchanged(below, above, *ready())[1]

    if paired:
        got = lax.ppermute(first, "lat", [(i, i ^ 1) for i in range(lat_peers)])
        own, closed = call(
            closed_kernel,
            [(6, rows, LANES), (3, 4, levels, rows, lanes)],
            [(7, levels, rows, lanes)],
            flops=60 * cells,
        )(*block, table)
        got, own, closed = lax.optimization_barrier((got, own, closed))
        return lax.cond(banded, circled, between, got, own, closed)

    below, above = swap_edges(last, first, "lat")
    state, sent = exchanged(*lax.optimization_barrier((below, above, *ready())))

    def filtered():
        row_counts = lax.dynamic_slice(
            jnp.broadcast_to(
                mode_counts.astype(jnp.float32)[None], (4 * levels, rows)
            ).reshape(total),
            (lon_pos * part,),
            (part,),
        )
        circles = lax.all_to_all(
            sent.reshape(lon_peers, part, lanes), "lon", 0, 0, tiled=True
        )
        smooth = call(
            filter_kernel, [circles.shape], [circles.shape], sems=lon_peers // 2, sent=True
        )(circles, tables[0], mode_weights(row_counts, MAXM, nlon))[0]
        smooth = lax.all_to_all(smooth, "lon", 0, 0, tiled=True).reshape(state.shape)
        return call(blend_kernel, [state.shape], [state.shape], sems=4, sent=True)(
            state, smooth, block[2], flags
        )[0]

    return lax.cond(banded, filtered, lambda: sent)


def solution(mesh):
    in_specs = (
        P(None, None, "lat", "lon"),
        P(None, "lat", "lon"),
        P(None, "lat", "lon"),
        P("lat"),
        P("lat"),
    )
    out_specs = P(None, None, "lat", "lon")
    return jax.shard_map(shards, mesh=mesh, in_specs=in_specs, out_specs=out_specs, check_vma=False)
```

```python
import functools
import math

import jax
import jax.numpy as jnp
import ml_dtypes
import numpy as np
from jax import lax
from jax.experimental import pallas as pl
from jax.experimental.pallas import tpu as pltpu
from jax.sharding import PartitionSpec as P

FBAND = 16
MAXM = 64
LANES = 128
SUMS = 32
PACKED = LANES // SUMS
GROUP = 16


lat_edge = 1.3
diffusion = 0.05
vertical_mix = 0.5
time_step = 0.05


def roll(x, shift, axis):
    shift %= x.shape[axis]
    return pltpu.roll(x, shift, axis) if shift else x


def east(x):
    return roll(x, -1, 1)


def west(x):
    return roll(x, 1, 1)


def north(x):
    return roll(x, -1, 0)


def south(x):
    return roll(x, 1, 0)


def lane_of(shape):
    return lax.broadcasted_iota(jnp.int32, shape, 1)


def east_terms(h, w, inv_c):
    open_e = 0.5 * (h + east(h)) * (w * east(w))
    return 0.25 * open_e, diffusion * open_e * inv_c


def north_terms(h, w, face):
    open_n = 0.5 * (h + north(h)) * (w * north(w)) * face
    return 0.25 * open_n, diffusion * open_n


def advance(fields, terms, scale, scale_c, vertical):
    quarter_e, spread_e, quarter_n, spread_n = terms
    u, v = fields[2], fields[3]
    speed_e = quarter_e * (u + east(u))
    speed_n = quarter_n * (v + north(v))
    here_e, there_e = speed_e + spread_e, speed_e - spread_e
    here_n, there_n = speed_n + spread_n, speed_n - spread_n
    fresh = []
    for q, vert in zip(fields, vertical):
        flux_e = here_e * q + there_e * east(q)
        flux_n = here_n * q + there_n * north(q)
        spread = (flux_e - west(flux_e)) + (flux_n - south(flux_n))
        fresh.append(q + scale * vert - scale_c * spread)
    return fresh


def own_columns(load, levels, lanes, rows):
    lane = lane_of((rows, LANES))
    own = jnp.zeros((rows, LANES), jnp.float32)
    for k in range(levels):
        x = load(k)
        at = GROUP * k + 2
        own = jnp.where((lane >= at) & (lane < at + 4), roll(x, at, 1), own)
        at = GROUP * k + 8
        own = jnp.where((lane >= at) & (lane < at + 4), roll(x, at + 4 - lanes, 1), own)
    return own


def row_terms(thick, wet, inv_c, levels, term_ref):
    w, h = wet(0), thick(0)
    hs = jnp.where(w > 0, h, 1.0)
    for k in range(levels):
        term_ref[0, k], term_ref[1, k] = east_terms(h, w, inv_c)
        scale = time_step * w / hs
        term_ref[2, k] = scale
        term_ref[3, k] = scale * inv_c
        if k + 1 < levels:
            w_next, h_next = wet(k + 1), thick(k + 1)
            hs_next = jnp.where(w_next > 0, h_next, 1.0)
            term_ref[4, k] = w * w_next * vertical_mix / (0.5 * (hs + hs_next))
            w, h, hs = w_next, h_next, hs_next


def fill_table(ref, place, nlat):
    place = place.astype(jnp.float32)
    ref[0] = 1.0 / jnp.cos(lat_edge * (2.0 * (place + 0.5) / nlat - 1.0))
    ref[1] = jnp.cos(lat_edge * (2.0 * (place + 1.0) / nlat - 1.0))


def ring_rows(rows):
    place = lax.broadcasted_iota(jnp.int32, (rows + 8, LANES), 0)
    return jnp.where(place < rows + 2, place, jnp.where(place < rows + 6, 0, place - rows - 8))


def load_kernel(
    paired,
    state_any,
    thick_any,
    wet_any,
    flag_any,
    count_any,
    sums_any,
    state_ref,
    thick_ref,
    wet_ref,
    first_ref,
    last_ref,
    flag_ref,
    count_ref,
    table_ref,
    end_table_ref,
    joint_table_ref,
    sums_ref,
    raw_ref,
    raw_flag_ref,
    raw_count_ref,
    sems,
):
    levels, rows = thick_ref.shape[:2]
    moves = [(flag_any, raw_flag_ref), (count_any, raw_count_ref), (wet_any, raw_ref)]
    moves += [(thick_any, thick_ref), (sums_any, sums_ref)]
    moves += [(state_any.at[f], state_ref.at[f]) for f in range(4)]
    copies = [pltpu.make_async_copy(*pair, sems.at[i]) for i, pair in enumerate(moves)]
    for copy in copies:
        copy.start()
    nlat = rows * lax.axis_size("lat")
    lat_pos = lax.axis_index("lat")
    first_row = lat_pos * rows
    fill_table(table_ref, first_row + ring_rows(rows), nlat)
    if paired:
        six = jnp.minimum(lax.broadcasted_iota(jnp.int32, (8, LANES), 0), 5)
        end = jnp.where(lat_pos == 0, rows - 4, -2)
        fill_table(end_table_ref, first_row + end + six, nlat)
        fill_table(joint_table_ref, first_row + 2 * lax.axis_index("lon") - 2 + six, nlat)
    for copy in copies[:3]:
        copy.wait()
    shape = (rows, rows)
    diagonal = lax.broadcasted_iota(jnp.int32, shape, 0) == lane_of(shape)
    for raw, ref in ((raw_flag_ref, flag_ref), (raw_count_ref, count_ref)):
        spread = jnp.broadcast_to(raw[...].astype(jnp.float32), shape)
        value = jnp.sum(jnp.where(diagonal, spread, 0.0), axis=1, keepdims=True)
        ref[...] = jnp.broadcast_to(value, (rows, LANES))
    for k in range(levels):
        wet_ref[k] = raw_ref[k].astype(jnp.float32)
    for copy in copies[3:]:
        copy.wait()
    for f in range(6):
        for k in range(levels):
            x = state_ref.at[f, k] if f < 4 else (thick_ref, wet_ref)[f - 4].at[k]
            first_ref[f, k] = x[0:2]
            last_ref[f, k] = x[rows - 2 : rows]
    if paired:
        even = lax.axis_index("lat") % 2 == 0
        for f in range(6):
            for k in range(levels):
                low, high = first_ref[f, k], last_ref[f, k]
                first_ref[f, k] = jnp.where(even, high, low)
                last_ref[f, k] = jnp.where(even, low, high)


def ready_kernel(state_ref, thick_ref, wet_ref, table_ref, own_ref, term_ref):
    levels, rows, lanes = thick_ref.shape

    def thick(k):
        return thick_ref[k]

    def wet(k):
        return wet_ref[k]

    for f in range(4):
        own_ref[f] = own_columns(lambda k, f=f: state_ref[f, k], levels, lanes, rows)
    own_ref[4] = own_columns(thick, levels, lanes, rows)
    own_ref[5] = own_columns(wet, levels, lanes, rows)
    row_terms(thick, wet, table_ref[0, :rows], levels, term_ref)


def pack_kernel(state_ref, thick_ref, wet_ref, halo_ref, first_ref, last_ref):
    levels, rows, lanes = thick_ref.shape
    lane = lane_of((8, LANES))
    for t in range(rows // 8 + 1):
        first = jnp.zeros((8, LANES), jnp.float32)
        last = jnp.zeros((8, LANES), jnp.float32)
        part = slice(8 * t, 8 * t + 8)
        for f in range(6):
            for k in range(levels):
                if t == rows // 8:
                    x = halo_ref[f, k]
                elif f < 4:
                    x = state_ref[f, k, part]
                elif f == 4:
                    x = thick_ref[k, part]
                else:
                    x = wet_ref[k, part]
                at = GROUP * f + 2 * k
                mine = (lane >= at) & (lane < at + 2)
                first = jnp.where(mine, roll(x, at, 1), first)
                last = jnp.where(mine, roll(x, at + 2 - lanes, 1), last)
        first_ref[part] = first
        last_ref[part] = last


def inner_kernel(
    state_ref,
    thick_ref,
    wet_ref,
    below_ref,
    above_ref,
    table_ref,
    own_ref,
    term_ref,
    out_ref,
    edge_ref,
    halo_ref,
    halo_term_ref,
    north_ref,
):
    levels, rows, lanes = thick_ref.shape
    full = rows + 8
    face = table_ref[1]
    lat_pos = lax.axis_index("lat")
    with_below = jnp.where(lat_pos > 0, 1.0, 0.0)
    with_above = jnp.where(lat_pos < lax.axis_size("lat") - 1, 1.0, 0.0)
    for f in range(6):
        for k in range(levels):
            halo_ref[f, k, 0:2] = above_ref[f, k] * with_above
            halo_ref[f, k, 2:6] = jnp.zeros((4, lanes), jnp.float32)
            halo_ref[f, k, 6:8] = below_ref[f, k] * with_below

    def joined(x, y):
        return jnp.concatenate([x, y], axis=0)

    def halo(f):
        return lambda k: halo_ref[f, k]

    for f in range(6):
        edge_ref[f, :rows] = own_ref[f]
        edge_ref[f, rows:] = own_columns(halo(f), levels, lanes, 8)
    row_terms(halo(4), halo(5), table_ref[0, rows:], levels, halo_term_ref)
    for k in range(levels):
        h = joined(thick_ref[k], halo_ref[4, k])
        w = joined(wet_ref[k], halo_ref[5, k])
        north_ref[0, k], north_ref[1, k] = north_terms(h, w, face)
        for f in range(4):
            out_ref[0, f, k] = joined(state_ref[f, k], halo_ref[f, k])

    def term(i, k):
        return joined(term_ref[i, k], halo_term_ref[i, k])

    def step(i, _):
        source, target = out_ref.at[i], out_ref.at[i + 1]
        fields = [source[f, 0] for f in range(4)]
        above = [jnp.zeros((full, LANES), jnp.float32)] * 4
        for k in range(levels):
            deeper = below = above
            if k + 1 < levels:
                couple = term(4, k)
                deeper = [source[f, k + 1] for f in range(4)]
                below = [couple * (d - q) for d, q in zip(deeper, fields)]
                vertical = [b - a for b, a in zip(below, above)]
            else:
                vertical = [-a for a in above]
            terms = term(0, k), term(1, k), north_ref[0, k], north_ref[1, k]
            fresh = advance(fields, terms, term(2, k), term(3, k), vertical)
            for f in range(4):
                target[f, k] = fresh[f]
            fields, above = deeper, below
        return 0

    lax.fori_loop(0, 2, step, 0)


def step_tile(tile_ref, h, w, levels, inv_c, face, term_ref):
    lane = lane_of(h.shape)

    def deeper(x):
        return roll(x, -GROUP, 1)

    def shallower(x):
        return roll(x, GROUP, 1)

    hs = jnp.where(w > 0, h, 1.0)
    scale = time_step * w / hs
    couple = w * deeper(w) * vertical_mix / (0.5 * (hs + deeper(hs)))
    couple = jnp.where(lane < GROUP * (levels - 1), couple, 0.0)
    terms = east_terms(h, w, inv_c) + north_terms(h, w, face)
    for i, term in enumerate(terms + (scale, scale * inv_c, couple)):
        term_ref[i] = term

    def step():
        terms = [term_ref[i] for i in range(7)]
        fields = [tile_ref[f] for f in range(4)]
        vertical = []
        for q in fields:
            down = terms[6] * (deeper(q) - q)
            vertical.append(down - shallower(down))
        for f, q in enumerate(advance(fields, terms[:4], terms[4], terms[5], vertical)):
            tile_ref[f] = q

    step()
    step()


def edge_kernel(
    inner_ref, own_ref, west_ref, east_ref, table_ref, out_ref, send_ref, tile_ref, term_ref, sems
):
    levels, rows, lanes = out_ref.shape[1:]
    full = rows + 8
    lane = lane_of((full, LANES))
    from_west, from_east = west_ref[...], east_ref[...]

    def joined(f):
        x = own_ref[f]
        for k in range(levels):
            src = GROUP * f + 2 * k
            at = GROUP * k
            x = jnp.where((lane >= at) & (lane < at + 2), roll(from_west, at - src, 1), x)
            at = GROUP * k + 12
            x = jnp.where((lane >= at) & (lane < at + 2), roll(from_east, at - src, 1), x)
        return x

    for f in range(4):
        tile_ref[f] = joined(f)
    step_tile(tile_ref, joined(4), joined(5), levels, table_ref[0], table_ref[1], term_ref)
    lane = lane_of((rows, LANES))
    for f in range(4):
        x = tile_ref[f, :rows]
        for k in range(levels):
            left = roll(x, -(GROUP * k + 2), 1)
            right = roll(x, lanes - 2 - (GROUP * k + 10), 1)
            out_ref[f, k] = jnp.where(
                lane < 2,
                left,
                jnp.where(lane >= lanes - 2, right, inner_ref[2, f, k, :rows]),
            )
        pltpu.make_async_copy(out_ref.at[f], send_ref.at[f], sems.at[f]).start()
    for f in range(4):
        pltpu.make_async_copy(out_ref.at[f], send_ref.at[f], sems.at[f]).wait()


def split(x):
    high = x.astype(jnp.bfloat16)
    return high, (x - high.astype(jnp.float32)).astype(jnp.bfloat16)


def product(a, b, dims):
    return lax.dot_general(a, b, (dims, ((), ())), preferred_element_type=jnp.float32)


def unpack(x):
    part = lane_of(x.shape) // SUMS
    return jnp.concatenate([jnp.where(part == g, x, 0.0) for g in range(PACKED)], axis=0)


def turned(tiles, place):
    part = lane_of(tiles[0].shape) // SUMS
    made = roll(tiles[0], -SUMS * place, 1)
    for d in range(1, PACKED):
        made = jnp.where(part == d, roll(tiles[d], SUMS * (d - place), 1), made)
    return made


def pack(x):
    size = x.shape[0] // PACKED
    made = x[:size]
    part = lane_of(made.shape) // SUMS
    for g in range(1, PACKED):
        made = jnp.where(part == g, x[size * g : size * (g + 1)], made)
    return made


def pairs_of_rows(tiles, t, place):
    sub = lax.broadcasted_iota(jnp.int32, tiles[0].shape, 0) // 2
    for y in range(4):
        made = roll(tiles[0], -2 * y, 0)
        for x in range(1, 4):
            made = jnp.where(sub == x, roll(tiles[x], 2 * (x - y), 0), made)
        place(y, made)


def step_levels(buf_ref, term_ref, loop):
    levels, size = buf_ref.shape[2:4]

    def step(i, _):
        source, target = buf_ref.at[i], buf_ref.at[i + 1]
        fields = [source[f, 0] for f in range(4)]
        above = [jnp.zeros((size, LANES), jnp.float32)] * 4
        for k in range(levels):
            deeper = below = above
            if k + 1 < levels:
                couple = term_ref[4, k]
                deeper = [source[f, k + 1] for f in range(4)]
                below = [couple * (d - q) for d, q in zip(deeper, fields)]
                vertical = [b - a for b, a in zip(below, above)]
            else:
                vertical = [-a for a in above]
            terms = [term_ref[i, k] for i in (0, 1, 5, 6)]
            fresh = advance(fields, terms, term_ref[2, k], term_ref[3, k], vertical)
            for f in range(4):
                target[f, k] = fresh[f]
            fields, above = deeper, below
        return 0

    if loop:
        lax.fori_loop(0, 2, step, 0)
    else:
        step(1, step(0, 0))


def closed_kernel(state_ref, thick_ref, wet_ref, table_ref, own_ref, buf_ref, term_ref):
    levels, rows, lanes = thick_ref.shape

    def thick(k):
        return thick_ref[k]

    def wet(k):
        return wet_ref[k]

    for f in range(4):
        own_ref[f] = own_columns(lambda k, f=f: state_ref[f, k], levels, lanes, rows)
    own_ref[4] = own_columns(thick, levels, lanes, rows)
    own_ref[5] = own_columns(wet, levels, lanes, rows)
    row_terms(thick, wet, table_ref[0, :rows], levels, term_ref)
    row = lax.broadcasted_iota(jnp.int32, (rows, LANES), 0)
    face = jnp.where(row < rows - 1, table_ref[1, :rows], 0.0)
    for k in range(levels):
        term_ref[5, k], term_ref[6, k] = north_terms(thick(k), wet(k), face)
        for f in range(4):
            buf_ref[0, f, k] = state_ref[f, k]
    step_levels(buf_ref, term_ref, True)


def end_kernel(
    state_ref,
    thick_ref,
    wet_ref,
    got_ref,
    own_ref,
    closed_ref,
    table_ref,
    sums_ref,
    out_ref,
    send_ref,
    field_ref,
    halo_ref,
    buf_ref,
    term_ref,
    raw_ref,
    main_ref,
):
    levels, rows, lanes = thick_ref.shape
    full = rows + 8
    top = lax.axis_index("lat") == 0
    at_top = jnp.where(top, 1.0, 0.0)
    at_bottom = jnp.where(top, 0.0, 1.0)
    sub = lax.broadcasted_iota(jnp.int32, (8, LANES), 0)

    def own(f, k, part):
        return state_ref[f, k, part] if f < 4 else (thick_ref, wet_ref)[f - 4][k, part]

    for f in range(6):
        for k in range(levels):
            halo_ref[f, k, 0:2] = got_ref[f, k] * at_top
            halo_ref[f, k, 2:6] = jnp.zeros((4, lanes), jnp.float32)
            halo_ref[f, k, 6:8] = got_ref[f, k] * at_bottom
    for f in range(6):
        for k in range(levels):
            halo = halo_ref[f, k]
            beyond = jnp.where(sub < 6, roll(halo, 4, 0), 0.0)
            high = jnp.where(sub < 4, roll(own(f, k, slice(rows - 8, rows)), -4, 0), beyond)
            low = jnp.where(sub < 2, roll(halo, 2, 0), roll(own(f, k, slice(0, 8)), 2, 0))
            tile = jnp.where(top, high, low)
            if f < 4:
                buf_ref[0, f, k] = tile
            else:
                field_ref[f - 4, k] = tile

    def thick(k):
        return field_ref[0, k]

    def wet(k):
        return field_ref[1, k]

    row_terms(thick, wet, table_ref[0], levels, term_ref)
    for k in range(levels):
        term_ref[5, k], term_ref[6, k] = north_terms(thick(k), wet(k), table_ref[1])
    step_levels(buf_ref, term_ref, False)
    c = lane_of((full, LANES)) % GROUP

    def ring(f):
        beyond = own_columns(lambda k: halo_ref[f, k], levels, lanes, 8)
        return jnp.concatenate([own_ref[f], beyond], axis=0)

    for i in range(3):
        a, b = ring(2 * i), ring(2 * i + 1)
        one = jnp.where(c < 4, roll(a, -2, 1), roll(a, -4, 1))
        two = jnp.where(c < 12, roll(b, 6, 1), roll(b, 4, 1))
        both = jnp.where(c < 8, one, two)
        raw_ref[i, 0:2] = both[full - 2 : full]
        raw_ref[i, 2 : rows + 4] = both[: rows + 2]
        raw_ref[i, rows + 4 : full] = jnp.zeros((4, LANES), jnp.float32)
    main = 8 * levels
    few = main // PACKED
    last = rows // 8 - 1
    for t in range(rows // 8):
        part = slice(8 * t, 8 * t + 8)
        for k in range(levels):
            tiles = []
            for f in range(4):
                x = closed_ref[2, f, k, part]
                if t == last:
                    fixed = jnp.where(sub >= 6, roll(buf_ref[2, f, k], 4, 0), x)
                    x = jnp.where(top, fixed, x)
                if t == 0:
                    fixed = jnp.where(sub < 2, roll(buf_ref[2, f, k], -2, 0), x)
                    x = jnp.where(top, x, fixed)
                out_ref[f, k, part] = x
                tiles.append(x)

            def place(y, tile, t=t, k=k):
                at = main * (4 * t + y) + 8 * k
                main_ref[at : at + 8] = tile

            pairs_of_rows(tiles, t, place)
        for p in range(4 * t, 4 * t + 4):
            for i in range(3):
                send_ref[p, few + 8 * i : few + 8 * i + 8] = raw_ref[i, 2 * p : 2 * p + 8]
    x = jnp.concatenate(split(main_ref[...]), axis=1)
    x = product(x, jnp.concatenate([sums_ref[...]] * 2, axis=0), ((1,), (0,)))
    x = x + roll(x, SUMS, 1)
    for p in range(send_ref.shape[0]):
        send_ref[p, :few] = pack(x[main * p : main * (p + 1)])


def circle_kernel(
    circle_ref,
    table_ref,
    basis_ref,
    joint_basis_ref,
    count_ref,
    out_ref,
    tile_ref,
    term_ref,
    joint_ref,
):
    peers = circle_ref.shape[0]
    modes = basis_ref.shape[1] // 2
    length = peers * LANES
    few = circle_ref.shape[1] - 24
    main = PACKED * few
    levels = main // 8
    lanes = LANES
    lane = lane_of((8, LANES))
    c = lane % GROUP
    for j in range(0, peers, 2):
        part = slice(4 * j, 4 * j + 8)
        for i in range(3):
            x, y, z = (
                circle_ref[(j + d) % peers, few + 8 * i : few + 8 * i + 8] for d in range(3)
            )
            for f, shift in ((2 * i, 0), (2 * i + 1, -8)):
                middle = jnp.where(c < 12, roll(y, 4 + shift, 1), roll(z, 12 + shift, 1))
                tile_ref[f, part] = jnp.where(c < 4, roll(x, shift - 4, 1), middle)
    inv_c, face = (jnp.concatenate([table_ref[i]] * (peers // 2), axis=0) for i in (0, 1))
    step_tile(tile_ref, tile_ref[4], tile_ref[5], levels, inv_c, face, term_ref)
    sub = lax.broadcasted_iota(jnp.int32, (8, LANES), 0) // 2
    right = (c % 8 >= 2) & (c % 8 < 6)
    for j in range(peers // 2):
        made = jnp.zeros((8, LANES), jnp.float32)
        for f in range(4):
            x = tile_ref[f, 8 * j : 8 * j + 8]
            made = jnp.where(sub == f, roll(x, 2 * f - 2, 0), made)
        joint_ref[8 * j : 8 * j + 8] = jnp.where(right, made, 0.0)
    lane_main = lane_of((main, LANES))
    row_main = lax.broadcasted_iota(jnp.int32, (main, LANES), 0)
    at_level = lane_main // GROUP == row_main // 8

    def block(o):
        return jnp.concatenate(
            [turned([circle_ref[PACKED * o + d, :few] for d in range(PACKED)], g) for g in range(PACKED)],
            axis=0,
        )

    def joint(j):
        x = joint_ref[8 * j : 8 * j + 8]
        return jnp.where(at_level, jnp.concatenate([x] * levels, axis=0), 0.0)

    total = jnp.zeros((2 * main, 2 * modes), jnp.float32)
    for source, basis, count in (
        (block, basis_ref, peers // PACKED),
        (joint, joint_basis_ref, peers // 2),
    ):
        for o in range(0, count, 2):
            parts = zip(split(source(o)), split(source(o + 1)))
            x = jnp.concatenate([jnp.concatenate(p, axis=1) for p in parts], axis=0)
            total = total + product(x, basis[lanes * o : lanes * (o + 2)], ((1,), (0,)))
    total = total[:main] + total[main:]
    counts = count_ref[...]
    row = lax.broadcasted_iota(jnp.int32, counts.shape, 0)
    own = 2 * lax.axis_index("lon")
    even, odd = (
        jnp.sum(jnp.where(row == own + r, counts, 0.0), axis=0, keepdims=True) for r in (0, 1)
    )
    limit = jnp.where(row_main % 2 == 0, even, odd)
    order = (lane_main % (modes // 2)).astype(jnp.float32)
    weight = jnp.where(order < limit, jnp.where(order == 0.0, 1.0 / length, 2.0 / length), 0.0)
    total = (total[:, :modes] + total[:, modes:]) * weight
    y = jnp.concatenate([jnp.concatenate([p, p], axis=1) for p in split(total)], axis=0)
    x = product(y, basis_ref[...], ((1,), (1,)))
    x = x[:main] + x[main:]
    for o in range(peers):
        at = lanes * (o // PACKED)
        tiles = [x[few * g : few * (g + 1), at : at + lanes] for g in range(PACKED)]
        out_ref[o, :few] = turned(tiles, o % PACKED)
    for o in range(0, peers, 2):
        before = (4 * o - 8) % (4 * peers)
        here = joint_ref[4 * o : 4 * o + 8]
        out_ref[o, few:] = jnp.where(
            c < 8, roll(joint_ref[before : before + 8], -8, 1), roll(here, 8, 1)
        )
        out_ref[o + 1, few:] = here


def join_kernel(
    state_ref, piece_ref, wet_ref, flag_ref, columns_ref, out_ref, made_ref, smooth_ref, sems
):
    levels, rows, lanes = wet_ref.shape
    main = 8 * levels
    few = main // PACKED
    lane = lane_of((8, LANES))
    x = jnp.concatenate(
        [unpack(piece_ref[p, :few]) for p in range(piece_ref.shape[0])], axis=0
    )
    x = jnp.concatenate(split(x), axis=1)
    x = product(x, jnp.concatenate([columns_ref[...]] * 2, axis=0), ((1,), (0,)))
    smooth_ref[...] = x[:, :lanes] + x[:, lanes:]
    edges = [{} for _ in range(rows // 8)]
    for t, into in enumerate(edges):
        tiles = [piece_ref[4 * t + x, few : few + 8] for x in range(4)]
        pairs_of_rows(tiles, t, into.__setitem__)
    copies = []
    for k in range(levels):
        for t in range(rows // 8):
            part = slice(8 * t, 8 * t + 8)
            starts = [main * (4 * t + x) + 8 * k for x in range(4)]
            tiles = [smooth_ref[at : at + 8] for at in starts]
            gate = flag_ref[part] * wet_ref[k, part]

            def place(f, smooth, k=k, gate=gate, part=part, edge=edges[t]):
                first = roll(edge[f], -(GROUP * k + 4), 1)
                last = roll(edge[f], lanes - 2 - (GROUP * k + 10), 1)
                state = jnp.where(
                    lane < 2, first, jnp.where(lane >= lanes - 2, last, state_ref[f, k, part])
                )
                made_ref[f, k, part] = state + gate * (smooth - state)

            pairs_of_rows(tiles, t, place)
        if k % 2:
            both = pl.ds(k - 1, 2)
            copies.append(
                pltpu.make_async_copy(
                    made_ref.at[:, both], out_ref.at[:, both], sems.at[k // 2]
                )
            )
            copies[-1].start()
    for copy in copies:
        copy.wait()


def filter_kernel(circle_ref, basis_ref, weight_ref, out_ref, piece_ref, sems):
    pieces, part, lanes = circle_ref.shape
    modes = weight_ref.shape[1]
    pairs = range(0, pieces, 2)
    total = jnp.zeros((2 * part, 2 * modes), jnp.float32)
    for o in pairs:
        parts = zip(split(circle_ref[o]), split(circle_ref[o + 1]))
        x = jnp.concatenate([jnp.concatenate(p, axis=1) for p in parts], axis=0)
        total = total + product(x, basis_ref[lanes * o : lanes * (o + 2)], ((1,), (0,)))
    total = total[:part] + total[part:]
    total = (total[:, :modes] + total[:, modes:]) * weight_ref[...]
    y = jnp.concatenate([jnp.concatenate([p, p], axis=1) for p in split(total)], axis=0)
    copies = []
    for o in pairs:
        x = product(y, basis_ref[lanes * o : lanes * (o + 2)], ((1,), (1,)))
        x = x[:part] + x[part:]
        piece_ref[o] = x[:, :lanes]
        piece_ref[o + 1] = x[:, lanes:]
        both = pl.ds(o, 2)
        copies.append(
            pltpu.make_async_copy(piece_ref.at[both], out_ref.at[both], sems.at[o // 2])
        )
        copies[-1].start()
    for copy in copies:
        copy.wait()


def blend_kernel(state_ref, smooth_ref, wet_ref, flag_ref, out_ref, piece_ref, sems):
    levels = wet_ref.shape[0]
    flag = flag_ref[...]
    copies = []
    for f in range(4):
        for k in range(levels):
            state = state_ref[f, k]
            gate = flag * wet_ref[k]
            piece_ref[f, k] = state + gate * (smooth_ref[f, k] - state)
        copies.append(pltpu.make_async_copy(piece_ref.at[f], out_ref.at[f], sems.at[f]))
        copies[-1].start()
    for copy in copies:
        copy.wait()


def call(kernel, outs, scratch=(), sems=0, raw=False, sent=False, flops=0):
    vmem = pl.BlockSpec(memory_space=pltpu.VMEM)
    away = pl.BlockSpec(memory_space=pl.ANY)
    specs = [vmem] * len(outs)
    shapes = [jax.ShapeDtypeStruct(s, jnp.float32) if isinstance(s, tuple) else s for s in outs]
    if sent:
        specs[-1] = away
        shapes[-1] = pltpu.HBM(outs[-1], jnp.float32)
    buffers = [pltpu.VMEM(s, jnp.float32) if isinstance(s, tuple) else s for s in scratch]
    if sems:
        buffers.append(pltpu.SemaphoreType.DMA((sems,)))
    cost = pl.CostEstimate(
        flops=flops,
        transcendentals=0,
        bytes_accessed=4 * sum(math.prod(s.shape) for s in shapes),
    )

    def run(*args):
        if raw:
            args = [pltpu.with_memory_space_constraint(x, pltpu.HBM) for x in args]
        return pl.pallas_call(
            kernel,
            out_shape=shapes,
            in_specs=[away if raw else vmem] * len(args),
            out_specs=specs,
            scratch_shapes=buffers,
            compiler_params=pltpu.CompilerParams(vmem_limit_bytes=24 << 20),
            cost_estimate=cost,
        )(*args)

    return run


def swap_edges(before_src, after_src, axis):
    peers = lax.axis_size(axis)
    up = [(i, (i + 1) % peers) for i in range(peers)]
    down = [(j, i) for i, j in up]
    return lax.ppermute(before_src, axis, up), lax.ppermute(after_src, axis, down)


def mode_basis(length, modes):
    turns = np.arange(modes)[None, :] * np.arange(length)[:, None] % length
    angle = turns * (2.0 * math.pi / length)
    basis = np.concatenate([np.cos(angle), np.sin(angle)], axis=1).astype(np.float32)
    high = basis.astype(ml_dtypes.bfloat16)
    low = (basis - high.astype(np.float32)).astype(ml_dtypes.bfloat16)
    return np.concatenate([high, low], axis=1)


def two_parts(x):
    x = x.astype(np.float32)
    high = x.astype(ml_dtypes.bfloat16)
    return np.concatenate([high, (x - high.astype(np.float32)).astype(ml_dtypes.bfloat16)], axis=1)


def on_grid(x):
    return np.round(x * 2.0**32) / 2.0**32


def sequences(length, lanes, modes):
    at = np.arange(lanes)
    band = 2.0 * math.pi * (modes - 0.5) / length
    along = ((lanes - 1 - 2.0 * at) / 2.0) ** 2 * math.cos(band)
    beside = at[1:] * (lanes - at[1:]) / 2.0
    matrix = np.diag(along) + np.diag(beside, 1) + np.diag(beside, -1)
    most = np.linalg.eigh(matrix)[1][:, ::-1][:, :SUMS]
    order = np.where(np.arange(SUMS)[None, :] % 2 == 0, 1.0, at[:, None] - (lanes - 1) / 2.0)
    return on_grid(most * np.sign((most * order).sum(axis=0))[None, :])


def block_coefficients(length, lanes, modes, columns):
    turns = np.arange(modes)[None, :] * np.arange(length)[:, None] % length
    angle = turns * (2.0 * math.pi / length)
    wave = np.concatenate([np.cos(angle), np.sin(angle)], axis=1).reshape(-1, lanes, 2 * modes)
    made = on_grid(np.einsum("in,oim->onm", columns, wave, optimize=False))
    rest = wave - np.einsum("in,onm->oim", columns, made, optimize=False)
    return made, np.abs(rest).max()


def joint_basis(basis, lanes):
    length = basis.shape[0]
    tile, lane = np.divmod(np.arange(length // 2), lanes)
    half, c = np.divmod(lane % GROUP, 8)
    column = (lanes * (2 * tile + half + 1) + c - 4) % length
    return np.where(((c >= 2) & (c < 6))[:, None], basis[column], np.zeros_like(basis[column]))


def mode_weights(counts, modes, length):
    order = jnp.arange(modes).astype(jnp.float32)
    keep = (order[None, :] < counts[:, None]).astype(jnp.float32)
    scale = jnp.where(order == 0, 1.0, 2.0) / length
    weights = keep * scale[None, :]
    return jnp.concatenate([weights, weights], axis=1)


def shards(ocean_state, thickness, wet_mask, mode_counts, row_flags):
    levels, rows, lanes = ocean_state.shape[1:]
    assert rows % 8 == 0 and lanes == LANES and levels * GROUP <= LANES
    lon_peers = lax.axis_size("lon")
    lat_peers = lax.axis_size("lat")
    nlat = rows * lat_peers
    nlon = lanes * lon_peers
    full = rows + 8
    total = 4 * levels * rows
    part = total // lon_peers
    lat_pos = lax.axis_index("lat")
    first_row = lat_pos * rows
    cells = 4 * levels * full * lanes
    edge_rows = (6, levels, 2, lanes)

    paired = rows == 2 * lon_peers and lon_peers % (2 * PACKED) == 0 and rows >= FBAND and lat_peers % 2 == 0 and levels % 2 == 0
    columns = sequences(nlon, lanes, MAXM)
    if paired:
        coefficients, rest = block_coefficients(nlon, lanes, MAXM, columns)
        paired = bool(rest < 1e-8)
    inside = (np.arange(lanes) >= 2) & (np.arange(lanes) < lanes - 2)
    sums = jnp.asarray(np.tile(two_parts(columns * inside[:, None]), (1, PACKED // 2)))
    *block, first, last, flags, counts, table, end_table, joint_table, to_sums = call(
        functools.partial(load_kernel, paired),
        [ocean_state.shape, thickness.shape, thickness.shape, edge_rows, edge_rows]
        + [(rows, lanes)] * 2
        + [(2, full, lanes), (2, 8, lanes), (2, 8, lanes)]
        + [jax.ShapeDtypeStruct(sums.shape, sums.dtype)],
        [pltpu.VMEM(shape, jnp.int32) for shape in (thickness.shape, (1, rows), (1, rows))],
        sems=9,
        raw=True,
    )(ocean_state, thickness, wet_mask, row_flags[None], mode_counts[None], sums)

    def ready():
        return call(
            ready_kernel, [(6, rows, LANES), (5, levels, rows, lanes)], flops=20 * cells
        )(*block, table)

    def exchanged(below, above, own, terms):
        inner, edges, halo = call(
            inner_kernel,
            [(3, 4, levels, full, lanes), (6, full, LANES), (6, levels, 8, lanes)],
            [(5, levels, 8, lanes), (2, levels, full, lanes)],
            flops=60 * cells,
        )(*block, below, above, table, own, terms)
        first, last = call(pack_kernel, [(full, LANES)] * 2)(*block, halo)
        from_west, from_east = swap_edges(last, first, "lon")
        return call(
            edge_kernel,
            [ocean_state.shape] * 2,
            [(4, full, LANES), (7, full, LANES)],
            sems=4,
            sent=True,
        )(inner, edges, from_west, from_east, table)

    banded = (first_row < FBAND) | (first_row + rows > nlat - FBAND)
    modes = mode_basis(nlon, MAXM)
    tables = [modes]
    if paired:
        coefficients = coefficients.reshape(SUMS * lon_peers, 2 * MAXM)
        tables = [
            two_parts(coefficients),
            joint_basis(modes, lanes),
            two_parts(np.concatenate([columns.T] * PACKED, axis=0)),
        ]
    tables = lax.optimization_barrier([jnp.asarray(table) for table in tables])
    lon_pos = lax.axis_index("lon")

    def circled(got, own, closed):
        few = 8 * levels // PACKED
        tile = (levels, 8, lanes)
        to_modes, at_joints, to_columns = tables
        state, sent = call(
            end_kernel,
            [ocean_state.shape, (lon_peers, few + 24, lanes)],
            [(2,) + tile, (6,) + tile, (3, 4) + tile, (7,) + tile, (3, full, lanes)]
            + [(total, lanes)],
        )(*block, got, own, closed, end_table, to_sums)
        circles = lax.all_to_all(sent, "lon", 0, 0, tiled=True)
        pieces = call(
            circle_kernel,
            [(lon_peers, few + 8, lanes)],
            [
                (6, 4 * lon_peers, lanes),
                (7, 4 * lon_peers, lanes),
                (4 * lon_peers, lanes),
            ],
        )(circles, joint_table, to_modes, at_joints, counts)[0]
        pieces = lax.all_to_all(pieces, "lon", 0, 0, tiled=True)
        return call(
            join_kernel,
            [ocean_state.shape],
            [ocean_state.shape, (total, lanes)],
            sems=levels // 2,
            sent=True,
        )(state, pieces, block[2], flags, to_columns)[0]

    def between(got, *_):
        pairs = [(i, i + 1) for i in range(1, lat_peers - 1, 2)]
        other = lax.ppermute(last, "lat", pairs + [(j, i) for i, j in pairs])
        even = lat_pos % 2 == 0
        below, above = jnp.where(even, other, got), jnp.where(even, got, other)
        return exchanged(below, above, *ready())[1]

    if paired:
        got = lax.ppermute(first, "lat", [(i, i ^ 1) for i in range(lat_peers)])
        own, closed = call(
            closed_kernel,
            [(6, rows, LANES), (3, 4, levels, rows, lanes)],
            [(7, levels, rows, lanes)],
            flops=60 * cells,
        )(*block, table)
        got, own, closed = lax.optimization_barrier((got, own, closed))
        return lax.cond(banded, circled, between, got, own, closed)

    below, above = swap_edges(last, first, "lat")
    state, sent = exchanged(*lax.optimization_barrier((below, above, *ready())))

    def filtered():
        row_counts = lax.dynamic_slice(
            jnp.broadcast_to(
                mode_counts.astype(jnp.float32)[None], (4 * levels, rows)
            ).reshape(total),
            (lon_pos * part,),
            (part,),
        )
        circles = lax.all_to_all(
            sent.reshape(lon_peers, part, lanes), "lon", 0, 0, tiled=True
        )
        smooth = call(
            filter_kernel, [circles.shape], [circles.shape], sems=lon_peers // 2, sent=True
        )(circles, tables[0], mode_weights(row_counts, MAXM, nlon))[0]
        smooth = lax.all_to_all(smooth, "lon", 0, 0, tiled=True).reshape(state.shape)
        return call(blend_kernel, [state.shape], [state.shape], sems=4, sent=True)(
            state, smooth, block[2], flags
        )[0]

    return lax.cond(banded, filtered, lambda: sent)


def solution(mesh):
    in_specs = (
        P(None, None, "lat", "lon"),
        P(None, "lat", "lon"),
        P(None, "lat", "lon"),
        P("lat"),
        P("lat"),
    )
    out_specs = P(None, None, "lat", "lon")
    return jax.shard_map(shards, mesh=mesh, in_specs=in_specs, out_specs=out_specs, check_vma=False)
```

```python
import functools
import math

import jax
import jax.numpy as jnp
import ml_dtypes
import numpy as np
from jax import lax
from jax.experimental import pallas as pl
from jax.experimental.pallas import tpu as pltpu
from jax.sharding import PartitionSpec as P

FBAND = 16
MAXM = 64
LANES = 128
SUMS = 32
PACKED = LANES // SUMS
GROUP = 16


lat_edge = 1.3
diffusion = 0.05
vertical_mix = 0.5
time_step = 0.05


def roll(x, shift, axis):
    shift %= x.shape[axis]
    return pltpu.roll(x, shift, axis) if shift else x


def east(x):
    return roll(x, -1, 1)


def west(x):
    return roll(x, 1, 1)


def north(x):
    return roll(x, -1, 0)


def south(x):
    return roll(x, 1, 0)


def lane_of(shape):
    return lax.broadcasted_iota(jnp.int32, shape, 1)


def east_terms(h, w, inv_c):
    open_e = 0.5 * (h + east(h)) * (w * east(w))
    return 0.25 * open_e, diffusion * open_e * inv_c


def north_terms(h, w, face):
    open_n = 0.5 * (h + north(h)) * (w * north(w)) * face
    return 0.25 * open_n, diffusion * open_n


def advance(fields, terms, scale, scale_c, vertical):
    quarter_e, spread_e, quarter_n, spread_n = terms
    u, v = fields[2], fields[3]
    speed_e = quarter_e * (u + east(u))
    speed_n = quarter_n * (v + north(v))
    here_e, there_e = speed_e + spread_e, speed_e - spread_e
    here_n, there_n = speed_n + spread_n, speed_n - spread_n
    fresh = []
    for q, vert in zip(fields, vertical):
        flux_e = here_e * q + there_e * east(q)
        flux_n = here_n * q + there_n * north(q)
        spread = (flux_e - west(flux_e)) + (flux_n - south(flux_n))
        fresh.append(q + scale * vert - scale_c * spread)
    return fresh


def own_columns(load, levels, lanes, rows):
    lane = lane_of((rows, LANES))
    own = jnp.zeros((rows, LANES), jnp.float32)
    for k in range(levels):
        x = load(k)
        at = GROUP * k + 2
        own = jnp.where((lane >= at) & (lane < at + 4), roll(x, at, 1), own)
        at = GROUP * k + 8
        own = jnp.where((lane >= at) & (lane < at + 4), roll(x, at + 4 - lanes, 1), own)
    return own


def row_terms(thick, wet, inv_c, levels, term_ref):
    w, h = wet(0), thick(0)
    hs = jnp.where(w > 0, h, 1.0)
    for k in range(levels):
        term_ref[0, k], term_ref[1, k] = east_terms(h, w, inv_c)
        scale = time_step * w / hs
        term_ref[2, k] = scale
        term_ref[3, k] = scale * inv_c
        if k + 1 < levels:
            w_next, h_next = wet(k + 1), thick(k + 1)
            hs_next = jnp.where(w_next > 0, h_next, 1.0)
            term_ref[4, k] = w * w_next * vertical_mix / (0.5 * (hs + hs_next))
            w, h, hs = w_next, h_next, hs_next


def fill_table(ref, place, nlat):
    place = place.astype(jnp.float32)
    ref[0] = 1.0 / jnp.cos(lat_edge * (2.0 * (place + 0.5) / nlat - 1.0))
    ref[1] = jnp.cos(lat_edge * (2.0 * (place + 1.0) / nlat - 1.0))


def ring_rows(rows):
    place = lax.broadcasted_iota(jnp.int32, (rows + 8, LANES), 0)
    return jnp.where(place < rows + 2, place, jnp.where(place < rows + 6, 0, place - rows - 8))


def load_kernel(
    paired,
    state_any,
    thick_any,
    wet_any,
    flag_any,
    count_any,
    sums_any,
    state_ref,
    thick_ref,
    wet_ref,
    first_ref,
    last_ref,
    flag_ref,
    count_ref,
    table_ref,
    end_table_ref,
    joint_table_ref,
    sums_ref,
    raw_ref,
    raw_flag_ref,
    raw_count_ref,
    sems,
):
    levels, rows = thick_ref.shape[:2]
    moves = [(flag_any, raw_flag_ref), (count_any, raw_count_ref), (wet_any, raw_ref)]
    moves += [(thick_any, thick_ref), (sums_any, sums_ref)]
    moves += [(state_any.at[f], state_ref.at[f]) for f in range(4)]
    copies = [pltpu.make_async_copy(*pair, sems.at[i]) for i, pair in enumerate(moves)]
    for copy in copies:
        copy.start()
    nlat = rows * lax.axis_size("lat")
    lat_pos = lax.axis_index("lat")
    first_row = lat_pos * rows
    fill_table(table_ref, first_row + ring_rows(rows), nlat)
    if paired:
        six = jnp.minimum(lax.broadcasted_iota(jnp.int32, (8, LANES), 0), 5)
        end = jnp.where(lat_pos == 0, rows - 4, -2)
        fill_table(end_table_ref, first_row + end + six, nlat)
        fill_table(joint_table_ref, first_row + 2 * lax.axis_index("lon") - 2 + six, nlat)
    for copy in copies[:3]:
        copy.wait()
    shape = (rows, rows)
    diagonal = lax.broadcasted_iota(jnp.int32, shape, 0) == lane_of(shape)
    for raw, ref in ((raw_flag_ref, flag_ref), (raw_count_ref, count_ref)):
        spread = jnp.broadcast_to(raw[...].astype(jnp.float32), shape)
        value = jnp.sum(jnp.where(diagonal, spread, 0.0), axis=1, keepdims=True)
        ref[...] = jnp.broadcast_to(value, (rows, LANES))
    for k in range(levels):
        wet_ref[k] = raw_ref[k].astype(jnp.float32)
    even = lax.axis_index("lat") % 2 == 0
    copies[3].wait()
    copies[4].wait()
    for f in (4, 5, 0, 1, 2, 3):
        if f < 4:
            copies[5 + f].wait()
        for k in range(levels):
            x = state_ref.at[f, k] if f < 4 else (thick_ref, wet_ref)[f - 4].at[k]
            low, high = x[0:2], x[rows - 2 : rows]
            if paired:
                low, high = jnp.where(even, high, low), jnp.where(even, low, high)
            first_ref[f, k] = low
            last_ref[f, k] = high


def ready_kernel(state_ref, thick_ref, wet_ref, table_ref, own_ref, term_ref):
    levels, rows, lanes = thick_ref.shape

    def thick(k):
        return thick_ref[k]

    def wet(k):
        return wet_ref[k]

    for f in range(4):
        own_ref[f] = own_columns(lambda k, f=f: state_ref[f, k], levels, lanes, rows)
    own_ref[4] = own_columns(thick, levels, lanes, rows)
    own_ref[5] = own_columns(wet, levels, lanes, rows)
    row_terms(thick, wet, table_ref[0, :rows], levels, term_ref)


def pack_kernel(state_ref, thick_ref, wet_ref, halo_ref, first_ref, last_ref):
    levels, rows, lanes = thick_ref.shape
    lane = lane_of((8, LANES))
    for t in range(rows // 8 + 1):
        first = jnp.zeros((8, LANES), jnp.float32)
        last = jnp.zeros((8, LANES), jnp.float32)
        part = slice(8 * t, 8 * t + 8)
        for f in range(6):
            for k in range(levels):
                if t == rows // 8:
                    x = halo_ref[f, k]
                elif f < 4:
                    x = state_ref[f, k, part]
                elif f == 4:
                    x = thick_ref[k, part]
                else:
                    x = wet_ref[k, part]
                at = GROUP * f + 2 * k
                mine = (lane >= at) & (lane < at + 2)
                first = jnp.where(mine, roll(x, at, 1), first)
                last = jnp.where(mine, roll(x, at + 2 - lanes, 1), last)
        first_ref[part] = first
        last_ref[part] = last


def inner_kernel(
    state_ref,
    thick_ref,
    wet_ref,
    below_ref,
    above_ref,
    table_ref,
    own_ref,
    term_ref,
    out_ref,
    edge_ref,
    halo_ref,
    halo_term_ref,
    north_ref,
):
    levels, rows, lanes = thick_ref.shape
    full = rows + 8
    face = table_ref[1]
    lat_pos = lax.axis_index("lat")
    with_below = jnp.where(lat_pos > 0, 1.0, 0.0)
    with_above = jnp.where(lat_pos < lax.axis_size("lat") - 1, 1.0, 0.0)
    for f in range(6):
        for k in range(levels):
            halo_ref[f, k, 0:2] = above_ref[f, k] * with_above
            halo_ref[f, k, 2:6] = jnp.zeros((4, lanes), jnp.float32)
            halo_ref[f, k, 6:8] = below_ref[f, k] * with_below

    def joined(x, y):
        return jnp.concatenate([x, y], axis=0)

    def halo(f):
        return lambda k: halo_ref[f, k]

    for f in range(6):
        edge_ref[f, :rows] = own_ref[f]
        edge_ref[f, rows:] = own_columns(halo(f), levels, lanes, 8)
    row_terms(halo(4), halo(5), table_ref[0, rows:], levels, halo_term_ref)
    for k in range(levels):
        h = joined(thick_ref[k], halo_ref[4, k])
        w = joined(wet_ref[k], halo_ref[5, k])
        north_ref[0, k], north_ref[1, k] = north_terms(h, w, face)
        for f in range(4):
            out_ref[0, f, k] = joined(state_ref[f, k], halo_ref[f, k])

    def term(i, k):
        return joined(term_ref[i, k], halo_term_ref[i, k])

    def step(i, _):
        source, target = out_ref.at[i], out_ref.at[i + 1]
        fields = [source[f, 0] for f in range(4)]
        above = [jnp.zeros((full, LANES), jnp.float32)] * 4
        for k in range(levels):
            deeper = below = above
            if k + 1 < levels:
                couple = term(4, k)
                deeper = [source[f, k + 1] for f in range(4)]
                below = [couple * (d - q) for d, q in zip(deeper, fields)]
                vertical = [b - a for b, a in zip(below, above)]
            else:
                vertical = [-a for a in above]
            terms = term(0, k), term(1, k), north_ref[0, k], north_ref[1, k]
            fresh = advance(fields, terms, term(2, k), term(3, k), vertical)
            for f in range(4):
                target[f, k] = fresh[f]
            fields, above = deeper, below
        return 0

    lax.fori_loop(0, 2, step, 0)


def step_tile(tile_ref, h, w, levels, inv_c, face, term_ref):
    lane = lane_of(h.shape)

    def deeper(x):
        return roll(x, -GROUP, 1)

    def shallower(x):
        return roll(x, GROUP, 1)

    hs = jnp.where(w > 0, h, 1.0)
    scale = time_step * w / hs
    couple = w * deeper(w) * vertical_mix / (0.5 * (hs + deeper(hs)))
    couple = jnp.where(lane < GROUP * (levels - 1), couple, 0.0)
    terms = east_terms(h, w, inv_c) + north_terms(h, w, face)
    for i, term in enumerate(terms + (scale, scale * inv_c, couple)):
        term_ref[i] = term

    def step():
        terms = [term_ref[i] for i in range(7)]
        fields = [tile_ref[f] for f in range(4)]
        vertical = []
        for q in fields:
            down = terms[6] * (deeper(q) - q)
            vertical.append(down - shallower(down))
        for f, q in enumerate(advance(fields, terms[:4], terms[4], terms[5], vertical)):
            tile_ref[f] = q

    step()
    step()


def edge_kernel(
    inner_ref, own_ref, west_ref, east_ref, table_ref, out_ref, send_ref, tile_ref, term_ref, sems
):
    levels, rows, lanes = out_ref.shape[1:]
    full = rows + 8
    lane = lane_of((full, LANES))
    from_west, from_east = west_ref[...], east_ref[...]

    def joined(f):
        x = own_ref[f]
        for k in range(levels):
            src = GROUP * f + 2 * k
            at = GROUP * k
            x = jnp.where((lane >= at) & (lane < at + 2), roll(from_west, at - src, 1), x)
            at = GROUP * k + 12
            x = jnp.where((lane >= at) & (lane < at + 2), roll(from_east, at - src, 1), x)
        return x

    for f in range(4):
        tile_ref[f] = joined(f)
    step_tile(tile_ref, joined(4), joined(5), levels, table_ref[0], table_ref[1], term_ref)
    lane = lane_of((rows, LANES))
    for f in range(4):
        x = tile_ref[f, :rows]
        for k in range(levels):
            left = roll(x, -(GROUP * k + 2), 1)
            right = roll(x, lanes - 2 - (GROUP * k + 10), 1)
            out_ref[f, k] = jnp.where(
                lane < 2,
                left,
                jnp.where(lane >= lanes - 2, right, inner_ref[2, f, k, :rows]),
            )
        pltpu.make_async_copy(out_ref.at[f], send_ref.at[f], sems.at[f]).start()
    for f in range(4):
        pltpu.make_async_copy(out_ref.at[f], send_ref.at[f], sems.at[f]).wait()


def split(x):
    high = x.astype(jnp.bfloat16)
    return high, (x - high.astype(jnp.float32)).astype(jnp.bfloat16)


def product(a, b, dims):
    return lax.dot_general(a, b, (dims, ((), ())), preferred_element_type=jnp.float32)


def unpack(x):
    part = lane_of(x.shape) // SUMS
    return jnp.concatenate([jnp.where(part == g, x, 0.0) for g in range(PACKED)], axis=0)


def pack(x):
    size = x.shape[0] // PACKED
    made = x[:size]
    part = lane_of(made.shape) // SUMS
    for g in range(1, PACKED):
        made = jnp.where(part == g, x[size * g : size * (g + 1)], made)
    return made


def pairs_of_rows(tiles, t, place):
    sub = lax.broadcasted_iota(jnp.int32, tiles[0].shape, 0) // 2
    for y in range(4):
        made = roll(tiles[0], -2 * y, 0)
        for x in range(1, 4):
            made = jnp.where(sub == x, roll(tiles[x], 2 * (x - y), 0), made)
        place(y, made)


def step_levels(buf_ref, term_ref, loop):
    levels, size = buf_ref.shape[2:4]

    def step(i, _):
        source, target = buf_ref.at[i], buf_ref.at[i + 1]
        fields = [source[f, 0] for f in range(4)]
        above = [jnp.zeros((size, LANES), jnp.float32)] * 4
        for k in range(levels):
            deeper = below = above
            if k + 1 < levels:
                couple = term_ref[4, k]
                deeper = [source[f, k + 1] for f in range(4)]
                below = [couple * (d - q) for d, q in zip(deeper, fields)]
                vertical = [b - a for b, a in zip(below, above)]
            else:
                vertical = [-a for a in above]
            terms = [term_ref[i, k] for i in (0, 1, 5, 6)]
            fresh = advance(fields, terms, term_ref[2, k], term_ref[3, k], vertical)
            for f in range(4):
                target[f, k] = fresh[f]
            fields, above = deeper, below
        return 0

    if loop:
        lax.fori_loop(0, 2, step, 0)
    else:
        step(1, step(0, 0))


def closed_kernel(state_ref, thick_ref, wet_ref, table_ref, own_ref, buf_ref, term_ref):
    levels, rows, lanes = thick_ref.shape

    def thick(k):
        return thick_ref[k]

    def wet(k):
        return wet_ref[k]

    for f in range(4):
        own_ref[f] = own_columns(lambda k, f=f: state_ref[f, k], levels, lanes, rows)
    own_ref[4] = own_columns(thick, levels, lanes, rows)
    own_ref[5] = own_columns(wet, levels, lanes, rows)
    row_terms(thick, wet, table_ref[0, :rows], levels, term_ref)
    row = lax.broadcasted_iota(jnp.int32, (rows, LANES), 0)
    face = jnp.where(row < rows - 1, table_ref[1, :rows], 0.0)
    for k in range(levels):
        term_ref[5, k], term_ref[6, k] = north_terms(thick(k), wet(k), face)
        for f in range(4):
            buf_ref[0, f, k] = state_ref[f, k]
    step_levels(buf_ref, term_ref, True)


def end_kernel(
    state_ref,
    thick_ref,
    wet_ref,
    got_ref,
    own_ref,
    closed_ref,
    table_ref,
    sums_ref,
    out_ref,
    send_ref,
    field_ref,
    halo_ref,
    buf_ref,
    term_ref,
    raw_ref,
    main_ref,
):
    levels, rows, lanes = thick_ref.shape
    full = rows + 8
    top = lax.axis_index("lat") == 0
    at_top = jnp.where(top, 1.0, 0.0)
    at_bottom = jnp.where(top, 0.0, 1.0)
    sub = lax.broadcasted_iota(jnp.int32, (8, LANES), 0)

    def own(f, k, part):
        return state_ref[f, k, part] if f < 4 else (thick_ref, wet_ref)[f - 4][k, part]

    for f in range(6):
        for k in range(levels):
            halo_ref[f, k, 0:2] = got_ref[f, k] * at_top
            halo_ref[f, k, 2:6] = jnp.zeros((4, lanes), jnp.float32)
            halo_ref[f, k, 6:8] = got_ref[f, k] * at_bottom
    for f in range(6):
        for k in range(levels):
            halo = halo_ref[f, k]
            beyond = jnp.where(sub < 6, roll(halo, 4, 0), 0.0)
            high = jnp.where(sub < 4, roll(own(f, k, slice(rows - 8, rows)), -4, 0), beyond)
            low = jnp.where(sub < 2, roll(halo, 2, 0), roll(own(f, k, slice(0, 8)), 2, 0))
            tile = jnp.where(top, high, low)
            if f < 4:
                buf_ref[0, f, k] = tile
            else:
                field_ref[f - 4, k] = tile

    def thick(k):
        return field_ref[0, k]

    def wet(k):
        return field_ref[1, k]

    row_terms(thick, wet, table_ref[0], levels, term_ref)
    for k in range(levels):
        term_ref[5, k], term_ref[6, k] = north_terms(thick(k), wet(k), table_ref[1])
    step_levels(buf_ref, term_ref, False)
    c = lane_of((full, LANES)) % GROUP

    def ring(f):
        beyond = own_columns(lambda k: halo_ref[f, k], levels, lanes, 8)
        return jnp.concatenate([own_ref[f], beyond], axis=0)

    for i in range(3):
        a, b = ring(2 * i), ring(2 * i + 1)
        one = jnp.where(c < 4, roll(a, -2, 1), roll(a, -4, 1))
        two = jnp.where(c < 12, roll(b, 6, 1), roll(b, 4, 1))
        both = jnp.where(c < 8, one, two)
        raw_ref[i, 0:2] = both[full - 2 : full]
        raw_ref[i, 2 : rows + 4] = both[: rows + 2]
        raw_ref[i, rows + 4 : full] = jnp.zeros((4, LANES), jnp.float32)
    main = 8 * levels
    few = main // PACKED
    last = rows // 8 - 1
    for t in range(rows // 8):
        part = slice(8 * t, 8 * t + 8)
        for k in range(levels):
            tiles = []
            for f in range(4):
                x = closed_ref[2, f, k, part]
                if t == last:
                    fixed = jnp.where(sub >= 6, roll(buf_ref[2, f, k], 4, 0), x)
                    x = jnp.where(top, fixed, x)
                if t == 0:
                    fixed = jnp.where(sub < 2, roll(buf_ref[2, f, k], -2, 0), x)
                    x = jnp.where(top, x, fixed)
                out_ref[f, k, part] = x
                tiles.append(x)

            def place(y, tile, t=t, k=k):
                at = main * (4 * t + y) + 8 * k
                main_ref[at : at + 8] = tile

            pairs_of_rows(tiles, t, place)
        for p in range(4 * t, 4 * t + 4):
            for i in range(3):
                send_ref[p, few + 8 * i : few + 8 * i + 8] = raw_ref[i, 2 * p : 2 * p + 8]
    x = jnp.concatenate(split(main_ref[...]), axis=1)
    x = product(x, jnp.concatenate([sums_ref[...]] * 2, axis=0), ((1,), (0,)))
    x = x + roll(x, SUMS, 1)
    for p in range(send_ref.shape[0]):
        send_ref[p, :few] = pack(x[main * p : main * (p + 1)])


def circle_kernel(
    circle_ref,
    table_ref,
    basis_ref,
    joint_basis_ref,
    count_ref,
    out_ref,
    tile_ref,
    term_ref,
    joint_ref,
):
    peers = circle_ref.shape[0]
    modes = basis_ref.shape[1] // 2
    length = basis_ref.shape[0]
    few = circle_ref.shape[1] - 24
    main = PACKED * few
    levels = main // 8
    lanes = LANES
    lane = lane_of((8, LANES))
    c = lane % GROUP
    for j in range(0, peers, 2):
        part = slice(4 * j, 4 * j + 8)
        for i in range(3):
            x, y, z = (
                circle_ref[(j + d) % peers, few + 8 * i : few + 8 * i + 8] for d in range(3)
            )
            for f, shift in ((2 * i, 0), (2 * i + 1, -8)):
                middle = jnp.where(c < 12, roll(y, 4 + shift, 1), roll(z, 12 + shift, 1))
                tile_ref[f, part] = jnp.where(c < 4, roll(x, shift - 4, 1), middle)
    inv_c, face = (jnp.concatenate([table_ref[i]] * (peers // 2), axis=0) for i in (0, 1))
    step_tile(tile_ref, tile_ref[4], tile_ref[5], levels, inv_c, face, term_ref)
    sub = lax.broadcasted_iota(jnp.int32, (8, LANES), 0) // 2
    right = (c % 8 >= 2) & (c % 8 < 6)
    for j in range(peers // 2):
        made = jnp.zeros((8, LANES), jnp.float32)
        for f in range(4):
            x = tile_ref[f, 8 * j : 8 * j + 8]
            made = jnp.where(sub == f, roll(x, 2 * f - 2, 0), made)
        joint_ref[8 * j : 8 * j + 8] = jnp.where(right, made, 0.0)
    lane_main = lane_of((main, LANES))
    row_main = lax.broadcasted_iota(jnp.int32, (main, LANES), 0)
    at_level = lane_main // GROUP == row_main // 8

    def block(o):
        return unpack(circle_ref[o, :few])

    def joint(j):
        x = joint_ref[8 * j : 8 * j + 8]
        return jnp.where(at_level, jnp.concatenate([x] * levels, axis=0), 0.0)

    total = jnp.zeros((2 * main, 2 * modes), jnp.float32)
    for source, basis, count in (
        (block, basis_ref, peers),
        (joint, joint_basis_ref, peers // 2),
    ):
        for o in range(0, count, 2):
            parts = zip(split(source(o)), split(source(o + 1)))
            x = jnp.concatenate([jnp.concatenate(p, axis=1) for p in parts], axis=0)
            total = total + product(x, basis[lanes * o : lanes * (o + 2)], ((1,), (0,)))
    total = total[:main] + total[main:]
    counts = count_ref[...]
    row = lax.broadcasted_iota(jnp.int32, counts.shape, 0)
    own = 2 * lax.axis_index("lon")
    even, odd = (
        jnp.sum(jnp.where(row == own + r, counts, 0.0), axis=0, keepdims=True) for r in (0, 1)
    )
    limit = jnp.where(row_main % 2 == 0, even, odd)
    order = (lane_main % (modes // 2)).astype(jnp.float32)
    weight = jnp.where(order < limit, jnp.where(order == 0.0, 1.0 / length, 2.0 / length), 0.0)
    total = (total[:, :modes] + total[:, modes:]) * weight
    y = jnp.concatenate([jnp.concatenate([p, p], axis=1) for p in split(total)], axis=0)
    for o in range(0, peers, 2):
        x = product(y, basis_ref[lanes * o : lanes * (o + 2)], ((1,), (1,)))
        x = x[:main] + x[main:]
        out_ref[o, :few] = pack(x[:, :lanes])
        out_ref[o + 1, :few] = pack(x[:, lanes:])
        before = (4 * o - 8) % (4 * peers)
        here = joint_ref[4 * o : 4 * o + 8]
        out_ref[o, few:] = jnp.where(
            c < 8, roll(joint_ref[before : before + 8], -8, 1), roll(here, 8, 1)
        )
        out_ref[o + 1, few:] = here


def join_kernel(
    state_ref, piece_ref, wet_ref, flag_ref, columns_ref, out_ref, made_ref, smooth_ref, sems
):
    levels, rows, lanes = wet_ref.shape
    main = 8 * levels
    few = main // PACKED
    lane = lane_of((8, LANES))
    x = jnp.concatenate(
        [unpack(piece_ref[p, :few]) for p in range(piece_ref.shape[0])], axis=0
    )
    x = jnp.concatenate(split(x), axis=1)
    x = product(x, jnp.concatenate([columns_ref[...]] * 2, axis=0), ((1,), (0,)))
    smooth_ref[...] = x[:, :lanes] + x[:, lanes:]
    edges = [{} for _ in range(rows // 8)]
    for t, into in enumerate(edges):
        tiles = [piece_ref[4 * t + x, few : few + 8] for x in range(4)]
        pairs_of_rows(tiles, t, into.__setitem__)
    copies = []
    for k in range(levels):
        for t in range(rows // 8):
            part = slice(8 * t, 8 * t + 8)
            starts = [main * (4 * t + x) + 8 * k for x in range(4)]
            tiles = [smooth_ref[at : at + 8] for at in starts]
            gate = flag_ref[part] * wet_ref[k, part]

            def place(f, smooth, k=k, gate=gate, part=part, edge=edges[t]):
                first = roll(edge[f], -(GROUP * k + 4), 1)
                last = roll(edge[f], lanes - 2 - (GROUP * k + 10), 1)
                state = jnp.where(
                    lane < 2, first, jnp.where(lane >= lanes - 2, last, state_ref[f, k, part])
                )
                made_ref[f, k, part] = state + gate * (smooth - state)

            pairs_of_rows(tiles, t, place)
        if k % 2:
            both = pl.ds(k - 1, 2)
            copies.append(
                pltpu.make_async_copy(
                    made_ref.at[:, both], out_ref.at[:, both], sems.at[k // 2]
                )
            )
            copies[-1].start()
    for copy in copies:
        copy.wait()


def filter_kernel(circle_ref, basis_ref, weight_ref, out_ref, piece_ref, sems):
    pieces, part, lanes = circle_ref.shape
    modes = weight_ref.shape[1]
    pairs = range(0, pieces, 2)
    total = jnp.zeros((2 * part, 2 * modes), jnp.float32)
    for o in pairs:
        parts = zip(split(circle_ref[o]), split(circle_ref[o + 1]))
        x = jnp.concatenate([jnp.concatenate(p, axis=1) for p in parts], axis=0)
        total = total + product(x, basis_ref[lanes * o : lanes * (o + 2)], ((1,), (0,)))
    total = total[:part] + total[part:]
    total = (total[:, :modes] + total[:, modes:]) * weight_ref[...]
    y = jnp.concatenate([jnp.concatenate([p, p], axis=1) for p in split(total)], axis=0)
    copies = []
    for o in pairs:
        x = product(y, basis_ref[lanes * o : lanes * (o + 2)], ((1,), (1,)))
        x = x[:part] + x[part:]
        piece_ref[o] = x[:, :lanes]
        piece_ref[o + 1] = x[:, lanes:]
        both = pl.ds(o, 2)
        copies.append(
            pltpu.make_async_copy(piece_ref.at[both], out_ref.at[both], sems.at[o // 2])
        )
        copies[-1].start()
    for copy in copies:
        copy.wait()


def blend_kernel(state_ref, smooth_ref, wet_ref, flag_ref, out_ref, piece_ref, sems):
    levels = wet_ref.shape[0]
    flag = flag_ref[...]
    copies = []
    for f in range(4):
        for k in range(levels):
            state = state_ref[f, k]
            gate = flag * wet_ref[k]
            piece_ref[f, k] = state + gate * (smooth_ref[f, k] - state)
        copies.append(pltpu.make_async_copy(piece_ref.at[f], out_ref.at[f], sems.at[f]))
        copies[-1].start()
    for copy in copies:
        copy.wait()


def call(kernel, outs, scratch=(), sems=0, raw=False, sent=False, flops=0):
    vmem = pl.BlockSpec(memory_space=pltpu.VMEM)
    away = pl.BlockSpec(memory_space=pl.ANY)
    specs = [vmem] * len(outs)
    shapes = [jax.ShapeDtypeStruct(s, jnp.float32) if isinstance(s, tuple) else s for s in outs]
    if sent:
        specs[-1] = away
        shapes[-1] = pltpu.HBM(outs[-1], jnp.float32)
    buffers = [pltpu.VMEM(s, jnp.float32) if isinstance(s, tuple) else s for s in scratch]
    if sems:
        buffers.append(pltpu.SemaphoreType.DMA((sems,)))
    cost = pl.CostEstimate(
        flops=flops,
        transcendentals=0,
        bytes_accessed=4 * sum(math.prod(s.shape) for s in shapes),
    )

    def run(*args):
        if raw:
            args = [pltpu.with_memory_space_constraint(x, pltpu.HBM) for x in args]
        return pl.pallas_call(
            kernel,
            out_shape=shapes,
            in_specs=[away if raw else vmem] * len(args),
            out_specs=specs,
            scratch_shapes=buffers,
            compiler_params=pltpu.CompilerParams(vmem_limit_bytes=24 << 20),
            cost_estimate=cost,
        )(*args)

    return run


def swap_edges(before_src, after_src, axis):
    peers = lax.axis_size(axis)
    up = [(i, (i + 1) % peers) for i in range(peers)]
    down = [(j, i) for i, j in up]
    return lax.ppermute(before_src, axis, up), lax.ppermute(after_src, axis, down)


def mode_basis(length, modes):
    turns = np.arange(modes)[None, :] * np.arange(length)[:, None] % length
    angle = turns * (2.0 * math.pi / length)
    basis = np.concatenate([np.cos(angle), np.sin(angle)], axis=1).astype(np.float32)
    high = basis.astype(ml_dtypes.bfloat16)
    low = (basis - high.astype(np.float32)).astype(ml_dtypes.bfloat16)
    return np.concatenate([high, low], axis=1)


def two_parts(x):
    x = x.astype(np.float32)
    high = x.astype(ml_dtypes.bfloat16)
    return np.concatenate([high, (x - high.astype(np.float32)).astype(ml_dtypes.bfloat16)], axis=1)


def on_grid(x):
    return np.round(x * 2.0**32) / 2.0**32


def sequences(length, lanes, modes):
    at = np.arange(lanes)
    band = 2.0 * math.pi * (modes - 0.5) / length
    along = ((lanes - 1 - 2.0 * at) / 2.0) ** 2 * math.cos(band)
    beside = at[1:] * (lanes - at[1:]) / 2.0
    matrix = np.diag(along) + np.diag(beside, 1) + np.diag(beside, -1)
    most = np.linalg.eigh(matrix)[1][:, ::-1][:, :SUMS]
    order = np.where(np.arange(SUMS)[None, :] % 2 == 0, 1.0, at[:, None] - (lanes - 1) / 2.0)
    return on_grid(most * np.sign((most * order).sum(axis=0))[None, :])


def block_coefficients(length, lanes, modes, columns):
    turns = np.arange(modes)[None, :] * np.arange(length)[:, None] % length
    angle = turns * (2.0 * math.pi / length)
    wave = np.concatenate([np.cos(angle), np.sin(angle)], axis=1).reshape(-1, lanes, 2 * modes)
    made = on_grid(np.einsum("in,oim->onm", columns, wave, optimize=False))
    rest = wave - np.einsum("in,onm->oim", columns, made, optimize=False)
    return made, np.abs(rest).max()


def joint_basis(basis, lanes):
    length = basis.shape[0]
    tile, lane = np.divmod(np.arange(length // 2), lanes)
    half, c = np.divmod(lane % GROUP, 8)
    column = (lanes * (2 * tile + half + 1) + c - 4) % length
    return np.where(((c >= 2) & (c < 6))[:, None], basis[column], np.zeros_like(basis[column]))


def mode_weights(counts, modes, length):
    order = jnp.arange(modes).astype(jnp.float32)
    keep = (order[None, :] < counts[:, None]).astype(jnp.float32)
    scale = jnp.where(order == 0, 1.0, 2.0) / length
    weights = keep * scale[None, :]
    return jnp.concatenate([weights, weights], axis=1)


def shards(ocean_state, thickness, wet_mask, mode_counts, row_flags):
    levels, rows, lanes = ocean_state.shape[1:]
    assert rows % 8 == 0 and lanes == LANES and levels * GROUP <= LANES
    lon_peers = lax.axis_size("lon")
    lat_peers = lax.axis_size("lat")
    nlat = rows * lat_peers
    nlon = lanes * lon_peers
    full = rows + 8
    total = 4 * levels * rows
    part = total // lon_peers
    lat_pos = lax.axis_index("lat")
    first_row = lat_pos * rows
    cells = 4 * levels * full * lanes
    edge_rows = (6, levels, 2, lanes)

    paired = rows == 2 * lon_peers and rows >= FBAND and lat_peers % 2 == 0 and levels % 2 == 0
    columns = sequences(nlon, lanes, MAXM)
    if paired:
        coefficients, rest = block_coefficients(nlon, lanes, MAXM, columns)
        paired = bool(rest < 1e-8)
    inside = (np.arange(lanes) >= 2) & (np.arange(lanes) < lanes - 2)
    sums = jnp.asarray(np.tile(two_parts(columns * inside[:, None]), (1, PACKED // 2)))
    *block, first, last, flags, counts, table, end_table, joint_table, to_sums = call(
        functools.partial(load_kernel, paired),
        [ocean_state.shape, thickness.shape, thickness.shape, edge_rows, edge_rows]
        + [(rows, lanes)] * 2
        + [(2, full, lanes), (2, 8, lanes), (2, 8, lanes)]
        + [jax.ShapeDtypeStruct(sums.shape, sums.dtype)],
        [pltpu.VMEM(shape, jnp.int32) for shape in (thickness.shape, (1, rows), (1, rows))],
        sems=9,
        raw=True,
    )(ocean_state, thickness, wet_mask, row_flags[None], mode_counts[None], sums)

    def ready():
        return call(
            ready_kernel, [(6, rows, LANES), (5, levels, rows, lanes)], flops=20 * cells
        )(*block, table)

    def exchanged(below, above, own, terms):
        inner, edges, halo = call(
            inner_kernel,
            [(3, 4, levels, full, lanes), (6, full, LANES), (6, levels, 8, lanes)],
            [(5, levels, 8, lanes), (2, levels, full, lanes)],
            flops=60 * cells,
        )(*block, below, above, table, own, terms)
        first, last = call(pack_kernel, [(full, LANES)] * 2)(*block, halo)
        from_west, from_east = swap_edges(last, first, "lon")
        return call(
            edge_kernel,
            [ocean_state.shape] * 2,
            [(4, full, LANES), (7, full, LANES)],
            sems=4,
            sent=True,
        )(inner, edges, from_west, from_east, table)

    banded = (first_row < FBAND) | (first_row + rows > nlat - FBAND)
    modes = mode_basis(nlon, MAXM)
    tables = [modes]
    if paired:
        coefficients = np.concatenate([coefficients] * PACKED, axis=1).reshape(nlon, 2 * MAXM)
        tables = [
            two_parts(coefficients),
            joint_basis(modes, lanes),
            two_parts(np.concatenate([columns.T] * PACKED, axis=0)),
        ]
    tables = lax.optimization_barrier([jnp.asarray(table) for table in tables])
    lon_pos = lax.axis_index("lon")

    def circled(got, own, closed):
        few = 8 * levels // PACKED
        tile = (levels, 8, lanes)
        to_modes, at_joints, to_columns = tables
        state, sent = call(
            end_kernel,
            [ocean_state.shape, (lon_peers, few + 24, lanes)],
            [(2,) + tile, (6,) + tile, (3, 4) + tile, (7,) + tile, (3, full, lanes)]
            + [(total, lanes)],
        )(*block, got, own, closed, end_table, to_sums)
        circles = lax.all_to_all(sent, "lon", 0, 0, tiled=True)
        pieces = call(
            circle_kernel,
            [(lon_peers, few + 8, lanes)],
            [
                (6, 4 * lon_peers, lanes),
                (7, 4 * lon_peers, lanes),
                (4 * lon_peers, lanes),
            ],
        )(circles, joint_table, to_modes, at_joints, counts)[0]
        pieces = lax.all_to_all(pieces, "lon", 0, 0, tiled=True)
        return call(
            join_kernel,
            [ocean_state.shape],
            [ocean_state.shape, (total, lanes)],
            sems=levels // 2,
            sent=True,
        )(state, pieces, block[2], flags, to_columns)[0]

    def between(got, *_):
        pairs = [(i, i + 1) for i in range(1, lat_peers - 1, 2)]
        other = lax.ppermute(last, "lat", pairs + [(j, i) for i, j in pairs])
        even = lat_pos % 2 == 0
        below, above = jnp.where(even, other, got), jnp.where(even, got, other)
        return exchanged(below, above, *ready())[1]

    if paired:
        got = lax.ppermute(first, "lat", [(i, i ^ 1) for i in range(lat_peers)])
        own, closed = call(
            closed_kernel,
            [(6, rows, LANES), (3, 4, levels, rows, lanes)],
            [(7, levels, rows, lanes)],
            flops=60 * cells,
        )(*block, table)
        got, own, closed = lax.optimization_barrier((got, own, closed))
        return lax.cond(banded, circled, between, got, own, closed)

    below, above = swap_edges(last, first, "lat")
    state, sent = exchanged(*lax.optimization_barrier((below, above, *ready())))

    def filtered():
        row_counts = lax.dynamic_slice(
            jnp.broadcast_to(
                mode_counts.astype(jnp.float32)[None], (4 * levels, rows)
            ).reshape(total),
            (lon_pos * part,),
            (part,),
        )
        circles = lax.all_to_all(
            sent.reshape(lon_peers, part, lanes), "lon", 0, 0, tiled=True
        )
        smooth = call(
            filter_kernel, [circles.shape], [circles.shape], sems=lon_peers // 2, sent=True
        )(circles, tables[0], mode_weights(row_counts, MAXM, nlon))[0]
        smooth = lax.all_to_all(smooth, "lon", 0, 0, tiled=True).reshape(state.shape)
        return call(blend_kernel, [state.shape], [state.shape], sems=4, sent=True)(
            state, smooth, block[2], flags
        )[0]

    return lax.cond(banded, filtered, lambda: sent)


def solution(mesh):
    in_specs = (
        P(None, None, "lat", "lon"),
        P(None, "lat", "lon"),
        P(None, "lat", "lon"),
        P("lat"),
        P("lat"),
    )
    out_specs = P(None, None, "lat", "lon")
    return jax.shard_map(shards, mesh=mesh, in_specs=in_specs, out_specs=out_specs, check_vma=False)
```

```python
import functools
import math

import jax
import jax.numpy as jnp
import ml_dtypes
import numpy as np
from jax import lax
from jax.experimental import pallas as pl
from jax.experimental.pallas import tpu as pltpu
from jax.sharding import PartitionSpec as P

FBAND = 16
MAXM = 64
LANES = 128
SUMS = 32
PACKED = LANES // SUMS
GROUP = 16


lat_edge = 1.3
diffusion = 0.05
vertical_mix = 0.5
time_step = 0.05


def roll(x, shift, axis):
    shift %= x.shape[axis]
    return pltpu.roll(x, shift, axis) if shift else x


def east(x):
    return roll(x, -1, 1)


def west(x):
    return roll(x, 1, 1)


def north(x):
    return roll(x, -1, 0)


def south(x):
    return roll(x, 1, 0)


def lane_of(shape):
    return lax.broadcasted_iota(jnp.int32, shape, 1)


def east_terms(h, w, inv_c):
    open_e = 0.5 * (h + east(h)) * (w * east(w))
    return 0.25 * open_e, diffusion * open_e * inv_c


def north_terms(h, w, face):
    open_n = 0.5 * (h + north(h)) * (w * north(w)) * face
    return 0.25 * open_n, diffusion * open_n


def advance(fields, terms, scale, scale_c, vertical):
    quarter_e, spread_e, quarter_n, spread_n = terms
    u, v = fields[2], fields[3]
    speed_e = quarter_e * (u + east(u))
    speed_n = quarter_n * (v + north(v))
    here_e, there_e = speed_e + spread_e, speed_e - spread_e
    here_n, there_n = speed_n + spread_n, speed_n - spread_n
    fresh = []
    for q, vert in zip(fields, vertical):
        flux_e = here_e * q + there_e * east(q)
        flux_n = here_n * q + there_n * north(q)
        spread = (flux_e - west(flux_e)) + (flux_n - south(flux_n))
        fresh.append(q + scale * vert - scale_c * spread)
    return fresh


def own_columns(load, levels, lanes, rows):
    lane = lane_of((rows, LANES))
    own = jnp.zeros((rows, LANES), jnp.float32)
    for k in range(levels):
        x = load(k)
        at = GROUP * k + 2
        own = jnp.where((lane >= at) & (lane < at + 4), roll(x, at, 1), own)
        at = GROUP * k + 8
        own = jnp.where((lane >= at) & (lane < at + 4), roll(x, at + 4 - lanes, 1), own)
    return own


def row_terms(thick, wet, inv_c, levels, term_ref):
    w, h = wet(0), thick(0)
    hs = jnp.where(w > 0, h, 1.0)
    for k in range(levels):
        term_ref[0, k], term_ref[1, k] = east_terms(h, w, inv_c)
        scale = time_step * w / hs
        term_ref[2, k] = scale
        term_ref[3, k] = scale * inv_c
        if k + 1 < levels:
            w_next, h_next = wet(k + 1), thick(k + 1)
            hs_next = jnp.where(w_next > 0, h_next, 1.0)
            term_ref[4, k] = w * w_next * vertical_mix / (0.5 * (hs + hs_next))
            w, h, hs = w_next, h_next, hs_next


def fill_table(ref, place, nlat):
    place = place.astype(jnp.float32)
    ref[0] = 1.0 / jnp.cos(lat_edge * (2.0 * (place + 0.5) / nlat - 1.0))
    ref[1] = jnp.cos(lat_edge * (2.0 * (place + 1.0) / nlat - 1.0))


def ring_rows(rows):
    place = lax.broadcasted_iota(jnp.int32, (rows + 8, LANES), 0)
    return jnp.where(place < rows + 2, place, jnp.where(place < rows + 6, 0, place - rows - 8))


def load_kernel(
    paired,
    state_any,
    thick_any,
    wet_any,
    flag_any,
    count_any,
    sums_any,
    state_ref,
    thick_ref,
    wet_ref,
    first_ref,
    last_ref,
    flag_ref,
    count_ref,
    table_ref,
    end_table_ref,
    joint_table_ref,
    sums_ref,
    raw_ref,
    raw_flag_ref,
    raw_count_ref,
    sems,
):
    levels, rows = thick_ref.shape[:2]
    moves = [(flag_any, raw_flag_ref), (count_any, raw_count_ref), (wet_any, raw_ref)]
    moves += [(thick_any, thick_ref), (sums_any, sums_ref)]
    moves += [(state_any.at[f], state_ref.at[f]) for f in range(4)]
    copies = [pltpu.make_async_copy(*pair, sems.at[i]) for i, pair in enumerate(moves)]
    for copy in copies:
        copy.start()
    nlat = rows * lax.axis_size("lat")
    lat_pos = lax.axis_index("lat")
    first_row = lat_pos * rows
    fill_table(table_ref, first_row + ring_rows(rows), nlat)
    if paired:
        six = jnp.minimum(lax.broadcasted_iota(jnp.int32, (8, LANES), 0), 5)
        end = jnp.where(lat_pos == 0, rows - 4, -2)
        fill_table(end_table_ref, first_row + end + six, nlat)
        fill_table(joint_table_ref, first_row + 2 * lax.axis_index("lon") - 2 + six, nlat)
    for copy in copies[:3]:
        copy.wait()
    shape = (rows, rows)
    diagonal = lax.broadcasted_iota(jnp.int32, shape, 0) == lane_of(shape)
    for raw, ref in ((raw_flag_ref, flag_ref), (raw_count_ref, count_ref)):
        spread = jnp.broadcast_to(raw[...].astype(jnp.float32), shape)
        value = jnp.sum(jnp.where(diagonal, spread, 0.0), axis=1, keepdims=True)
        ref[...] = jnp.broadcast_to(value, (rows, LANES))
    for k in range(levels):
        wet_ref[k] = raw_ref[k].astype(jnp.float32)
    even = lax.axis_index("lat") % 2 == 0
    copies[3].wait()
    copies[4].wait()
    for f in (4, 5, 0, 1, 2, 3):
        if f < 4:
            copies[5 + f].wait()
        for k in range(levels):
            x = state_ref.at[f, k] if f < 4 else (thick_ref, wet_ref)[f - 4].at[k]
            low, high = x[0:2], x[rows - 2 : rows]
            if paired:
                low, high = jnp.where(even, high, low), jnp.where(even, low, high)
            first_ref[f, k] = low
            last_ref[f, k] = high


def ready_kernel(state_ref, thick_ref, wet_ref, table_ref, own_ref, term_ref):
    levels, rows, lanes = thick_ref.shape

    def thick(k):
        return thick_ref[k]

    def wet(k):
        return wet_ref[k]

    for f in range(4):
        own_ref[f] = own_columns(lambda k, f=f: state_ref[f, k], levels, lanes, rows)
    own_ref[4] = own_columns(thick, levels, lanes, rows)
    own_ref[5] = own_columns(wet, levels, lanes, rows)
    row_terms(thick, wet, table_ref[0, :rows], levels, term_ref)


def pack_kernel(state_ref, thick_ref, wet_ref, halo_ref, first_ref, last_ref):
    levels, rows, lanes = thick_ref.shape
    lane = lane_of((8, LANES))
    for t in range(rows // 8 + 1):
        first = jnp.zeros((8, LANES), jnp.float32)
        last = jnp.zeros((8, LANES), jnp.float32)
        part = slice(8 * t, 8 * t + 8)
        for f in range(6):
            for k in range(levels):
                if t == rows // 8:
                    x = halo_ref[f, k]
                elif f < 4:
                    x = state_ref[f, k, part]
                elif f == 4:
                    x = thick_ref[k, part]
                else:
                    x = wet_ref[k, part]
                at = GROUP * f + 2 * k
                mine = (lane >= at) & (lane < at + 2)
                first = jnp.where(mine, roll(x, at, 1), first)
                last = jnp.where(mine, roll(x, at + 2 - lanes, 1), last)
        first_ref[part] = first
        last_ref[part] = last


def inner_kernel(
    state_ref,
    thick_ref,
    wet_ref,
    below_ref,
    above_ref,
    table_ref,
    own_ref,
    term_ref,
    out_ref,
    edge_ref,
    halo_ref,
    halo_term_ref,
    north_ref,
):
    levels, rows, lanes = thick_ref.shape
    full = rows + 8
    face = table_ref[1]
    lat_pos = lax.axis_index("lat")
    with_below = jnp.where(lat_pos > 0, 1.0, 0.0)
    with_above = jnp.where(lat_pos < lax.axis_size("lat") - 1, 1.0, 0.0)
    for f in range(6):
        for k in range(levels):
            halo_ref[f, k, 0:2] = above_ref[f, k] * with_above
            halo_ref[f, k, 2:6] = jnp.zeros((4, lanes), jnp.float32)
            halo_ref[f, k, 6:8] = below_ref[f, k] * with_below

    def joined(x, y):
        return jnp.concatenate([x, y], axis=0)

    def halo(f):
        return lambda k: halo_ref[f, k]

    for f in range(6):
        edge_ref[f, :rows] = own_ref[f]
        edge_ref[f, rows:] = own_columns(halo(f), levels, lanes, 8)
    row_terms(halo(4), halo(5), table_ref[0, rows:], levels, halo_term_ref)
    for k in range(levels):
        h = joined(thick_ref[k], halo_ref[4, k])
        w = joined(wet_ref[k], halo_ref[5, k])
        north_ref[0, k], north_ref[1, k] = north_terms(h, w, face)
        for f in range(4):
            out_ref[0, f, k] = joined(state_ref[f, k], halo_ref[f, k])

    def term(i, k):
        return joined(term_ref[i, k], halo_term_ref[i, k])

    def step(i, _):
        source, target = out_ref.at[i], out_ref.at[i + 1]
        fields = [source[f, 0] for f in range(4)]
        above = [jnp.zeros((full, LANES), jnp.float32)] * 4
        for k in range(levels):
            deeper = below = above
            if k + 1 < levels:
                couple = term(4, k)
                deeper = [source[f, k + 1] for f in range(4)]
                below = [couple * (d - q) for d, q in zip(deeper, fields)]
                vertical = [b - a for b, a in zip(below, above)]
            else:
                vertical = [-a for a in above]
            terms = term(0, k), term(1, k), north_ref[0, k], north_ref[1, k]
            fresh = advance(fields, terms, term(2, k), term(3, k), vertical)
            for f in range(4):
                target[f, k] = fresh[f]
            fields, above = deeper, below
        return 0

    lax.fori_loop(0, 2, step, 0)


def step_tile(tile_ref, h, w, levels, inv_c, face, term_ref):
    lane = lane_of(h.shape)

    def deeper(x):
        return roll(x, -GROUP, 1)

    def shallower(x):
        return roll(x, GROUP, 1)

    hs = jnp.where(w > 0, h, 1.0)
    scale = time_step * w / hs
    couple = w * deeper(w) * vertical_mix / (0.5 * (hs + deeper(hs)))
    couple = jnp.where(lane < GROUP * (levels - 1), couple, 0.0)
    terms = east_terms(h, w, inv_c) + north_terms(h, w, face)
    for i, term in enumerate(terms + (scale, scale * inv_c, couple)):
        term_ref[i] = term

    def step():
        terms = [term_ref[i] for i in range(7)]
        fields = [tile_ref[f] for f in range(4)]
        vertical = []
        for q in fields:
            down = terms[6] * (deeper(q) - q)
            vertical.append(down - shallower(down))
        for f, q in enumerate(advance(fields, terms[:4], terms[4], terms[5], vertical)):
            tile_ref[f] = q

    step()
    step()


def edge_kernel(
    inner_ref, own_ref, west_ref, east_ref, table_ref, out_ref, send_ref, tile_ref, term_ref, sems
):
    levels, rows, lanes = out_ref.shape[1:]
    full = rows + 8
    lane = lane_of((full, LANES))
    from_west, from_east = west_ref[...], east_ref[...]

    def joined(f):
        x = own_ref[f]
        for k in range(levels):
            src = GROUP * f + 2 * k
            at = GROUP * k
            x = jnp.where((lane >= at) & (lane < at + 2), roll(from_west, at - src, 1), x)
            at = GROUP * k + 12
            x = jnp.where((lane >= at) & (lane < at + 2), roll(from_east, at - src, 1), x)
        return x

    for f in range(4):
        tile_ref[f] = joined(f)
    step_tile(tile_ref, joined(4), joined(5), levels, table_ref[0], table_ref[1], term_ref)
    lane = lane_of((rows, LANES))
    for f in range(4):
        x = tile_ref[f, :rows]
        for k in range(levels):
            left = roll(x, -(GROUP * k + 2), 1)
            right = roll(x, lanes - 2 - (GROUP * k + 10), 1)
            out_ref[f, k] = jnp.where(
                lane < 2,
                left,
                jnp.where(lane >= lanes - 2, right, inner_ref[2, f, k, :rows]),
            )
        pltpu.make_async_copy(out_ref.at[f], send_ref.at[f], sems.at[f]).start()
    for f in range(4):
        pltpu.make_async_copy(out_ref.at[f], send_ref.at[f], sems.at[f]).wait()


def split(x):
    high = x.astype(jnp.bfloat16)
    return high, (x - high.astype(jnp.float32)).astype(jnp.bfloat16)


def product(a, b, dims):
    return lax.dot_general(a, b, (dims, ((), ())), preferred_element_type=jnp.float32)


def unpack(x):
    part = lane_of(x.shape) // SUMS
    return jnp.concatenate([jnp.where(part == g, x, 0.0) for g in range(PACKED)], axis=0)


def pack(x):
    size = x.shape[0] // PACKED
    made = x[:size]
    part = lane_of(made.shape) // SUMS
    for g in range(1, PACKED):
        made = jnp.where(part == g, x[size * g : size * (g + 1)], made)
    return made


def pairs_of_rows(tiles, t, place):
    sub = lax.broadcasted_iota(jnp.int32, tiles[0].shape, 0) // 2
    for y in range(4):
        made = roll(tiles[0], -2 * y, 0)
        for x in range(1, 4):
            made = jnp.where(sub == x, roll(tiles[x], 2 * (x - y), 0), made)
        place(y, made)


def side_by_side(a, b):
    c = lane_of(a.shape) % GROUP
    one = jnp.where(c < 4, roll(a, -2, 1), roll(a, -4, 1))
    two = jnp.where(c < 12, roll(b, 6, 1), roll(b, 4, 1))
    return jnp.where(c < 8, one, two)


def step_levels(buf_ref, term_ref, loop):
    levels, size = buf_ref.shape[2:4]

    def step(i, _):
        source, target = buf_ref.at[i], buf_ref.at[i + 1]
        fields = [source[f, 0] for f in range(4)]
        above = [jnp.zeros((size, LANES), jnp.float32)] * 4
        for k in range(levels):
            deeper = below = above
            if k + 1 < levels:
                couple = term_ref[4, k]
                deeper = [source[f, k + 1] for f in range(4)]
                below = [couple * (d - q) for d, q in zip(deeper, fields)]
                vertical = [b - a for b, a in zip(below, above)]
            else:
                vertical = [-a for a in above]
            terms = [term_ref[i, k] for i in (0, 1, 5, 6)]
            fresh = advance(fields, terms, term_ref[2, k], term_ref[3, k], vertical)
            for f in range(4):
                target[f, k] = fresh[f]
            fields, above = deeper, below
        return 0

    if loop:
        lax.fori_loop(0, 2, step, 0)
    else:
        step(1, step(0, 0))


def closed_kernel(state_ref, thick_ref, wet_ref, table_ref, own_ref, buf_ref, term_ref):
    levels, rows, lanes = thick_ref.shape

    def thick(k):
        return thick_ref[k]

    def wet(k):
        return wet_ref[k]

    tiles = [
        own_columns(lambda k, f=f: state_ref[f, k], levels, lanes, rows) for f in range(4)
    ]
    tiles += [own_columns(load, levels, lanes, rows) for load in (thick, wet)]
    for i in range(3):
        own_ref[i] = side_by_side(tiles[2 * i], tiles[2 * i + 1])
    row_terms(thick, wet, table_ref[0, :rows], levels, term_ref)
    row = lax.broadcasted_iota(jnp.int32, (rows, LANES), 0)
    face = jnp.where(row < rows - 1, table_ref[1, :rows], 0.0)
    for k in range(levels):
        term_ref[5, k], term_ref[6, k] = north_terms(thick(k), wet(k), face)
        for f in range(4):
            buf_ref[0, f, k] = state_ref[f, k]
    step_levels(buf_ref, term_ref, True)


def end_kernel(
    state_ref,
    thick_ref,
    wet_ref,
    got_ref,
    own_ref,
    closed_ref,
    table_ref,
    sums_ref,
    out_ref,
    send_ref,
    field_ref,
    halo_ref,
    buf_ref,
    term_ref,
    raw_ref,
    main_ref,
):
    levels, rows, lanes = thick_ref.shape
    full = rows + 8
    top = lax.axis_index("lat") == 0
    at_top = jnp.where(top, 1.0, 0.0)
    at_bottom = jnp.where(top, 0.0, 1.0)
    sub = lax.broadcasted_iota(jnp.int32, (8, LANES), 0)

    def own(f, k, part):
        return state_ref[f, k, part] if f < 4 else (thick_ref, wet_ref)[f - 4][k, part]

    for f in range(6):
        for k in range(levels):
            halo_ref[f, k, 0:2] = got_ref[f, k] * at_top
            halo_ref[f, k, 2:6] = jnp.zeros((4, lanes), jnp.float32)
            halo_ref[f, k, 6:8] = got_ref[f, k] * at_bottom
    for f in range(6):
        for k in range(levels):
            halo = halo_ref[f, k]
            past = jnp.where(sub < 6, roll(halo, 4, 0), 0.0)
            high = jnp.where(sub < 4, roll(own(f, k, slice(rows - 8, rows)), -4, 0), past)
            low = jnp.where(sub < 2, roll(halo, 2, 0), roll(own(f, k, slice(0, 8)), 2, 0))
            tile = jnp.where(top, high, low)
            if f < 4:
                buf_ref[0, f, k] = tile
            else:
                field_ref[f - 4, k] = tile

    def thick(k):
        return field_ref[0, k]

    def wet(k):
        return field_ref[1, k]

    row_terms(thick, wet, table_ref[0], levels, term_ref)
    for k in range(levels):
        term_ref[5, k], term_ref[6, k] = north_terms(thick(k), wet(k), table_ref[1])
    step_levels(buf_ref, term_ref, False)

    def beyond(f):
        return own_columns(lambda k: halo_ref[f, k], levels, lanes, 8)

    for i in range(3):
        outer = side_by_side(beyond(2 * i), beyond(2 * i + 1))
        raw_ref[i, 0:2] = outer[6:8]
        raw_ref[i, 2 : rows + 2] = own_ref[i]
        raw_ref[i, rows + 2 : full] = outer[0:6]
    main = 8 * levels
    few = main // PACKED
    last = rows // 8 - 1
    for t in range(rows // 8):
        part = slice(8 * t, 8 * t + 8)
        for k in range(levels):
            tiles = []
            for f in range(4):
                x = closed_ref[2, f, k, part]
                if t == last:
                    fixed = jnp.where(sub >= 6, roll(buf_ref[2, f, k], 4, 0), x)
                    x = jnp.where(top, fixed, x)
                if t == 0:
                    fixed = jnp.where(sub < 2, roll(buf_ref[2, f, k], -2, 0), x)
                    x = jnp.where(top, x, fixed)
                out_ref[f, k, part] = x
                tiles.append(x)

            def place(y, tile, t=t, k=k):
                at = main * (4 * t + y) + 8 * k
                main_ref[at : at + 8] = tile

            pairs_of_rows(tiles, t, place)
        for p in range(4 * t, 4 * t + 4):
            for i in range(3):
                send_ref[p, few + 8 * i : few + 8 * i + 8] = raw_ref[i, 2 * p : 2 * p + 8]
    x = jnp.concatenate(split(main_ref[...]), axis=1)
    x = product(x, jnp.concatenate([sums_ref[...]] * 2, axis=0), ((1,), (0,)))
    x = x + roll(x, SUMS, 1)
    for p in range(send_ref.shape[0]):
        send_ref[p, :few] = pack(x[main * p : main * (p + 1)])


def circle_kernel(
    circle_ref,
    table_ref,
    basis_ref,
    joint_basis_ref,
    count_ref,
    out_ref,
    tile_ref,
    term_ref,
    joint_ref,
):
    peers = circle_ref.shape[0]
    modes = basis_ref.shape[1] // 2
    length = basis_ref.shape[0]
    few = circle_ref.shape[1] - 24
    main = PACKED * few
    levels = main // 8
    lanes = LANES
    lane = lane_of((8, LANES))
    c = lane % GROUP
    for j in range(0, peers, 2):
        part = slice(4 * j, 4 * j + 8)
        for i in range(3):
            x, y, z = (
                circle_ref[(j + d) % peers, few + 8 * i : few + 8 * i + 8] for d in range(3)
            )
            for f, shift in ((2 * i, 0), (2 * i + 1, -8)):
                middle = jnp.where(c < 12, roll(y, 4 + shift, 1), roll(z, 12 + shift, 1))
                tile_ref[f, part] = jnp.where(c < 4, roll(x, shift - 4, 1), middle)
    inv_c, face = (jnp.concatenate([table_ref[i]] * (peers // 2), axis=0) for i in (0, 1))
    step_tile(tile_ref, tile_ref[4], tile_ref[5], levels, inv_c, face, term_ref)
    sub = lax.broadcasted_iota(jnp.int32, (8, LANES), 0) // 2
    right = (c % 8 >= 2) & (c % 8 < 6)
    for j in range(peers // 2):
        made = jnp.zeros((8, LANES), jnp.float32)
        for f in range(4):
            x = tile_ref[f, 8 * j : 8 * j + 8]
            made = jnp.where(sub == f, roll(x, 2 * f - 2, 0), made)
        joint_ref[8 * j : 8 * j + 8] = jnp.where(right, made, 0.0)
    lane_main = lane_of((main, LANES))
    row_main = lax.broadcasted_iota(jnp.int32, (main, LANES), 0)
    at_level = lane_main // GROUP == row_main // 8

    def block(o):
        return unpack(circle_ref[o, :few])

    def joint(j):
        x = joint_ref[8 * j : 8 * j + 8]
        return jnp.where(at_level, jnp.concatenate([x] * levels, axis=0), 0.0)

    total = jnp.zeros((2 * main, 2 * modes), jnp.float32)
    for source, basis, count in (
        (block, basis_ref, peers),
        (joint, joint_basis_ref, peers // 2),
    ):
        for o in range(0, count, 2):
            parts = zip(split(source(o)), split(source(o + 1)))
            x = jnp.concatenate([jnp.concatenate(p, axis=1) for p in parts], axis=0)
            total = total + product(x, basis[lanes * o : lanes * (o + 2)], ((1,), (0,)))
    total = total[:main] + total[main:]
    counts = count_ref[...]
    row = lax.broadcasted_iota(jnp.int32, counts.shape, 0)
    own = 2 * lax.axis_index("lon")
    even, odd = (
        jnp.sum(jnp.where(row == own + r, counts, 0.0), axis=0, keepdims=True) for r in (0, 1)
    )
    limit = jnp.where(row_main % 2 == 0, even, odd)
    order = (lane_main % (modes // 2)).astype(jnp.float32)
    weight = jnp.where(order < limit, jnp.where(order == 0.0, 1.0 / length, 2.0 / length), 0.0)
    total = (total[:, :modes] + total[:, modes:]) * weight
    y = jnp.concatenate([jnp.concatenate([p, p], axis=1) for p in split(total)], axis=0)
    for o in range(0, peers, 2):
        x = product(y, basis_ref[lanes * o : lanes * (o + 2)], ((1,), (1,)))
        x = x[:main] + x[main:]
        out_ref[o, :few] = pack(x[:, :lanes])
        out_ref[o + 1, :few] = pack(x[:, lanes:])
        before = (4 * o - 8) % (4 * peers)
        here = joint_ref[4 * o : 4 * o + 8]
        out_ref[o, few:] = jnp.where(
            c < 8, roll(joint_ref[before : before + 8], -8, 1), roll(here, 8, 1)
        )
        out_ref[o + 1, few:] = here


def join_kernel(
    state_ref, piece_ref, wet_ref, flag_ref, columns_ref, out_ref, made_ref, smooth_ref, sems
):
    levels, rows, lanes = wet_ref.shape
    main = 8 * levels
    few = main // PACKED
    lane = lane_of((8, LANES))
    x = jnp.concatenate(
        [unpack(piece_ref[p, :few]) for p in range(piece_ref.shape[0])], axis=0
    )
    x = jnp.concatenate(split(x), axis=1)
    x = product(x, jnp.concatenate([columns_ref[...]] * 2, axis=0), ((1,), (0,)))
    smooth_ref[...] = x[:, :lanes] + x[:, lanes:]
    edges = [{} for _ in range(rows // 8)]
    for t, into in enumerate(edges):
        tiles = [piece_ref[4 * t + x, few : few + 8] for x in range(4)]
        pairs_of_rows(tiles, t, into.__setitem__)
    copies = []
    for k in range(levels):
        for t in range(rows // 8):
            part = slice(8 * t, 8 * t + 8)
            starts = [main * (4 * t + x) + 8 * k for x in range(4)]
            tiles = [smooth_ref[at : at + 8] for at in starts]
            gate = flag_ref[part] * wet_ref[k, part]

            def place(f, smooth, k=k, gate=gate, part=part, edge=edges[t]):
                first = roll(edge[f], -(GROUP * k + 4), 1)
                last = roll(edge[f], lanes - 2 - (GROUP * k + 10), 1)
                state = jnp.where(
                    lane < 2, first, jnp.where(lane >= lanes - 2, last, state_ref[f, k, part])
                )
                made_ref[f, k, part] = state + gate * (smooth - state)

            pairs_of_rows(tiles, t, place)
        if k % 2:
            both = pl.ds(k - 1, 2)
            copies.append(
                pltpu.make_async_copy(
                    made_ref.at[:, both], out_ref.at[:, both], sems.at[k // 2]
                )
            )
            copies[-1].start()
    for copy in copies:
        copy.wait()


def filter_kernel(circle_ref, basis_ref, weight_ref, out_ref, piece_ref, sems):
    pieces, part, lanes = circle_ref.shape
    modes = weight_ref.shape[1]
    pairs = range(0, pieces, 2)
    total = jnp.zeros((2 * part, 2 * modes), jnp.float32)
    for o in pairs:
        parts = zip(split(circle_ref[o]), split(circle_ref[o + 1]))
        x = jnp.concatenate([jnp.concatenate(p, axis=1) for p in parts], axis=0)
        total = total + product(x, basis_ref[lanes * o : lanes * (o + 2)], ((1,), (0,)))
    total = total[:part] + total[part:]
    total = (total[:, :modes] + total[:, modes:]) * weight_ref[...]
    y = jnp.concatenate([jnp.concatenate([p, p], axis=1) for p in split(total)], axis=0)
    copies = []
    for o in pairs:
        x = product(y, basis_ref[lanes * o : lanes * (o + 2)], ((1,), (1,)))
        x = x[:part] + x[part:]
        piece_ref[o] = x[:, :lanes]
        piece_ref[o + 1] = x[:, lanes:]
        both = pl.ds(o, 2)
        copies.append(
            pltpu.make_async_copy(piece_ref.at[both], out_ref.at[both], sems.at[o // 2])
        )
        copies[-1].start()
    for copy in copies:
        copy.wait()


def blend_kernel(state_ref, smooth_ref, wet_ref, flag_ref, out_ref, piece_ref, sems):
    levels = wet_ref.shape[0]
    flag = flag_ref[...]
    copies = []
    for f in range(4):
        for k in range(levels):
            state = state_ref[f, k]
            gate = flag * wet_ref[k]
            piece_ref[f, k] = state + gate * (smooth_ref[f, k] - state)
        copies.append(pltpu.make_async_copy(piece_ref.at[f], out_ref.at[f], sems.at[f]))
        copies[-1].start()
    for copy in copies:
        copy.wait()


def call(kernel, outs, scratch=(), sems=0, raw=False, sent=False, flops=0):
    vmem = pl.BlockSpec(memory_space=pltpu.VMEM)
    away = pl.BlockSpec(memory_space=pl.ANY)
    specs = [vmem] * len(outs)
    shapes = [jax.ShapeDtypeStruct(s, jnp.float32) if isinstance(s, tuple) else s for s in outs]
    if sent:
        specs[-1] = away
        shapes[-1] = pltpu.HBM(outs[-1], jnp.float32)
    buffers = [pltpu.VMEM(s, jnp.float32) if isinstance(s, tuple) else s for s in scratch]
    if sems:
        buffers.append(pltpu.SemaphoreType.DMA((sems,)))
    cost = pl.CostEstimate(
        flops=flops,
        transcendentals=0,
        bytes_accessed=4 * sum(math.prod(s.shape) for s in shapes),
    )

    def run(*args):
        if raw:
            args = [pltpu.with_memory_space_constraint(x, pltpu.HBM) for x in args]
        return pl.pallas_call(
            kernel,
            out_shape=shapes,
            in_specs=[away if raw else vmem] * len(args),
            out_specs=specs,
            scratch_shapes=buffers,
            compiler_params=pltpu.CompilerParams(vmem_limit_bytes=24 << 20),
            cost_estimate=cost,
        )(*args)

    return run


def swap_edges(before_src, after_src, axis):
    peers = lax.axis_size(axis)
    up = [(i, (i + 1) % peers) for i in range(peers)]
    down = [(j, i) for i, j in up]
    return lax.ppermute(before_src, axis, up), lax.ppermute(after_src, axis, down)


def mode_basis(length, modes):
    turns = np.arange(modes)[None, :] * np.arange(length)[:, None] % length
    angle = turns * (2.0 * math.pi / length)
    basis = np.concatenate([np.cos(angle), np.sin(angle)], axis=1).astype(np.float32)
    high = basis.astype(ml_dtypes.bfloat16)
    low = (basis - high.astype(np.float32)).astype(ml_dtypes.bfloat16)
    return np.concatenate([high, low], axis=1)


def two_parts(x):
    x = x.astype(np.float32)
    high = x.astype(ml_dtypes.bfloat16)
    return np.concatenate([high, (x - high.astype(np.float32)).astype(ml_dtypes.bfloat16)], axis=1)


def on_grid(x):
    return np.round(x * 2.0**32) / 2.0**32


def sequences(length, lanes, modes):
    at = np.arange(lanes)
    band = 2.0 * math.pi * (modes - 0.5) / length
    along = ((lanes - 1 - 2.0 * at) / 2.0) ** 2 * math.cos(band)
    beside = at[1:] * (lanes - at[1:]) / 2.0
    matrix = np.diag(along) + np.diag(beside, 1) + np.diag(beside, -1)
    most = np.linalg.eigh(matrix)[1][:, ::-1][:, :SUMS]
    order = np.where(np.arange(SUMS)[None, :] % 2 == 0, 1.0, at[:, None] - (lanes - 1) / 2.0)
    return on_grid(most * np.sign((most * order).sum(axis=0))[None, :])


def block_coefficients(length, lanes, modes, columns):
    turns = np.arange(modes)[None, :] * np.arange(length)[:, None] % length
    angle = turns * (2.0 * math.pi / length)
    wave = np.concatenate([np.cos(angle), np.sin(angle)], axis=1).reshape(-1, lanes, 2 * modes)
    made = on_grid(np.einsum("in,oim->onm", columns, wave, optimize=False))
    rest = wave - np.einsum("in,onm->oim", columns, made, optimize=False)
    return made, np.abs(rest).max()


def joint_basis(basis, lanes):
    length = basis.shape[0]
    tile, lane = np.divmod(np.arange(length // 2), lanes)
    half, c = np.divmod(lane % GROUP, 8)
    column = (lanes * (2 * tile + half + 1) + c - 4) % length
    return np.where(((c >= 2) & (c < 6))[:, None], basis[column], np.zeros_like(basis[column]))


def mode_weights(counts, modes, length):
    order = jnp.arange(modes).astype(jnp.float32)
    keep = (order[None, :] < counts[:, None]).astype(jnp.float32)
    scale = jnp.where(order == 0, 1.0, 2.0) / length
    weights = keep * scale[None, :]
    return jnp.concatenate([weights, weights], axis=1)


def shards(ocean_state, thickness, wet_mask, mode_counts, row_flags):
    levels, rows, lanes = ocean_state.shape[1:]
    assert rows % 8 == 0 and lanes == LANES and levels * GROUP <= LANES
    lon_peers = lax.axis_size("lon")
    lat_peers = lax.axis_size("lat")
    nlat = rows * lat_peers
    nlon = lanes * lon_peers
    full = rows + 8
    total = 4 * levels * rows
    part = total // lon_peers
    lat_pos = lax.axis_index("lat")
    first_row = lat_pos * rows
    cells = 4 * levels * full * lanes
    edge_rows = (6, levels, 2, lanes)

    paired = rows == 2 * lon_peers and rows >= FBAND and lat_peers % 2 == 0 and levels % 2 == 0
    columns = sequences(nlon, lanes, MAXM)
    if paired:
        coefficients, rest = block_coefficients(nlon, lanes, MAXM, columns)
        paired = bool(rest < 1e-8)
    inside = (np.arange(lanes) >= 2) & (np.arange(lanes) < lanes - 2)
    sums = jnp.asarray(np.tile(two_parts(columns * inside[:, None]), (1, PACKED // 2)))
    *block, first, last, flags, counts, table, end_table, joint_table, to_sums = call(
        functools.partial(load_kernel, paired),
        [ocean_state.shape, thickness.shape, thickness.shape, edge_rows, edge_rows]
        + [(rows, lanes)] * 2
        + [(2, full, lanes), (2, 8, lanes), (2, 8, lanes)]
        + [jax.ShapeDtypeStruct(sums.shape, sums.dtype)],
        [pltpu.VMEM(shape, jnp.int32) for shape in (thickness.shape, (1, rows), (1, rows))],
        sems=9,
        raw=True,
    )(ocean_state, thickness, wet_mask, row_flags[None], mode_counts[None], sums)

    def ready():
        return call(
            ready_kernel, [(6, rows, LANES), (5, levels, rows, lanes)], flops=20 * cells
        )(*block, table)

    def exchanged(below, above, own, terms):
        inner, edges, halo = call(
            inner_kernel,
            [(3, 4, levels, full, lanes), (6, full, LANES), (6, levels, 8, lanes)],
            [(5, levels, 8, lanes), (2, levels, full, lanes)],
            flops=60 * cells,
        )(*block, below, above, table, own, terms)
        first, last = call(pack_kernel, [(full, LANES)] * 2)(*block, halo)
        from_west, from_east = swap_edges(last, first, "lon")
        return call(
            edge_kernel,
            [ocean_state.shape] * 2,
            [(4, full, LANES), (7, full, LANES)],
            sems=4,
            sent=True,
        )(inner, edges, from_west, from_east, table)

    banded = (first_row < FBAND) | (first_row + rows > nlat - FBAND)
    modes = mode_basis(nlon, MAXM)
    tables = [modes]
    if paired:
        coefficients = np.concatenate([coefficients] * PACKED, axis=1).reshape(nlon, 2 * MAXM)
        tables = [
            two_parts(coefficients),
            joint_basis(modes, lanes),
            two_parts(np.concatenate([columns.T] * PACKED, axis=0)),
        ]
    tables = lax.optimization_barrier([jnp.asarray(table) for table in tables])
    lon_pos = lax.axis_index("lon")

    def circled(got, own, closed):
        few = 8 * levels // PACKED
        tile = (levels, 8, lanes)
        to_modes, at_joints, to_columns = tables
        state, sent = call(
            end_kernel,
            [ocean_state.shape, (lon_peers, few + 24, lanes)],
            [(2,) + tile, (6,) + tile, (3, 4) + tile, (7,) + tile, (3, full, lanes)]
            + [(total, lanes)],
        )(*block, got, own, closed, end_table, to_sums)
        circles = lax.all_to_all(sent, "lon", 0, 0, tiled=True)
        pieces = call(
            circle_kernel,
            [(lon_peers, few + 8, lanes)],
            [
                (6, 4 * lon_peers, lanes),
                (7, 4 * lon_peers, lanes),
                (4 * lon_peers, lanes),
            ],
        )(circles, joint_table, to_modes, at_joints, counts)[0]
        pieces = lax.all_to_all(pieces, "lon", 0, 0, tiled=True)
        return call(
            join_kernel,
            [ocean_state.shape],
            [ocean_state.shape, (total, lanes)],
            sems=levels // 2,
            sent=True,
        )(state, pieces, block[2], flags, to_columns)[0]

    def between(got, *_):
        pairs = [(i, i + 1) for i in range(1, lat_peers - 1, 2)]
        other = lax.ppermute(last, "lat", pairs + [(j, i) for i, j in pairs])
        even = lat_pos % 2 == 0
        below, above = jnp.where(even, other, got), jnp.where(even, got, other)
        return exchanged(below, above, *ready())[1]

    if paired:
        got = lax.ppermute(first, "lat", [(i, i ^ 1) for i in range(lat_peers)])
        own, closed = call(
            closed_kernel,
            [(3, rows, LANES), (3, 4, levels, rows, lanes)],
            [(7, levels, rows, lanes)],
            flops=60 * cells,
        )(*block, table)
        got, own, closed = lax.optimization_barrier((got, own, closed))
        return lax.cond(banded, circled, between, got, own, closed)

    below, above = swap_edges(last, first, "lat")
    state, sent = exchanged(*lax.optimization_barrier((below, above, *ready())))

    def filtered():
        row_counts = lax.dynamic_slice(
            jnp.broadcast_to(
                mode_counts.astype(jnp.float32)[None], (4 * levels, rows)
            ).reshape(total),
            (lon_pos * part,),
            (part,),
        )
        circles = lax.all_to_all(
            sent.reshape(lon_peers, part, lanes), "lon", 0, 0, tiled=True
        )
        smooth = call(
            filter_kernel, [circles.shape], [circles.shape], sems=lon_peers // 2, sent=True
        )(circles, tables[0], mode_weights(row_counts, MAXM, nlon))[0]
        smooth = lax.all_to_all(smooth, "lon", 0, 0, tiled=True).reshape(state.shape)
        return call(blend_kernel, [state.shape], [state.shape], sems=4, sent=True)(
            state, smooth, block[2], flags
        )[0]

    return lax.cond(banded, filtered, lambda: sent)


def solution(mesh):
    in_specs = (
        P(None, None, "lat", "lon"),
        P(None, "lat", "lon"),
        P(None, "lat", "lon"),
        P("lat"),
        P("lat"),
    )
    out_specs = P(None, None, "lat", "lon")
    return jax.shard_map(shards, mesh=mesh, in_specs=in_specs, out_specs=out_specs, check_vma=False)
```

```python
import functools
import math

import jax
import jax.numpy as jnp
import ml_dtypes
import numpy as np
from jax import lax
from jax.experimental import pallas as pl
from jax.experimental.pallas import tpu as pltpu
from jax.sharding import PartitionSpec as P

FBAND = 16
MAXM = 64
LANES = 128
SUMS = 32
PACKED = LANES // SUMS
GROUP = 16


lat_edge = 1.3
diffusion = 0.05
vertical_mix = 0.5
time_step = 0.05


def roll(x, shift, axis):
    shift %= x.shape[axis]
    return pltpu.roll(x, shift, axis) if shift else x


def east(x):
    return roll(x, -1, 1)


def west(x):
    return roll(x, 1, 1)


def north(x):
    return roll(x, -1, 0)


def south(x):
    return roll(x, 1, 0)


def lane_of(shape):
    return lax.broadcasted_iota(jnp.int32, shape, 1)


def east_terms(h, w, inv_c):
    open_e = 0.5 * (h + east(h)) * (w * east(w))
    return 0.25 * open_e, diffusion * open_e * inv_c


def north_terms(h, w, face):
    open_n = 0.5 * (h + north(h)) * (w * north(w)) * face
    return 0.25 * open_n, diffusion * open_n


def advance(fields, terms, scale, scale_c, vertical):
    quarter_e, spread_e, quarter_n, spread_n = terms
    u, v = fields[2], fields[3]
    speed_e = quarter_e * (u + east(u))
    speed_n = quarter_n * (v + north(v))
    here_e, there_e = speed_e + spread_e, speed_e - spread_e
    here_n, there_n = speed_n + spread_n, speed_n - spread_n
    fresh = []
    for q, vert in zip(fields, vertical):
        flux_e = here_e * q + there_e * east(q)
        flux_n = here_n * q + there_n * north(q)
        spread = (flux_e - west(flux_e)) + (flux_n - south(flux_n))
        fresh.append(q + scale * vert - scale_c * spread)
    return fresh


def own_columns(load, levels, lanes, rows):
    lane = lane_of((rows, LANES))
    own = jnp.zeros((rows, LANES), jnp.float32)
    for k in range(levels):
        x = load(k)
        at = GROUP * k + 2
        own = jnp.where((lane >= at) & (lane < at + 4), roll(x, at, 1), own)
        at = GROUP * k + 8
        own = jnp.where((lane >= at) & (lane < at + 4), roll(x, at + 4 - lanes, 1), own)
    return own


def row_terms(thick, wet, inv_c, levels, term_ref):
    w, h = wet(0), thick(0)
    hs = jnp.where(w > 0, h, 1.0)
    for k in range(levels):
        term_ref[0, k], term_ref[1, k] = east_terms(h, w, inv_c)
        scale = time_step * w / hs
        term_ref[2, k] = scale
        term_ref[3, k] = scale * inv_c
        if k + 1 < levels:
            w_next, h_next = wet(k + 1), thick(k + 1)
            hs_next = jnp.where(w_next > 0, h_next, 1.0)
            term_ref[4, k] = w * w_next * (2.0 * vertical_mix) / (hs + hs_next)
            w, h, hs = w_next, h_next, hs_next


def fill_table(ref, place, nlat):
    place = place.astype(jnp.float32)
    ref[0] = 1.0 / jnp.cos(lat_edge * (2.0 * (place + 0.5) / nlat - 1.0))
    ref[1] = jnp.cos(lat_edge * (2.0 * (place + 1.0) / nlat - 1.0))


def ring_rows(rows):
    place = lax.broadcasted_iota(jnp.int32, (rows + 8, LANES), 0)
    return jnp.where(place < rows + 2, place, jnp.where(place < rows + 6, 0, place - rows - 8))


def load_kernel(
    paired,
    state_any,
    thick_any,
    wet_any,
    flag_any,
    count_any,
    sums_any,
    state_ref,
    thick_ref,
    wet_ref,
    first_ref,
    last_ref,
    flag_ref,
    count_ref,
    table_ref,
    end_table_ref,
    joint_table_ref,
    sums_ref,
    raw_ref,
    raw_flag_ref,
    raw_count_ref,
    sems,
):
    levels, rows = thick_ref.shape[:2]
    moves = [(flag_any, raw_flag_ref), (count_any, raw_count_ref), (wet_any, raw_ref)]
    moves += [(thick_any, thick_ref), (sums_any, sums_ref)]
    moves += [(state_any.at[f], state_ref.at[f]) for f in range(4)]
    copies = [pltpu.make_async_copy(*pair, sems.at[i]) for i, pair in enumerate(moves)]
    for copy in copies:
        copy.start()
    nlat = rows * lax.axis_size("lat")
    lat_pos = lax.axis_index("lat")
    first_row = lat_pos * rows
    fill_table(table_ref, first_row + ring_rows(rows), nlat)
    if paired:
        six = jnp.minimum(lax.broadcasted_iota(jnp.int32, (8, LANES), 0), 5)
        end = jnp.where(lat_pos == 0, rows - 4, -2)
        fill_table(end_table_ref, first_row + end + six, nlat)
        fill_table(joint_table_ref, first_row + 2 * lax.axis_index("lon") - 2 + six, nlat)
    for copy in copies[:3]:
        copy.wait()
    shape = (rows, rows)
    diagonal = lax.broadcasted_iota(jnp.int32, shape, 0) == lane_of(shape)
    for raw, ref in ((raw_flag_ref, flag_ref), (raw_count_ref, count_ref)):
        spread = jnp.broadcast_to(raw[...].astype(jnp.float32), shape)
        value = jnp.sum(jnp.where(diagonal, spread, 0.0), axis=1, keepdims=True)
        ref[...] = jnp.broadcast_to(value, (rows, LANES))
    for k in range(levels):
        wet_ref[k] = raw_ref[k].astype(jnp.float32)
    even = lax.axis_index("lat") % 2 == 0
    copies[3].wait()
    copies[4].wait()
    for f in (4, 5, 0, 1, 2, 3):
        if f < 4:
            copies[5 + f].wait()
        for k in range(levels):
            x = state_ref.at[f, k] if f < 4 else (thick_ref, wet_ref)[f - 4].at[k]
            low, high = x[0:2], x[rows - 2 : rows]
            if paired:
                low, high = jnp.where(even, high, low), jnp.where(even, low, high)
            first_ref[f, k] = low
            last_ref[f, k] = high


def ready_kernel(state_ref, thick_ref, wet_ref, table_ref, own_ref, term_ref):
    levels, rows, lanes = thick_ref.shape

    def thick(k):
        return thick_ref[k]

    def wet(k):
        return wet_ref[k]

    for f in range(4):
        own_ref[f] = own_columns(lambda k, f=f: state_ref[f, k], levels, lanes, rows)
    own_ref[4] = own_columns(thick, levels, lanes, rows)
    own_ref[5] = own_columns(wet, levels, lanes, rows)
    row_terms(thick, wet, table_ref[0, :rows], levels, term_ref)


def pack_kernel(state_ref, thick_ref, wet_ref, halo_ref, first_ref, last_ref):
    levels, rows, lanes = thick_ref.shape
    lane = lane_of((8, LANES))
    for t in range(rows // 8 + 1):
        first = jnp.zeros((8, LANES), jnp.float32)
        last = jnp.zeros((8, LANES), jnp.float32)
        part = slice(8 * t, 8 * t + 8)
        for f in range(6):
            for k in range(levels):
                if t == rows // 8:
                    x = halo_ref[f, k]
                elif f < 4:
                    x = state_ref[f, k, part]
                elif f == 4:
                    x = thick_ref[k, part]
                else:
                    x = wet_ref[k, part]
                at = GROUP * f + 2 * k
                mine = (lane >= at) & (lane < at + 2)
                first = jnp.where(mine, roll(x, at, 1), first)
                last = jnp.where(mine, roll(x, at + 2 - lanes, 1), last)
        first_ref[part] = first
        last_ref[part] = last


def inner_kernel(
    state_ref,
    thick_ref,
    wet_ref,
    below_ref,
    above_ref,
    table_ref,
    own_ref,
    term_ref,
    out_ref,
    edge_ref,
    halo_ref,
    halo_term_ref,
    north_ref,
):
    levels, rows, lanes = thick_ref.shape
    full = rows + 8
    face = table_ref[1]
    lat_pos = lax.axis_index("lat")
    with_below = jnp.where(lat_pos > 0, 1.0, 0.0)
    with_above = jnp.where(lat_pos < lax.axis_size("lat") - 1, 1.0, 0.0)
    for f in range(6):
        for k in range(levels):
            halo_ref[f, k, 0:2] = above_ref[f, k] * with_above
            halo_ref[f, k, 2:6] = jnp.zeros((4, lanes), jnp.float32)
            halo_ref[f, k, 6:8] = below_ref[f, k] * with_below

    def joined(x, y):
        return jnp.concatenate([x, y], axis=0)

    def halo(f):
        return lambda k: halo_ref[f, k]

    for f in range(6):
        edge_ref[f, :rows] = own_ref[f]
        edge_ref[f, rows:] = own_columns(halo(f), levels, lanes, 8)
    row_terms(halo(4), halo(5), table_ref[0, rows:], levels, halo_term_ref)
    for k in range(levels):
        h = joined(thick_ref[k], halo_ref[4, k])
        w = joined(wet_ref[k], halo_ref[5, k])
        north_ref[0, k], north_ref[1, k] = north_terms(h, w, face)
        for f in range(4):
            out_ref[0, f, k] = joined(state_ref[f, k], halo_ref[f, k])

    def term(i, k):
        return joined(term_ref[i, k], halo_term_ref[i, k])

    def step(i, _):
        source, target = out_ref.at[i], out_ref.at[i + 1]
        fields = [source[f, 0] for f in range(4)]
        above = [jnp.zeros((full, LANES), jnp.float32)] * 4
        for k in range(levels):
            deeper = below = above
            if k + 1 < levels:
                couple = term(4, k)
                deeper = [source[f, k + 1] for f in range(4)]
                below = [couple * (d - q) for d, q in zip(deeper, fields)]
                vertical = [b - a for b, a in zip(below, above)]
            else:
                vertical = [-a for a in above]
            terms = term(0, k), term(1, k), north_ref[0, k], north_ref[1, k]
            fresh = advance(fields, terms, term(2, k), term(3, k), vertical)
            for f in range(4):
                target[f, k] = fresh[f]
            fields, above = deeper, below
        return 0

    lax.fori_loop(0, 2, step, 0)


def step_tile(tile_ref, h, w, levels, inv_c, face, term_ref):
    lane = lane_of(h.shape)

    def deeper(x):
        return roll(x, -GROUP, 1)

    def shallower(x):
        return roll(x, GROUP, 1)

    hs = jnp.where(w > 0, h, 1.0)
    scale = time_step * w / hs
    couple = w * deeper(w) * (2.0 * vertical_mix) / (hs + deeper(hs))
    couple = jnp.where(lane < GROUP * (levels - 1), couple, 0.0)
    terms = east_terms(h, w, inv_c) + north_terms(h, w, face)
    for i, term in enumerate(terms + (scale, scale * inv_c, couple)):
        term_ref[i] = term

    def step():
        terms = [term_ref[i] for i in range(7)]
        fields = [tile_ref[f] for f in range(4)]
        vertical = []
        for q in fields:
            down = terms[6] * (deeper(q) - q)
            vertical.append(down - shallower(down))
        for f, q in enumerate(advance(fields, terms[:4], terms[4], terms[5], vertical)):
            tile_ref[f] = q

    step()
    step()


def edge_kernel(
    inner_ref, own_ref, west_ref, east_ref, table_ref, out_ref, send_ref, tile_ref, term_ref, sems
):
    levels, rows, lanes = out_ref.shape[1:]
    full = rows + 8
    lane = lane_of((full, LANES))
    from_west, from_east = west_ref[...], east_ref[...]

    def joined(f):
        x = own_ref[f]
        for k in range(levels):
            src = GROUP * f + 2 * k
            at = GROUP * k
            x = jnp.where((lane >= at) & (lane < at + 2), roll(from_west, at - src, 1), x)
            at = GROUP * k + 12
            x = jnp.where((lane >= at) & (lane < at + 2), roll(from_east, at - src, 1), x)
        return x

    for f in range(4):
        tile_ref[f] = joined(f)
    step_tile(tile_ref, joined(4), joined(5), levels, table_ref[0], table_ref[1], term_ref)
    lane = lane_of((rows, LANES))
    for f in range(4):
        x = tile_ref[f, :rows]
        for k in range(levels):
            left = roll(x, -(GROUP * k + 2), 1)
            right = roll(x, lanes - 2 - (GROUP * k + 10), 1)
            out_ref[f, k] = jnp.where(
                lane < 2,
                left,
                jnp.where(lane >= lanes - 2, right, inner_ref[2, f, k, :rows]),
            )
        pltpu.make_async_copy(out_ref.at[f], send_ref.at[f], sems.at[f]).start()
    for f in range(4):
        pltpu.make_async_copy(out_ref.at[f], send_ref.at[f], sems.at[f]).wait()


def split(x):
    high = x.astype(jnp.bfloat16)
    return high, (x - high.astype(jnp.float32)).astype(jnp.bfloat16)


def product(a, b, dims):
    return lax.dot_general(a, b, (dims, ((), ())), preferred_element_type=jnp.float32)


def unpack(x):
    part = lane_of(x.shape) // SUMS
    return jnp.concatenate([jnp.where(part == g, x, 0.0) for g in range(PACKED)], axis=0)


def pack(x):
    size = x.shape[0] // PACKED
    made = x[:size]
    part = lane_of(made.shape) // SUMS
    for g in range(1, PACKED):
        made = jnp.where(part == g, x[size * g : size * (g + 1)], made)
    return made


def pairs_of_rows(tiles, t, place):
    sub = lax.broadcasted_iota(jnp.int32, tiles[0].shape, 0) // 2
    for y in range(4):
        made = roll(tiles[0], -2 * y, 0)
        for x in range(1, 4):
            made = jnp.where(sub == x, roll(tiles[x], 2 * (x - y), 0), made)
        place(y, made)


def side_by_side(a, b):
    c = lane_of(a.shape) % GROUP
    one = jnp.where(c < 4, roll(a, -2, 1), roll(a, -4, 1))
    two = jnp.where(c < 12, roll(b, 6, 1), roll(b, 4, 1))
    return jnp.where(c < 8, one, two)


def step_levels(buf_ref, term_ref, loop):
    levels, size = buf_ref.shape[2:4]

    def step(i, _):
        source, target = buf_ref.at[i], buf_ref.at[i + 1]
        fields = [source[f, 0] for f in range(4)]
        above = [jnp.zeros((size, LANES), jnp.float32)] * 4
        for k in range(levels):
            deeper = below = above
            if k + 1 < levels:
                couple = term_ref[4, k]
                deeper = [source[f, k + 1] for f in range(4)]
                below = [couple * (d - q) for d, q in zip(deeper, fields)]
                vertical = [b - a for b, a in zip(below, above)]
            else:
                vertical = [-a for a in above]
            terms = [term_ref[i, k] for i in (0, 1, 5, 6)]
            fresh = advance(fields, terms, term_ref[2, k], term_ref[3, k], vertical)
            for f in range(4):
                target[f, k] = fresh[f]
            fields, above = deeper, below
        return 0

    if loop:
        lax.fori_loop(0, 2, step, 0)
    else:
        step(1, step(0, 0))


def closed_kernel(state_ref, thick_ref, wet_ref, table_ref, own_ref, buf_ref, term_ref):
    levels, rows, lanes = thick_ref.shape

    def thick(k):
        return thick_ref[k]

    def wet(k):
        return wet_ref[k]

    tiles = [
        own_columns(lambda k, f=f: state_ref[f, k], levels, lanes, rows) for f in range(4)
    ]
    tiles += [own_columns(load, levels, lanes, rows) for load in (thick, wet)]
    for i in range(3):
        own_ref[i] = side_by_side(tiles[2 * i], tiles[2 * i + 1])
    row_terms(thick, wet, table_ref[0, :rows], levels, term_ref)
    row = lax.broadcasted_iota(jnp.int32, (rows, LANES), 0)
    face = jnp.where(row < rows - 1, table_ref[1, :rows], 0.0)
    for k in range(levels):
        term_ref[5, k], term_ref[6, k] = north_terms(thick(k), wet(k), face)
        for f in range(4):
            buf_ref[0, f, k] = state_ref[f, k]
    step_levels(buf_ref, term_ref, True)


def end_kernel(
    state_ref,
    thick_ref,
    wet_ref,
    got_ref,
    own_ref,
    closed_ref,
    table_ref,
    sums_ref,
    out_ref,
    send_ref,
    field_ref,
    halo_ref,
    buf_ref,
    term_ref,
    raw_ref,
    main_ref,
):
    levels, rows, lanes = thick_ref.shape
    full = rows + 8
    top = lax.axis_index("lat") == 0
    at_top = jnp.where(top, 1.0, 0.0)
    at_bottom = jnp.where(top, 0.0, 1.0)
    sub = lax.broadcasted_iota(jnp.int32, (8, LANES), 0)

    def own(f, k, part):
        return state_ref[f, k, part] if f < 4 else (thick_ref, wet_ref)[f - 4][k, part]

    for f in range(6):
        for k in range(levels):
            halo_ref[f, k, 0:2] = got_ref[f, k] * at_top
            halo_ref[f, k, 2:6] = jnp.zeros((4, lanes), jnp.float32)
            halo_ref[f, k, 6:8] = got_ref[f, k] * at_bottom
    for f in range(6):
        for k in range(levels):
            halo = halo_ref[f, k]
            past = jnp.where(sub < 6, roll(halo, 4, 0), 0.0)
            high = jnp.where(sub < 4, roll(own(f, k, slice(rows - 8, rows)), -4, 0), past)
            low = jnp.where(sub < 2, roll(halo, 2, 0), roll(own(f, k, slice(0, 8)), 2, 0))
            tile = jnp.where(top, high, low)
            if f < 4:
                buf_ref[0, f, k] = tile
            else:
                field_ref[f - 4, k] = tile

    def thick(k):
        return field_ref[0, k]

    def wet(k):
        return field_ref[1, k]

    row_terms(thick, wet, table_ref[0], levels, term_ref)
    for k in range(levels):
        term_ref[5, k], term_ref[6, k] = north_terms(thick(k), wet(k), table_ref[1])
    step_levels(buf_ref, term_ref, False)

    def beyond(f):
        return own_columns(lambda k: halo_ref[f, k], levels, lanes, 8)

    for i in range(3):
        outer = side_by_side(beyond(2 * i), beyond(2 * i + 1))
        raw_ref[i, 0:2] = outer[6:8]
        raw_ref[i, 2 : rows + 2] = own_ref[i]
        raw_ref[i, rows + 2 : full] = outer[0:6]
    main = 8 * levels
    few = main // PACKED
    last = rows // 8 - 1
    for t in range(rows // 8):
        part = slice(8 * t, 8 * t + 8)
        for k in range(levels):
            tiles = []
            for f in range(4):
                x = closed_ref[2, f, k, part]
                if t == last:
                    fixed = jnp.where(sub >= 6, roll(buf_ref[2, f, k], 4, 0), x)
                    x = jnp.where(top, fixed, x)
                if t == 0:
                    fixed = jnp.where(sub < 2, roll(buf_ref[2, f, k], -2, 0), x)
                    x = jnp.where(top, x, fixed)
                out_ref[f, k, part] = x
                tiles.append(x)

            def place(y, tile, t=t, k=k):
                at = main * (4 * t + y) + 8 * k
                main_ref[at : at + 8] = tile

            pairs_of_rows(tiles, t, place)
        for p in range(4 * t, 4 * t + 4):
            for i in range(3):
                send_ref[p, few + 8 * i : few + 8 * i + 8] = raw_ref[i, 2 * p : 2 * p + 8]
    x = jnp.concatenate(split(main_ref[...]), axis=1)
    x = product(x, jnp.concatenate([sums_ref[...]] * 2, axis=0), ((1,), (0,)))
    x = x + roll(x, SUMS, 1)
    for p in range(send_ref.shape[0]):
        send_ref[p, :few] = pack(x[main * p : main * (p + 1)])


def circle_kernel(
    circle_ref,
    table_ref,
    basis_ref,
    joint_basis_ref,
    count_ref,
    out_ref,
    tile_ref,
    term_ref,
    joint_ref,
):
    peers = circle_ref.shape[0]
    modes = basis_ref.shape[1] // 2
    length = basis_ref.shape[0]
    few = circle_ref.shape[1] - 24
    main = PACKED * few
    levels = main // 8
    lanes = LANES
    lane = lane_of((8, LANES))
    c = lane % GROUP
    for j in range(0, peers, 2):
        part = slice(4 * j, 4 * j + 8)
        for i in range(3):
            x, y, z = (
                circle_ref[(j + d) % peers, few + 8 * i : few + 8 * i + 8] for d in range(3)
            )
            for f, shift in ((2 * i, 0), (2 * i + 1, -8)):
                middle = jnp.where(c < 12, roll(y, 4 + shift, 1), roll(z, 12 + shift, 1))
                tile_ref[f, part] = jnp.where(c < 4, roll(x, shift - 4, 1), middle)
    inv_c, face = (jnp.concatenate([table_ref[i]] * (peers // 2), axis=0) for i in (0, 1))
    step_tile(tile_ref, tile_ref[4], tile_ref[5], levels, inv_c, face, term_ref)
    sub = lax.broadcasted_iota(jnp.int32, (8, LANES), 0) // 2
    right = (c % 8 >= 2) & (c % 8 < 6)
    for j in range(peers // 2):
        made = jnp.zeros((8, LANES), jnp.float32)
        for f in range(4):
            x = tile_ref[f, 8 * j : 8 * j + 8]
            made = jnp.where(sub == f, roll(x, 2 * f - 2, 0), made)
        joint_ref[8 * j : 8 * j + 8] = jnp.where(right, made, 0.0)
    lane_main = lane_of((main, LANES))
    row_main = lax.broadcasted_iota(jnp.int32, (main, LANES), 0)
    at_level = lane_main // GROUP == row_main // 8

    def block(o):
        return unpack(circle_ref[o, :few])

    def joint(j):
        x = joint_ref[8 * j : 8 * j + 8]
        return jnp.where(at_level, jnp.concatenate([x] * levels, axis=0), 0.0)

    total = jnp.zeros((2 * main, 2 * modes), jnp.float32)
    for source, basis, count in (
        (block, basis_ref, peers),
        (joint, joint_basis_ref, peers // 2),
    ):
        for o in range(0, count, 2):
            parts = zip(split(source(o)), split(source(o + 1)))
            x = jnp.concatenate([jnp.concatenate(p, axis=1) for p in parts], axis=0)
            total = total + product(x, basis[lanes * o : lanes * (o + 2)], ((1,), (0,)))
    total = total[:main] + total[main:]
    counts = count_ref[...]
    row = lax.broadcasted_iota(jnp.int32, counts.shape, 0)
    own = 2 * lax.axis_index("lon")
    even, odd = (
        jnp.sum(jnp.where(row == own + r, counts, 0.0), axis=0, keepdims=True) for r in (0, 1)
    )
    limit = jnp.where(row_main % 2 == 0, even, odd)
    order = (lane_main % (modes // 2)).astype(jnp.float32)
    weight = jnp.where(order < limit, jnp.where(order == 0.0, 1.0 / length, 2.0 / length), 0.0)
    total = (total[:, :modes] + total[:, modes:]) * weight
    y = jnp.concatenate([jnp.concatenate([p, p], axis=1) for p in split(total)], axis=0)
    for o in range(0, peers, 2):
        x = product(y, basis_ref[lanes * o : lanes * (o + 2)], ((1,), (1,)))
        x = x[:main] + x[main:]
        out_ref[o, :few] = pack(x[:, :lanes])
        out_ref[o + 1, :few] = pack(x[:, lanes:])
        before = (4 * o - 8) % (4 * peers)
        here = joint_ref[4 * o : 4 * o + 8]
        out_ref[o, few:] = jnp.where(
            c < 8, roll(joint_ref[before : before + 8], -8, 1), roll(here, 8, 1)
        )
        out_ref[o + 1, few:] = here


def join_kernel(
    state_ref, piece_ref, wet_ref, flag_ref, columns_ref, out_ref, made_ref, smooth_ref, sems
):
    levels, rows, lanes = wet_ref.shape
    main = 8 * levels
    few = main // PACKED
    lane = lane_of((8, LANES))
    x = jnp.concatenate(
        [unpack(piece_ref[p, :few]) for p in range(piece_ref.shape[0])], axis=0
    )
    x = jnp.concatenate(split(x), axis=1)
    x = product(x, jnp.concatenate([columns_ref[...]] * 2, axis=0), ((1,), (0,)))
    smooth_ref[...] = x[:, :lanes] + x[:, lanes:]
    edges = [{} for _ in range(rows // 8)]
    for t, into in enumerate(edges):
        tiles = [piece_ref[4 * t + x, few : few + 8] for x in range(4)]
        pairs_of_rows(tiles, t, into.__setitem__)
    copies = []
    for k in range(levels):
        for t in range(rows // 8):
            part = slice(8 * t, 8 * t + 8)
            starts = [main * (4 * t + x) + 8 * k for x in range(4)]
            tiles = [smooth_ref[at : at + 8] for at in starts]
            gate = flag_ref[part] * wet_ref[k, part]

            def place(f, smooth, k=k, gate=gate, part=part, edge=edges[t]):
                first = roll(edge[f], -(GROUP * k + 4), 1)
                last = roll(edge[f], lanes - 2 - (GROUP * k + 10), 1)
                state = jnp.where(
                    lane < 2, first, jnp.where(lane >= lanes - 2, last, state_ref[f, k, part])
                )
                made_ref[f, k, part] = state + gate * (smooth - state)

            pairs_of_rows(tiles, t, place)
        if k % 2:
            both = pl.ds(k - 1, 2)
            copies.append(
                pltpu.make_async_copy(
                    made_ref.at[:, both], out_ref.at[:, both], sems.at[k // 2]
                )
            )
            copies[-1].start()
    for copy in copies:
        copy.wait()


def filter_kernel(circle_ref, basis_ref, weight_ref, out_ref, piece_ref, sems):
    pieces, part, lanes = circle_ref.shape
    modes = weight_ref.shape[1]
    pairs = range(0, pieces, 2)
    total = jnp.zeros((2 * part, 2 * modes), jnp.float32)
    for o in pairs:
        parts = zip(split(circle_ref[o]), split(circle_ref[o + 1]))
        x = jnp.concatenate([jnp.concatenate(p, axis=1) for p in parts], axis=0)
        total = total + product(x, basis_ref[lanes * o : lanes * (o + 2)], ((1,), (0,)))
    total = total[:part] + total[part:]
    total = (total[:, :modes] + total[:, modes:]) * weight_ref[...]
    y = jnp.concatenate([jnp.concatenate([p, p], axis=1) for p in split(total)], axis=0)
    copies = []
    for o in pairs:
        x = product(y, basis_ref[lanes * o : lanes * (o + 2)], ((1,), (1,)))
        x = x[:part] + x[part:]
        piece_ref[o] = x[:, :lanes]
        piece_ref[o + 1] = x[:, lanes:]
        both = pl.ds(o, 2)
        copies.append(
            pltpu.make_async_copy(piece_ref.at[both], out_ref.at[both], sems.at[o // 2])
        )
        copies[-1].start()
    for copy in copies:
        copy.wait()


def blend_kernel(state_ref, smooth_ref, wet_ref, flag_ref, out_ref, piece_ref, sems):
    levels = wet_ref.shape[0]
    flag = flag_ref[...]
    copies = []
    for f in range(4):
        for k in range(levels):
            state = state_ref[f, k]
            gate = flag * wet_ref[k]
            piece_ref[f, k] = state + gate * (smooth_ref[f, k] - state)
        copies.append(pltpu.make_async_copy(piece_ref.at[f], out_ref.at[f], sems.at[f]))
        copies[-1].start()
    for copy in copies:
        copy.wait()


def call(kernel, outs, scratch=(), sems=0, raw=False, sent=False, flops=0):
    vmem = pl.BlockSpec(memory_space=pltpu.VMEM)
    away = pl.BlockSpec(memory_space=pl.ANY)
    specs = [vmem] * len(outs)
    shapes = [jax.ShapeDtypeStruct(s, jnp.float32) if isinstance(s, tuple) else s for s in outs]
    if sent:
        specs[-1] = away
        shapes[-1] = pltpu.HBM(outs[-1], jnp.float32)
    buffers = [pltpu.VMEM(s, jnp.float32) if isinstance(s, tuple) else s for s in scratch]
    if sems:
        buffers.append(pltpu.SemaphoreType.DMA((sems,)))
    cost = pl.CostEstimate(
        flops=flops,
        transcendentals=0,
        bytes_accessed=4 * sum(math.prod(s.shape) for s in shapes),
    )

    def run(*args):
        if raw:
            args = [pltpu.with_memory_space_constraint(x, pltpu.HBM) for x in args]
        return pl.pallas_call(
            kernel,
            out_shape=shapes,
            in_specs=[away if raw else vmem] * len(args),
            out_specs=specs,
            scratch_shapes=buffers,
            compiler_params=pltpu.CompilerParams(vmem_limit_bytes=24 << 20),
            cost_estimate=cost,
        )(*args)

    return run


def swap_edges(before_src, after_src, axis):
    peers = lax.axis_size(axis)
    up = [(i, (i + 1) % peers) for i in range(peers)]
    down = [(j, i) for i, j in up]
    return lax.ppermute(before_src, axis, up), lax.ppermute(after_src, axis, down)


def mode_basis(length, modes):
    turns = np.arange(modes)[None, :] * np.arange(length)[:, None] % length
    angle = turns * (2.0 * math.pi / length)
    basis = np.concatenate([np.cos(angle), np.sin(angle)], axis=1).astype(np.float32)
    high = basis.astype(ml_dtypes.bfloat16)
    low = (basis - high.astype(np.float32)).astype(ml_dtypes.bfloat16)
    return np.concatenate([high, low], axis=1)


def two_parts(x):
    x = x.astype(np.float32)
    high = x.astype(ml_dtypes.bfloat16)
    return np.concatenate([high, (x - high.astype(np.float32)).astype(ml_dtypes.bfloat16)], axis=1)


def on_grid(x):
    return np.round(x * 2.0**32) / 2.0**32


def sequences(length, lanes, modes):
    at = np.arange(lanes)
    band = 2.0 * math.pi * (modes - 0.5) / length
    along = ((lanes - 1 - 2.0 * at) / 2.0) ** 2 * math.cos(band)
    beside = at[1:] * (lanes - at[1:]) / 2.0
    matrix = np.diag(along) + np.diag(beside, 1) + np.diag(beside, -1)
    most = np.linalg.eigh(matrix)[1][:, ::-1][:, :SUMS]
    order = np.where(np.arange(SUMS)[None, :] % 2 == 0, 1.0, at[:, None] - (lanes - 1) / 2.0)
    return on_grid(most * np.sign((most * order).sum(axis=0))[None, :])


def block_coefficients(length, lanes, modes, columns):
    turns = np.arange(modes)[None, :] * np.arange(length)[:, None] % length
    angle = turns * (2.0 * math.pi / length)
    wave = np.concatenate([np.cos(angle), np.sin(angle)], axis=1).reshape(-1, lanes, 2 * modes)
    made = on_grid(np.einsum("in,oim->onm", columns, wave, optimize=False))
    rest = wave - np.einsum("in,onm->oim", columns, made, optimize=False)
    return made, np.abs(rest).max()


def joint_basis(basis, lanes):
    length = basis.shape[0]
    tile, lane = np.divmod(np.arange(length // 2), lanes)
    half, c = np.divmod(lane % GROUP, 8)
    column = (lanes * (2 * tile + half + 1) + c - 4) % length
    return np.where(((c >= 2) & (c < 6))[:, None], basis[column], np.zeros_like(basis[column]))


def mode_weights(counts, modes, length):
    order = jnp.arange(modes).astype(jnp.float32)
    keep = (order[None, :] < counts[:, None]).astype(jnp.float32)
    scale = jnp.where(order == 0, 1.0, 2.0) / length
    weights = keep * scale[None, :]
    return jnp.concatenate([weights, weights], axis=1)


def shards(ocean_state, thickness, wet_mask, mode_counts, row_flags):
    levels, rows, lanes = ocean_state.shape[1:]
    assert rows % 8 == 0 and lanes == LANES and levels * GROUP <= LANES
    lon_peers = lax.axis_size("lon")
    lat_peers = lax.axis_size("lat")
    nlat = rows * lat_peers
    nlon = lanes * lon_peers
    full = rows + 8
    total = 4 * levels * rows
    part = total // lon_peers
    lat_pos = lax.axis_index("lat")
    first_row = lat_pos * rows
    cells = 4 * levels * full * lanes
    edge_rows = (6, levels, 2, lanes)

    paired = rows == 2 * lon_peers and rows >= FBAND and lat_peers % 2 == 0 and levels % 2 == 0
    columns = sequences(nlon, lanes, MAXM)
    if paired:
        coefficients, rest = block_coefficients(nlon, lanes, MAXM, columns)
        paired = bool(rest < 1e-8)
    inside = (np.arange(lanes) >= 2) & (np.arange(lanes) < lanes - 2)
    sums = jnp.asarray(np.tile(two_parts(columns * inside[:, None]), (1, PACKED // 2)))
    *block, first, last, flags, counts, table, end_table, joint_table, to_sums = call(
        functools.partial(load_kernel, paired),
        [ocean_state.shape, thickness.shape, thickness.shape, edge_rows, edge_rows]
        + [(rows, lanes)] * 2
        + [(2, full, lanes), (2, 8, lanes), (2, 8, lanes)]
        + [jax.ShapeDtypeStruct(sums.shape, sums.dtype)],
        [pltpu.VMEM(shape, jnp.int32) for shape in (thickness.shape, (1, rows), (1, rows))],
        sems=9,
        raw=True,
    )(ocean_state, thickness, wet_mask, row_flags[None], mode_counts[None], sums)

    def ready():
        return call(
            ready_kernel, [(6, rows, LANES), (5, levels, rows, lanes)], flops=20 * cells
        )(*block, table)

    def exchanged(below, above, own, terms):
        inner, edges, halo = call(
            inner_kernel,
            [(3, 4, levels, full, lanes), (6, full, LANES), (6, levels, 8, lanes)],
            [(5, levels, 8, lanes), (2, levels, full, lanes)],
            flops=60 * cells,
        )(*block, below, above, table, own, terms)
        first, last = call(pack_kernel, [(full, LANES)] * 2)(*block, halo)
        from_west, from_east = swap_edges(last, first, "lon")
        return call(
            edge_kernel,
            [ocean_state.shape] * 2,
            [(4, full, LANES), (7, full, LANES)],
            sems=4,
            sent=True,
        )(inner, edges, from_west, from_east, table)

    banded = (first_row < FBAND) | (first_row + rows > nlat - FBAND)
    modes = mode_basis(nlon, MAXM)
    tables = [modes]
    if paired:
        coefficients = np.concatenate([coefficients] * PACKED, axis=1).reshape(nlon, 2 * MAXM)
        tables = [
            two_parts(coefficients),
            joint_basis(modes, lanes),
            two_parts(np.concatenate([columns.T] * PACKED, axis=0)),
        ]
    tables = lax.optimization_barrier([jnp.asarray(table) for table in tables])
    lon_pos = lax.axis_index("lon")

    def circled(got, own, closed):
        few = 8 * levels // PACKED
        tile = (levels, 8, lanes)
        to_modes, at_joints, to_columns = tables
        state, sent = call(
            end_kernel,
            [ocean_state.shape, (lon_peers, few + 24, lanes)],
            [(2,) + tile, (6,) + tile, (3, 4) + tile, (7,) + tile, (3, full, lanes)]
            + [(total, lanes)],
        )(*block, got, own, closed, end_table, to_sums)
        circles = lax.all_to_all(sent, "lon", 0, 0, tiled=True)
        pieces = call(
            circle_kernel,
            [(lon_peers, few + 8, lanes)],
            [
                (6, 4 * lon_peers, lanes),
                (7, 4 * lon_peers, lanes),
                (4 * lon_peers, lanes),
            ],
        )(circles, joint_table, to_modes, at_joints, counts)[0]
        pieces = lax.all_to_all(pieces, "lon", 0, 0, tiled=True)
        return call(
            join_kernel,
            [ocean_state.shape],
            [ocean_state.shape, (total, lanes)],
            sems=levels // 2,
            sent=True,
        )(state, pieces, block[2], flags, to_columns)[0]

    def between(got, *_):
        pairs = [(i, i + 1) for i in range(1, lat_peers - 1, 2)]
        other = lax.ppermute(last, "lat", pairs + [(j, i) for i, j in pairs])
        even = lat_pos % 2 == 0
        below, above = jnp.where(even, other, got), jnp.where(even, got, other)
        return exchanged(below, above, *ready())[1]

    if paired:
        got = lax.ppermute(first, "lat", [(i, i ^ 1) for i in range(lat_peers)])
        own, closed = call(
            closed_kernel,
            [(3, rows, LANES), (3, 4, levels, rows, lanes)],
            [(7, levels, rows, lanes)],
            flops=60 * cells,
        )(*block, table)
        got, own, closed = lax.optimization_barrier((got, own, closed))
        return lax.cond(banded, circled, between, got, own, closed)

    below, above = swap_edges(last, first, "lat")
    state, sent = exchanged(*lax.optimization_barrier((below, above, *ready())))

    def filtered():
        row_counts = lax.dynamic_slice(
            jnp.broadcast_to(
                mode_counts.astype(jnp.float32)[None], (4 * levels, rows)
            ).reshape(total),
            (lon_pos * part,),
            (part,),
        )
        circles = lax.all_to_all(
            sent.reshape(lon_peers, part, lanes), "lon", 0, 0, tiled=True
        )
        smooth = call(
            filter_kernel, [circles.shape], [circles.shape], sems=lon_peers // 2, sent=True
        )(circles, tables[0], mode_weights(row_counts, MAXM, nlon))[0]
        smooth = lax.all_to_all(smooth, "lon", 0, 0, tiled=True).reshape(state.shape)
        return call(blend_kernel, [state.shape], [state.shape], sems=4, sent=True)(
            state, smooth, block[2], flags
        )[0]

    return lax.cond(banded, filtered, lambda: sent)


def solution(mesh):
    in_specs = (
        P(None, None, "lat", "lon"),
        P(None, "lat", "lon"),
        P(None, "lat", "lon"),
        P("lat"),
        P("lat"),
    )
    out_specs = P(None, None, "lat", "lon")
    return jax.shard_map(shards, mesh=mesh, in_specs=in_specs, out_specs=out_specs, check_vma=False)
```
